32 devices in a mesh: dp: 2 (over y), fsdp: 16 (over z, x, core).
Axes of the slice: x: 2, y: 2, z: 4, core: 2. Of those that a mesh axis runs over, the one named last changes fastest.
Arguments:
- tokens: bfloat16 [32768, 768], P(('dp', 'fsdp')), may hold values from -6 to 6
- image_counts: int32 [32, 2], P(('dp', 'fsdp')), may hold values from 0 to 5, as said below
- cotangent: bfloat16 [32768, 768], P(('dp', 'fsdp')), may hold values from -6 to 6
- first_gain: bfloat16 [768], P('fsdp'), may hold values from 0.5 to 1.5
- first_shift: bfloat16 [768], P('fsdp'), may hold values from -3 to 3
- query_weight: bfloat16 [768, 768], P('fsdp'), may hold values from -0.21875 to 0.21875
- query_bias: bfloat16 [768], P('fsdp'), may hold values from -3 to 3
- key_weight: bfloat16 [768, 768], P('fsdp'), may hold values from -0.21875 to 0.21875
- value_weight: bfloat16 [768, 768], P('fsdp'), may hold values from -0.21875 to 0.21875
- value_bias: bfloat16 [768], P('fsdp'), may hold values from -3 to 3
- out_weight: bfloat16 [768, 768], P('fsdp'), may hold values from -0.625 to 0.625
- out_bias: bfloat16 [768], P('fsdp'), may hold values from -3 to 3
- second_gain: bfloat16 [768], P('fsdp'), may hold values from 0.5 to 1.5
- second_shift: bfloat16 [768], P('fsdp'), may hold values from -3 to 3
- up_weight: bfloat16 [768, 3072], P('fsdp'), may hold values from -0.21875 to 0.21875
- up_bias: bfloat16 [3072], P('fsdp'), may hold values from -3 to 3
- down_weight: bfloat16 [3072, 768], P('fsdp'), may hold values from -0.109375 to 0.109375
- down_bias: bfloat16 [768], P('fsdp'), may hold values from -3 to 3
Outputs:
- layer_out: bfloat16 [32768, 768], P(('dp', 'fsdp'))
- grad_tokens: float32 [32768, 768], P(('dp', 'fsdp'))
- grad_first_gain: float32 [768], P('fsdp')
- grad_first_shift: float32 [768], P('fsdp')
- grad_query_weight: float32 [768, 768], P('fsdp')
- grad_query_bias: float32 [768], P('fsdp')
- grad_key_weight: float32 [768, 768], P('fsdp')
- grad_value_weight: float32 [768, 768], P('fsdp')
- grad_value_bias: float32 [768], P('fsdp')
- grad_out_weight: float32 [768, 768], P('fsdp')
- grad_out_bias: float32 [768], P('fsdp')
- grad_second_gain: float32 [768], P('fsdp')
- grad_second_shift: float32 [768], P('fsdp')
- grad_up_weight: float32 [768, 3072], P('fsdp')
- grad_up_bias: float32 [3072], P('fsdp')
- grad_down_weight: float32 [3072, 768], P('fsdp')
- grad_down_bias: float32 [768], P('fsdp')
The draws below stay inside these ranges and needn't reach their ends.
Inputs may be any that keep to these rules, and one draw needn't show every extreme that they name: `image_counts`: row b holds s, the count of 197-row images, and l, the count of 325-row images, of the b-th block of 1024 rows, with 197 s + 325 l <= 1024. In every draw some block holds 3 large images and some other block 5 small ones and no large one.
All inputs are finite; a program needn't handle non-finite values.
Results may differ from the reference program's by a relative error of at most 0.02.
Values may be sent and summed in bfloat16 or wider, within the bound.
A program may use at most 256 MiB of HBM per device.

```python
import jax
import jax.numpy as jnp
from jax import lax

D = 768
HEADS = 12
HEAD_DIM = 64
FF = 3072
SMALL_ROWS = 197
LARGE_ROWS = 325
ROWS_DEV = 1024
TOKENS = 32768
N_DP = 2
N_FSDP = 16


def draw_image_counts(key, part):
    key_large = jax.random.fold_in(key, 11)
    key_drop = jax.random.fold_in(key, 12)
    key_pick = jax.random.fold_in(key, 13)
    device_total = N_DP * N_FSDP
    most_large = ROWS_DEV // LARGE_ROWS
    large_count = jax.random.randint(key_large, (device_total,), 0, most_large + 1)
    ranking = jax.random.permutation(key_pick, device_total)
    large_count = large_count.at[ranking[0]].set(most_large).at[ranking[1]].set(0)
    dropped = jax.random.randint(key_drop, (device_total,), 0, 2).at[ranking[1]].set(0)
    small_count = jnp.maximum((ROWS_DEV - LARGE_ROWS * large_count) // SMALL_ROWS - dropped, 0)
    return jnp.stack([small_count, large_count], axis=1).astype(jnp.int32)


def with_spikes(values, stream_key, source, target, parts, factor):
    def block_of(axis_at):
        return (jnp.arange(values.shape[axis_at]) // (values.shape[axis_at] // parts)).reshape((-1,) + (1,) * (values.ndim - 1 - axis_at))

    near = jax.random.permutation(stream_key, parts)[block_of(target)]
    second = (block_of(target) + parts // 2) % parts
    return jnp.where((block_of(source) == near) | (block_of(source) == second), factor * values, values)


def block_scale(own_key, dims, pieces, smallest, top_value):
    level = 1.0
    for dim, blocks in pieces:
        draws = jax.random.uniform(jax.random.fold_in(jax.random.fold_in(own_key, 6), dim), (blocks,), jnp.float32, smallest / len(pieces), top_value / len(pieces))
        level = level * jnp.repeat(jnp.exp(draws), dims[dim] // blocks).reshape((-1,) + (1,) * (len(dims) - 1 - dim))
    return level


def gaussian(rng, dims, spread, bound, pieces=(), dtype=jnp.bfloat16):
    drawn = jax.random.normal(rng, dims, jnp.float32) * spread
    if len(pieces) > 0:
        drawn = block_scale(rng, dims, pieces, -0.22, 0.18) * drawn
    return jnp.clip(drawn, min=-bound, max=bound).astype(dtype)


def gaussian_with(stream_key, dims, scale, limit, split, heavy, kind=jnp.bfloat16):
    drawn = scale * jax.random.normal(stream_key, dims, jnp.float32)
    if split:
        drawn = drawn * block_scale(stream_key, dims, split, -0.22, 0.18)
    return jnp.clip(with_spikes(drawn, jax.random.fold_in(stream_key, 3), *heavy), -limit, limit).astype(kind)


def setup_inputs(seed: int = 0) -> dict:
    splits = jax.random.split(jax.random.key(seed), 19)
    tokens = gaussian(splits[0], (TOKENS, D), 1.0, 6.0, ((0, 32),))
    image_counts = draw_image_counts(jax.random.fold_in(splits[18], 71), 0)
    cotangent = gaussian_with(splits[2], (TOKENS, D), 1.0, 6.0, ((0, 32),), (0, 1, 32, 2.75))
    first_gain = jnp.clip(1.0 + 0.1 * jax.random.normal(splits[3], (D,), jnp.float32), 0.5, 1.5).astype(jnp.bfloat16)
    first_shift = gaussian(splits[4], (D,), 0.5, 3.0, ((0, 16),))
    query_weight = gaussian(splits[5], (D, D), D ** -0.5, 0.21875, ((0, 16),))
    query_bias = gaussian(splits[6], (D,), 0.5, 3.0, ((0, 16),))
    key_weight = gaussian(splits[7], (D, D), D ** -0.5, 0.21875, ((0, 16),))
    value_weight = gaussian(splits[8], (D, D), D ** -0.5, 0.21875, ((0, 16),))
    value_bias = gaussian(splits[9], (D,), 0.5, 3.0, ((0, 16),))
    out_weight = gaussian(splits[10], (D, D), (D // 8) ** -0.5, 0.625, ((0, 16),))
    out_bias = gaussian(splits[11], (D,), 0.5, 3.0, ((0, 16),))
    second_gain = jnp.clip(1.0 + 0.1 * jax.random.normal(splits[12], (D,), jnp.float32), 0.5, 1.5).astype(jnp.bfloat16)
    second_shift = gaussian(splits[13], (D,), 0.5, 3.0, ((0, 16),))
    up_weight = gaussian(splits[14], (D, FF), D ** -0.5, 0.21875, ((0, 16),))
    up_bias = gaussian(splits[15], (FF,), 0.5, 3.0, ((0, 16),))
    down_weight = gaussian(splits[16], (FF, D), FF ** -0.5, 0.109375, ((0, 16),))
    down_bias = gaussian(splits[17], (D,), 0.5, 3.0, ((0, 16),))
    return {"tokens": tokens, "image_counts": image_counts, "cotangent": cotangent, "first_gain": first_gain, "first_shift": first_shift, "query_weight": query_weight, "query_bias": query_bias, "key_weight": key_weight, "value_weight": value_weight, "value_bias": value_bias, "out_weight": out_weight, "out_bias": out_bias, "second_gain": second_gain, "second_shift": second_shift, "up_weight": up_weight, "up_bias": up_bias, "down_weight": down_weight, "down_bias": down_bias}


@jax.custom_vjp
def low(v):
    return lax.optimization_barrier(v.astype(jnp.bfloat16)).astype(jnp.float32)

@jax.custom_vjp
def low_back(v):
    return v

def low_keep(v):
    return (low(v), None)

def low_pass(kept, grad):
    return (grad,)

def back_keep(v):
    return (v, None)

def back_low(kept, grad):
    return (low(grad),)
low.defvjp(low_keep, low_pass)
low_back.defvjp(back_keep, back_low)
EPS = 1e-06
HIGH = lax.Precision.HIGHEST

def matmul_high(left, right):
    return jnp.dot(left, right, precision=HIGH)

def layer_norm(values, gain_vec, shift_vec):
    row_mean = lax.optimization_barrier(jnp.mean(values, axis=-1, keepdims=True))
    centred = values - row_mean
    row_var = lax.optimization_barrier(jnp.mean(centred * centred, axis=-1, keepdims=True))
    return centred * lax.rsqrt(row_var + EPS) * gain_vec + shift_vec

def image_ids(count_row, row_total):
    places = lax.iota(jnp.int32, row_total)
    small_count = count_row[0]
    large_count = count_row[1]
    offset = small_count * SMALL_ROWS
    live_rows = places < offset + large_count * LARGE_ROWS
    image_of = jnp.where(places < offset, places // SMALL_ROWS, jnp.where(live_rows, small_count + (places - offset) // LARGE_ROWS, -1))
    return (image_of.astype(jnp.int32), live_rows)

def device_layer(inputs, count_row, params):
    first_gain, first_shift, query_weight, query_bias, key_weight, value_weight, value_bias, out_weight, out_bias, second_gain, second_shift, up_weight, up_bias, down_weight, down_bias = params
    row_total = inputs.shape[0]
    feat_width = inputs.shape[1]
    image_of, live_rows = image_ids(count_row, row_total)
    first_in = low(layer_norm(inputs, first_gain, first_shift))
    query = low_back(low(matmul_high(first_in, query_weight) + query_bias))
    key_rows = low_back(low(matmul_high(first_in, key_weight)))
    value_rows = low_back(low(matmul_high(first_in, value_weight) + value_bias))
    query_h = query.reshape(row_total, HEADS, HEAD_DIM)
    key_h = key_rows.reshape(row_total, HEADS, HEAD_DIM)
    value_h = value_rows.reshape(row_total, HEADS, HEAD_DIM)
    scores = low_back(jnp.einsum('qhd,khd->hqk', query_h, key_h, precision=HIGH) * HEAD_DIM ** (-0.5))
    allowed = image_of[:, None] == image_of[None, :]
    attn_probs = jax.nn.softmax(jnp.where(allowed[None], scores, -1e+30), axis=-1)
    attn_mixed = jnp.einsum('hqk,khd->qhd', low(attn_probs), value_h, precision=HIGH).reshape(row_total, feat_width)
    attn_mixed = low_back(low(attn_mixed))
    residual = inputs + low_back(matmul_high(attn_mixed, out_weight) + out_bias)
    second_in = low(layer_norm(residual, second_gain, second_shift))
    pre_gelu = low_back(matmul_high(second_in, up_weight) + up_bias)
    hidden = low(jax.nn.gelu(pre_gelu, approximate=False))
    result = residual + low_back(matmul_high(hidden, down_weight) + down_bias)
    return jnp.where(live_rows[:, None], result, 0.0)

def reference(tokens, image_counts, cotangent, first_gain, first_shift, query_weight, query_bias, key_weight, value_weight, value_bias, out_weight, out_bias, second_gain, second_shift, up_weight, up_bias, down_weight, down_bias):
    params = (first_gain.astype(jnp.float32), first_shift.astype(jnp.float32), query_weight.astype(jnp.float32), query_bias.astype(jnp.float32), key_weight.astype(jnp.float32), value_weight.astype(jnp.float32), value_bias.astype(jnp.float32), out_weight.astype(jnp.float32), out_bias.astype(jnp.float32), second_gain.astype(jnp.float32), second_shift.astype(jnp.float32), up_weight.astype(jnp.float32), up_bias.astype(jnp.float32), down_weight.astype(jnp.float32), down_bias.astype(jnp.float32))
    blocks = tokens.astype(jnp.float32).reshape(-1, ROWS_DEV, D)
    cot_blocks = cotangent.astype(jnp.float32).reshape(-1, ROWS_DEV, D)

    def forward(block_rows, param_set):

        def per_device(paired):
            return device_layer(paired[0], paired[1], param_set)
        return lax.map(jax.checkpoint(per_device), (block_rows, image_counts))
    result, pullback = jax.vjp(forward, blocks, params)
    grad_blocks, grads = pullback(cot_blocks)
    layer_out = result.reshape(-1, D).astype(jnp.bfloat16)
    grad_tokens = grad_blocks.reshape(-1, D)
    return (layer_out, grad_tokens, grads[0], grads[1], grads[2], grads[3], grads[4], grads[5], grads[6], grads[7], grads[8], grads[9], grads[10], grads[11], grads[12], grads[13], grads[14])
```

```python
import functools
import math

import jax
import jax.numpy as jnp
from jax import lax
from jax.experimental import pallas as pl
from jax.experimental.pallas import tpu as pltpu
from jax.sharding import PartitionSpec as P

EPS = 1e-06
NT = (((1,), (1,)), ((), ()))
TN = (((0,), (0,)), ((), ()))


SMALL_ROWS=197; LARGE_ROWS=325
QB=256
KB=128
NEG=-1e30

def image_ends(small, large, rows):
    ends=[]
    for i in range(1, rows//SMALL_ROWS+1):
        e = jnp.minimum(i, small)*SMALL_ROWS + jnp.maximum(i-small,0)*LARGE_ROWS
        ends.append(jnp.where(i<=small+large, e, 2*rows))
    return ends

def image_of(places, ends):
    idx = jnp.zeros(places.shape, jnp.int32)
    for e in ends:
        idx = idx + (places>=e).astype(jnp.int32)
    return idx

def key_range(ends, first, last, rows):
    lo = jnp.int32(0); hi = jnp.int32(rows)
    for e in ends:
        lo = jnp.maximum(lo, jnp.where(e<=first, e, 0))
        hi = jnp.minimum(hi, jnp.where(e>last, e, rows))
    return lo, hi

def widths_of(rows):
    ws = [w*KB for w in range(3, rows//KB)]
    ws = [w for w in ws if w<=768]
    return ws+[rows]

def with_window(counts_ref, rows, first, body):
    small=counts_ref[0]; large=counts_ref[1]
    ends=image_ends(small, large, rows)
    lo,hi=key_range(ends, first, first+QB-1, rows)
    base=lo//KB
    need=(hi+KB-1)//KB - base
    done=jnp.int32(0)
    for w in widths_of(rows):
        n=w//KB
        use = (need<=n) & (need>done)
        start = jnp.minimum(base, (rows-w)//KB)*KB
        @pl.when(use)
        def _(start=start, w=w):
            body(pl.multiple_of(start,KB), w, ends)
        done=jnp.int32(n)

def fwd_kernel(counts_ref, q_ref, k_ref, v_ref, o_ref, lse_ref):
    rows=q_ref.shape[0]
    lane=lax.broadcasted_iota(jnp.int32,(QB,128),1)
    def block(b, _):
        first=pl.multiple_of(b*QB,QB)
        def body(start, w, ends):
            q=q_ref[pl.ds(first,QB),:]
            k=k_ref[pl.ds(start,w),:]
            v=v_ref[pl.ds(start,w),:]
            rid=image_of(first+lax.broadcasted_iota(jnp.int32,(QB,1),0), ends)
            cid=image_of(start+lax.broadcasted_iota(jnp.int32,(1,w),1), ends)
            bias=jnp.where(rid==cid, 0.0, NEG)
            outs=[];lses=[]
            for e in range(2):
                qm=jnp.where((lane<64)==(e==0), q, jnp.zeros_like(q))
                s=lax.dot_general(qm,k,(((1,),(1,)),((),())),preferred_element_type=jnp.float32)+bias
                m=jnp.max(s,axis=1,keepdims=True)
                p=jnp.exp(s-m)
                l=jnp.sum(p,axis=1,keepdims=True)
                o=jnp.dot(p.astype(jnp.bfloat16),v,preferred_element_type=jnp.float32)
                outs.append(o*(1.0/l)); lses.append(m+jnp.log(l))
            o_ref[pl.ds(first,QB),:]=jnp.where(lane<64,outs[0],outs[1]).astype(jnp.bfloat16)
            both=jnp.where(lane<64,jnp.broadcast_to(lses[0],(QB,128)),jnp.broadcast_to(lses[1],(QB,128)))
            t=both.T
            lse_ref[0,0:1,pl.ds(first,QB)]=t[0:1,:]
            lse_ref[0,1:2,pl.ds(first,QB)]=t[64:65,:]
        with_window(counts_ref, rows, first, body)
        return 0
    lax.fori_loop(0,rows//QB,block,0)

def attn_fwd(counts,q,k,v):
    rows,feat=q.shape
    pairs=feat//128
    spec=pl.BlockSpec((rows,128),lambda p,c:(0,p))
    return pl.pallas_call(fwd_kernel,
        grid_spec=pltpu.PrefetchScalarGridSpec(num_scalar_prefetch=1,grid=(pairs,),
            in_specs=[spec]*3,out_specs=[spec,pl.BlockSpec((1,2,rows),lambda p,c:(p,0,0))]),
        out_shape=[jax.ShapeDtypeStruct((rows,feat),jnp.bfloat16),jax.ShapeDtypeStruct((pairs,2,rows),jnp.float32)],
        name="attend",
        )(counts,q,k,v)

def bwd_kernel(counts_ref, q_ref, k_ref, v_ref, do_ref, lse_ref, dq_ref, dk_ref, dv_ref, dk_acc, dv_acc):
    rows=q_ref.shape[0]
    lane=lax.broadcasted_iota(jnp.int32,(QB,128),1)
    dk_acc[...]=jnp.zeros_like(dk_acc)
    dv_acc[...]=jnp.zeros_like(dv_acc)
    nt=(((1,),(1,)),((),()))
    tn=(((0,),(0,)),((),()))
    def block(b,_):
        first=pl.multiple_of(b*QB,QB)
        def body(start,w,ends):
            q=q_ref[pl.ds(first,QB),:]
            do=do_ref[pl.ds(first,QB),:]
            k=k_ref[pl.ds(start,w),:]
            v=v_ref[pl.ds(start,w),:]
            rid=image_of(start+lax.broadcasted_iota(jnp.int32,(w,1),0), ends)
            cid=image_of(first+lax.broadcasted_iota(jnp.int32,(1,QB),1), ends)
            bias=jnp.where(rid==cid,0.0,NEG)
            dqs=[]
            dks=None;dvs=None
            for e in range(2):
                mask=(lane<64)==(e==0)
                qm=jnp.where(mask,q,jnp.zeros_like(q))
                dom=jnp.where(mask,do,jnp.zeros_like(do))
                s=lax.dot_general(k,qm,nt,preferred_element_type=jnp.float32)+bias
                p=jnp.exp(s-lse_ref[0,e:e+1,pl.ds(first,QB)])
                dp=lax.dot_general(v,dom,nt,preferred_element_type=jnp.float32)
                delta=jnp.sum(p*dp,axis=0,keepdims=True)
                ds=(p*(dp-delta)).astype(jnp.bfloat16)
                pb=p.astype(jnp.bfloat16)
                dv_e=jnp.dot(pb,dom,preferred_element_type=jnp.float32)
                dk_e=jnp.dot(ds,qm,preferred_element_type=jnp.float32)
                dq_e=lax.dot_general(ds,k,tn,preferred_element_type=jnp.float32)
                dvs=dv_e if dvs is None else dvs+dv_e
                dks=dk_e if dks is None else dks+dk_e
                dqs.append(dq_e)
            dv_acc[pl.ds(start,w),:]+=dvs
            dk_acc[pl.ds(start,w),:]+=dks
            dq_ref[pl.ds(first,QB),:]=(jnp.where(lane<64,dqs[0],dqs[1])*0.125).astype(jnp.bfloat16)
        with_window(counts_ref,rows,first,body)
        return 0
    lax.fori_loop(0,rows//QB,block,0)
    dk_ref[...]=dk_acc[...].astype(jnp.bfloat16)
    dv_ref[...]=dv_acc[...].astype(jnp.bfloat16)

def attn_bwd(counts,q,k,v,do,lse):
    rows,feat=q.shape
    pairs=feat//128
    spec=pl.BlockSpec((rows,128),lambda p,c:(0,p))
    return pl.pallas_call(bwd_kernel,
        grid_spec=pltpu.PrefetchScalarGridSpec(num_scalar_prefetch=1,grid=(pairs,),
            in_specs=[spec]*4+[pl.BlockSpec((1,2,rows),lambda p,c:(p,0,0))],out_specs=[spec]*3,
            scratch_shapes=[pltpu.VMEM((rows,128),jnp.float32)]*2),
        out_shape=[jax.ShapeDtypeStruct((rows,feat),jnp.bfloat16)]*3,
        name="attend_back",
        )(counts,q,k,v,do,lse)

f32=jnp.float32; bf16=jnp.bfloat16
RB=256
INV_SQRT2=1/math.sqrt(2.0); INV_SQRT2PI=1/math.sqrt(2*math.pi)

def dot(a,b): return jnp.dot(a,b,preferred_element_type=f32)
def dot_nt(a,b): return lax.dot_general(a,b,NT,preferred_element_type=f32)
def dot_tn(a,b): return lax.dot_general(a,b,TN,preferred_element_type=f32)

def norm_parts(x):
    mean=jnp.mean(x,axis=-1,keepdims=True)
    cen=x-mean
    var=jnp.mean(cen*cen,axis=-1,keepdims=True)
    q=lax.rsqrt(var+EPS)
    return cen*q, q

def live_mask(counts_ref, first, n):
    end=counts_ref[0]*197+counts_ref[1]*325
    r=first+lax.broadcasted_iota(jnp.int32,(n,1),0)
    return r<end

def mid_kernel(counts_ref, mixed_ref, tokens_ref, cot_ref, outw_ref, vec_ref, up_ref, ub_ref, down_ref,
        layer_ref, gres_ref, gmix_ref, gup_ref, gub_ref, gdown_ref, gout_ref, gvec_ref,
        res_s, si_s, gb_s, accout_s, accgs_s, hid_s, gi_s):
    rows=tokens_ref.shape[0]
    j=pl.program_id(0); nj=pl.num_programs(0)
    obias=vec_ref[0:1,:]; gain=vec_ref[1:2,:]; shift=vec_ref[2:3,:]; dbias=vec_ref[3:4,:]
    @pl.when(j==0)
    def _():
        def step(i,_):
            first=pl.multiple_of(i*RB,RB); sl=pl.ds(first,RB)
            res=tokens_ref[sl,:].astype(f32)+(dot(mixed_ref[sl,:],outw_ref[...])+obias)
            res_s[sl,:]=res
            xhat,_q=norm_parts(res)
            si_s[sl,:]=(xhat*gain+shift).astype(bf16)
            live=live_mask(counts_ref,first,RB)
            gb_s[sl,:]=jnp.where(live,cot_ref[sl,:],jnp.zeros((),bf16))
            return 0
        lax.fori_loop(0,rows//RB,step,0)
        accout_s[...]=jnp.zeros_like(accout_s)
        accgs_s[...]=jnp.zeros_like(accgs_s)
    gub=jnp.zeros(gub_ref.shape,f32)
    for i in range(rows//RB):
        sl=slice(i*RB,(i+1)*RB)
        pre=dot(si_s[sl,:],up_ref[...])+ub_ref[...]
        cdf=0.5+0.5*lax.erf(pre*INV_SQRT2)
        pdf=jnp.exp(-0.5*pre*pre)*INV_SQRT2PI
        hid_s[sl,:]=(pre*cdf).astype(bf16)
        gh=dot_nt(gb_s[sl,:],down_ref[...])
        gi=(gh*(cdf+pre*pdf)).astype(bf16)
        gi_s[sl,:]=gi
        gub=gub+jnp.sum(gi.astype(f32),axis=0,keepdims=True)
    gub_ref[...]=gub
    accout_s[...]+=dot(hid_s[...],down_ref[...])
    accgs_s[...]+=dot_nt(gi_s[...],up_ref[...])
    gdown_ref[...]=dot_tn(hid_s[...],gb_s[...]).astype(bf16)
    gup_ref[...]=dot_tn(si_s[...],gi_s[...]).astype(bf16)
    @pl.when(j==nj-1)
    def _():
        gvec_ref[...]=jnp.zeros_like(gvec_ref)
        def step(i,_):
            first=pl.multiple_of(i*RB,RB); sl=pl.ds(first,RB)
            live=live_mask(counts_ref,first,RB)
            res=res_s[sl,:]
            layer=res+(accout_s[sl,:]+dbias)
            layer_ref[sl,:]=jnp.where(live,layer,0.0).astype(bf16)
            xhat,q=norm_parts(res)
            gs=accgs_s[sl,:]
            t=gs*gain
            gb=gb_s[sl,:].astype(f32)
            gres=gb+q*(t-jnp.mean(t,axis=-1,keepdims=True)-xhat*jnp.mean(t*xhat,axis=-1,keepdims=True))
            gres_ref[sl,:]=gres
            ga=gres.astype(bf16)
            mixed_unused=None
            si_s[sl,:]=ga
            gvec_ref[0:1,:]+=jnp.sum(gb,axis=0,keepdims=True)
            gvec_ref[1:2,:]+=jnp.sum(gs*xhat,axis=0,keepdims=True)
            gvec_ref[2:3,:]+=jnp.sum(gs,axis=0,keepdims=True)
            gvec_ref[3:4,:]+=jnp.sum(ga.astype(f32),axis=0,keepdims=True)
            gmix_ref[sl,:]=dot_nt(ga,outw_ref[...]).astype(bf16)
            return 0
        lax.fori_loop(0,rows//RB,step,0)
        gout_ref[...]=dot_tn(mixed_ref[...],si_s[...]).astype(bf16)

def middle(counts,mixed,tokens,cot,outw,vec,up,ub,down,FB=512):
    rows,D=tokens.shape; FF=up.shape[1]
    nj=FF//FB
    full=lambda a: pl.BlockSpec(a.shape,lambda j,c:(0,)*len(a.shape),pipeline_mode=pl.Buffered(1))
    fo=lambda s: pl.BlockSpec(s,lambda j,c:(0,)*len(s),pipeline_mode=pl.Buffered(1))
    return pl.pallas_call(mid_kernel,
        grid_spec=pltpu.PrefetchScalarGridSpec(num_scalar_prefetch=1,grid=(nj,),
            in_specs=[full(mixed),full(tokens),full(cot),full(outw),full(vec),
                pl.BlockSpec((D,FB),lambda j,c:(0,j)),pl.BlockSpec((1,FB),lambda j,c:(0,j)),pl.BlockSpec((FB,D),lambda j,c:(j,0))],
            out_specs=[fo((rows,D)),fo((rows,D)),fo((rows,D)),
                pl.BlockSpec((D,FB),lambda j,c:(0,j)),pl.BlockSpec((1,FB),lambda j,c:(0,j)),pl.BlockSpec((FB,D),lambda j,c:(j,0)),
                fo((D,D)),fo((8,D))],
            scratch_shapes=[pltpu.VMEM((rows,D),f32),pltpu.VMEM((rows,D),bf16),pltpu.VMEM((rows,D),bf16),
                pltpu.VMEM((rows,D),f32),pltpu.VMEM((rows,D),f32),pltpu.VMEM((rows,FB),bf16),pltpu.VMEM((rows,FB),bf16)]),
        out_shape=[jax.ShapeDtypeStruct((rows,D),bf16),jax.ShapeDtypeStruct((rows,D),f32),jax.ShapeDtypeStruct((rows,D),bf16),
            jax.ShapeDtypeStruct((D,FF),bf16),jax.ShapeDtypeStruct((1,FF),f32),jax.ShapeDtypeStruct((FF,D),bf16),
            jax.ShapeDtypeStruct((D,D),bf16),jax.ShapeDtypeStruct((8,D),f32)],
        compiler_params=pltpu.CompilerParams(vmem_limit_bytes=60*2**20),
        name="feed_forward",
        )(counts,mixed,tokens,cot,outw,vec,up,ub,down)


def qkv_kernel(tokens_ref, vec_ref, qw_ref, kw_ref, vw_ref, fi_ref, q_ref, k_ref, v_ref):
    rows=tokens_ref.shape[0]
    gain=vec_ref[0:1,:]; shift=vec_ref[1:2,:]; qb=vec_ref[2:3,:]; vb=vec_ref[3:4,:]
    for i in range(rows//RB):
        sl=slice(i*RB,(i+1)*RB)
        xhat,_=norm_parts(tokens_ref[sl,:].astype(f32))
        fi=(xhat*gain+shift).astype(bf16)
        fi_ref[sl,:]=fi
        q_ref[sl,:]=((dot(fi,qw_ref[...])+qb).astype(bf16).astype(f32)*0.125).astype(bf16)
        k_ref[sl,:]=dot(fi,kw_ref[...]).astype(bf16)
        v_ref[sl,:]=(dot(fi,vw_ref[...])+vb).astype(bf16)

def project(tokens,vec,qw,kw,vw):
    rows,D=tokens.shape
    return pl.pallas_call(qkv_kernel,out_shape=[jax.ShapeDtypeStruct((rows,D),bf16)]*4,
        compiler_params=pltpu.CompilerParams(vmem_limit_bytes=60*2**20),name="project")(tokens,vec,qw,kw,vw)

def back_kernel(tokens_ref, vec_ref, gres_ref, fi_ref, dq_ref, dk_ref, dv_ref, qw_ref, kw_ref, vw_ref,
        gtok_ref, gq_ref, gk_ref, gv_ref, gvec_ref):
    rows=tokens_ref.shape[0]
    gain=vec_ref[0:1,:]
    gvec=[jnp.zeros((1,tokens_ref.shape[1]),f32)]*4
    for i in range(rows//RB):
        sl=slice(i*RB,(i+1)*RB)
        dq=dq_ref[sl,:];dk=dk_ref[sl,:];dv=dv_ref[sl,:]
        gs=dot_nt(dq,qw_ref[...])+dot_nt(dk,kw_ref[...])+dot_nt(dv,vw_ref[...])
        xhat,q=norm_parts(tokens_ref[sl,:].astype(f32))
        t=gs*gain
        gtok_ref[sl,:]=gres_ref[sl,:]+q*(t-jnp.mean(t,axis=-1,keepdims=True)-xhat*jnp.mean(t*xhat,axis=-1,keepdims=True))
        for n,a in enumerate((gs*xhat,gs,dq.astype(f32),dv.astype(f32))):
            gvec[n]=gvec[n]+jnp.sum(a,axis=0,keepdims=True)
    gvec_ref[...]=jnp.zeros_like(gvec_ref)
    for n in range(4): gvec_ref[n:n+1,:]=gvec[n]
    fi=fi_ref[...]
    gq_ref[...]=dot_tn(fi,dq_ref[...]).astype(bf16)
    gk_ref[...]=dot_tn(fi,dk_ref[...]).astype(bf16)
    gv_ref[...]=dot_tn(fi,dv_ref[...]).astype(bf16)

def project_back(tokens,vec,gres,fi,dq,dk,dv,qw,kw,vw):
    rows,D=tokens.shape
    s=jax.ShapeDtypeStruct
    return pl.pallas_call(back_kernel,out_shape=[s((rows,D),f32),s((D,D),bf16),s((D,D),bf16),s((D,D),bf16),s((8,D),f32)],
        compiler_params=pltpu.CompilerParams(vmem_limit_bytes=60*2**20),name="project_back")(tokens,vec,gres,fi,dq,dk,dv,qw,kw,vw)

FSDP="fsdp"

def on_device(tokens, image_counts, cotangent, first_gain, first_shift, query_weight, query_bias, key_weight,
              value_weight, value_bias, out_weight, out_bias, second_gain, second_shift, up_weight, up_bias,
              down_weight, down_bias):
    rows, feat = tokens.shape
    own = query_weight.shape[0]
    n = feat // own
    counts = image_counts[0]
    gather = lambda a: lax.all_gather(a, FSDP, axis=0, tiled=False)
    small = jnp.concatenate([jnp.stack([first_gain, first_shift, query_bias, value_bias, out_bias, second_gain, second_shift, down_bias]),
        up_bias.reshape(-1, own)])
    small_all = gather(small)
    attn_all = gather(jnp.stack([query_weight, key_weight, value_weight, out_weight]))
    full = lambda i: attn_all[:, i].reshape(feat, feat)
    qw, kw, vw, ow = full(0), full(1), full(2), full(3)
    up = gather(up_weight).reshape(feat, -1)
    down = gather(down_weight).reshape(-1, feat)
    wide = jnp.transpose(small_all[:, :8], (1, 0, 2)).reshape(8, feat).astype(f32)
    ub = small_all[:, 8:].reshape(1, -1).astype(f32)
    vec1 = wide[0:4]
    vec2 = wide[4:8]
    fi, q, k, v = project(tokens, vec1, qw, kw, vw)
    mixed, lse = attn_fwd(counts, q, k, v)
    layer_out, gres, gmix, gup, gub, gdown, gout, gv2 = middle(counts, mixed, tokens, cotangent, ow, vec2, up, ub, down)
    dq, dk, dv = attn_bwd(counts, q, k, v, gmix, lse)
    gtok, gq, gk, gv, gv1 = project_back(tokens, vec1, gres, fi, dq, dk, dv, qw, kw, vw)
    scatter = lambda a: lax.psum_scatter(a, FSDP, scatter_dimension=0, tiled=False)
    pair = lambda a: lax.psum(a, "dp").astype(f32)
    su = scatter(gup.reshape(n, own, -1))
    sd = scatter(gdown.reshape(n, -1, feat))
    sa = scatter(jnp.stack([g.reshape(n, own, feat) for g in (gq, gk, gv, gout)], axis=1))
    smalls = jnp.concatenate([gv1[0:4], gv2[0:4]]).reshape(8, n, own)
    smalls = jnp.concatenate([jnp.transpose(smalls, (1, 0, 2)), gub.reshape(n, -1, own)], axis=1).astype(bf16)
    ss = scatter(smalls)
    su, sd, sa, ss = (pair(a) for a in (su, sd, sa, ss))
    return (layer_out, gtok, ss[0], ss[1], sa[0], ss[2], sa[1], sa[2], ss[3], sa[3], ss[7], ss[5], ss[6], su,
            ss[8:].reshape(-1), sd, ss[4])


def solution(mesh):
    rows = P(("dp", "fsdp"), None)
    mat = P("fsdp", None)
    vec = P("fsdp")
    return jax.shard_map(
        on_device,
        mesh=mesh,
        in_specs=(rows, rows, rows, vec, vec, mat, vec, mat, mat, vec, mat, vec, vec, vec, mat, vec, mat, vec),
        out_specs=(rows, rows, vec, vec, mat, vec, mat, mat, vec, mat, vec, vec, vec, mat, vec, mat, vec),
        check_vma=False,
    )
```

```python
import functools
import math

import jax
import jax.numpy as jnp
from jax import lax
from jax.experimental import pallas as pl
from jax.experimental.pallas import tpu as pltpu
from jax.sharding import PartitionSpec as P

EPS = 1e-06
NT = (((1,), (1,)), ((), ()))
TN = (((0,), (0,)), ((), ()))


SMALL_ROWS=197; LARGE_ROWS=325
QB=256
KB=128
NEG=-1e30

def image_ends(small, large, rows):
    ends=[]
    for i in range(1, rows//SMALL_ROWS+1):
        e = jnp.minimum(i, small)*SMALL_ROWS + jnp.maximum(i-small,0)*LARGE_ROWS
        ends.append(jnp.where(i<=small+large, e, 2*rows))
    return ends

def image_of(places, ends):
    idx = jnp.zeros(places.shape, jnp.int32)
    for e in ends:
        idx = idx + (places>=e).astype(jnp.int32)
    return idx

def key_range(ends, first, last, rows):
    lo = jnp.int32(0); hi = jnp.int32(rows)
    for e in ends:
        lo = jnp.maximum(lo, jnp.where(e<=first, e, 0))
        hi = jnp.minimum(hi, jnp.where(e>last, e, rows))
    return lo, hi

def widths_of(rows):
    ws = [w*KB for w in range(3, rows//KB)]
    ws = [w for w in ws if w<=768]
    return ws+[rows]

def with_window(counts_ref, rows, first, body):
    small=counts_ref[0]; large=counts_ref[1]
    ends=image_ends(small, large, rows)
    lo,hi=key_range(ends, first, first+QB-1, rows)
    base=lo//KB
    need=(hi+KB-1)//KB - base
    done=jnp.int32(0)
    for w in widths_of(rows):
        n=w//KB
        use = (need<=n) & (need>done)
        start = jnp.minimum(base, (rows-w)//KB)*KB
        @pl.when(use)
        def _(start=start, w=w):
            body(pl.multiple_of(start,KB), w, ends)
        done=jnp.int32(n)

def fwd_kernel(counts_ref, q_ref, k_ref, v_ref, o_ref, lse_ref):
    rows=q_ref.shape[0]
    lane=lax.broadcasted_iota(jnp.int32,(QB,128),1)
    def block(b, _):
        first=pl.multiple_of(b*QB,QB)
        def body(start, w, ends):
            q=q_ref[pl.ds(first,QB),:]
            k=k_ref[pl.ds(start,w),:]
            v=v_ref[pl.ds(start,w),:]
            rid=image_of(first+lax.broadcasted_iota(jnp.int32,(QB,1),0), ends)
            cid=image_of(start+lax.broadcasted_iota(jnp.int32,(1,w),1), ends)
            bias=jnp.where(rid==cid, 0.0, NEG)
            outs=[];lses=[]
            for e in range(2):
                qm=jnp.where((lane<64)==(e==0), q, jnp.zeros_like(q))
                s=lax.dot_general(qm,k,(((1,),(1,)),((),())),preferred_element_type=jnp.float32)+bias
                m=jnp.max(s,axis=1,keepdims=True)
                p=jnp.exp(s-m)
                l=jnp.sum(p,axis=1,keepdims=True)
                o=jnp.dot(p.astype(jnp.bfloat16),v,preferred_element_type=jnp.float32)
                outs.append(o*(1.0/l)); lses.append(m+jnp.log(l))
            o_ref[pl.ds(first,QB),:]=jnp.where(lane<64,outs[0],outs[1]).astype(jnp.bfloat16)
            both=jnp.where(lane<64,jnp.broadcast_to(lses[0],(QB,128)),jnp.broadcast_to(lses[1],(QB,128)))
            t=both.T
            lse_ref[0,0:1,pl.ds(first,QB)]=t[0:1,:]
            lse_ref[0,1:2,pl.ds(first,QB)]=t[64:65,:]
        with_window(counts_ref, rows, first, body)
        return 0
    lax.fori_loop(0,rows//QB,block,0)

def attn_fwd(counts,q,k,v):
    rows,feat=q.shape
    pairs=feat//128
    spec=pl.BlockSpec((rows,128),lambda p,c:(0,p))
    return pl.pallas_call(fwd_kernel,
        grid_spec=pltpu.PrefetchScalarGridSpec(num_scalar_prefetch=1,grid=(pairs,),
            in_specs=[spec]*3,out_specs=[spec,pl.BlockSpec((1,2,rows),lambda p,c:(p,0,0))]),
        out_shape=[jax.ShapeDtypeStruct((rows,feat),jnp.bfloat16),jax.ShapeDtypeStruct((pairs,2,rows),jnp.float32)],
        name="attend",
        )(counts,q,k,v)

def bwd_kernel(counts_ref, q_ref, k_ref, v_ref, do_ref, lse_ref, dq_ref, dk_ref, dv_ref, dk_acc, dv_acc):
    rows=q_ref.shape[0]
    lane=lax.broadcasted_iota(jnp.int32,(QB,128),1)
    dk_acc[...]=jnp.zeros_like(dk_acc)
    dv_acc[...]=jnp.zeros_like(dv_acc)
    nt=(((1,),(1,)),((),()))
    tn=(((0,),(0,)),((),()))
    def block(b,_):
        first=pl.multiple_of(b*QB,QB)
        def body(start,w,ends):
            q=q_ref[pl.ds(first,QB),:]
            do=do_ref[pl.ds(first,QB),:]
            k=k_ref[pl.ds(start,w),:]
            v=v_ref[pl.ds(start,w),:]
            rid=image_of(start+lax.broadcasted_iota(jnp.int32,(w,1),0), ends)
            cid=image_of(first+lax.broadcasted_iota(jnp.int32,(1,QB),1), ends)
            bias=jnp.where(rid==cid,0.0,NEG)
            dqs=[]
            dks=None;dvs=None
            for e in range(2):
                mask=(lane<64)==(e==0)
                qm=jnp.where(mask,q,jnp.zeros_like(q))
                dom=jnp.where(mask,do,jnp.zeros_like(do))
                s=lax.dot_general(k,qm,nt,preferred_element_type=jnp.float32)+bias
                p=jnp.exp(s-lse_ref[0,e:e+1,pl.ds(first,QB)])
                dp=lax.dot_general(v,dom,nt,preferred_element_type=jnp.float32)
                delta=jnp.sum(p*dp,axis=0,keepdims=True)
                ds=(p*(dp-delta)).astype(jnp.bfloat16)
                pb=p.astype(jnp.bfloat16)
                dv_e=jnp.dot(pb,dom,preferred_element_type=jnp.float32)
                dk_e=jnp.dot(ds,qm,preferred_element_type=jnp.float32)
                dq_e=lax.dot_general(ds,k,tn,preferred_element_type=jnp.float32)
                dvs=dv_e if dvs is None else dvs+dv_e
                dks=dk_e if dks is None else dks+dk_e
                dqs.append(dq_e)
            dv_acc[pl.ds(start,w),:]+=dvs
            dk_acc[pl.ds(start,w),:]+=dks
            dq_ref[pl.ds(first,QB),:]=(jnp.where(lane<64,dqs[0],dqs[1])*0.125).astype(jnp.bfloat16)
        with_window(counts_ref,rows,first,body)
        return 0
    lax.fori_loop(0,rows//QB,block,0)
    dk_ref[...]=dk_acc[...].astype(jnp.bfloat16)
    dv_ref[...]=dv_acc[...].astype(jnp.bfloat16)

def attn_bwd(counts,q,k,v,do,lse):
    rows,feat=q.shape
    pairs=feat//128
    spec=pl.BlockSpec((rows,128),lambda p,c:(0,p))
    return pl.pallas_call(bwd_kernel,
        grid_spec=pltpu.PrefetchScalarGridSpec(num_scalar_prefetch=1,grid=(pairs,),
            in_specs=[spec]*4+[pl.BlockSpec((1,2,rows),lambda p,c:(p,0,0))],out_specs=[spec]*3,
            scratch_shapes=[pltpu.VMEM((rows,128),jnp.float32)]*2),
        out_shape=[jax.ShapeDtypeStruct((rows,feat),jnp.bfloat16)]*3,
        name="attend_back",
        )(counts,q,k,v,do,lse)

f32=jnp.float32; bf16=jnp.bfloat16
RB=256
INV_SQRT2=1/math.sqrt(2.0); INV_SQRT2PI=1/math.sqrt(2*math.pi)

def dot(a,b): return jnp.dot(a,b,preferred_element_type=f32)
def dot_nt(a,b): return lax.dot_general(a,b,NT,preferred_element_type=f32)
def dot_tn(a,b): return lax.dot_general(a,b,TN,preferred_element_type=f32)

def norm_parts(x):
    mean=jnp.mean(x,axis=-1,keepdims=True)
    cen=x-mean
    var=jnp.mean(cen*cen,axis=-1,keepdims=True)
    q=lax.rsqrt(var+EPS)
    return cen*q, q

def live_mask(counts_ref, first, n):
    end=counts_ref[0]*197+counts_ref[1]*325
    r=first+lax.broadcasted_iota(jnp.int32,(n,1),0)
    return r<end

def mid_kernel(counts_ref, mixed_ref, tokens_ref, cot_ref, outw_ref, vec_ref, up_ref, ub_ref, down_ref,
        layer_ref, gres_ref, gmix_ref, gup_ref, gub_ref, gdown_ref, gout_ref, gvec_ref,
        res_s, si_s, gb_s, accout_s, accgs_s, hid_s, gi_s):
    rows=tokens_ref.shape[0]
    j=pl.program_id(0); nj=pl.num_programs(0)
    obias=vec_ref[0:1,:]; gain=vec_ref[1:2,:]; shift=vec_ref[2:3,:]; dbias=vec_ref[3:4,:]
    @pl.when(j==0)
    def _():
        def step(i,_):
            first=pl.multiple_of(i*RB,RB); sl=pl.ds(first,RB)
            res=tokens_ref[sl,:].astype(f32)+(dot(mixed_ref[sl,:],outw_ref[...])+obias)
            res_s[sl,:]=res
            xhat,_q=norm_parts(res)
            si_s[sl,:]=(xhat*gain+shift).astype(bf16)
            live=live_mask(counts_ref,first,RB)
            gb_s[sl,:]=jnp.where(live,cot_ref[sl,:],jnp.zeros((),bf16))
            return 0
        lax.fori_loop(0,rows//RB,step,0)
        accout_s[...]=jnp.zeros_like(accout_s)
        accgs_s[...]=jnp.zeros_like(accgs_s)
    gub=jnp.zeros(gub_ref.shape,f32)
    for i in range(rows//RB):
        sl=slice(i*RB,(i+1)*RB)
        pre=dot(si_s[sl,:],up_ref[...])+ub_ref[...]
        cdf=0.5+0.5*lax.erf(pre*INV_SQRT2)
        pdf=jnp.exp(-0.5*pre*pre)*INV_SQRT2PI
        hid_s[sl,:]=(pre*cdf).astype(bf16)
        gh=dot_nt(gb_s[sl,:],down_ref[...])
        gi=(gh*(cdf+pre*pdf)).astype(bf16)
        gi_s[sl,:]=gi
        gub=gub+jnp.sum(gi.astype(f32),axis=0,keepdims=True)
    gub_ref[...]=gub
    accout_s[...]+=dot(hid_s[...],down_ref[...])
    accgs_s[...]+=dot_nt(gi_s[...],up_ref[...])
    gdown_ref[...]=dot_tn(hid_s[...],gb_s[...]).astype(bf16)
    gup_ref[...]=dot_tn(si_s[...],gi_s[...]).astype(bf16)
    @pl.when(j==nj-1)
    def _():
        gvec_ref[...]=jnp.zeros_like(gvec_ref)
        def step(i,_):
            first=pl.multiple_of(i*RB,RB); sl=pl.ds(first,RB)
            live=live_mask(counts_ref,first,RB)
            res=res_s[sl,:]
            layer=res+(accout_s[sl,:]+dbias)
            layer_ref[sl,:]=jnp.where(live,layer,0.0).astype(bf16)
            xhat,q=norm_parts(res)
            gs=accgs_s[sl,:]
            t=gs*gain
            gb=gb_s[sl,:].astype(f32)
            gres=gb+q*(t-jnp.mean(t,axis=-1,keepdims=True)-xhat*jnp.mean(t*xhat,axis=-1,keepdims=True))
            gres_ref[sl,:]=gres
            ga=gres.astype(bf16)
            mixed_unused=None
            si_s[sl,:]=ga
            gvec_ref[0:1,:]+=jnp.sum(gb,axis=0,keepdims=True)
            gvec_ref[1:2,:]+=jnp.sum(gs*xhat,axis=0,keepdims=True)
            gvec_ref[2:3,:]+=jnp.sum(gs,axis=0,keepdims=True)
            gvec_ref[3:4,:]+=jnp.sum(ga.astype(f32),axis=0,keepdims=True)
            gmix_ref[sl,:]=dot_nt(ga,outw_ref[...]).astype(bf16)
            return 0
        lax.fori_loop(0,rows//RB,step,0)
        gout_ref[...]=dot_tn(mixed_ref[...],si_s[...]).astype(bf16)

def middle(counts,mixed,tokens,cot,outw,vec,up,ub,down,FB=512):
    rows,D=tokens.shape; FF=up.shape[1]
    nj=FF//FB
    full=lambda a: pl.BlockSpec(a.shape,lambda j,c:(0,)*len(a.shape),pipeline_mode=pl.Buffered(1))
    fo=lambda s: pl.BlockSpec(s,lambda j,c:(0,)*len(s),pipeline_mode=pl.Buffered(1))
    return pl.pallas_call(mid_kernel,
        grid_spec=pltpu.PrefetchScalarGridSpec(num_scalar_prefetch=1,grid=(nj,),
            in_specs=[full(mixed),full(tokens),full(cot),full(outw),full(vec),
                pl.BlockSpec((D,FB),lambda j,c:(0,j)),pl.BlockSpec((1,FB),lambda j,c:(0,j)),pl.BlockSpec((FB,D),lambda j,c:(j,0))],
            out_specs=[fo((rows,D)),fo((rows,D)),fo((rows,D)),
                pl.BlockSpec((D,FB),lambda j,c:(0,j)),pl.BlockSpec((1,FB),lambda j,c:(0,j)),pl.BlockSpec((FB,D),lambda j,c:(j,0)),
                fo((D,D)),fo((8,D))],
            scratch_shapes=[pltpu.VMEM((rows,D),f32),pltpu.VMEM((rows,D),bf16),pltpu.VMEM((rows,D),bf16),
                pltpu.VMEM((rows,D),f32),pltpu.VMEM((rows,D),f32),pltpu.VMEM((rows,FB),bf16),pltpu.VMEM((rows,FB),bf16)]),
        out_shape=[jax.ShapeDtypeStruct((rows,D),bf16),jax.ShapeDtypeStruct((rows,D),f32),jax.ShapeDtypeStruct((rows,D),bf16),
            jax.ShapeDtypeStruct((D,FF),bf16),jax.ShapeDtypeStruct((1,FF),f32),jax.ShapeDtypeStruct((FF,D),bf16),
            jax.ShapeDtypeStruct((D,D),bf16),jax.ShapeDtypeStruct((8,D),f32)],
        compiler_params=pltpu.CompilerParams(vmem_limit_bytes=60*2**20),
        name="feed_forward",
        )(counts,mixed,tokens,cot,outw,vec,up,ub,down)


def qkv_kernel(tokens_ref, vec_ref, qw_ref, kw_ref, vw_ref, fi_ref, q_ref, k_ref, v_ref):
    rows=tokens_ref.shape[0]
    gain=vec_ref[0:1,:]; shift=vec_ref[1:2,:]; qb=vec_ref[2:3,:]; vb=vec_ref[3:4,:]
    for i in range(rows//RB):
        sl=slice(i*RB,(i+1)*RB)
        xhat,_=norm_parts(tokens_ref[sl,:].astype(f32))
        fi=(xhat*gain+shift).astype(bf16)
        fi_ref[sl,:]=fi
        q_ref[sl,:]=((dot(fi,qw_ref[...])+qb).astype(bf16).astype(f32)*0.125).astype(bf16)
        k_ref[sl,:]=dot(fi,kw_ref[...]).astype(bf16)
        v_ref[sl,:]=(dot(fi,vw_ref[...])+vb).astype(bf16)

def project(tokens,vec,qw,kw,vw):
    rows,D=tokens.shape
    return pl.pallas_call(qkv_kernel,out_shape=[jax.ShapeDtypeStruct((rows,D),bf16)]*4,
        compiler_params=pltpu.CompilerParams(vmem_limit_bytes=60*2**20),name="project")(tokens,vec,qw,kw,vw)

def back_kernel(tokens_ref, vec_ref, gres_ref, fi_ref, dq_ref, dk_ref, dv_ref, qw_ref, kw_ref, vw_ref,
        gtok_ref, gq_ref, gk_ref, gv_ref, gvec_ref):
    rows=tokens_ref.shape[0]
    gain=vec_ref[0:1,:]
    gvec=[jnp.zeros((1,tokens_ref.shape[1]),f32)]*4
    for i in range(rows//RB):
        sl=slice(i*RB,(i+1)*RB)
        dq=dq_ref[sl,:];dk=dk_ref[sl,:];dv=dv_ref[sl,:]
        gs=dot_nt(dq,qw_ref[...])+dot_nt(dk,kw_ref[...])+dot_nt(dv,vw_ref[...])
        xhat,q=norm_parts(tokens_ref[sl,:].astype(f32))
        t=gs*gain
        gtok_ref[sl,:]=gres_ref[sl,:]+q*(t-jnp.mean(t,axis=-1,keepdims=True)-xhat*jnp.mean(t*xhat,axis=-1,keepdims=True))
        for n,a in enumerate((gs*xhat,gs,dq.astype(f32),dv.astype(f32))):
            gvec[n]=gvec[n]+jnp.sum(a,axis=0,keepdims=True)
    gvec_ref[...]=jnp.zeros_like(gvec_ref)
    for n in range(4): gvec_ref[n:n+1,:]=gvec[n]
    fi=fi_ref[...]
    gq_ref[...]=dot_tn(fi,dq_ref[...]).astype(bf16)
    gk_ref[...]=dot_tn(fi,dk_ref[...]).astype(bf16)
    gv_ref[...]=dot_tn(fi,dv_ref[...]).astype(bf16)

def project_back(tokens,vec,gres,fi,dq,dk,dv,qw,kw,vw):
    rows,D=tokens.shape
    s=jax.ShapeDtypeStruct
    return pl.pallas_call(back_kernel,out_shape=[s((rows,D),f32),s((D,D),bf16),s((D,D),bf16),s((D,D),bf16),s((8,D),f32)],
        compiler_params=pltpu.CompilerParams(vmem_limit_bytes=60*2**20),name="project_back")(tokens,vec,gres,fi,dq,dk,dv,qw,kw,vw)


MESH = pl.DeviceIdType.MESH


class Place:
    def __init__(self, dp_total, fsdp_total):
        half = fsdp_total // 2
        self.outer_total = 4 if half % 4 == 0 else half
        self.inner_total = half // self.outer_total
        self.d = lax.axis_index("dp")
        self.f = lax.axis_index("fsdp")
        self.core = self.f % 2
        self.inner = (self.f // 2) % self.inner_total
        self.outer = self.f // (2 * self.inner_total)
        self.side = self.d % 2
        self.twin = self.d + 1 - 2 * self.side

    def index(self, outer, inner, core):
        return (outer * self.inner_total + inner) * 2 + core

    def slot(self, s, t, core=None):
        return self.index((self.outer + s) % self.outer_total, (self.inner + t) % self.inner_total,
                          self.core if core is None else core)

    def neighbours(self):
        out = [(self.d, self.slot(s, 0)) for s in range(1, self.outer_total)]
        out += [(self.d, self.slot(0, t)) for t in range(1, self.inner_total)]
        out += [(self.twin, self.f), (self.d, self.slot(0, 0, 1 - self.core))]
        return out


def greet(place):
    barrier = pltpu.get_barrier_semaphore()
    others = place.neighbours()
    for other in others:
        pl.semaphore_signal(barrier, inc=1, device_id=other, device_id_type=MESH)
    pl.semaphore_wait(barrier, len(others))


class Gather:
    def __init__(self, place, view, rows, edge, sems, base):
        self.place, self.view, self.rows, self.edge = place, view, rows, edge
        self.send_sem, self.recv_sem = sems
        A, B = place.outer_total, place.inner_total
        self.base = base
        self.keys = {}
        for s in range(1, A):
            self.keys["z", s] = len(self.keys)
        for s in range(A):
            for t in range(1, B):
                self.keys["x", s, t] = len(self.keys)
        if edge:
            for s in range(A):
                for t in range(B):
                    if s or t:
                        self.keys["y", s, t] = len(self.keys)
        for s in range(A):
            for t in range(B):
                self.keys["c", s, t] = len(self.keys)
        self.sent = []

    @staticmethod
    def count(A, B, edge):
        return (A - 1) + A * (B - 1) + (A * B - 1 if edge else 0) + A * B

    def part(self, slot, kind):
        if not self.edge:
            return self.view(slot, 0, self.rows)
        p = self.place.side
        if kind == "plane":
            return self.view(slot, p * self.edge, self.rows - self.edge)
        if kind == "mine":
            return self.view(slot, p * (self.rows - self.edge), self.edge)
        if kind == "theirs":
            return self.view(slot, (1 - p) * (self.rows - self.edge), self.edge)
        return self.view(slot, 0, self.rows)

    def copy(self, key, ref, to):
        i = self.base + self.keys[key]
        return pltpu.make_async_remote_copy(src_ref=ref, dst_ref=ref, send_sem=self.send_sem.at[i],
                                            recv_sem=self.recv_sem.at[i], device_id=to, device_id_type=MESH)

    def send(self, key, ref, to):
        c = self.copy(key, ref, to)
        c.start()
        self.sent.append(c)

    def got(self, key, ref):
        self.copy(key, ref, (self.place.d, self.place.f)).wait_recv()

    def start_outer(self):
        p = self.place
        for s in range(1, p.outer_total):
            self.send(("z", s), self.part(p.f, "plane"), (p.d, p.slot(-s, 0)))

    def pass_inner(self, s):
        p = self.place
        for t in range(1, p.inner_total):
            self.send(("x", s, t), self.part(p.slot(s, 0), "plane"), (p.d, p.slot(0, -t)))

    def pass_twin(self, s, t):
        p = self.place
        if self.edge:
            self.send(("y", s, t), self.part(p.slot(s, t), "mine"), (p.twin, p.f))

    def pass_core(self, s, t):
        p = self.place
        self.send(("c", s, t), self.part(p.slot(s, t), "all"), (p.d, p.slot(0, 0, 1 - p.core)))

    def start_inner(self):
        self.pass_inner(0)
        self.pass_core(0, 0)

    def from_outer(self):
        p = self.place
        for s in range(1, p.outer_total):
            self.got(("z", s), self.part(p.slot(s, 0), "plane"))
            self.pass_inner(s)
            self.pass_twin(s, 0)

    def from_inner(self):
        p = self.place
        for s in range(p.outer_total):
            for t in range(1, p.inner_total):
                self.got(("x", s, t), self.part(p.slot(s, t), "plane"))
                self.pass_twin(s, t)

    def from_twin(self):
        p = self.place
        for s in range(p.outer_total):
            for t in range(p.inner_total):
                if s or t:
                    if self.edge:
                        self.got(("y", s, t), self.part(p.slot(s, t), "theirs"))
                    self.pass_core(s, t)

    def from_core(self):
        p = self.place
        for s in range(p.outer_total):
            for t in range(p.inner_total):
                self.got(("c", s, t), self.part(p.slot(s, t, 1 - p.core), "all"))

    def finish(self):
        for c in self.sent:
            c.wait_send()


def local(src, dst, sem):
    c = pltpu.make_async_copy(src, dst, sem)
    c.start()
    return c


def gather_kernel(dp_total, fsdp_total, tokens_ref, small_ref, qo_ref, ko_ref, vo_ref, oo_ref, uo_ref, do_ref,
                  fi_ref, q_ref, k_ref, v_ref, vec_ref, qkv_all, o_all, up_all, down_all, small_all,
                  w_s, small_s, send_sem, recv_sem, loc_sem):
    place = Place(dp_total, fsdp_total)
    A, B = place.outer_total, place.inner_total
    n = fsdp_total
    own = qo_ref.shape[0]
    down_own = do_ref.shape[0]
    ff = uo_ref.shape[1]
    me = place.f
    greet(place)
    fill = [local(small_ref, small_all.at[me], loc_sem.at[0])]
    for i, r in enumerate((qo_ref, ko_ref, vo_ref)):
        fill.append(local(r, qkv_all.at[me, pl.ds(i * own, own)], loc_sem.at[1 + i]))
    fill.append(local(oo_ref, o_all.at[me], loc_sem.at[4]))
    fill.append(local(uo_ref, up_all.at[me], loc_sem.at[5]))
    fill.append(local(do_ref, down_all.at[me], loc_sem.at[6]))
    sems = (send_sem, recv_sem)
    third = own // 3

    def rows_view(ref, offset=0, cols=None):
        def view(slot, start, rows):
            at = pl.ds(pl.multiple_of(offset + start, 8), rows)
            return ref.at[slot, at] if cols is None else ref.at[slot, at, cols]
        return view

    specs = [(rows_view(small_all), small_all.shape[1], 0),
             (rows_view(qkv_all), 3 * own, own),
             (rows_view(o_all), own, third),
             (rows_view(up_all, 0, pl.ds(0, ff // 2)), own, third),
             (rows_view(up_all, 0, pl.ds(ff // 2, ff // 2)), own, third),
             (rows_view(down_all, 0), down_own // 2, down_own // 6),
             (rows_view(down_all, down_own // 2), down_own // 2, down_own // 6)]
    units = []
    base = 0
    for view, rows, edge in specs:
        units.append(Gather(place, view, rows, edge, sems, base))
        base += Gather.count(A, B, edge)
    for c in fill:
        c.wait()
    for u in units:
        u.start_outer()
    sm, u0, rest = units[0], units[1], units[2:]
    sm.start_inner()
    u0.start_inner()
    sm.from_outer()
    sm.from_inner()
    sm.from_twin()
    u0.from_outer()
    rest[0].start_inner()
    rest[1].start_inner()
    sm.from_core()
    cs = local(small_all, small_s, loc_sem.at[0])
    u0.from_inner()
    rest[0].from_outer()
    cs.wait()
    total = jnp.zeros(vec_ref.shape, f32)
    for i in range(n):
        total = total + small_s[i].astype(f32)
    vec_ref[...] = total
    u0.from_twin()
    rest[1].from_outer()
    u0.from_core()
    cw = local(qkv_all, w_s, loc_sem.at[1])
    rest[2].start_inner()
    rest[0].from_inner()
    cw.wait()
    rows = tokens_ref.shape[0]
    todo = [rest[2].from_outer, rest[0].from_twin, rest[1].from_inner, rest[3].start_inner,
            rest[3].from_outer, rest[1].from_twin, rest[0].from_core, rest[2].from_inner, rest[4].start_inner,
            rest[4].from_outer, rest[2].from_twin, rest[1].from_core, rest[3].from_inner, rest[3].from_twin,
            rest[4].from_inner, rest[2].from_core, rest[4].from_twin, rest[3].from_core, rest[4].from_core]
    gain = vec_ref[0:1, :]
    shift = vec_ref[1:2, :]
    qbias = vec_ref[2:3, :]
    vbias = vec_ref[3:4, :]
    feat = tokens_ref.shape[1]
    for i in range(rows // RB):
        sl = slice(i * RB, (i + 1) * RB)
        xhat, _ = norm_parts(tokens_ref[sl, :].astype(f32))
        fi = (xhat * gain + shift).astype(bf16)
        fi_ref[sl, :] = fi
        weight = lambda i: w_s[:, i * own:(i + 1) * own, :].reshape(feat, feat)
        q_ref[sl, :] = ((dot(fi, weight(0)) + qbias).astype(bf16).astype(f32) * 0.125).astype(bf16)
        k_ref[sl, :] = dot(fi, weight(1)).astype(bf16)
        v_ref[sl, :] = (dot(fi, weight(2)) + vbias).astype(bf16)
        for _ in range(2):
            todo.pop(0)()
    for t in todo:
        t()
    for u in units:
        u.finish()


def gather_project(sizes, tokens, small, qw, kw, vw, ow, up, down):
    dp_total, n = sizes
    rows, feat = tokens.shape
    own = qw.shape[0]
    half = n // 2
    A = 4 if half % 4 == 0 else half
    B = half // A
    copies = Gather.count(A, B, 0) + 6 * Gather.count(A, B, 1)
    s = jax.ShapeDtypeStruct
    vm = pl.BlockSpec(memory_space=pltpu.VMEM)
    anyspec = pl.BlockSpec(memory_space=pl.ANY)
    return pl.pallas_call(
        functools.partial(gather_kernel, dp_total, n),
        in_specs=[vm] * 8,
        out_specs=[vm] * 5 + [anyspec] * 5,
        out_shape=[s((rows, feat), bf16)] * 4 + [s(small.shape, f32), s((n, 3 * own, feat), bf16), s((n, own, feat), bf16),
                   s((n,) + up.shape, bf16), s((n,) + down.shape, bf16), s((n,) + small.shape, bf16)],
        scratch_shapes=[pltpu.VMEM((n, 3 * own, feat), bf16), pltpu.VMEM((n,) + small.shape, bf16),
                        pltpu.SemaphoreType.DMA((copies,)), pltpu.SemaphoreType.DMA((copies,)),
                        pltpu.SemaphoreType.DMA((8,))],
        compiler_params=pltpu.CompilerParams(collective_id=1, has_side_effects=True, vmem_limit_bytes=60 * 2**20),
        name="gather_project",
    )(tokens, small, qw, kw, vw, ow, up, down)

FSDP="fsdp"

def spread(vectors, index, total):
    own = vectors.shape[-1]
    at = lax.broadcasted_iota(jnp.int32, (1, total, own), 1)
    wide = jnp.where(at == index, vectors[:, None, :], jnp.zeros((), vectors.dtype))
    return wide.reshape(vectors.shape[0], total * own)

def on_device(sizes, tokens, image_counts, cotangent, first_gain, first_shift, query_weight, query_bias, key_weight,
              value_weight, value_bias, out_weight, out_bias, second_gain, second_shift, up_weight, up_bias,
              down_weight, down_bias):
    rows, feat = tokens.shape
    own = query_weight.shape[0]
    n = feat // own
    counts = image_counts[0]
    me = lax.axis_index(FSDP)
    eight = jnp.stack([first_gain, first_shift, query_bias, value_bias, out_bias, second_gain, second_shift, down_bias])
    small = jnp.concatenate([spread(eight, me, n), spread(up_bias[None], me, n).reshape(-1, feat)])
    small = jnp.concatenate([small, jnp.zeros((16 - small.shape[0], feat), bf16)])
    fi, q, k, v, vec, qkv_all, o_all, up_all, down_all, _ = gather_project(
        sizes, tokens, small, query_weight, key_weight, value_weight, out_weight, up_weight, down_weight)
    full = lambda i: qkv_all[:, i * own:(i + 1) * own].reshape(feat, feat)
    qw, kw, vw = full(0), full(1), full(2)
    ow = o_all.reshape(feat, feat)
    up = up_all.reshape(feat, -1)
    down = down_all.reshape(-1, feat)
    vec1 = vec[0:8]
    vec2 = vec[4:12]
    ub = vec[8:12].reshape(1, -1)
    mixed, lse = attn_fwd(counts, q, k, v)
    layer_out, gres, gmix, gup, gub, gdown, gout, gv2 = middle(counts, mixed, tokens, cotangent, ow, vec2, up, ub, down)
    dq, dk, dv = attn_bwd(counts, q, k, v, gmix, lse)
    gtok, gq, gk, gv, gv1 = project_back(tokens, vec1, gres, fi, dq, dk, dv, qw, kw, vw)
    scatter = lambda a: lax.psum_scatter(a, FSDP, scatter_dimension=0, tiled=False)
    pair = lambda a: lax.psum(a, "dp").astype(f32)
    su = scatter(gup.reshape(n, own, -1))
    sd = scatter(gdown.reshape(n, -1, feat))
    sa = scatter(jnp.stack([g.reshape(n, own, feat) for g in (gq, gk, gv, gout)], axis=1))
    smalls = jnp.concatenate([gv1[0:4], gv2[0:4]]).reshape(8, n, own)
    smalls = jnp.concatenate([jnp.transpose(smalls, (1, 0, 2)), gub.reshape(n, -1, own)], axis=1).astype(bf16)
    ss = scatter(smalls)
    su, sd, sa, ss = (pair(a) for a in (su, sd, sa, ss))
    return (layer_out, gtok, ss[0], ss[1], sa[0], ss[2], sa[1], sa[2], ss[3], sa[3], ss[7], ss[5], ss[6], su,
            ss[8:].reshape(-1), sd, ss[4])


def solution(mesh):
    rows = P(("dp", "fsdp"), None)
    mat = P("fsdp", None)
    vec = P("fsdp")
    return jax.shard_map(
        functools.partial(on_device, (mesh.shape["dp"], mesh.shape["fsdp"])),
        mesh=mesh,
        in_specs=(rows, rows, rows, vec, vec, mat, vec, mat, mat, vec, mat, vec, vec, vec, mat, vec, mat, vec),
        out_specs=(rows, rows, vec, vec, mat, vec, mat, mat, vec, mat, vec, vec, vec, mat, vec, mat, vec),
        check_vma=False,
    )
```

```python
import functools
import math

import jax
import jax.numpy as jnp
from jax import lax
from jax.experimental import pallas as pl
from jax.experimental.pallas import tpu as pltpu
from jax.sharding import PartitionSpec as P

EPS = 1e-06
NT = (((1,), (1,)), ((), ()))
TN = (((0,), (0,)), ((), ()))


SMALL_ROWS=197; LARGE_ROWS=325
QB=256
KB=128
NEG=-1e30

def image_ends(small, large, rows):
    ends=[]
    for i in range(1, rows//SMALL_ROWS+1):
        e = jnp.minimum(i, small)*SMALL_ROWS + jnp.maximum(i-small,0)*LARGE_ROWS
        ends.append(jnp.where(i<=small+large, e, 2*rows))
    return ends

def image_of(places, ends):
    idx = jnp.zeros(places.shape, jnp.int32)
    for e in ends:
        idx = idx + (places>=e).astype(jnp.int32)
    return idx

def key_range(ends, first, last, rows):
    lo = jnp.int32(0); hi = jnp.int32(rows)
    for e in ends:
        lo = jnp.maximum(lo, jnp.where(e<=first, e, 0))
        hi = jnp.minimum(hi, jnp.where(e>last, e, rows))
    return lo, hi

def widths_of(rows):
    ws = [w*KB for w in range(3, rows//KB)]
    ws = [w for w in ws if w<=768]
    return ws+[rows]

def with_window(counts_ref, rows, first, body):
    small=counts_ref[0]; large=counts_ref[1]
    ends=image_ends(small, large, rows)
    lo,hi=key_range(ends, first, first+QB-1, rows)
    base=lo//KB
    need=(hi+KB-1)//KB - base
    done=jnp.int32(0)
    for w in widths_of(rows):
        n=w//KB
        use = (need<=n) & (need>done)
        start = jnp.minimum(base, (rows-w)//KB)*KB
        @pl.when(use)
        def _(start=start, w=w):
            body(pl.multiple_of(start,KB), w, ends)
        done=jnp.int32(n)

def fwd_kernel(counts_ref, q_ref, k_ref, v_ref, o_ref, lse_ref):
    rows=q_ref.shape[0]
    lane=lax.broadcasted_iota(jnp.int32,(QB,128),1)
    def block(b, _):
        first=pl.multiple_of(b*QB,QB)
        def body(start, w, ends):
            q=q_ref[pl.ds(first,QB),:]
            k=k_ref[pl.ds(start,w),:]
            v=v_ref[pl.ds(start,w),:]
            rid=image_of(first+lax.broadcasted_iota(jnp.int32,(QB,1),0), ends)
            cid=image_of(start+lax.broadcasted_iota(jnp.int32,(1,w),1), ends)
            bias=jnp.where(rid==cid, 0.0, NEG)
            outs=[];lses=[]
            for e in range(2):
                qm=jnp.where((lane<64)==(e==0), q, jnp.zeros_like(q))
                s=lax.dot_general(qm,k,(((1,),(1,)),((),())),preferred_element_type=jnp.float32)+bias
                m=jnp.max(s,axis=1,keepdims=True)
                p=jnp.exp(s-m)
                l=jnp.sum(p,axis=1,keepdims=True)
                o=jnp.dot(p.astype(jnp.bfloat16),v,preferred_element_type=jnp.float32)
                outs.append(o*(1.0/l)); lses.append(m+jnp.log(l))
            o_ref[pl.ds(first,QB),:]=jnp.where(lane<64,outs[0],outs[1]).astype(jnp.bfloat16)
            both=jnp.where(lane<64,jnp.broadcast_to(lses[0],(QB,128)),jnp.broadcast_to(lses[1],(QB,128)))
            t=both.T
            lse_ref[0,0:1,pl.ds(first,QB)]=t[0:1,:]
            lse_ref[0,1:2,pl.ds(first,QB)]=t[64:65,:]
        with_window(counts_ref, rows, first, body)
        return 0
    lax.fori_loop(0,rows//QB,block,0)

def attn_fwd(counts,q,k,v):
    rows,feat=q.shape
    pairs=feat//128
    spec=pl.BlockSpec((rows,128),lambda p,c:(0,p))
    return pl.pallas_call(fwd_kernel,
        grid_spec=pltpu.PrefetchScalarGridSpec(num_scalar_prefetch=1,grid=(pairs,),
            in_specs=[spec]*3,out_specs=[spec,pl.BlockSpec((1,2,rows),lambda p,c:(p,0,0))]),
        out_shape=[jax.ShapeDtypeStruct((rows,feat),jnp.bfloat16),jax.ShapeDtypeStruct((pairs,2,rows),jnp.float32)],
        name="attend",
        )(counts,q,k,v)

def bwd_kernel(counts_ref, q_ref, k_ref, v_ref, do_ref, lse_ref, dq_ref, dk_ref, dv_ref, dk_acc, dv_acc):
    rows=q_ref.shape[0]
    lane=lax.broadcasted_iota(jnp.int32,(QB,128),1)
    dk_acc[...]=jnp.zeros_like(dk_acc)
    dv_acc[...]=jnp.zeros_like(dv_acc)
    nt=(((1,),(1,)),((),()))
    tn=(((0,),(0,)),((),()))
    def block(b,_):
        first=pl.multiple_of(b*QB,QB)
        def body(start,w,ends):
            q=q_ref[pl.ds(first,QB),:]
            do=do_ref[pl.ds(first,QB),:]
            k=k_ref[pl.ds(start,w),:]
            v=v_ref[pl.ds(start,w),:]
            rid=image_of(start+lax.broadcasted_iota(jnp.int32,(w,1),0), ends)
            cid=image_of(first+lax.broadcasted_iota(jnp.int32,(1,QB),1), ends)
            bias=jnp.where(rid==cid,0.0,NEG)
            dqs=[]
            dks=None;dvs=None
            for e in range(2):
                mask=(lane<64)==(e==0)
                qm=jnp.where(mask,q,jnp.zeros_like(q))
                dom=jnp.where(mask,do,jnp.zeros_like(do))
                s=lax.dot_general(k,qm,nt,preferred_element_type=jnp.float32)+bias
                p=jnp.exp(s-lse_ref[0,e:e+1,pl.ds(first,QB)])
                dp=lax.dot_general(v,dom,nt,preferred_element_type=jnp.float32)
                delta=jnp.sum(p*dp,axis=0,keepdims=True)
                ds=(p*(dp-delta)).astype(jnp.bfloat16)
                pb=p.astype(jnp.bfloat16)
                dv_e=jnp.dot(pb,dom,preferred_element_type=jnp.float32)
                dk_e=jnp.dot(ds,qm,preferred_element_type=jnp.float32)
                dq_e=lax.dot_general(ds,k,tn,preferred_element_type=jnp.float32)
                dvs=dv_e if dvs is None else dvs+dv_e
                dks=dk_e if dks is None else dks+dk_e
                dqs.append(dq_e)
            dv_acc[pl.ds(start,w),:]+=dvs
            dk_acc[pl.ds(start,w),:]+=dks
            dq_ref[pl.ds(first,QB),:]=(jnp.where(lane<64,dqs[0],dqs[1])*0.125).astype(jnp.bfloat16)
        with_window(counts_ref,rows,first,body)
        return 0
    lax.fori_loop(0,rows//QB,block,0)
    dk_ref[...]=dk_acc[...].astype(jnp.bfloat16)
    dv_ref[...]=dv_acc[...].astype(jnp.bfloat16)

def attn_bwd(counts,q,k,v,do,lse):
    rows,feat=q.shape
    pairs=feat//128
    spec=pl.BlockSpec((rows,128),lambda p,c:(0,p))
    return pl.pallas_call(bwd_kernel,
        grid_spec=pltpu.PrefetchScalarGridSpec(num_scalar_prefetch=1,grid=(pairs,),
            in_specs=[spec]*4+[pl.BlockSpec((1,2,rows),lambda p,c:(p,0,0))],out_specs=[spec]*3,
            scratch_shapes=[pltpu.VMEM((rows,128),jnp.float32)]*2),
        out_shape=[jax.ShapeDtypeStruct((rows,feat),jnp.bfloat16)]*3,
        name="attend_back",
        )(counts,q,k,v,do,lse)

f32=jnp.float32; bf16=jnp.bfloat16
RB=256
INV_SQRT2=1/math.sqrt(2.0); INV_SQRT2PI=1/math.sqrt(2*math.pi)

def dot(a,b): return jnp.dot(a,b,preferred_element_type=f32)
def dot_nt(a,b): return lax.dot_general(a,b,NT,preferred_element_type=f32)
def dot_tn(a,b): return lax.dot_general(a,b,TN,preferred_element_type=f32)

def norm_parts(x):
    mean=jnp.mean(x,axis=-1,keepdims=True)
    cen=x-mean
    var=jnp.mean(cen*cen,axis=-1,keepdims=True)
    q=lax.rsqrt(var+EPS)
    return cen*q, q

def live_mask(counts_ref, first, n):
    end=counts_ref[0]*197+counts_ref[1]*325
    r=first+lax.broadcasted_iota(jnp.int32,(n,1),0)
    return r<end

def mid_kernel(counts_ref, mixed_ref, tokens_ref, cot_ref, outw_ref, vec_ref, up_ref, ub_ref, down_ref,
        layer_ref, gres_ref, gmix_ref, gup_ref, gub_ref, gdown_ref, gout_ref, gvec_ref,
        res_s, si_s, gb_s, accout_s, accgs_s, hid_s, gi_s):
    rows=tokens_ref.shape[0]
    j=pl.program_id(0); nj=pl.num_programs(0)
    obias=vec_ref[0:1,:]; gain=vec_ref[1:2,:]; shift=vec_ref[2:3,:]; dbias=vec_ref[3:4,:]
    @pl.when(j==0)
    def _():
        def step(i,_):
            first=pl.multiple_of(i*RB,RB); sl=pl.ds(first,RB)
            res=tokens_ref[sl,:].astype(f32)+(dot(mixed_ref[sl,:],outw_ref[...])+obias)
            res_s[sl,:]=res
            xhat,_q=norm_parts(res)
            si_s[sl,:]=(xhat*gain+shift).astype(bf16)
            live=live_mask(counts_ref,first,RB)
            gb_s[sl,:]=jnp.where(live,cot_ref[sl,:],jnp.zeros((),bf16))
            return 0
        lax.fori_loop(0,rows//RB,step,0)
        accout_s[...]=jnp.zeros_like(accout_s)
        accgs_s[...]=jnp.zeros_like(accgs_s)
    gub=jnp.zeros(gub_ref.shape,f32)
    for i in range(rows//RB):
        sl=slice(i*RB,(i+1)*RB)
        pre=dot(si_s[sl,:],up_ref[...])+ub_ref[...]
        cdf=0.5+0.5*lax.erf(pre*INV_SQRT2)
        pdf=jnp.exp(-0.5*pre*pre)*INV_SQRT2PI
        hid_s[sl,:]=(pre*cdf).astype(bf16)
        gh=dot_nt(gb_s[sl,:],down_ref[...])
        gi=(gh*(cdf+pre*pdf)).astype(bf16)
        gi_s[sl,:]=gi
        gub=gub+jnp.sum(gi.astype(f32),axis=0,keepdims=True)
    gub_ref[...]=gub
    accout_s[...]+=dot(hid_s[...],down_ref[...])
    accgs_s[...]+=dot_nt(gi_s[...],up_ref[...])
    gdown_ref[...]=dot_tn(hid_s[...],gb_s[...]).astype(bf16)
    gup_ref[...]=dot_tn(si_s[...],gi_s[...]).astype(bf16)
    @pl.when(j==nj-1)
    def _():
        gvec_ref[...]=jnp.zeros_like(gvec_ref)
        def step(i,_):
            first=pl.multiple_of(i*RB,RB); sl=pl.ds(first,RB)
            live=live_mask(counts_ref,first,RB)
            res=res_s[sl,:]
            layer=res+(accout_s[sl,:]+dbias)
            layer_ref[sl,:]=jnp.where(live,layer,0.0).astype(bf16)
            xhat,q=norm_parts(res)
            gs=accgs_s[sl,:]
            t=gs*gain
            gb=gb_s[sl,:].astype(f32)
            gres=gb+q*(t-jnp.mean(t,axis=-1,keepdims=True)-xhat*jnp.mean(t*xhat,axis=-1,keepdims=True))
            gres_ref[sl,:]=gres
            ga=gres.astype(bf16)
            mixed_unused=None
            si_s[sl,:]=ga
            gvec_ref[0:1,:]+=jnp.sum(gb,axis=0,keepdims=True)
            gvec_ref[1:2,:]+=jnp.sum(gs*xhat,axis=0,keepdims=True)
            gvec_ref[2:3,:]+=jnp.sum(gs,axis=0,keepdims=True)
            gvec_ref[3:4,:]+=jnp.sum(ga.astype(f32),axis=0,keepdims=True)
            gmix_ref[sl,:]=dot_nt(ga,outw_ref[...]).astype(bf16)
            return 0
        lax.fori_loop(0,rows//RB,step,0)
        gout_ref[...]=dot_tn(mixed_ref[...],si_s[...]).astype(bf16)

def middle(counts,mixed,tokens,cot,outw,vec,up,ub,down,FB=512):
    rows,D=tokens.shape; FF=up.shape[1]
    nj=FF//FB
    full=lambda a: pl.BlockSpec(a.shape,lambda j,c:(0,)*len(a.shape),pipeline_mode=pl.Buffered(1))
    fo=lambda s: pl.BlockSpec(s,lambda j,c:(0,)*len(s),pipeline_mode=pl.Buffered(1))
    return pl.pallas_call(mid_kernel,
        grid_spec=pltpu.PrefetchScalarGridSpec(num_scalar_prefetch=1,grid=(nj,),
            in_specs=[full(mixed),full(tokens),full(cot),full(outw),full(vec),
                pl.BlockSpec((D,FB),lambda j,c:(0,j)),pl.BlockSpec((1,FB),lambda j,c:(0,j)),pl.BlockSpec((FB,D),lambda j,c:(j,0))],
            out_specs=[fo((rows,D)),fo((rows,D)),fo((rows,D)),
                pl.BlockSpec((D,FB),lambda j,c:(0,j)),pl.BlockSpec((1,FB),lambda j,c:(0,j)),pl.BlockSpec((FB,D),lambda j,c:(j,0)),
                fo((D,D)),fo((8,D))],
            scratch_shapes=[pltpu.VMEM((rows,D),f32),pltpu.VMEM((rows,D),bf16),pltpu.VMEM((rows,D),bf16),
                pltpu.VMEM((rows,D),f32),pltpu.VMEM((rows,D),f32),pltpu.VMEM((rows,FB),bf16),pltpu.VMEM((rows,FB),bf16)]),
        out_shape=[jax.ShapeDtypeStruct((rows,D),bf16),jax.ShapeDtypeStruct((rows,D),f32),jax.ShapeDtypeStruct((rows,D),bf16),
            jax.ShapeDtypeStruct((D,FF),bf16),jax.ShapeDtypeStruct((1,FF),f32),jax.ShapeDtypeStruct((FF,D),bf16),
            jax.ShapeDtypeStruct((D,D),bf16),jax.ShapeDtypeStruct((8,D),f32)],
        compiler_params=pltpu.CompilerParams(vmem_limit_bytes=60*2**20),
        name="feed_forward",
        )(counts,mixed,tokens,cot,outw,vec,up,ub,down)


def qkv_kernel(tokens_ref, vec_ref, qw_ref, kw_ref, vw_ref, fi_ref, q_ref, k_ref, v_ref):
    rows=tokens_ref.shape[0]
    gain=vec_ref[0:1,:]; shift=vec_ref[1:2,:]; qb=vec_ref[2:3,:]; vb=vec_ref[3:4,:]
    for i in range(rows//RB):
        sl=slice(i*RB,(i+1)*RB)
        xhat,_=norm_parts(tokens_ref[sl,:].astype(f32))
        fi=(xhat*gain+shift).astype(bf16)
        fi_ref[sl,:]=fi
        q_ref[sl,:]=((dot(fi,qw_ref[...])+qb).astype(bf16).astype(f32)*0.125).astype(bf16)
        k_ref[sl,:]=dot(fi,kw_ref[...]).astype(bf16)
        v_ref[sl,:]=(dot(fi,vw_ref[...])+vb).astype(bf16)

def project(tokens,vec,qw,kw,vw):
    rows,D=tokens.shape
    return pl.pallas_call(qkv_kernel,out_shape=[jax.ShapeDtypeStruct((rows,D),bf16)]*4,
        compiler_params=pltpu.CompilerParams(vmem_limit_bytes=60*2**20),name="project")(tokens,vec,qw,kw,vw)

def back_kernel(tokens_ref, vec_ref, gres_ref, fi_ref, dq_ref, dk_ref, dv_ref, qw_ref, kw_ref, vw_ref,
        gtok_ref, gq_ref, gk_ref, gv_ref, gvec_ref):
    rows=tokens_ref.shape[0]
    gain=vec_ref[0:1,:]
    gvec=[jnp.zeros((1,tokens_ref.shape[1]),f32)]*4
    for i in range(rows//RB):
        sl=slice(i*RB,(i+1)*RB)
        dq=dq_ref[sl,:];dk=dk_ref[sl,:];dv=dv_ref[sl,:]
        gs=dot_nt(dq,qw_ref[...])+dot_nt(dk,kw_ref[...])+dot_nt(dv,vw_ref[...])
        xhat,q=norm_parts(tokens_ref[sl,:].astype(f32))
        t=gs*gain
        gtok_ref[sl,:]=gres_ref[sl,:]+q*(t-jnp.mean(t,axis=-1,keepdims=True)-xhat*jnp.mean(t*xhat,axis=-1,keepdims=True))
        for n,a in enumerate((gs*xhat,gs,dq.astype(f32),dv.astype(f32))):
            gvec[n]=gvec[n]+jnp.sum(a,axis=0,keepdims=True)
    gvec_ref[...]=jnp.zeros_like(gvec_ref)
    for n in range(4): gvec_ref[n:n+1,:]=gvec[n]
    fi=fi_ref[...]
    gq_ref[...]=dot_tn(fi,dq_ref[...]).astype(bf16)
    gk_ref[...]=dot_tn(fi,dk_ref[...]).astype(bf16)
    gv_ref[...]=dot_tn(fi,dv_ref[...]).astype(bf16)

def project_back(tokens,vec,gres,fi,dq,dk,dv,qw,kw,vw):
    rows,D=tokens.shape
    s=jax.ShapeDtypeStruct
    return pl.pallas_call(back_kernel,out_shape=[s((rows,D),f32),s((D,D),bf16),s((D,D),bf16),s((D,D),bf16),s((8,D),f32)],
        compiler_params=pltpu.CompilerParams(vmem_limit_bytes=60*2**20),name="project_back")(tokens,vec,gres,fi,dq,dk,dv,qw,kw,vw)


MESH = pl.DeviceIdType.MESH


class Place:
    def __init__(self, dp_total, fsdp_total):
        half = fsdp_total // 2
        self.outer_total = 4 if half % 4 == 0 else half
        self.inner_total = half // self.outer_total
        self.d = lax.axis_index("dp")
        self.f = lax.axis_index("fsdp")
        self.core = self.f % 2
        self.inner = (self.f // 2) % self.inner_total
        self.outer = self.f // (2 * self.inner_total)
        self.side = self.d % 2
        self.twin = self.d + 1 - 2 * self.side
        self.pairs = dp_total // 2

    def index(self, outer, inner, core):
        return (outer * self.inner_total + inner) * 2 + core

    def slot(self, s, t, core=None):
        return self.index((self.outer + s) % self.outer_total, (self.inner + t) % self.inner_total,
                          self.core if core is None else core)

    def neighbours(self):
        out = [(self.d, self.slot(s, 0)) for s in range(1, self.outer_total)]
        out += [(self.d, self.slot(0, t)) for t in range(1, self.inner_total)]
        out += [(self.twin, self.f), (self.d, self.slot(0, 0, 1 - self.core))]
        return out


def greet(place):
    barrier = pltpu.get_barrier_semaphore()
    others = place.neighbours()
    for other in others:
        pl.semaphore_signal(barrier, inc=1, device_id=other, device_id_type=MESH)
    pl.semaphore_wait(barrier, len(others))


class Gather:
    def __init__(self, place, view, rows, edge, sems, base):
        self.place, self.view, self.rows, self.edge = place, view, rows, edge
        self.send_sem, self.recv_sem = sems
        A, B = place.outer_total, place.inner_total
        self.base = base
        self.keys = {}
        for s in range(1, A):
            self.keys["z", s] = len(self.keys)
        for s in range(A):
            for t in range(1, B):
                self.keys["x", s, t] = len(self.keys)
        if edge:
            for s in range(A):
                for t in range(B):
                    if s or t:
                        self.keys["y", s, t] = len(self.keys)
        for s in range(A):
            for t in range(B):
                self.keys["c", s, t] = len(self.keys)
        self.sent = []

    @staticmethod
    def count(A, B, edge):
        return (A - 1) + A * (B - 1) + (A * B - 1 if edge else 0) + A * B

    def part(self, slot, kind):
        if not self.edge:
            return self.view(slot, 0, self.rows)
        p = self.place.side
        if kind == "plane":
            return self.view(slot, p * self.edge, self.rows - self.edge)
        if kind == "mine":
            return self.view(slot, p * (self.rows - self.edge), self.edge)
        if kind == "theirs":
            return self.view(slot, (1 - p) * (self.rows - self.edge), self.edge)
        return self.view(slot, 0, self.rows)

    def copy(self, key, ref, to):
        i = self.base + self.keys[key]
        return pltpu.make_async_remote_copy(src_ref=ref, dst_ref=ref, send_sem=self.send_sem.at[i],
                                            recv_sem=self.recv_sem.at[i], device_id=to, device_id_type=MESH)

    def send(self, key, ref, to):
        c = self.copy(key, ref, to)
        c.start()
        self.sent.append(c)

    def got(self, key, ref):
        self.copy(key, ref, (self.place.d, self.place.f)).wait_recv()

    def start_outer(self):
        p = self.place
        for s in range(1, p.outer_total):
            self.send(("z", s), self.part(p.f, "plane"), (p.d, p.slot(-s, 0)))

    def pass_inner(self, s):
        p = self.place
        for t in range(1, p.inner_total):
            self.send(("x", s, t), self.part(p.slot(s, 0), "plane"), (p.d, p.slot(0, -t)))

    def pass_twin(self, s, t):
        p = self.place
        if self.edge:
            self.send(("y", s, t), self.part(p.slot(s, t), "mine"), (p.twin, p.f))

    def pass_core(self, s, t):
        p = self.place
        self.send(("c", s, t), self.part(p.slot(s, t), "all"), (p.d, p.slot(0, 0, 1 - p.core)))

    def start_inner(self):
        self.pass_inner(0)
        self.pass_core(0, 0)

    def from_outer(self):
        p = self.place
        for s in range(1, p.outer_total):
            self.got(("z", s), self.part(p.slot(s, 0), "plane"))
            self.pass_inner(s)
            self.pass_twin(s, 0)

    def from_inner(self):
        p = self.place
        for s in range(p.outer_total):
            for t in range(1, p.inner_total):
                self.got(("x", s, t), self.part(p.slot(s, t), "plane"))
                self.pass_twin(s, t)

    def from_twin(self):
        p = self.place
        for s in range(p.outer_total):
            for t in range(p.inner_total):
                if s or t:
                    if self.edge:
                        self.got(("y", s, t), self.part(p.slot(s, t), "theirs"))
                    self.pass_core(s, t)

    def from_core(self):
        p = self.place
        for s in range(p.outer_total):
            for t in range(p.inner_total):
                self.got(("c", s, t), self.part(p.slot(s, t, 1 - p.core), "all"))

    def finish(self):
        for c in self.sent:
            c.wait_send()


def local(src, dst, sem):
    c = pltpu.make_async_copy(src, dst, sem)
    c.start()
    return c


def gather_kernel(dp_total, fsdp_total, tokens_ref, small_ref, qo_ref, ko_ref, vo_ref, oo_ref, uo_ref, do_ref,
                  fi_ref, q_ref, k_ref, v_ref, vec_ref, qkv_all, o_all, up_all, down_all, small_all,
                  w_s, small_s, send_sem, recv_sem, loc_sem):
    place = Place(dp_total, fsdp_total)
    A, B = place.outer_total, place.inner_total
    n = fsdp_total
    own = qo_ref.shape[0]
    down_own = do_ref.shape[0]
    ff = uo_ref.shape[1]
    me = place.f
    greet(place)
    fill = [local(small_ref, small_all.at[me], loc_sem.at[0])]
    for i, r in enumerate((qo_ref, ko_ref, vo_ref)):
        fill.append(local(r, qkv_all.at[me, pl.ds(i * own, own)], loc_sem.at[1 + i]))
    fill.append(local(oo_ref, o_all.at[me], loc_sem.at[4]))
    fill.append(local(uo_ref, up_all.at[me], loc_sem.at[5]))
    fill.append(local(do_ref, down_all.at[me], loc_sem.at[6]))
    sems = (send_sem, recv_sem)
    third = own // 3

    def rows_view(ref, offset=0, cols=None):
        def view(slot, start, rows):
            at = pl.ds(pl.multiple_of(offset + start, 8), rows)
            return ref.at[slot, at] if cols is None else ref.at[slot, at, cols]
        return view

    specs = [(rows_view(small_all), small_all.shape[1], 0),
             (rows_view(qkv_all), 3 * own, own),
             (rows_view(o_all), own, third),
             (rows_view(up_all, 0, pl.ds(0, ff // 2)), own, third),
             (rows_view(up_all, 0, pl.ds(ff // 2, ff // 2)), own, third),
             (rows_view(down_all, 0), down_own // 2, down_own // 6),
             (rows_view(down_all, down_own // 2), down_own // 2, down_own // 6)]
    units = []
    base = 0
    for view, rows, edge in specs:
        units.append(Gather(place, view, rows, edge, sems, base))
        base += Gather.count(A, B, edge)
    for c in fill:
        c.wait()
    for u in units:
        u.start_outer()
    sm, u0, rest = units[0], units[1], units[2:]
    sm.start_inner()
    u0.start_inner()
    sm.from_outer()
    sm.from_inner()
    sm.from_twin()
    u0.from_outer()
    rest[0].start_inner()
    rest[1].start_inner()
    sm.from_core()
    cs = local(small_all, small_s, loc_sem.at[0])
    u0.from_inner()
    rest[0].from_outer()
    cs.wait()
    total = jnp.zeros(vec_ref.shape, f32)
    for i in range(n):
        total = total + small_s[i].astype(f32)
    vec_ref[...] = total
    u0.from_twin()
    rest[1].from_outer()
    u0.from_core()
    cw = local(qkv_all, w_s, loc_sem.at[1])
    rest[2].start_inner()
    rest[0].from_inner()
    cw.wait()
    rows = tokens_ref.shape[0]
    todo = [rest[2].from_outer, rest[0].from_twin, rest[1].from_inner, rest[3].start_inner,
            rest[3].from_outer, rest[1].from_twin, rest[0].from_core, rest[2].from_inner, rest[4].start_inner,
            rest[4].from_outer, rest[2].from_twin, rest[1].from_core, rest[3].from_inner, rest[3].from_twin,
            rest[4].from_inner, rest[2].from_core, rest[4].from_twin, rest[3].from_core, rest[4].from_core]
    gain = vec_ref[0:1, :]
    shift = vec_ref[1:2, :]
    qbias = vec_ref[2:3, :]
    vbias = vec_ref[3:4, :]
    feat = tokens_ref.shape[1]
    for i in range(rows // RB):
        sl = slice(i * RB, (i + 1) * RB)
        xhat, _ = norm_parts(tokens_ref[sl, :].astype(f32))
        fi = (xhat * gain + shift).astype(bf16)
        fi_ref[sl, :] = fi
        weight = lambda i: w_s[:, i * own:(i + 1) * own, :].reshape(feat, feat)
        q_ref[sl, :] = ((dot(fi, weight(0)) + qbias).astype(bf16).astype(f32) * 0.125).astype(bf16)
        k_ref[sl, :] = dot(fi, weight(1)).astype(bf16)
        v_ref[sl, :] = (dot(fi, weight(2)) + vbias).astype(bf16)
        for _ in range(2):
            todo.pop(0)()
    for t in todo:
        t()
    for u in units:
        u.finish()


def gather_project(sizes, tokens, small, qw, kw, vw, ow, up, down):
    dp_total, n = sizes
    rows, feat = tokens.shape
    own = qw.shape[0]
    half = n // 2
    A = 4 if half % 4 == 0 else half
    B = half // A
    copies = Gather.count(A, B, 0) + 6 * Gather.count(A, B, 1)
    s = jax.ShapeDtypeStruct
    vm = pl.BlockSpec(memory_space=pltpu.VMEM)
    anyspec = pl.BlockSpec(memory_space=pl.ANY)
    return pl.pallas_call(
        functools.partial(gather_kernel, dp_total, n),
        in_specs=[vm] * 8,
        out_specs=[vm] * 5 + [anyspec] * 5,
        out_shape=[s((rows, feat), bf16)] * 4 + [s(small.shape, f32), s((n, 3 * own, feat), bf16), s((n, own, feat), bf16),
                   s((n,) + up.shape, bf16), s((n,) + down.shape, bf16), s((n,) + small.shape, bf16)],
        scratch_shapes=[pltpu.VMEM((n, 3 * own, feat), bf16), pltpu.VMEM((n,) + small.shape, bf16),
                        pltpu.SemaphoreType.DMA((copies,)), pltpu.SemaphoreType.DMA((copies,)),
                        pltpu.SemaphoreType.DMA((8,))],
        compiler_params=pltpu.CompilerParams(collective_id=1, has_side_effects=True, vmem_limit_bytes=60 * 2**20),
        name="gather_project",
    )(tokens, small, qw, kw, vw, ow, up, down)


def plan_neighbours(place):
    out = place.neighbours()
    out += [(place.side + 2 * ((place.d // 2 + k) % place.pairs), place.f) for k in range(1, place.pairs)]
    return out


def greet_all(place):
    barrier = pltpu.get_barrier_semaphore()
    others = plan_neighbours(place)
    for other in others:
        pl.semaphore_signal(barrier, inc=1, device_id=other, device_id_type=MESH)
    pl.semaphore_wait(barrier, len(others))


def scatter_copies(A, B, pairs):
    return 1 + 1 + (B - 1) + (A - 1) + 1 + (pairs - 1)


def scatter_shapes(A, B, pairs, rows, width, edge):
    out = [pltpu.VMEM((A, B, rows, width), bf16), pltpu.VMEM((A, B, rows, edge), bf16),
           pltpu.VMEM((B - 1, A, rows, width), bf16), pltpu.VMEM((A - 1, rows, width), bf16),
           pltpu.VMEM((rows, width), bf16)]
    if pairs > 1:
        out += [pltpu.VMEM((rows, width), bf16), pltpu.VMEM((pairs - 1, rows, width), bf16)]
    return out


class Scatter:
    def __init__(self, place, terms, bufs, edge, out, sems, base):
        self.place, self.terms, self.edge, self.out = place, terms, edge, out
        self.sums, self.from_twin_buf, self.from_inner_buf, self.from_outer_buf, self.last_buf = bufs[:5]
        self.pair_bufs = bufs[5:]
        self.width = terms.shape[-1]
        self.rows = terms.shape[-2]
        self.send_sem, self.recv_sem = sems
        self.base = base
        self.sent = []
        p = place.side
        e, w = edge, self.width
        at = lambda start, size: pl.ds(pl.multiple_of(start, 128), size)
        self.plane = at(p * e, w - e)
        self.mine = at(p * (w - e), e)
        self.theirs = at((1 - p) * (w - e), e)
        self.twin_plane = at((1 - p) * e, w - e)
        self.middle = pl.ds(e, w - 2 * e)

    def copy(self, i, src, dst, to):
        return pltpu.make_async_remote_copy(src_ref=src, dst_ref=dst, send_sem=self.send_sem.at[self.base + i],
                                            recv_sem=self.recv_sem.at[self.base + i], device_id=to, device_id_type=MESH)

    def send(self, i, src, dst, to):
        c = self.copy(i, src, dst, to)
        c.start()
        self.sent.append(c)

    def got(self, i, dst):
        self.copy(i, dst, dst, (self.place.d, self.place.f)).wait_recv()

    def start(self):
        p = self.place
        self.send(0, self.terms.at[:, :, 1 - p.core], self.sums, (p.d, p.slot(0, 0, 1 - p.core)))

    def from_core(self):
        p = self.place
        self.got(0, self.sums)
        B = p.inner_total

        def add(i, _):
            a, b = i // B, i % B
            self.sums[a, b] = (self.sums[a, b].astype(f32) + self.terms[a, b, p.core].astype(f32)).astype(bf16)
            return 0

        lax.fori_loop(0, p.outer_total * B, add, 0)
        self.send(1, self.sums.at[:, :, :, self.theirs], self.from_twin_buf, (p.twin, p.f))

    def from_twin(self):
        p = self.place
        B = p.inner_total
        self.got(1, self.from_twin_buf)

        def add(i, _):
            a, b = i // B, i % B
            self.sums[a, b, :, self.mine] = (self.sums[a, b, :, self.mine].astype(f32)
                                             + self.from_twin_buf[a, b].astype(f32)).astype(bf16)
            return 0

        lax.fori_loop(0, p.outer_total * B, add, 0)
        for t in range(1, B):
            to = (p.inner + B - t) % B
            self.send(1 + t, self.sums.at[:, to, :, self.plane], self.from_inner_buf.at[t - 1, :, :, self.plane],
                      (p.d, p.slot(0, -t)))

    def from_inner(self):
        p = self.place
        A, B = p.outer_total, p.inner_total
        for t in range(1, B):
            self.got(1 + t, self.from_inner_buf.at[t - 1, :, :, self.plane])

        def add(a, _):
            total = self.sums[a, p.inner, :, self.plane].astype(f32)
            for t in range(1, B):
                total = total + self.from_inner_buf[t - 1, a, :, self.plane].astype(f32)
            self.sums[a, p.inner, :, self.plane] = total.astype(bf16)
            return 0

        lax.fori_loop(0, A, add, 0)
        for s in range(1, A):
            to = (p.outer + A - s) % A
            self.send(B + s, self.sums.at[to, p.inner, :, self.plane], self.from_outer_buf.at[s - 1, :, self.plane],
                      (p.d, p.slot(-s, 0)))

    def from_outer(self):
        p = self.place
        A, B = p.outer_total, p.inner_total
        for s in range(1, A):
            self.got(B + s, self.from_outer_buf.at[s - 1, :, self.plane])
        total = self.sums[p.outer, p.inner, :, self.plane].astype(f32)
        for s in range(1, A):
            total = total + self.from_outer_buf[s - 1, :, self.plane].astype(f32)
        self.sums[p.outer, p.inner, :, self.plane] = total.astype(bf16)
        self.send(A + B, self.sums.at[p.outer, p.inner, :, self.plane], self.last_buf.at[:, self.plane],
                  (p.twin, p.f))

    def from_last(self):
        p = self.place
        A, B = p.outer_total, p.inner_total
        self.got(A + B, self.last_buf.at[:, self.twin_plane])
        own = lambda cols: self.sums[p.outer, p.inner, :, cols].astype(f32)
        last = lambda cols: self.last_buf[:, cols].astype(f32)
        if p.pairs == 1:
            self.out[:, self.mine] = own(self.mine)
            self.out[:, self.middle] = own(self.middle) + last(self.middle)
            self.out[:, self.theirs] = last(self.theirs)
            return
        half, others = self.pair_bufs
        half[:, self.mine] = own(self.mine).astype(bf16)
        half[:, self.middle] = (own(self.middle) + last(self.middle)).astype(bf16)
        half[:, self.theirs] = last(self.theirs).astype(bf16)
        for k in range(1, p.pairs):
            to = p.side + 2 * ((p.d // 2 + p.pairs - k) % p.pairs)
            self.send(A + B + k, half, others.at[k - 1], (to, p.f))

    def from_pairs(self):
        p = self.place
        if p.pairs == 1:
            return
        half, others = self.pair_bufs
        total = half[...].astype(f32)
        for k in range(1, p.pairs):
            self.got(p.outer_total + p.inner_total + k, others.at[k - 1])
            total = total + others[k - 1].astype(f32)
        self.out[...] = total

    def steps(self):
        return [self.start, self.from_core, self.from_twin, self.from_inner, self.from_outer, self.from_last,
                self.from_pairs]

    def finish(self):
        for c in self.sent:
            c.wait_send()


class Total:
    def __init__(self, place, value, bufs, out, sems, base):
        self.place, self.value, self.bufs, self.out = place, value, bufs, out
        self.send_sem, self.recv_sem = sems
        p = place
        core = [(p.d, p.slot(0, 0, 1 - p.core))]
        inner = [(p.d, p.slot(0, t)) for t in range(1, p.inner_total)]
        outer = [(p.d, p.slot(s, 0)) for s in range(1, p.outer_total)]
        twin = [(p.twin, p.f)]
        pairs = [(p.side + 2 * ((p.d // 2 + k) % p.pairs), p.f) for k in range(1, p.pairs)]
        back = [(p.d, p.slot(0, -t)) for t in range(1, p.inner_total)]
        self.rounds = [r for r in (core, inner, outer, twin, pairs) if r]
        self.base = base
        self.sent = []

    @staticmethod
    def copies(A, B, pairs):
        return 1 + (B - 1) + (A - 1) + 1 + (pairs - 1)

    @staticmethod
    def shapes(A, B, pairs, shape):
        n = Total.copies(A, B, pairs)
        return [pltpu.VMEM((n,) + shape, f32), pltpu.VMEM((5,) + shape, f32)]

    def send_round(self, r):
        landing, held = self.bufs
        i = sum(len(x) for x in self.rounds[:r])
        for k, to in enumerate(self.rounds[r]):
            c = pltpu.make_async_remote_copy(src_ref=held.at[r], dst_ref=landing.at[i + k],
                                             send_sem=self.send_sem.at[self.base + i + k],
                                             recv_sem=self.recv_sem.at[self.base + i + k], device_id=to,
                                             device_id_type=MESH)
            c.start()
            self.sent.append(c)

    def start(self):
        self.bufs[1][0] = self.value[...]
        self.send_round(0)

    def step(self, r):
        landing, held = self.bufs
        i = sum(len(x) for x in self.rounds[:r])
        p = self.place
        total = held[r]
        for k in range(len(self.rounds[r])):
            pltpu.make_async_remote_copy(src_ref=held.at[r], dst_ref=landing.at[i + k],
                                         send_sem=self.send_sem.at[self.base + i + k],
                                         recv_sem=self.recv_sem.at[self.base + i + k], device_id=(p.d, p.f),
                                         device_id_type=MESH).wait_recv()
            total = total + landing[i + k]
        if r + 1 < len(self.rounds):
            held[r + 1] = total
            self.send_round(r + 1)
        else:
            self.out[...] = total

    def steps(self):
        return [self.start] + [functools.partial(self.step, r) for r in range(len(self.rounds))]

    def finish(self):
        for c in self.sent:
            c.wait_send()


def reduce_kernel(dp_total, n, edges, *refs):
    place = Place(dp_total, n)
    A, B, pairs = place.outer_total, place.inner_total, place.pairs
    k = len(edges)
    small_ref = refs[0]
    terms = refs[1:1 + k]
    small_out = refs[1 + k]
    outs = refs[2 + k:2 + 2 * k]
    rest = refs[2 + 2 * k:]
    per = 5 if pairs == 1 else 7
    send_sem, recv_sem = rest[-2:]
    sems = (send_sem, recv_sem)
    greet_all(place)
    base = 0
    units = []
    for i in range(k):
        units.append(Scatter(place, terms[i], rest[i * per:(i + 1) * per], edges[i], outs[i], sems, base))
        base += scatter_copies(A, B, pairs)
    small = Total(place, small_ref, rest[k * per:k * per + 2], small_out, sems, base)
    chains = [u.steps() for u in units] + [small.steps()]
    depth = max(len(c) for c in chains)
    for tick in range(len(chains) + depth):
        for i, c in enumerate(chains):
            if 0 <= tick - i < len(c):
                c[tick - i]()
    for u in units + [small]:
        u.finish()


def reduce_all(sizes, small, terms, edges):
    dp_total, n = sizes
    half = n // 2
    A = 4 if half % 4 == 0 else half
    B = half // A
    pairs = dp_total // 2
    k = len(terms)
    terms = [t.reshape(A, B, 2, *t.shape[1:]) for t in terms]
    scratch = []
    for t, e in zip(terms, edges):
        scratch += scatter_shapes(A, B, pairs, t.shape[-2], t.shape[-1], e)
    scratch += Total.shapes(A, B, pairs, small.shape)
    copies = k * scatter_copies(A, B, pairs) + Total.copies(A, B, pairs)
    scratch += [pltpu.SemaphoreType.DMA((copies,))] * 2
    vm = pl.BlockSpec(memory_space=pltpu.VMEM)
    return pl.pallas_call(
        functools.partial(reduce_kernel, dp_total, n, edges),
        in_specs=[vm] * (k + 1), out_specs=[vm] * (k + 1),
        out_shape=[jax.ShapeDtypeStruct(small.shape, f32)] + [jax.ShapeDtypeStruct(t.shape[-2:], f32) for t in terms],
        scratch_shapes=scratch,
        compiler_params=pltpu.CompilerParams(collective_id=2, has_side_effects=True, vmem_limit_bytes=62 * 2**20),
        name="reduce_gradients",
    )(small, *terms)

FSDP="fsdp"

def spread(vectors, index, total):
    own = vectors.shape[-1]
    at = lax.broadcasted_iota(jnp.int32, (1, total, own), 1)
    wide = jnp.where(at == index, vectors[:, None, :], jnp.zeros((), vectors.dtype))
    return wide.reshape(vectors.shape[0], total * own)

def on_device(sizes, tokens, image_counts, cotangent, first_gain, first_shift, query_weight, query_bias, key_weight,
              value_weight, value_bias, out_weight, out_bias, second_gain, second_shift, up_weight, up_bias,
              down_weight, down_bias):
    rows, feat = tokens.shape
    own = query_weight.shape[0]
    n = feat // own
    counts = image_counts[0]
    me = lax.axis_index(FSDP)
    eight = jnp.stack([first_gain, first_shift, query_bias, value_bias, out_bias, second_gain, second_shift, down_bias])
    small = jnp.concatenate([spread(eight, me, n), spread(up_bias[None], me, n).reshape(-1, feat)])
    small = jnp.concatenate([small, jnp.zeros((16 - small.shape[0], feat), bf16)])
    fi, q, k, v, vec, qkv_all, o_all, up_all, down_all, _ = gather_project(
        sizes, tokens, small, query_weight, key_weight, value_weight, out_weight, up_weight, down_weight)
    full = lambda i: qkv_all[:, i * own:(i + 1) * own].reshape(feat, feat)
    qw, kw, vw = full(0), full(1), full(2)
    ow = o_all.reshape(feat, feat)
    up = up_all.reshape(feat, -1)
    down = down_all.reshape(-1, feat)
    vec1 = vec[0:8]
    vec2 = vec[4:12]
    ub = vec[8:12].reshape(1, -1)
    mixed, lse = attn_fwd(counts, q, k, v)
    layer_out, gres, gmix, gup, gub, gdown, gout, gv2 = middle(counts, mixed, tokens, cotangent, ow, vec2, up, ub, down)
    dq, dk, dv = attn_bwd(counts, q, k, v, gmix, lse)
    gtok, gq, gk, gv, gv1 = project_back(tokens, vec1, gres, fi, dq, dk, dv, qw, kw, vw)
    smalls = jnp.concatenate([gv1[0:4], gv2[0:4], gub.reshape(-1, feat)])
    smalls = jnp.concatenate([smalls, jnp.zeros((16 - smalls.shape[0], feat), f32)])
    cut = lambda g: g.reshape(n, -1, g.shape[1])
    gdown3 = cut(gdown)
    gup3 = cut(gup)
    half_down = gdown3.shape[1] // 2
    half_up = gup3.shape[2] // 2
    terms = [gdown3[:, :half_down], gdown3[:, half_down:], gup3[:, :, :half_up], gup3[:, :, half_up:], cut(gout), cut(gq), cut(gk), cut(gv)]
    edges = (128, 128, 384, 384, 256, 256, 256, 256)
    total, d0, d1, u0, u1, go, gq, gk, gv = reduce_all(sizes, smalls, terms, edges)
    mine = lax.dynamic_index_in_dim(total[:8].reshape(8, n, own), me, 1, keepdims=False)
    ub_mine = lax.dynamic_index_in_dim(total[8:12].reshape(n, -1), me, 0, keepdims=False)
    return (layer_out, gtok, mine[0], mine[1], gq, mine[2], gk, gv, mine[3], go, mine[7], mine[5], mine[6],
            jnp.concatenate([u0, u1], axis=1), ub_mine, jnp.concatenate([d0, d1]), mine[4])


def solution(mesh):
    rows = P(("dp", "fsdp"), None)
    mat = P("fsdp", None)
    vec = P("fsdp")
    return jax.shard_map(
        functools.partial(on_device, (mesh.shape["dp"], mesh.shape["fsdp"])),
        mesh=mesh,
        in_specs=(rows, rows, rows, vec, vec, mat, vec, mat, mat, vec, mat, vec, vec, vec, mat, vec, mat, vec),
        out_specs=(rows, rows, vec, vec, mat, vec, mat, mat, vec, mat, vec, vec, vec, mat, vec, mat, vec),
        check_vma=False,
    )
```

```python
import functools
import math

import jax
import jax.numpy as jnp
from jax import lax
from jax.experimental import pallas as pl
from jax.experimental.pallas import tpu as pltpu
from jax.sharding import PartitionSpec as P

EPS = 1e-06
NT = (((1,), (1,)), ((), ()))
TN = (((0,), (0,)), ((), ()))


SMALL_ROWS=197; LARGE_ROWS=325
QB=256
KB=128
NEG=-1e30

def image_ends(small, large, rows):
    ends=[]
    for i in range(1, rows//SMALL_ROWS+1):
        e = jnp.minimum(i, small)*SMALL_ROWS + jnp.maximum(i-small,0)*LARGE_ROWS
        ends.append(jnp.where(i<=small+large, e, 2*rows))
    return ends

def image_of(places, ends):
    idx = jnp.zeros(places.shape, jnp.int32)
    for e in ends:
        idx = idx + (places>=e).astype(jnp.int32)
    return idx

def key_range(ends, first, last, rows):
    lo = jnp.int32(0); hi = jnp.int32(rows)
    for e in ends:
        lo = jnp.maximum(lo, jnp.where(e<=first, e, 0))
        hi = jnp.minimum(hi, jnp.where(e>last, e, rows))
    return lo, hi

def widths_of(rows):
    ws = [w*KB for w in range(3, rows//KB)]
    ws = [w for w in ws if w<=768]
    return ws+[rows]

def with_window(counts_ref, rows, first, body):
    small=counts_ref[0]; large=counts_ref[1]
    ends=image_ends(small, large, rows)
    lo,hi=key_range(ends, first, first+QB-1, rows)
    base=lo//KB
    need=(hi+KB-1)//KB - base
    done=jnp.int32(0)
    for w in widths_of(rows):
        n=w//KB
        use = (need<=n) & (need>done)
        start = jnp.minimum(base, (rows-w)//KB)*KB
        @pl.when(use)
        def _(start=start, w=w):
            body(pl.multiple_of(start,KB), w, ends)
        done=jnp.int32(n)

def fwd_kernel(counts_ref, q_ref, k_ref, v_ref, o_ref, lse_ref):
    rows=q_ref.shape[0]
    lane=lax.broadcasted_iota(jnp.int32,(QB,128),1)
    def block(b, _):
        first=pl.multiple_of(b*QB,QB)
        def body(start, w, ends):
            q=q_ref[pl.ds(first,QB),:]
            k=k_ref[pl.ds(start,w),:]
            v=v_ref[pl.ds(start,w),:]
            rid=image_of(first+lax.broadcasted_iota(jnp.int32,(QB,1),0), ends)
            cid=image_of(start+lax.broadcasted_iota(jnp.int32,(1,w),1), ends)
            bias=jnp.where(rid==cid, 0.0, NEG)
            outs=[];lses=[]
            for e in range(2):
                qm=jnp.where((lane<64)==(e==0), q, jnp.zeros_like(q))
                s=lax.dot_general(qm,k,(((1,),(1,)),((),())),preferred_element_type=jnp.float32)+bias
                m=jnp.max(s,axis=1,keepdims=True)
                p=jnp.exp(s-m)
                l=jnp.sum(p,axis=1,keepdims=True)
                o=jnp.dot(p.astype(jnp.bfloat16),v,preferred_element_type=jnp.float32)
                outs.append(o*(1.0/l)); lses.append(m+jnp.log(l))
            o_ref[pl.ds(first,QB),:]=jnp.where(lane<64,outs[0],outs[1]).astype(jnp.bfloat16)
            both=jnp.where(lane<64,jnp.broadcast_to(lses[0],(QB,128)),jnp.broadcast_to(lses[1],(QB,128)))
            t=both.T
            lse_ref[0,0:1,pl.ds(first,QB)]=t[0:1,:]
            lse_ref[0,1:2,pl.ds(first,QB)]=t[64:65,:]
        with_window(counts_ref, rows, first, body)
        return 0
    lax.fori_loop(0,rows//QB,block,0)

def attn_fwd(counts,q,k,v):
    rows,feat=q.shape
    pairs=feat//128
    spec=pl.BlockSpec((rows,128),lambda p,c:(0,p))
    return pl.pallas_call(fwd_kernel,
        grid_spec=pltpu.PrefetchScalarGridSpec(num_scalar_prefetch=1,grid=(pairs,),
            in_specs=[spec]*3,out_specs=[spec,pl.BlockSpec((1,2,rows),lambda p,c:(p,0,0))]),
        out_shape=[jax.ShapeDtypeStruct((rows,feat),jnp.bfloat16),jax.ShapeDtypeStruct((pairs,2,rows),jnp.float32)],
        name="attend",
        )(counts,q,k,v)

def bwd_kernel(counts_ref, q_ref, k_ref, v_ref, do_ref, lse_ref, dq_ref, dk_ref, dv_ref, dk_acc, dv_acc):
    rows=q_ref.shape[0]
    lane=lax.broadcasted_iota(jnp.int32,(QB,128),1)
    dk_acc[...]=jnp.zeros_like(dk_acc)
    dv_acc[...]=jnp.zeros_like(dv_acc)
    nt=(((1,),(1,)),((),()))
    tn=(((0,),(0,)),((),()))
    def block(b,_):
        first=pl.multiple_of(b*QB,QB)
        def body(start,w,ends):
            q=q_ref[pl.ds(first,QB),:]
            do=do_ref[pl.ds(first,QB),:]
            k=k_ref[pl.ds(start,w),:]
            v=v_ref[pl.ds(start,w),:]
            rid=image_of(start+lax.broadcasted_iota(jnp.int32,(w,1),0), ends)
            cid=image_of(first+lax.broadcasted_iota(jnp.int32,(1,QB),1), ends)
            bias=jnp.where(rid==cid,0.0,NEG)
            dqs=[]
            dks=None;dvs=None
            for e in range(2):
                mask=(lane<64)==(e==0)
                qm=jnp.where(mask,q,jnp.zeros_like(q))
                dom=jnp.where(mask,do,jnp.zeros_like(do))
                s=lax.dot_general(k,qm,nt,preferred_element_type=jnp.float32)+bias
                p=jnp.exp(s-lse_ref[0,e:e+1,pl.ds(first,QB)])
                dp=lax.dot_general(v,dom,nt,preferred_element_type=jnp.float32)
                delta=jnp.sum(p*dp,axis=0,keepdims=True)
                ds=(p*(dp-delta)).astype(jnp.bfloat16)
                pb=p.astype(jnp.bfloat16)
                dv_e=jnp.dot(pb,dom,preferred_element_type=jnp.float32)
                dk_e=jnp.dot(ds,qm,preferred_element_type=jnp.float32)
                dq_e=lax.dot_general(ds,k,tn,preferred_element_type=jnp.float32)
                dvs=dv_e if dvs is None else dvs+dv_e
                dks=dk_e if dks is None else dks+dk_e
                dqs.append(dq_e)
            dv_acc[pl.ds(start,w),:]+=dvs
            dk_acc[pl.ds(start,w),:]+=dks
            dq_ref[pl.ds(first,QB),:]=(jnp.where(lane<64,dqs[0],dqs[1])*0.125).astype(jnp.bfloat16)
        with_window(counts_ref,rows,first,body)
        return 0
    lax.fori_loop(0,rows//QB,block,0)
    dk_ref[...]=dk_acc[...].astype(jnp.bfloat16)
    dv_ref[...]=dv_acc[...].astype(jnp.bfloat16)

def attn_bwd(counts,q,k,v,do,lse):
    rows,feat=q.shape
    pairs=feat//128
    spec=pl.BlockSpec((rows,128),lambda p,c:(0,p))
    return pl.pallas_call(bwd_kernel,
        grid_spec=pltpu.PrefetchScalarGridSpec(num_scalar_prefetch=1,grid=(pairs,),
            in_specs=[spec]*4+[pl.BlockSpec((1,2,rows),lambda p,c:(p,0,0))],out_specs=[spec]*3,
            scratch_shapes=[pltpu.VMEM((rows,128),jnp.float32)]*2),
        out_shape=[jax.ShapeDtypeStruct((rows,feat),jnp.bfloat16)]*3,
        name="attend_back",
        )(counts,q,k,v,do,lse)

f32=jnp.float32; bf16=jnp.bfloat16
RB=256
INV_SQRT2=1/math.sqrt(2.0); INV_SQRT2PI=1/math.sqrt(2*math.pi)

def dot(a,b): return jnp.dot(a,b,preferred_element_type=f32)
def dot_nt(a,b): return lax.dot_general(a,b,NT,preferred_element_type=f32)
def dot_tn(a,b): return lax.dot_general(a,b,TN,preferred_element_type=f32)

def norm_parts(x):
    mean=jnp.mean(x,axis=-1,keepdims=True)
    cen=x-mean
    var=jnp.mean(cen*cen,axis=-1,keepdims=True)
    q=lax.rsqrt(var+EPS)
    return cen*q, q

def live_mask(counts_ref, first, n):
    end=counts_ref[0]*197+counts_ref[1]*325
    r=first+lax.broadcasted_iota(jnp.int32,(n,1),0)
    return r<end

def mid_kernel(counts_ref, mixed_ref, tokens_ref, cot_ref, outw_ref, vec_ref, up_ref, ub_ref, down_ref,
        layer_ref, gres_ref, gmix_ref, gup_ref, gub_ref, gdown_ref, gout_ref, gvec_ref,
        res_s, si_s, gb_s, accout_s, accgs_s, hid_s, gi_s):
    rows=tokens_ref.shape[0]
    j=pl.program_id(0); nj=pl.num_programs(0)
    obias=vec_ref[0:1,:]; gain=vec_ref[1:2,:]; shift=vec_ref[2:3,:]; dbias=vec_ref[3:4,:]
    @pl.when(j==0)
    def _():
        def step(i,_):
            first=pl.multiple_of(i*RB,RB); sl=pl.ds(first,RB)
            res=tokens_ref[sl,:].astype(f32)+(dot(mixed_ref[sl,:],outw_ref[...])+obias)
            res_s[sl,:]=res
            xhat,_q=norm_parts(res)
            si_s[sl,:]=(xhat*gain+shift).astype(bf16)
            live=live_mask(counts_ref,first,RB)
            gb_s[sl,:]=jnp.where(live,cot_ref[sl,:],jnp.zeros((),bf16))
            return 0
        lax.fori_loop(0,rows//RB,step,0)
        accout_s[...]=jnp.zeros_like(accout_s)
        accgs_s[...]=jnp.zeros_like(accgs_s)
    gub=jnp.zeros(gub_ref.shape,f32)
    for i in range(rows//RB):
        sl=slice(i*RB,(i+1)*RB)
        pre=dot(si_s[sl,:],up_ref[...])+ub_ref[...]
        cdf=0.5+0.5*lax.erf(pre*INV_SQRT2)
        pdf=jnp.exp(-0.5*pre*pre)*INV_SQRT2PI
        hid_s[sl,:]=(pre*cdf).astype(bf16)
        gh=dot_nt(gb_s[sl,:],down_ref[...])
        gi=(gh*(cdf+pre*pdf)).astype(bf16)
        gi_s[sl,:]=gi
        gub=gub+jnp.sum(gi.astype(f32),axis=0,keepdims=True)
    gub_ref[...]=gub
    accout_s[...]+=dot(hid_s[...],down_ref[...])
    accgs_s[...]+=dot_nt(gi_s[...],up_ref[...])
    gdown_ref[...]=dot_tn(hid_s[...],gb_s[...]).astype(bf16)
    gup_ref[...]=dot_tn(si_s[...],gi_s[...]).astype(bf16)
    @pl.when(j==nj-1)
    def _():
        gvec_ref[...]=jnp.zeros_like(gvec_ref)
        def step(i,_):
            first=pl.multiple_of(i*RB,RB); sl=pl.ds(first,RB)
            live=live_mask(counts_ref,first,RB)
            res=res_s[sl,:]
            layer=res+(accout_s[sl,:]+dbias)
            layer_ref[sl,:]=jnp.where(live,layer,0.0).astype(bf16)
            xhat,q=norm_parts(res)
            gs=accgs_s[sl,:]
            t=gs*gain
            gb=gb_s[sl,:].astype(f32)
            gres=gb+q*(t-jnp.mean(t,axis=-1,keepdims=True)-xhat*jnp.mean(t*xhat,axis=-1,keepdims=True))
            gres_ref[sl,:]=gres
            ga=gres.astype(bf16)
            mixed_unused=None
            si_s[sl,:]=ga
            gvec_ref[0:1,:]+=jnp.sum(gb,axis=0,keepdims=True)
            gvec_ref[1:2,:]+=jnp.sum(gs*xhat,axis=0,keepdims=True)
            gvec_ref[2:3,:]+=jnp.sum(gs,axis=0,keepdims=True)
            gvec_ref[3:4,:]+=jnp.sum(ga.astype(f32),axis=0,keepdims=True)
            gmix_ref[sl,:]=dot_nt(ga,outw_ref[...]).astype(bf16)
            return 0
        lax.fori_loop(0,rows//RB,step,0)
        gout_ref[...]=dot_tn(mixed_ref[...],si_s[...]).astype(bf16)

def middle(counts,mixed,tokens,cot,outw,vec,up,ub,down,FB=512):
    rows,D=tokens.shape; FF=up.shape[1]
    nj=FF//FB
    full=lambda a: pl.BlockSpec(a.shape,lambda j,c:(0,)*len(a.shape),pipeline_mode=pl.Buffered(1))
    fo=lambda s: pl.BlockSpec(s,lambda j,c:(0,)*len(s),pipeline_mode=pl.Buffered(1))
    return pl.pallas_call(mid_kernel,
        grid_spec=pltpu.PrefetchScalarGridSpec(num_scalar_prefetch=1,grid=(nj,),
            in_specs=[full(mixed),full(tokens),full(cot),full(outw),full(vec),
                pl.BlockSpec((D,FB),lambda j,c:(0,j)),pl.BlockSpec((1,FB),lambda j,c:(0,j)),pl.BlockSpec((FB,D),lambda j,c:(j,0))],
            out_specs=[fo((rows,D)),fo((rows,D)),fo((rows,D)),
                pl.BlockSpec((D,FB),lambda j,c:(0,j)),pl.BlockSpec((1,FB),lambda j,c:(0,j)),pl.BlockSpec((FB,D),lambda j,c:(j,0)),
                fo((D,D)),fo((8,D))],
            scratch_shapes=[pltpu.VMEM((rows,D),f32),pltpu.VMEM((rows,D),bf16),pltpu.VMEM((rows,D),bf16),
                pltpu.VMEM((rows,D),f32),pltpu.VMEM((rows,D),f32),pltpu.VMEM((rows,FB),bf16),pltpu.VMEM((rows,FB),bf16)]),
        out_shape=[jax.ShapeDtypeStruct((rows,D),bf16),jax.ShapeDtypeStruct((rows,D),f32),jax.ShapeDtypeStruct((rows,D),bf16),
            jax.ShapeDtypeStruct((D,FF),bf16),jax.ShapeDtypeStruct((1,FF),f32),jax.ShapeDtypeStruct((FF,D),bf16),
            jax.ShapeDtypeStruct((D,D),bf16),jax.ShapeDtypeStruct((8,D),f32)],
        compiler_params=pltpu.CompilerParams(vmem_limit_bytes=60*2**20),
        name="feed_forward",
        )(counts,mixed,tokens,cot,outw,vec,up,ub,down)


def qkv_kernel(tokens_ref, vec_ref, qw_ref, kw_ref, vw_ref, fi_ref, q_ref, k_ref, v_ref):
    rows=tokens_ref.shape[0]
    gain=vec_ref[0:1,:]; shift=vec_ref[1:2,:]; qb=vec_ref[2:3,:]; vb=vec_ref[3:4,:]
    for i in range(rows//RB):
        sl=slice(i*RB,(i+1)*RB)
        xhat,_=norm_parts(tokens_ref[sl,:].astype(f32))
        fi=(xhat*gain+shift).astype(bf16)
        fi_ref[sl,:]=fi
        q_ref[sl,:]=((dot(fi,qw_ref[...])+qb).astype(bf16).astype(f32)*0.125).astype(bf16)
        k_ref[sl,:]=dot(fi,kw_ref[...]).astype(bf16)
        v_ref[sl,:]=(dot(fi,vw_ref[...])+vb).astype(bf16)

def project(tokens,vec,qw,kw,vw):
    rows,D=tokens.shape
    return pl.pallas_call(qkv_kernel,out_shape=[jax.ShapeDtypeStruct((rows,D),bf16)]*4,
        compiler_params=pltpu.CompilerParams(vmem_limit_bytes=60*2**20),name="project")(tokens,vec,qw,kw,vw)

def back_kernel(tokens_ref, vec_ref, gres_ref, fi_ref, dq_ref, dk_ref, dv_ref, qw_ref, kw_ref, vw_ref,
        gtok_ref, gq_ref, gk_ref, gv_ref, gvec_ref):
    rows=tokens_ref.shape[0]
    gain=vec_ref[0:1,:]
    gvec=[jnp.zeros((1,tokens_ref.shape[1]),f32)]*4
    for i in range(rows//RB):
        sl=slice(i*RB,(i+1)*RB)
        dq=dq_ref[sl,:];dk=dk_ref[sl,:];dv=dv_ref[sl,:]
        gs=dot_nt(dq,qw_ref[...])+dot_nt(dk,kw_ref[...])+dot_nt(dv,vw_ref[...])
        xhat,q=norm_parts(tokens_ref[sl,:].astype(f32))
        t=gs*gain
        gtok_ref[sl,:]=gres_ref[sl,:]+q*(t-jnp.mean(t,axis=-1,keepdims=True)-xhat*jnp.mean(t*xhat,axis=-1,keepdims=True))
        for n,a in enumerate((gs*xhat,gs,dq.astype(f32),dv.astype(f32))):
            gvec[n]=gvec[n]+jnp.sum(a,axis=0,keepdims=True)
    gvec_ref[...]=jnp.zeros_like(gvec_ref)
    for n in range(4): gvec_ref[n:n+1,:]=gvec[n]
    fi=fi_ref[...]
    gq_ref[...]=dot_tn(fi,dq_ref[...]).astype(bf16)
    gk_ref[...]=dot_tn(fi,dk_ref[...]).astype(bf16)
    gv_ref[...]=dot_tn(fi,dv_ref[...]).astype(bf16)

def project_back(tokens,vec,gres,fi,dq,dk,dv,qw,kw,vw):
    rows,D=tokens.shape
    s=jax.ShapeDtypeStruct
    return pl.pallas_call(back_kernel,out_shape=[s((rows,D),f32),s((D,D),bf16),s((D,D),bf16),s((D,D),bf16),s((8,D),f32)],
        compiler_params=pltpu.CompilerParams(vmem_limit_bytes=60*2**20),name="project_back")(tokens,vec,gres,fi,dq,dk,dv,qw,kw,vw)


MESH = pl.DeviceIdType.MESH


class Place:
    def __init__(self, dp_total, fsdp_total):
        half = fsdp_total // 2
        self.outer_total = 4
        self.inner_total = half // 4
        assert half % 4 == 0
        self.pairs = dp_total // 2
        self.d = lax.axis_index("dp")
        self.f = lax.axis_index("fsdp")
        self.core = self.f % 2
        self.inner = (self.f // 2) % self.inner_total
        self.outer = self.f // (2 * self.inner_total)
        self.side = self.d % 2
        self.twin = self.d + 1 - 2 * self.side
        self.flip = self.outer // 2
        self.mirror = self.unmirror(self.outer)

    def unmirror(self, at):
        return at + self.flip * (3 - 2 * at)

    def arrival(self, step):
        return self.unmirror(step - self.mirror if step == 1 else step)

    def at_outer(self, outer):
        return (self.d, self.index(outer, self.inner, self.core))

    def index(self, outer, inner, core):
        return (outer * self.inner_total + inner) * 2 + core

    def slot(self, s, t, core=None):
        return self.index((self.outer + s) % self.outer_total, (self.inner + t) % self.inner_total,
                          self.core if core is None else core)

    def neighbours(self):
        out = [(self.d, self.slot(s, 0)) for s in range(1, self.outer_total)]
        out += [(self.d, self.slot(0, t)) for t in range(1, self.inner_total)]
        out += [(self.twin, self.f), (self.d, self.slot(0, 0, 1 - self.core))]
        return out


def greet(others):
    barrier = pltpu.get_barrier_semaphore()
    for other in others:
        pl.semaphore_signal(barrier, inc=1, device_id=other, device_id_type=MESH)
    pl.semaphore_wait(barrier, len(others))


class Gather:
    def __init__(self, place, view, rows, edge, sems, base):
        self.place, self.view, self.rows, self.edge = place, view, rows, edge
        self.send_sem, self.recv_sem = sems
        A, B = place.outer_total, place.inner_total
        self.base = base
        keys = [("z", s) for s in range(1, A)] + [("Z", s) for s in range(1, A)]
        keys += [("x", s, t) for s in range(A) for t in range(1, B)]
        if edge:
            keys += [("y", s, t) for s in range(A) for t in range(B) if s or t]
        keys += [("c", s, t) for s in range(A) for t in range(B)]
        self.keys = {key: i for i, key in enumerate(keys)}
        self.sent = []
        self.sent_inside = []

    @staticmethod
    def count(A, B, edge):
        return 2 * (A - 1) + A * (B - 1) + (A * B - 1 if edge else 0) + A * B

    def part(self, slot, kind):
        if not self.edge:
            return self.view(slot, 0, self.rows)
        p = self.place.side
        if kind == "plane":
            return self.view(slot, p * self.edge, self.rows - self.edge)
        if kind == "mine":
            return self.view(slot, p * (self.rows - self.edge), self.edge)
        if kind == "theirs":
            return self.view(slot, (1 - p) * (self.rows - self.edge), self.edge)
        return self.view(slot, 0, self.rows)

    def copy(self, key, ref, to):
        i = self.base + self.keys[key]
        into = i
        if key[0] == "Z":
            into = self.base + self.keys["z", 2 if key[1] == 2 else 3]
        return pltpu.make_async_remote_copy(src_ref=ref, dst_ref=ref, send_sem=self.send_sem.at[i],
                                            recv_sem=self.recv_sem.at[into], device_id=to, device_id_type=MESH)

    def send(self, key, make):
        self.copy(key, *make()).start()
        self.sent.append((key, make))

    def send_inside(self, key, make):
        @pl.when(self.place.mirror == 1)
        def _():
            self.copy(key, *make()).start()

        self.sent_inside.append((key, make))

    def got(self, key, ref):
        self.copy(key, ref, (self.place.d, self.place.f)).wait_recv()

    def slot_of(self, step, t, core):
        p = self.place
        outer = p.outer if step == 0 else p.arrival(step)
        return p.index(outer, (p.inner + t) % p.inner_total, core)

    def start_outer(self):
        p = self.place
        self.send(("z", 1), lambda: (self.part(p.f, "plane"), p.at_outer(p.unmirror(1 - p.mirror))))
        self.send_inside(("z", 2), lambda: (self.part(p.f, "plane"), p.at_outer(p.unmirror(2))))

    def start_inner(self):
        self.pass_inner(0)
        self.pass_core(0, 0)

    def start(self):
        self.start_outer()
        self.start_inner()

    def from_outer_step(self, step):
        p = self.place
        self.got(("z", step), self.part(self.slot_of(step, 0, p.core), "plane"))
        self.send_inside(("Z", step), lambda: (self.part(self.slot_of(step, 0, p.core), "plane"),
                                               p.at_outer(p.unmirror(2 if step == 1 else 0))))
        self.pass_inner(step)
        self.pass_twin(step, 0)

    def from_outer(self):
        for step in range(1, self.place.outer_total):
            self.from_outer_step(step)

    def pass_inner(self, step):
        p = self.place
        for t in range(1, p.inner_total):
            self.send(("x", step, t), lambda t=t: (self.part(self.slot_of(step, 0, p.core), "plane"),
                                                   (p.d, p.slot(0, -t))))

    def pass_twin(self, step, t):
        p = self.place
        if self.edge:
            self.send(("y", step, t), lambda: (self.part(self.slot_of(step, t, p.core), "mine"), (p.twin, p.f)))

    def pass_core(self, step, t):
        p = self.place
        self.send(("c", step, t), lambda: (self.part(self.slot_of(step, t, p.core), "all"),
                                           (p.d, p.slot(0, 0, 1 - p.core))))

    def from_inner(self):
        p = self.place
        for step in range(p.outer_total):
            for t in range(1, p.inner_total):
                self.got(("x", step, t), self.part(self.slot_of(step, t, p.core), "plane"))
                self.pass_twin(step, t)

    def from_twin(self):
        p = self.place
        for step in range(p.outer_total):
            for t in range(p.inner_total):
                if step or t:
                    if self.edge:
                        self.got(("y", step, t), self.part(self.slot_of(step, t, p.core), "theirs"))
                    self.pass_core(step, t)

    def from_core(self):
        p = self.place
        for step in range(p.outer_total):
            for t in range(p.inner_total):
                self.got(("c", step, t), self.part(self.slot_of(step, t, 1 - p.core), "all"))

    def finish(self):
        for key, make in self.sent:
            self.copy(key, *make()).wait_send()

        @pl.when(self.place.mirror == 1)
        def _():
            for key, make in self.sent_inside:
                self.copy(key, *make()).wait_send()


def local(src, dst, sem):
    c = pltpu.make_async_copy(src, dst, sem)
    c.start()
    return c


def attend_block(counts_ref, q_ref, k_ref, v_ref, mixed_ref, lse_ref, pair, block):
    rows = q_ref.shape[0]
    lane = lax.broadcasted_iota(jnp.int32, (QB, 128), 1)
    first = pl.multiple_of(block * QB, QB)
    cols = pl.ds(pl.multiple_of(pair * 128, 128), 128)
    q = q_ref[pl.ds(first, QB), cols]
    k = k_ref[:, cols]
    v = v_ref[:, cols]
    ends = image_ends(counts_ref[0], counts_ref[1], rows)
    rid = image_of(first + lax.broadcasted_iota(jnp.int32, (QB, 1), 0), ends)
    cid = image_of(lax.broadcasted_iota(jnp.int32, (1, rows), 1), ends)
    bias = jnp.where(rid == cid, 0.0, NEG)
    outs = []
    lses = []
    for e in range(2):
        qm = jnp.where((lane < 64) == (e == 0), q, jnp.zeros_like(q))
        s = dot_nt(qm, k) + bias
        m = jnp.max(s, axis=1, keepdims=True)
        p = jnp.exp(s - m)
        l = jnp.sum(p, axis=1, keepdims=True)
        o = dot(p.astype(bf16), v)
        outs.append(o * (1.0 / l))
        lses.append(m + jnp.log(l))
    mixed_ref[pl.ds(first, QB), cols] = jnp.where(lane < 64, outs[0], outs[1]).astype(bf16)
    both = jnp.where(lane < 64, jnp.broadcast_to(lses[0], (QB, 128)), jnp.broadcast_to(lses[1], (QB, 128)))
    t = both.T
    lse_ref[pair, 0:1, pl.ds(first, QB)] = t[0:1, :]
    lse_ref[pair, 1:2, pl.ds(first, QB)] = t[64:65, :]


def gather_units(place, own, down_own, ff, small_all, qkv_all, o_all, up_all, down_all, sems):
    A, B = place.outer_total, place.inner_total

    def rows_view(ref, offset=0, cols=None):
        def view(slot, start, rows):
            at = pl.ds(pl.multiple_of(offset + start, 8), rows)
            return ref.at[slot, at] if cols is None else ref.at[slot, at, cols]
        return view

    third = own // 3
    half = down_own // 2
    five = half * 5 // 12 // 8 * 8
    specs = [(rows_view(small_all), small_all.shape[1], 0),
             (rows_view(qkv_all), 3 * own, own),
             (rows_view(o_all), own, third),
             (rows_view(up_all, 0, pl.ds(0, ff // 2)), own, third),
             (rows_view(up_all, 0, pl.ds(ff // 2, ff // 2)), own, third),
             (rows_view(down_all, 0), half, five),
             (rows_view(down_all, half), half, five)]
    units = []
    base = 0
    for view, rows, edge in specs:
        units.append(Gather(place, view, rows, edge, sems, base))
        base += Gather.count(A, B, edge)
    return units


def gather_kernel(dp_total, fsdp_total, counts_ref, tokens_ref, small_ref, qo_ref, ko_ref, vo_ref, oo_ref, uo_ref,
                  do_ref, fi_ref, q_ref, k_ref, v_ref, vec_ref, mixed_ref, lse_ref, qkv_all, o_all, up_all, down_all,
                  small_all, w_s, small_s, send_sem, recv_sem, loc_sem):
    place = Place(dp_total, fsdp_total)
    n = fsdp_total
    own = qo_ref.shape[0]
    me = place.f
    greet(place.neighbours())
    fill = [local(small_ref, small_all.at[me], loc_sem.at[0])]
    for i, r in enumerate((qo_ref, ko_ref, vo_ref)):
        fill.append(local(r, qkv_all.at[me, pl.ds(i * own, own)], loc_sem.at[1 + i]))
    fill.append(local(oo_ref, o_all.at[me], loc_sem.at[4]))
    fill.append(local(uo_ref, up_all.at[me], loc_sem.at[5]))
    fill.append(local(do_ref, down_all.at[me], loc_sem.at[6]))
    units = gather_units(place, own, do_ref.shape[0], uo_ref.shape[1], small_all, qkv_all, o_all, up_all, down_all,
                         (send_sem, recv_sem))
    for c in fill:
        c.wait()
    sm, u = units[0], units[1:]
    for x in (sm, u[0], u[1]):
        x.start()
    sm.from_outer()
    sm.from_inner()
    sm.from_twin()
    u[2].start()
    u[0].from_outer()
    sm.from_core()
    take = local(small_all, small_s, loc_sem.at[0])
    u[0].from_inner()
    take.wait()
    total = jnp.zeros(vec_ref.shape, f32)
    for i in range(n):
        total = total + small_s[i].astype(f32)
    vec_ref[...] = total
    u[3].start()
    u[1].from_outer()
    u[0].from_twin()
    u[0].from_core()
    take = local(qkv_all, w_s, loc_sem.at[1])
    u[1].from_inner()
    take.wait()
    rows, feat = tokens_ref.shape

    def project_rows(i, _):
        sl = pl.ds(pl.multiple_of(i * RB, RB), RB)
        xhat, _q = norm_parts(tokens_ref[sl, :].astype(f32))
        fi = (xhat * vec_ref[0:1, :] + vec_ref[1:2, :]).astype(bf16)
        fi_ref[sl, :] = fi
        weight = lambda i: w_s[:, i * own:(i + 1) * own, :].reshape(feat, feat)
        q_ref[sl, :] = ((dot(fi, weight(0)) + vec_ref[2:3, :]).astype(bf16).astype(f32) * 0.125).astype(bf16)
        k_ref[sl, :] = dot(fi, weight(1)).astype(bf16)
        v_ref[sl, :] = (dot(fi, weight(2)) + vec_ref[3:4, :]).astype(bf16)
        return 0

    half = rows // RB // 2
    lax.fori_loop(0, half, project_rows, 0)
    u[2].from_outer()
    lax.fori_loop(half, 2 * half, project_rows, 0)
    u[4].start()
    u[1].from_twin()
    u[2].from_inner()
    blocks = rows // QB
    step = lambda unit, s: functools.partial(unit.from_outer_step, s)
    batches = [
        [step(u[3], 1), u[5].start],
        [step(u[3], 2), u[1].from_core],
        [step(u[3], 3), u[2].from_twin],
        [u[3].from_inner],
        [step(u[4], 1), u[2].from_core],
        [step(u[4], 2), u[3].from_twin],
        [step(u[4], 3)],
        [u[4].from_inner, u[3].from_core],
        [step(u[5], 1)],
        [step(u[5], 2), u[4].from_twin],
        [step(u[5], 3)],
        [u[5].from_inner, u[4].from_core],
        [u[5].from_twin],
        [],
        [u[5].from_core]]
    pieces = feat // 128 * blocks

    def piece(i, _):
        attend_block(counts_ref, q_ref, k_ref, v_ref, mixed_ref, lse_ref, i // blocks, i % blocks)
        for k, batch in enumerate(batches):
            if batch:
                @pl.when(i == (k + 1) * (pieces - 1) // len(batches))
                def _(batch=batch):
                    for one in batch:
                        one()
        return 0

    lax.fori_loop(0, pieces, piece, 0)
    for x in units:
        x.finish()


def gather_attend(sizes, counts, tokens, small, qw, kw, vw, ow, up, down):
    dp_total, n = sizes
    rows, feat = tokens.shape
    own = qw.shape[0]
    A, B = 4, n // 8
    pairs = feat // 128
    copies = Gather.count(A, B, 0) + 6 * Gather.count(A, B, 1)
    s = jax.ShapeDtypeStruct
    vm = pl.BlockSpec(memory_space=pltpu.VMEM)
    anyspec = pl.BlockSpec(memory_space=pl.ANY)
    return pl.pallas_call(
        functools.partial(gather_kernel, dp_total, n),
        in_specs=[pl.BlockSpec(memory_space=pltpu.SMEM)] + [vm] * 8,
        out_specs=[vm] * 7 + [anyspec] * 5,
        out_shape=[s((rows, feat), bf16)] * 4 + [s(small.shape, f32), s((rows, feat), bf16), s((pairs, 2, rows), f32),
                   s((n, 3 * own, feat), bf16), s((n, own, feat), bf16),
                   s((n,) + up.shape, bf16), s((n,) + down.shape, bf16), s((n,) + small.shape, bf16)],
        scratch_shapes=[pltpu.VMEM((n, 3 * own, feat), bf16), pltpu.VMEM((n,) + small.shape, bf16),
                        pltpu.SemaphoreType.DMA((copies,)), pltpu.SemaphoreType.DMA((copies,)),
                        pltpu.SemaphoreType.DMA((8,))],
        compiler_params=pltpu.CompilerParams(collective_id=1, has_side_effects=True, vmem_limit_bytes=60 * 2**20),
        name="gather_attend",
    )(counts, tokens, small, qw, kw, vw, ow, up, down)


def plan_neighbours(place):
    out = place.neighbours()
    out += [(place.side + 2 * ((place.d // 2 + k) % place.pairs), place.f) for k in range(1, place.pairs)]
    return out


def scatter_copies(A, B, pairs):
    return 1 + 1 + (B - 1) + (A - 1) + 1 + (pairs - 1)


def scatter_shapes(A, B, pairs, rows, width, edge):
    out = [pltpu.VMEM((A, B, rows, width), bf16), pltpu.VMEM((A, B, rows, edge), bf16),
           pltpu.VMEM((B - 1, A, rows, width), bf16), pltpu.VMEM((A - 1, rows, width), bf16),
           pltpu.VMEM((rows, width), bf16)]
    if pairs > 1:
        out += [pltpu.VMEM((rows, width), bf16), pltpu.VMEM((pairs - 1, rows, width), bf16)]
    return out


class Scatter:
    def __init__(self, place, terms, bufs, edge, out, sems, base):
        self.place, self.terms, self.edge, self.out = place, terms, edge, out
        self.sums, self.from_twin_buf, self.from_inner_buf, self.from_outer_buf, self.last_buf = bufs[:5]
        self.pair_bufs = bufs[5:]
        self.width = terms.shape[-1]
        self.rows = terms.shape[-2]
        self.send_sem, self.recv_sem = sems
        self.base = base
        self.sent = []
        p = place.side
        e, w = edge, self.width
        at = lambda start, size: pl.ds(pl.multiple_of(start, 128), size)
        self.plane = at(p * e, w - e)
        self.mine = at(p * (w - e), e)
        self.theirs = at((1 - p) * (w - e), e)
        self.twin_plane = at((1 - p) * e, w - e)
        self.middle = pl.ds(e, w - 2 * e)

    def copy(self, i, src, dst, to):
        return pltpu.make_async_remote_copy(src_ref=src, dst_ref=dst, send_sem=self.send_sem.at[self.base + i],
                                            recv_sem=self.recv_sem.at[self.base + i], device_id=to, device_id_type=MESH)

    def send(self, i, src, dst, to):
        c = self.copy(i, src, dst, to)
        c.start()
        self.sent.append(c)

    def got(self, i, dst):
        self.copy(i, dst, dst, (self.place.d, self.place.f)).wait_recv()

    def start(self):
        p = self.place
        self.send(0, self.terms.at[:, :, 1 - p.core], self.sums, (p.d, p.slot(0, 0, 1 - p.core)))

    def from_core(self):
        p = self.place
        self.got(0, self.sums)
        B = p.inner_total

        def add(i, _):
            a, b = i // B, i % B
            self.sums[a, b] = (self.sums[a, b].astype(f32) + self.terms[a, b, p.core].astype(f32)).astype(bf16)
            return 0

        lax.fori_loop(0, p.outer_total * B, add, 0)
        self.send(1, self.sums.at[:, :, :, self.theirs], self.from_twin_buf, (p.twin, p.f))

    def from_twin(self):
        p = self.place
        B = p.inner_total
        self.got(1, self.from_twin_buf)

        def add(i, _):
            a, b = i // B, i % B
            self.sums[a, b, :, self.mine] = (self.sums[a, b, :, self.mine].astype(f32)
                                             + self.from_twin_buf[a, b].astype(f32)).astype(bf16)
            return 0

        lax.fori_loop(0, p.outer_total * B, add, 0)
        for t in range(1, B):
            to = (p.inner + B - t) % B
            self.send(1 + t, self.sums.at[:, to, :, self.plane], self.from_inner_buf.at[t - 1, :, :, self.plane],
                      (p.d, p.slot(0, -t)))

    def from_inner(self):
        p = self.place
        A, B = p.outer_total, p.inner_total
        for t in range(1, B):
            self.got(1 + t, self.from_inner_buf.at[t - 1, :, :, self.plane])

        def add(a, _):
            total = self.sums[a, p.inner, :, self.plane].astype(f32)
            for t in range(1, B):
                total = total + self.from_inner_buf[t - 1, a, :, self.plane].astype(f32)
            self.sums[a, p.inner, :, self.plane] = total.astype(bf16)
            return 0

        lax.fori_loop(0, A, add, 0)
        for s in range(1, A):
            to = (p.outer + A - s) % A
            self.send(B + s, self.sums.at[to, p.inner, :, self.plane], self.from_outer_buf.at[s - 1, :, self.plane],
                      (p.d, p.slot(-s, 0)))

    def from_outer(self):
        p = self.place
        A, B = p.outer_total, p.inner_total
        for s in range(1, A):
            self.got(B + s, self.from_outer_buf.at[s - 1, :, self.plane])
        total = self.sums[p.outer, p.inner, :, self.plane].astype(f32)
        for s in range(1, A):
            total = total + self.from_outer_buf[s - 1, :, self.plane].astype(f32)
        self.sums[p.outer, p.inner, :, self.plane] = total.astype(bf16)
        self.send(A + B, self.sums.at[p.outer, p.inner, :, self.plane], self.last_buf.at[:, self.plane],
                  (p.twin, p.f))

    def from_last(self):
        p = self.place
        A, B = p.outer_total, p.inner_total
        self.got(A + B, self.last_buf.at[:, self.twin_plane])
        own = lambda cols: self.sums[p.outer, p.inner, :, cols].astype(f32)
        last = lambda cols: self.last_buf[:, cols].astype(f32)
        if p.pairs == 1:
            self.out[:, self.mine] = own(self.mine)
            self.out[:, self.middle] = own(self.middle) + last(self.middle)
            self.out[:, self.theirs] = last(self.theirs)
            return
        half, others = self.pair_bufs
        half[:, self.mine] = own(self.mine).astype(bf16)
        half[:, self.middle] = (own(self.middle) + last(self.middle)).astype(bf16)
        half[:, self.theirs] = last(self.theirs).astype(bf16)
        for k in range(1, p.pairs):
            to = p.side + 2 * ((p.d // 2 + p.pairs - k) % p.pairs)
            self.send(A + B + k, half, others.at[k - 1], (to, p.f))

    def from_pairs(self):
        p = self.place
        if p.pairs == 1:
            return
        half, others = self.pair_bufs
        total = half[...].astype(f32)
        for k in range(1, p.pairs):
            self.got(p.outer_total + p.inner_total + k, others.at[k - 1])
            total = total + others[k - 1].astype(f32)
        self.out[...] = total

    def steps(self):
        return [self.start, self.from_core, self.from_twin, self.from_inner, self.from_outer, self.from_last,
                self.from_pairs]

    def finish(self):
        for c in self.sent:
            c.wait_send()


class Total:
    def __init__(self, place, value, bufs, out, sems, base):
        self.place, self.value, self.bufs, self.out = place, value, bufs, out
        self.send_sem, self.recv_sem = sems
        p = place
        core = [(p.d, p.slot(0, 0, 1 - p.core))]
        inner = [(p.d, p.slot(0, t)) for t in range(1, p.inner_total)]
        outer = [(p.d, p.slot(s, 0)) for s in range(1, p.outer_total)]
        twin = [(p.twin, p.f)]
        pairs = [(p.side + 2 * ((p.d // 2 + k) % p.pairs), p.f) for k in range(1, p.pairs)]
        back = [(p.d, p.slot(0, -t)) for t in range(1, p.inner_total)]
        self.rounds = [r for r in (core, inner, outer, twin, pairs) if r]
        self.base = base
        self.sent = []

    @staticmethod
    def copies(A, B, pairs):
        return 1 + (B - 1) + (A - 1) + 1 + (pairs - 1)

    @staticmethod
    def shapes(A, B, pairs, shape):
        n = Total.copies(A, B, pairs)
        return [pltpu.VMEM((n,) + shape, f32), pltpu.VMEM((5,) + shape, f32)]

    def send_round(self, r):
        landing, held = self.bufs
        i = sum(len(x) for x in self.rounds[:r])
        for k, to in enumerate(self.rounds[r]):
            c = pltpu.make_async_remote_copy(src_ref=held.at[r], dst_ref=landing.at[i + k],
                                             send_sem=self.send_sem.at[self.base + i + k],
                                             recv_sem=self.recv_sem.at[self.base + i + k], device_id=to,
                                             device_id_type=MESH)
            c.start()
            self.sent.append(c)

    def start(self):
        self.bufs[1][0] = self.value[...]
        self.send_round(0)

    def step(self, r):
        landing, held = self.bufs
        i = sum(len(x) for x in self.rounds[:r])
        p = self.place
        total = held[r]
        for k in range(len(self.rounds[r])):
            pltpu.make_async_remote_copy(src_ref=held.at[r], dst_ref=landing.at[i + k],
                                         send_sem=self.send_sem.at[self.base + i + k],
                                         recv_sem=self.recv_sem.at[self.base + i + k], device_id=(p.d, p.f),
                                         device_id_type=MESH).wait_recv()
            total = total + landing[i + k]
        if r + 1 < len(self.rounds):
            held[r + 1] = total
            self.send_round(r + 1)
        else:
            self.out[...] = total

    def steps(self):
        return [self.start] + [functools.partial(self.step, r) for r in range(len(self.rounds))]

    def finish(self):
        for c in self.sent:
            c.wait_send()


def reduce_kernel(dp_total, n, edges, *refs):
    place = Place(dp_total, n)
    A, B, pairs = place.outer_total, place.inner_total, place.pairs
    k = len(edges)
    small_ref = refs[0]
    terms = refs[1:1 + k]
    small_out = refs[1 + k]
    outs = refs[2 + k:2 + 2 * k]
    rest = refs[2 + 2 * k:]
    per = 5 if pairs == 1 else 7
    send_sem, recv_sem = rest[-2:]
    sems = (send_sem, recv_sem)
    greet(plan_neighbours(place))
    base = 0
    units = []
    for i in range(k):
        units.append(Scatter(place, terms[i], rest[i * per:(i + 1) * per], edges[i], outs[i], sems, base))
        base += scatter_copies(A, B, pairs)
    small = Total(place, small_ref, rest[k * per:k * per + 2], small_out, sems, base)
    chains = [u.steps() for u in units] + [small.steps()]
    depth = max(len(c) for c in chains)
    for tick in range(len(chains) + depth):
        for i, c in enumerate(chains):
            if 0 <= tick - i < len(c):
                c[tick - i]()
    for u in units + [small]:
        u.finish()


def reduce_all(sizes, small, terms, edges):
    dp_total, n = sizes
    half = n // 2
    A = 4 if half % 4 == 0 else half
    B = half // A
    pairs = dp_total // 2
    k = len(terms)
    terms = [t.reshape(A, B, 2, *t.shape[1:]) for t in terms]
    scratch = []
    for t, e in zip(terms, edges):
        scratch += scatter_shapes(A, B, pairs, t.shape[-2], t.shape[-1], e)
    scratch += Total.shapes(A, B, pairs, small.shape)
    copies = k * scatter_copies(A, B, pairs) + Total.copies(A, B, pairs)
    scratch += [pltpu.SemaphoreType.DMA((copies,))] * 2
    vm = pl.BlockSpec(memory_space=pltpu.VMEM)
    return pl.pallas_call(
        functools.partial(reduce_kernel, dp_total, n, edges),
        in_specs=[vm] * (k + 1), out_specs=[vm] * (k + 1),
        out_shape=[jax.ShapeDtypeStruct(small.shape, f32)] + [jax.ShapeDtypeStruct(t.shape[-2:], f32) for t in terms],
        scratch_shapes=scratch,
        compiler_params=pltpu.CompilerParams(collective_id=2, has_side_effects=True, vmem_limit_bytes=62 * 2**20),
        name="reduce_gradients",
    )(small, *terms)

FSDP="fsdp"

def spread(vectors, index, total):
    own = vectors.shape[-1]
    at = lax.broadcasted_iota(jnp.int32, (1, total, own), 1)
    wide = jnp.where(at == index, vectors[:, None, :], jnp.zeros((), vectors.dtype))
    return wide.reshape(vectors.shape[0], total * own)

def on_device(sizes, tokens, image_counts, cotangent, first_gain, first_shift, query_weight, query_bias, key_weight,
              value_weight, value_bias, out_weight, out_bias, second_gain, second_shift, up_weight, up_bias,
              down_weight, down_bias):
    rows, feat = tokens.shape
    own = query_weight.shape[0]
    n = feat // own
    counts = image_counts[0]
    me = lax.axis_index(FSDP)
    eight = jnp.stack([first_gain, first_shift, query_bias, value_bias, out_bias, second_gain, second_shift, down_bias])
    small = jnp.concatenate([spread(eight, me, n), spread(up_bias[None], me, n).reshape(-1, feat)])
    small = jnp.concatenate([small, jnp.zeros((16 - small.shape[0], feat), bf16)])
    fi, q, k, v, vec, mixed, lse, qkv_all, o_all, up_all, down_all, _ = gather_attend(
        sizes, counts, tokens, small, query_weight, key_weight, value_weight, out_weight, up_weight, down_weight)
    full = lambda i: qkv_all[:, i * own:(i + 1) * own].reshape(feat, feat)
    qw, kw, vw = full(0), full(1), full(2)
    ow = o_all.reshape(feat, feat)
    up = up_all.reshape(feat, -1)
    down = down_all.reshape(-1, feat)
    vec1 = vec[0:8]
    vec2 = vec[4:12]
    ub = vec[8:12].reshape(1, -1)
    layer_out, gres, gmix, gup, gub, gdown, gout, gv2 = middle(counts, mixed, tokens, cotangent, ow, vec2, up, ub, down)
    dq, dk, dv = attn_bwd(counts, q, k, v, gmix, lse)
    gtok, gq, gk, gv, gv1 = project_back(tokens, vec1, gres, fi, dq, dk, dv, qw, kw, vw)
    smalls = jnp.concatenate([gv1[0:4], gv2[0:4], gub.reshape(-1, feat)])
    smalls = jnp.concatenate([smalls, jnp.zeros((16 - smalls.shape[0], feat), f32)])
    cut = lambda g: g.reshape(n, -1, g.shape[1])
    gdown3 = cut(gdown)
    gup3 = cut(gup)
    half_down = gdown3.shape[1] // 2
    half_up = gup3.shape[2] // 2
    terms = [gdown3[:, :half_down], gdown3[:, half_down:], gup3[:, :, :half_up], gup3[:, :, half_up:], cut(gout), cut(gq), cut(gk), cut(gv)]
    edges = (128, 128, 384, 384, 256, 256, 256, 256)
    total, d0, d1, u0, u1, go, gq, gk, gv = reduce_all(sizes, smalls, terms, edges)
    mine = lax.dynamic_index_in_dim(total[:8].reshape(8, n, own), me, 1, keepdims=False)
    ub_mine = lax.dynamic_index_in_dim(total[8:12].reshape(n, -1), me, 0, keepdims=False)
    return (layer_out, gtok, mine[0], mine[1], gq, mine[2], gk, gv, mine[3], go, mine[7], mine[5], mine[6],
            jnp.concatenate([u0, u1], axis=1), ub_mine, jnp.concatenate([d0, d1]), mine[4])


def solution(mesh):
    rows = P(("dp", "fsdp"), None)
    mat = P("fsdp", None)
    vec = P("fsdp")
    return jax.shard_map(
        functools.partial(on_device, (mesh.shape["dp"], mesh.shape["fsdp"])),
        mesh=mesh,
        in_specs=(rows, rows, rows, vec, vec, mat, vec, mat, mat, vec, mat, vec, vec, vec, mat, vec, mat, vec),
        out_specs=(rows, rows, vec, vec, mat, vec, mat, mat, vec, mat, vec, vec, vec, mat, vec, mat, vec),
        check_vma=False,
    )
```

```python
import functools
import math

import jax
import jax.numpy as jnp
from jax import lax
from jax.experimental import pallas as pl
from jax.experimental.pallas import tpu as pltpu
from jax.sharding import PartitionSpec as P

EPS = 1e-06
NT = (((1,), (1,)), ((), ()))
TN = (((0,), (0,)), ((), ()))


SMALL_ROWS=197; LARGE_ROWS=325
QB=256
KB=128
NEG=-1e30

def image_ends(small, large, rows):
    ends=[]
    for i in range(1, rows//SMALL_ROWS+1):
        e = jnp.minimum(i, small)*SMALL_ROWS + jnp.maximum(i-small,0)*LARGE_ROWS
        ends.append(jnp.where(i<=small+large, e, 2*rows))
    return ends

def image_of(places, ends):
    idx = jnp.zeros(places.shape, jnp.int32)
    for e in ends:
        idx = idx + (places>=e).astype(jnp.int32)
    return idx

def key_range(ends, first, last, rows):
    lo = jnp.int32(0); hi = jnp.int32(rows)
    for e in ends:
        lo = jnp.maximum(lo, jnp.where(e<=first, e, 0))
        hi = jnp.minimum(hi, jnp.where(e>last, e, rows))
    return lo, hi

def widths_of(rows):
    ws = [w*KB for w in range(3, rows//KB)]
    ws = [w for w in ws if w<=768]
    return ws+[rows]

def with_window(counts_ref, rows, first, body):
    small=counts_ref[0]; large=counts_ref[1]
    ends=image_ends(small, large, rows)
    lo,hi=key_range(ends, first, first+QB-1, rows)
    base=lo//KB
    need=(hi+KB-1)//KB - base
    done=jnp.int32(0)
    for w in widths_of(rows):
        n=w//KB
        use = (need<=n) & (need>done)
        start = jnp.minimum(base, (rows-w)//KB)*KB
        @pl.when(use)
        def _(start=start, w=w):
            body(pl.multiple_of(start,KB), w, ends)
        done=jnp.int32(n)

def fwd_kernel(counts_ref, q_ref, k_ref, v_ref, o_ref, lse_ref):
    rows=q_ref.shape[0]
    lane=lax.broadcasted_iota(jnp.int32,(QB,128),1)
    def block(b, _):
        first=pl.multiple_of(b*QB,QB)
        def body(start, w, ends):
            q=q_ref[pl.ds(first,QB),:]
            k=k_ref[pl.ds(start,w),:]
            v=v_ref[pl.ds(start,w),:]
            rid=image_of(first+lax.broadcasted_iota(jnp.int32,(QB,1),0), ends)
            cid=image_of(start+lax.broadcasted_iota(jnp.int32,(1,w),1), ends)
            bias=jnp.where(rid==cid, 0.0, NEG)
            outs=[];lses=[]
            for e in range(2):
                qm=jnp.where((lane<64)==(e==0), q, jnp.zeros_like(q))
                s=lax.dot_general(qm,k,(((1,),(1,)),((),())),preferred_element_type=jnp.float32)+bias
                m=jnp.max(s,axis=1,keepdims=True)
                p=jnp.exp(s-m)
                l=jnp.sum(p,axis=1,keepdims=True)
                o=jnp.dot(p.astype(jnp.bfloat16),v,preferred_element_type=jnp.float32)
                outs.append(o*(1.0/l)); lses.append(m+jnp.log(l))
            o_ref[pl.ds(first,QB),:]=jnp.where(lane<64,outs[0],outs[1]).astype(jnp.bfloat16)
            both=jnp.where(lane<64,jnp.broadcast_to(lses[0],(QB,128)),jnp.broadcast_to(lses[1],(QB,128)))
            t=both.T
            lse_ref[0,0:1,pl.ds(first,QB)]=t[0:1,:]
            lse_ref[0,1:2,pl.ds(first,QB)]=t[64:65,:]
        with_window(counts_ref, rows, first, body)
        return 0
    lax.fori_loop(0,rows//QB,block,0)

def attn_fwd(counts,q,k,v):
    rows,feat=q.shape
    pairs=feat//128
    spec=pl.BlockSpec((rows,128),lambda p,c:(0,p))
    return pl.pallas_call(fwd_kernel,
        grid_spec=pltpu.PrefetchScalarGridSpec(num_scalar_prefetch=1,grid=(pairs,),
            in_specs=[spec]*3,out_specs=[spec,pl.BlockSpec((1,2,rows),lambda p,c:(p,0,0))]),
        out_shape=[jax.ShapeDtypeStruct((rows,feat),jnp.bfloat16),jax.ShapeDtypeStruct((pairs,2,rows),jnp.float32)],
        name="attend",
        )(counts,q,k,v)

def bwd_kernel(counts_ref, q_ref, k_ref, v_ref, do_ref, lse_ref, dq_ref, dk_ref, dv_ref, dk_acc, dv_acc):
    rows=q_ref.shape[0]
    lane=lax.broadcasted_iota(jnp.int32,(QB,128),1)
    dk_acc[...]=jnp.zeros_like(dk_acc)
    dv_acc[...]=jnp.zeros_like(dv_acc)
    nt=(((1,),(1,)),((),()))
    tn=(((0,),(0,)),((),()))
    def block(b,_):
        first=pl.multiple_of(b*QB,QB)
        def body(start,w,ends):
            q=q_ref[pl.ds(first,QB),:]
            do=do_ref[pl.ds(first,QB),:]
            k=k_ref[pl.ds(start,w),:]
            v=v_ref[pl.ds(start,w),:]
            rid=image_of(start+lax.broadcasted_iota(jnp.int32,(w,1),0), ends)
            cid=image_of(first+lax.broadcasted_iota(jnp.int32,(1,QB),1), ends)
            bias=jnp.where(rid==cid,0.0,NEG)
            dqs=[]
            dks=None;dvs=None
            for e in range(2):
                mask=(lane<64)==(e==0)
                qm=jnp.where(mask,q,jnp.zeros_like(q))
                dom=jnp.where(mask,do,jnp.zeros_like(do))
                s=lax.dot_general(k,qm,nt,preferred_element_type=jnp.float32)+bias
                p=jnp.exp(s-lse_ref[0,e:e+1,pl.ds(first,QB)])
                dp=lax.dot_general(v,dom,nt,preferred_element_type=jnp.float32)
                delta=jnp.sum(p*dp,axis=0,keepdims=True)
                ds=(p*(dp-delta)).astype(jnp.bfloat16)
                pb=p.astype(jnp.bfloat16)
                dv_e=jnp.dot(pb,dom,preferred_element_type=jnp.float32)
                dk_e=jnp.dot(ds,qm,preferred_element_type=jnp.float32)
                dq_e=lax.dot_general(ds,k,tn,preferred_element_type=jnp.float32)
                dvs=dv_e if dvs is None else dvs+dv_e
                dks=dk_e if dks is None else dks+dk_e
                dqs.append(dq_e)
            dv_acc[pl.ds(start,w),:]+=dvs
            dk_acc[pl.ds(start,w),:]+=dks
            dq_ref[pl.ds(first,QB),:]=(jnp.where(lane<64,dqs[0],dqs[1])*0.125).astype(jnp.bfloat16)
        with_window(counts_ref,rows,first,body)
        return 0
    lax.fori_loop(0,rows//QB,block,0)
    dk_ref[...]=dk_acc[...].astype(jnp.bfloat16)
    dv_ref[...]=dv_acc[...].astype(jnp.bfloat16)

def attn_bwd(counts,q,k,v,do,lse):
    rows,feat=q.shape
    pairs=feat//128
    spec=pl.BlockSpec((rows,128),lambda p,c:(0,p))
    return pl.pallas_call(bwd_kernel,
        grid_spec=pltpu.PrefetchScalarGridSpec(num_scalar_prefetch=1,grid=(pairs,),
            in_specs=[spec]*4+[pl.BlockSpec((1,2,rows),lambda p,c:(p,0,0))],out_specs=[spec]*3,
            scratch_shapes=[pltpu.VMEM((rows,128),jnp.float32)]*2),
        out_shape=[jax.ShapeDtypeStruct((rows,feat),jnp.bfloat16)]*3,
        name="attend_back",
        )(counts,q,k,v,do,lse)

f32=jnp.float32; bf16=jnp.bfloat16
RB=256
INV_SQRT2=1/math.sqrt(2.0); INV_SQRT2PI=1/math.sqrt(2*math.pi)

def dot(a,b): return jnp.dot(a,b,preferred_element_type=f32)
def dot_nt(a,b): return lax.dot_general(a,b,NT,preferred_element_type=f32)
def dot_tn(a,b): return lax.dot_general(a,b,TN,preferred_element_type=f32)

def norm_parts(x):
    mean=jnp.mean(x,axis=-1,keepdims=True)
    cen=x-mean
    var=jnp.mean(cen*cen,axis=-1,keepdims=True)
    q=lax.rsqrt(var+EPS)
    return cen*q, q

def live_mask(counts_ref, first, n):
    end=counts_ref[0]*197+counts_ref[1]*325
    r=first+lax.broadcasted_iota(jnp.int32,(n,1),0)
    return r<end

def mid_kernel(counts_ref, mixed_ref, tokens_ref, cot_ref, outw_ref, vec_ref, up_ref, ub_ref, down_ref,
        layer_ref, gres_ref, gmix_ref, gup_ref, gub_ref, gdown_ref, gout_ref, gvec_ref,
        res_s, si_s, gb_s, accout_s, accgs_s, hid_s, gi_s):
    rows=tokens_ref.shape[0]
    j=pl.program_id(0); nj=pl.num_programs(0)
    obias=vec_ref[0:1,:]; gain=vec_ref[1:2,:]; shift=vec_ref[2:3,:]; dbias=vec_ref[3:4,:]
    @pl.when(j==0)
    def _():
        def step(i,_):
            first=pl.multiple_of(i*RB,RB); sl=pl.ds(first,RB)
            res=tokens_ref[sl,:].astype(f32)+(dot(mixed_ref[sl,:],outw_ref[...])+obias)
            res_s[sl,:]=res
            xhat,_q=norm_parts(res)
            si_s[sl,:]=(xhat*gain+shift).astype(bf16)
            live=live_mask(counts_ref,first,RB)
            gb_s[sl,:]=jnp.where(live,cot_ref[sl,:],jnp.zeros((),bf16))
            return 0
        lax.fori_loop(0,rows//RB,step,0)
        accout_s[...]=jnp.zeros_like(accout_s)
        accgs_s[...]=jnp.zeros_like(accgs_s)
    gub=jnp.zeros(gub_ref.shape,f32)
    for i in range(rows//RB):
        sl=slice(i*RB,(i+1)*RB)
        pre=dot(si_s[sl,:],up_ref[...])+ub_ref[...]
        cdf=0.5+0.5*lax.erf(pre*INV_SQRT2)
        pdf=jnp.exp(-0.5*pre*pre)*INV_SQRT2PI
        hid_s[sl,:]=(pre*cdf).astype(bf16)
        gh=dot_nt(gb_s[sl,:],down_ref[...])
        gi=(gh*(cdf+pre*pdf)).astype(bf16)
        gi_s[sl,:]=gi
        gub=gub+jnp.sum(gi.astype(f32),axis=0,keepdims=True)
    gub_ref[...]=gub
    accout_s[...]+=dot(hid_s[...],down_ref[...])
    accgs_s[...]+=dot_nt(gi_s[...],up_ref[...])
    gdown_ref[...]=dot_tn(hid_s[...],gb_s[...]).astype(bf16)
    gup_ref[...]=dot_tn(si_s[...],gi_s[...]).astype(bf16)
    @pl.when(j==nj-1)
    def _():
        gvec_ref[...]=jnp.zeros_like(gvec_ref)
        def step(i,_):
            first=pl.multiple_of(i*RB,RB); sl=pl.ds(first,RB)
            live=live_mask(counts_ref,first,RB)
            res=res_s[sl,:]
            layer=res+(accout_s[sl,:]+dbias)
            layer_ref[sl,:]=jnp.where(live,layer,0.0).astype(bf16)
            xhat,q=norm_parts(res)
            gs=accgs_s[sl,:]
            t=gs*gain
            gb=gb_s[sl,:].astype(f32)
            gres=gb+q*(t-jnp.mean(t,axis=-1,keepdims=True)-xhat*jnp.mean(t*xhat,axis=-1,keepdims=True))
            gres_ref[sl,:]=gres
            ga=gres.astype(bf16)
            mixed_unused=None
            si_s[sl,:]=ga
            gvec_ref[0:1,:]+=jnp.sum(gb,axis=0,keepdims=True)
            gvec_ref[1:2,:]+=jnp.sum(gs*xhat,axis=0,keepdims=True)
            gvec_ref[2:3,:]+=jnp.sum(gs,axis=0,keepdims=True)
            gvec_ref[3:4,:]+=jnp.sum(ga.astype(f32),axis=0,keepdims=True)
            gmix_ref[sl,:]=dot_nt(ga,outw_ref[...]).astype(bf16)
            return 0
        lax.fori_loop(0,rows//RB,step,0)
        gout_ref[...]=dot_tn(mixed_ref[...],si_s[...]).astype(bf16)

def middle(counts,mixed,tokens,cot,outw,vec,up,ub,down,FB=512):
    rows,D=tokens.shape; FF=up.shape[1]
    nj=FF//FB
    full=lambda a: pl.BlockSpec(a.shape,lambda j,c:(0,)*len(a.shape),pipeline_mode=pl.Buffered(1))
    fo=lambda s: pl.BlockSpec(s,lambda j,c:(0,)*len(s),pipeline_mode=pl.Buffered(1))
    return pl.pallas_call(mid_kernel,
        grid_spec=pltpu.PrefetchScalarGridSpec(num_scalar_prefetch=1,grid=(nj,),
            in_specs=[full(mixed),full(tokens),full(cot),full(outw),full(vec),
                pl.BlockSpec((D,FB),lambda j,c:(0,j)),pl.BlockSpec((1,FB),lambda j,c:(0,j)),pl.BlockSpec((FB,D),lambda j,c:(j,0))],
            out_specs=[fo((rows,D)),fo((rows,D)),fo((rows,D)),
                pl.BlockSpec((D,FB),lambda j,c:(0,j)),pl.BlockSpec((1,FB),lambda j,c:(0,j)),pl.BlockSpec((FB,D),lambda j,c:(j,0)),
                fo((D,D)),fo((8,D))],
            scratch_shapes=[pltpu.VMEM((rows,D),f32),pltpu.VMEM((rows,D),bf16),pltpu.VMEM((rows,D),bf16),
                pltpu.VMEM((rows,D),f32),pltpu.VMEM((rows,D),f32),pltpu.VMEM((rows,FB),bf16),pltpu.VMEM((rows,FB),bf16)]),
        out_shape=[jax.ShapeDtypeStruct((rows,D),bf16),jax.ShapeDtypeStruct((rows,D),f32),jax.ShapeDtypeStruct((rows,D),bf16),
            jax.ShapeDtypeStruct((D,FF),bf16),jax.ShapeDtypeStruct((1,FF),f32),jax.ShapeDtypeStruct((FF,D),bf16),
            jax.ShapeDtypeStruct((D,D),bf16),jax.ShapeDtypeStruct((8,D),f32)],
        compiler_params=pltpu.CompilerParams(vmem_limit_bytes=60*2**20),
        name="feed_forward",
        )(counts,mixed,tokens,cot,outw,vec,up,ub,down)


def qkv_kernel(tokens_ref, vec_ref, qw_ref, kw_ref, vw_ref, fi_ref, q_ref, k_ref, v_ref):
    rows=tokens_ref.shape[0]
    gain=vec_ref[0:1,:]; shift=vec_ref[1:2,:]; qb=vec_ref[2:3,:]; vb=vec_ref[3:4,:]
    for i in range(rows//RB):
        sl=slice(i*RB,(i+1)*RB)
        xhat,_=norm_parts(tokens_ref[sl,:].astype(f32))
        fi=(xhat*gain+shift).astype(bf16)
        fi_ref[sl,:]=fi
        q_ref[sl,:]=((dot(fi,qw_ref[...])+qb).astype(bf16).astype(f32)*0.125).astype(bf16)
        k_ref[sl,:]=dot(fi,kw_ref[...]).astype(bf16)
        v_ref[sl,:]=(dot(fi,vw_ref[...])+vb).astype(bf16)

def project(tokens,vec,qw,kw,vw):
    rows,D=tokens.shape
    return pl.pallas_call(qkv_kernel,out_shape=[jax.ShapeDtypeStruct((rows,D),bf16)]*4,
        compiler_params=pltpu.CompilerParams(vmem_limit_bytes=60*2**20),name="project")(tokens,vec,qw,kw,vw)

def back_kernel(tokens_ref, vec_ref, gres_ref, fi_ref, dq_ref, dk_ref, dv_ref, qw_ref, kw_ref, vw_ref,
        gtok_ref, gq_ref, gk_ref, gv_ref, gvec_ref):
    rows=tokens_ref.shape[0]
    gain=vec_ref[0:1,:]
    gvec=[jnp.zeros((1,tokens_ref.shape[1]),f32)]*4
    for i in range(rows//RB):
        sl=slice(i*RB,(i+1)*RB)
        dq=dq_ref[sl,:];dk=dk_ref[sl,:];dv=dv_ref[sl,:]
        gs=dot_nt(dq,qw_ref[...])+dot_nt(dk,kw_ref[...])+dot_nt(dv,vw_ref[...])
        xhat,q=norm_parts(tokens_ref[sl,:].astype(f32))
        t=gs*gain
        gtok_ref[sl,:]=gres_ref[sl,:]+q*(t-jnp.mean(t,axis=-1,keepdims=True)-xhat*jnp.mean(t*xhat,axis=-1,keepdims=True))
        for n,a in enumerate((gs*xhat,gs,dq.astype(f32),dv.astype(f32))):
            gvec[n]=gvec[n]+jnp.sum(a,axis=0,keepdims=True)
    gvec_ref[...]=jnp.zeros_like(gvec_ref)
    for n in range(4): gvec_ref[n:n+1,:]=gvec[n]
    fi=fi_ref[...]
    gq_ref[...]=dot_tn(fi,dq_ref[...]).astype(bf16)
    gk_ref[...]=dot_tn(fi,dk_ref[...]).astype(bf16)
    gv_ref[...]=dot_tn(fi,dv_ref[...]).astype(bf16)

def project_back(tokens,vec,gres,fi,dq,dk,dv,qw,kw,vw):
    rows,D=tokens.shape
    s=jax.ShapeDtypeStruct
    return pl.pallas_call(back_kernel,out_shape=[s((rows,D),f32),s((D,D),bf16),s((D,D),bf16),s((D,D),bf16),s((8,D),f32)],
        compiler_params=pltpu.CompilerParams(vmem_limit_bytes=60*2**20),name="project_back")(tokens,vec,gres,fi,dq,dk,dv,qw,kw,vw)


MESH = pl.DeviceIdType.MESH


class Place:
    def __init__(self, dp_total, fsdp_total):
        half = fsdp_total // 2
        self.outer_total = 4
        self.inner_total = half // 4
        assert half % 4 == 0
        self.pairs = dp_total // 2
        self.d = lax.axis_index("dp")
        self.f = lax.axis_index("fsdp")
        self.core = self.f % 2
        self.inner = (self.f // 2) % self.inner_total
        self.outer = self.f // (2 * self.inner_total)
        self.side = self.d % 2
        self.twin = self.d + 1 - 2 * self.side
        self.flip = self.outer // 2
        self.mirror = self.unmirror(self.outer)

    def unmirror(self, at):
        return at + self.flip * (3 - 2 * at)

    def arrival(self, step):
        return self.unmirror(step - self.mirror if step == 1 else step)

    def device(self, outer, inner, core):
        return (self.d, (outer * self.inner_total + inner) * 2 + core)

    def at_outer(self, outer):
        return self.device(outer, self.inner, self.core)

    def at_inner(self, t):
        return self.device(self.outer, (self.inner + t) % self.inner_total, self.core)

    def other_core(self):
        return self.device(self.outer, self.inner, 1 - self.core)

    def at_twin(self):
        return (self.twin, self.f)

    def me(self):
        return (self.d, self.f)

    def at_pair(self, k):
        return (self.side + 2 * ((self.d // 2 + k) % self.pairs), self.f)

    def neighbours(self, pairs=False):
        out = [self.at_outer((self.outer + s) % 4) for s in range(1, 4)]
        out += [self.at_inner(t) for t in range(1, self.inner_total)]
        out += [self.at_twin(), self.other_core()]
        if pairs:
            out += [self.at_pair(k) for k in range(1, self.pairs)]
        return out


def greet(others):
    barrier = pltpu.get_barrier_semaphore()
    for other in others:
        pl.semaphore_signal(barrier, inc=1, device_id=other, device_id_type=MESH)
    pl.semaphore_wait(barrier, len(others))


class Gather:
    def __init__(self, place, ref, edge, sems, base):
        self.place, self.ref, self.edge = place, ref, edge
        self.rows = ref.shape[-2]
        self.send_sem, self.recv_sem = sems
        self.base = base
        A, B = place.outer_total, place.inner_total
        keys = [("z", s) for s in range(1, A)] + [("Z", s) for s in range(1, A)]
        keys += [("x", s, t) for s in range(A) for t in range(1, B)]
        keys += [("y", t) for t in range(B)]
        keys += [("c",)]
        self.keys = {key: i for i, key in enumerate(keys)}
        self.sent = []
        self.sent_inside = []

    @staticmethod
    def count(B):
        return 6 + 4 * (B - 1) + B + 1

    def rows_of(self, kind):
        e, r, p = self.edge, self.rows, self.place.side
        if not e or kind == "all":
            return pl.ds(0, r)
        start, size = {"plane": (p * e, r - e), "mine": (p * (r - e), e), "theirs": ((1 - p) * (r - e), e)}[kind]
        return pl.ds(pl.multiple_of(start, 8), size)

    def part(self, outer, inner, core, kind):
        return self.ref.at[outer, inner, core, self.rows_of(kind)]

    def copy(self, key, ref, to):
        i = self.base + self.keys[key]
        into = i
        if key[0] == "Z":
            into = self.base + self.keys["z", 2 if key[1] == 2 else 3]
        return pltpu.make_async_remote_copy(src_ref=ref, dst_ref=ref, send_sem=self.send_sem.at[i],
                                            recv_sem=self.recv_sem.at[into], device_id=to, device_id_type=MESH)

    def send(self, key, make):
        self.copy(key, *make()).start()
        self.sent.append((key, make))

    def send_inside(self, key, make):
        @pl.when(self.place.mirror == 1)
        def _():
            self.copy(key, *make()).start()

        self.sent_inside.append((key, make))

    def got(self, key, ref):
        self.copy(key, ref, self.place.me()).wait_recv()

    def outer_of(self, step):
        return self.place.outer if step == 0 else self.place.arrival(step)

    def own_line(self, step):
        p = self.place
        return self.part(self.outer_of(step), p.inner, p.core, "plane")

    def start(self):
        p = self.place
        self.send(("z", 1), lambda: (self.own_line(0), p.at_outer(p.unmirror(1 - p.mirror))))
        self.send_inside(("z", 2), lambda: (self.own_line(0), p.at_outer(p.unmirror(2))))
        self.pass_inner(0)

    def pass_inner(self, step):
        p = self.place
        for t in range(1, p.inner_total):
            self.send(("x", step, t), lambda t=t: (self.own_line(step), p.at_inner(-t)))

    def from_outer_step(self, step):
        p = self.place
        self.got(("z", step), self.own_line(step))
        self.send_inside(("Z", step), lambda: (self.own_line(step), p.at_outer(p.unmirror(2 if step == 1 else 0))))
        self.pass_inner(step)
        if step == 3:
            self.pass_twin(0)

    def from_outer(self):
        for step in range(1, 4):
            self.from_outer_step(step)

    def line(self, t, kind):
        p = self.place
        return self.part(slice(None), (p.inner + t) % p.inner_total, p.core, kind)

    def pass_twin(self, t):
        if self.edge:
            self.send(("y", t), lambda: (self.line(t, "mine"), self.place.at_twin()))

    def from_inner(self):
        p = self.place
        for t in range(1, p.inner_total):
            for step in range(4):
                self.got(("x", step, t), self.part(self.outer_of(step), (p.inner + t) % p.inner_total, p.core, "plane"))
            self.pass_twin(t)

    def half(self, core):
        return self.part(slice(None), slice(None), core, "all")

    def from_twin(self):
        p = self.place
        if self.edge:
            for t in range(p.inner_total):
                self.got(("y", t), self.line(t, "theirs"))
        self.send(("c",), lambda: (self.half(p.core), p.other_core()))

    def from_core(self):
        self.got(("c",), self.half(1 - self.place.core))

    def finish(self):
        for key, make in self.sent:
            self.copy(key, *make()).wait_send()

        @pl.when(self.place.mirror == 1)
        def _():
            for key, make in self.sent_inside:
                self.copy(key, *make()).wait_send()


class Scatter:
    def __init__(self, place, terms, bufs, edge, emit, sems, base):
        self.place, self.terms, self.edge, self.emit = place, terms, edge, emit
        self.sums, self.twin_buf, self.inner_buf, self.outer_buf, self.last_buf = bufs[:5]
        self.pair_bufs = bufs[5:]
        self.send_sem, self.recv_sem = sems
        self.base = base
        p, e, w = place.side, edge, terms.shape[-1]
        at = lambda start, size: pl.ds(pl.multiple_of(start, 128), size)
        self.plane = at(p * e, w - e)
        self.mine = at(p * (w - e), e)
        self.theirs = at((1 - p) * (w - e), e)
        self.twin_plane = at((1 - p) * e, w - e)
        self.middle = pl.ds(e, w - 2 * e)

    @staticmethod
    def count(B, pairs):
        return 1 + 1 + (B - 1) + 3 + 1 + (pairs - 1)

    @staticmethod
    def shapes(B, pairs, rows, width, edge, lead=()):
        out = [(4, B, rows, width), (4, B, rows, edge), (B - 1, 4, rows, width), (3, rows, width), (rows, width)]
        if pairs > 1:
            out += [(rows, width), (pairs - 1, rows, width)]
        return [pltpu.VMEM(tuple(lead) + s, bf16) for s in out]

    def copy(self, i, src, dst, to):
        return pltpu.make_async_remote_copy(src_ref=src, dst_ref=dst, send_sem=self.send_sem.at[self.base + i],
                                            recv_sem=self.recv_sem.at[self.base + i], device_id=to, device_id_type=MESH)

    def copies(self, stage):
        p = self.place
        A, B = 4, p.inner_total
        if stage == "core":
            return [self.copy(0, self.terms.at[:, :, 1 - p.core], self.sums, p.other_core())]
        if stage == "twin":
            return [self.copy(1, self.sums.at[:, :, :, self.theirs], self.twin_buf, p.at_twin())]
        if stage == "inner":
            return [self.copy(1 + t, self.sums.at[:, (p.inner + B - t) % B, :, self.plane],
                              self.inner_buf.at[t - 1, :, :, self.plane], p.at_inner(-t)) for t in range(1, B)]
        if stage == "outer":
            return [self.copy(B + s, self.sums.at[(p.outer + A - s) % A, p.inner, :, self.plane],
                              self.outer_buf.at[s - 1, :, self.plane], p.at_outer((p.outer + A - s) % A))
                    for s in range(1, A)]
        if stage == "last":
            return [self.copy(A + B, self.sums.at[p.outer, p.inner, :, self.plane], self.last_buf.at[:, self.plane],
                              p.at_twin())]
        half, others = self.pair_bufs
        return [self.copy(A + B + k, half, others.at[k - 1], p.at_pair(p.pairs - k)) for k in range(1, p.pairs)]

    def go(self, stage):
        for c in self.copies(stage):
            c.start()

    def got(self, i, dst):
        self.copy(i, dst, dst, self.place.me()).wait_recv()

    def start(self):
        self.go("core")

    def from_core(self):
        p = self.place
        B = p.inner_total
        self.got(0, self.sums)

        def add(i, _):
            a, b = i // B, i % B
            self.sums[a, b] = (self.sums[a, b].astype(f32) + self.terms[a, b, p.core].astype(f32)).astype(bf16)
            return 0

        lax.fori_loop(0, 4 * B, add, 0)
        self.go("twin")

    def from_twin(self):
        p = self.place
        B = p.inner_total
        self.got(1, self.twin_buf)

        def add(i, _):
            a, b = i // B, i % B
            self.sums[a, b, :, self.mine] = (self.sums[a, b, :, self.mine].astype(f32)
                                             + self.twin_buf[a, b].astype(f32)).astype(bf16)
            return 0

        lax.fori_loop(0, 4 * B, add, 0)
        self.go("inner")

    def from_inner(self):
        p = self.place
        B = p.inner_total
        for t in range(1, B):
            self.got(1 + t, self.inner_buf.at[t - 1, :, :, self.plane])

        def add(a, _):
            total = self.sums[a, p.inner, :, self.plane].astype(f32)
            for t in range(1, B):
                total = total + self.inner_buf[t - 1, a, :, self.plane].astype(f32)
            self.sums[a, p.inner, :, self.plane] = total.astype(bf16)
            return 0

        lax.fori_loop(0, 4, add, 0)
        self.go("outer")

    def from_outer(self):
        p = self.place
        B = p.inner_total
        for s in range(1, 4):
            self.got(B + s, self.outer_buf.at[s - 1, :, self.plane])
        total = self.sums[p.outer, p.inner, :, self.plane].astype(f32)
        for s in range(1, 4):
            total = total + self.outer_buf[s - 1, :, self.plane].astype(f32)
        self.sums[p.outer, p.inner, :, self.plane] = total.astype(bf16)
        self.go("last")

    def from_last(self):
        p = self.place
        self.got(4 + p.inner_total, self.last_buf.at[:, self.twin_plane])
        own = lambda cols: self.sums[p.outer, p.inner, :, cols].astype(f32)
        last = lambda cols: self.last_buf[:, cols].astype(f32)
        if p.pairs == 1:
            self.emit(self.mine, own(self.mine))
            self.emit(self.middle, own(self.middle) + last(self.middle))
            self.emit(self.theirs, last(self.theirs))
            return
        half, others = self.pair_bufs
        half[:, self.mine] = own(self.mine).astype(bf16)
        half[:, self.middle] = (own(self.middle) + last(self.middle)).astype(bf16)
        half[:, self.theirs] = last(self.theirs).astype(bf16)
        self.go("pairs")

    def from_pairs(self):
        p = self.place
        if p.pairs == 1:
            return
        half, others = self.pair_bufs
        total = half[...].astype(f32)
        for k in range(1, p.pairs):
            self.got(4 + p.inner_total + k, others.at[k - 1])
            total = total + others[k - 1].astype(f32)
        self.emit(pl.ds(0, self.terms.shape[-1]), total)

    def finish(self):
        for stage in ("core", "twin", "inner", "outer", "last") + (("pairs",) if self.place.pairs > 1 else ()):
            for c in self.copies(stage):
                c.wait_send()


class Total:
    def __init__(self, place, value, bufs, out, sems, base):
        self.place, self.value, self.bufs, self.out = place, value, bufs, out
        self.send_sem, self.recv_sem = sems
        p = place
        rounds = [[p.other_core()], [p.at_inner(t) for t in range(1, p.inner_total)],
                  [p.at_outer((p.outer + s) % 4) for s in range(1, 4)], [p.at_twin()],
                  [p.at_pair(k) for k in range(1, p.pairs)]]
        self.rounds = [r for r in rounds if r]
        self.base = base

    @staticmethod
    def count(B, pairs):
        return 1 + (B - 1) + 3 + 1 + (pairs - 1)

    @staticmethod
    def shapes(B, pairs, shape):
        return [pltpu.VMEM((Total.count(B, pairs),) + shape, f32), pltpu.VMEM((5,) + shape, f32)]

    def copies(self, r):
        landing, held = self.bufs
        i = sum(len(x) for x in self.rounds[:r])
        return [(pltpu.make_async_remote_copy(src_ref=held.at[r], dst_ref=landing.at[i + k],
                                              send_sem=self.send_sem.at[self.base + i + k],
                                              recv_sem=self.recv_sem.at[self.base + i + k], device_id=to,
                                              device_id_type=MESH), i + k) for k, to in enumerate(self.rounds[r])]

    def start(self):
        self.bufs[1][0] = self.value[...]
        for c, _ in self.copies(0):
            c.start()

    def step(self, r):
        landing, held = self.bufs
        total = held[r]
        for c, i in self.copies(r):
            c.wait_recv()
            total = total + landing[i]
        if r + 1 < len(self.rounds):
            held[r + 1] = total
            for c, _ in self.copies(r + 1):
                c.start()
        else:
            self.out[...] = total

    def steps(self):
        return [functools.partial(self.step, r) for r in range(len(self.rounds))]

    def finish(self):
        for r in range(len(self.rounds)):
            for c, _ in self.copies(r):
                c.wait_send()


def local(src, dst, sem):
    c = pltpu.make_async_copy(src, dst, sem)
    c.start()
    return c


BLOCKS = 3


def lane_tile(source, moves):
    lane = None
    out = None
    for col, to, size in moves:
        tile = source[:, col // 128 * 128:col // 128 * 128 + 128]
        shift = (to - col) % 128
        if shift:
            tile = pltpu.roll(tile, shift, 1)
        if out is None:
            out = tile
            lane = lax.broadcasted_iota(jnp.int32, tile.shape, 1)
        else:
            out = jnp.where((lane >= to) & (lane < to + size), tile, out)
    return out


def split_columns(source, owners):
    piece = source.shape[1] // owners // BLOCKS
    per = 128 // piece
    out = []
    for j in range(BLOCKS):
        tiles = [lane_tile(source, [(((t * per + q) * BLOCKS + j) * piece, q * piece, piece) for q in range(per)])
                 for t in range(owners // per)]
        out.append(jnp.concatenate(tiles, axis=1))
    return out


def join_columns(parts, owners):
    source = jnp.concatenate(parts, axis=1)
    width = parts[0].shape[1]
    piece = width // owners
    per = 128 // piece
    tiles = []
    for t in range(source.shape[1] // 128):
        moves = []
        for q in range(per):
            unit = t * per + q
            moves.append(((unit % BLOCKS) * width + unit // BLOCKS * piece, q * piece, piece))
        tiles.append(lane_tile(source, moves))
    return jnp.concatenate(tiles, axis=1)


CFG = {}


def attend_block(counts_ref, q_ref, k_ref, v_ref, mixed_ref, lse_ref, pair, block):
    rows = q_ref.shape[0]
    lane = lax.broadcasted_iota(jnp.int32, (QB, 128), 1)
    first = pl.multiple_of(block * QB, QB)
    cols = pl.ds(pl.multiple_of(pair * 128, 128), 128)
    q = q_ref[pl.ds(first, QB), cols]
    k = k_ref[:, cols]
    v = v_ref[:, cols]
    ends = image_ends(counts_ref[0], counts_ref[1], rows)
    rid = image_of(first + lax.broadcasted_iota(jnp.int32, (QB, 1), 0), ends)
    cid = image_of(lax.broadcasted_iota(jnp.int32, (1, rows), 1), ends)
    bias = jnp.where(rid == cid, 0.0, NEG)
    outs = []
    lses = []
    for e in range(2):
        qm = jnp.where((lane < 64) == (e == 0), q, jnp.zeros_like(q))
        s = dot_nt(qm, k) + bias
        m = jnp.max(s, axis=1, keepdims=True)
        p = jnp.exp(s - m)
        l = jnp.sum(p, axis=1, keepdims=True)
        o = dot(p.astype(bf16), v)
        outs.append(o * (1.0 / l))
        lses.append(m + jnp.log(l))
    mixed_ref[pl.ds(first, QB), cols] = jnp.where(lane < 64, outs[0], outs[1]).astype(bf16)
    both = jnp.where(lane < 64, jnp.broadcast_to(lses[0], (QB, 128)), jnp.broadcast_to(lses[1], (QB, 128)))
    t = both.T
    lse_ref[pair, 0:1, pl.ds(first, QB)] = t[0:1, :]
    lse_ref[pair, 1:2, pl.ds(first, QB)] = t[64:65, :]


def gather_edge(rows, last=False):
    return rows // 3 if rows % 24 == 0 else rows // 4 if last or rows < 64 else rows * 3 // 8


def gather_plan(sm, u, vectors):
    step = lambda unit, s: functools.partial(unit.from_outer_step, s)
    head = [sm.start, u[0].start, sm.from_outer, u[1].start, u[0].from_outer, sm.from_inner, u[2].start,
            u[1].from_outer, u[0].from_inner, sm.from_twin, u[3].start, u[2].from_outer, u[1].from_inner,
            u[0].from_twin, sm.from_core, vectors, u[4].start, step(u[3], 1), u[0].from_core]
    middle = [[step(u[3], 2)], [step(u[3], 3), u[5].start], [u[2].from_inner], [u[1].from_twin]]
    rest = []
    for t in range(4, len(u)):
        rest += [[step(u[t], 1)] + ([u[t + 2].start] if t + 2 < len(u) else []), [step(u[t], 2)], [step(u[t], 3)],
                 [u[t - 1].from_inner], [u[t - 2].from_twin, u[t - 3].from_core]]
    n = len(u)
    rest += [[u[n - 1].from_inner], [u[n - 2].from_twin, u[n - 3].from_core], [u[n - 1].from_twin, u[n - 2].from_core],
             [u[n - 1].from_core]]
    return head, middle, rest


def gather_kernel(dp_total, n, counts_ref, tokens_hbm, small_ref, qo_ref, ko_ref, vo_ref, oo_ref, uo_ref, do_ref,
                  q_hbm, k_hbm, v_hbm, vec_ref, mixed_hbm, lse_ref, qkv_all, o_all, up_all, down_all, small_all,
                  tokens_s, q_s, k_s, v_s, mixed_s, w_s, small_s, up_own, send_sem, recv_sem, loc_sem):
    place = Place(dp_total, n)
    B = place.inner_total
    own = qo_ref.shape[0]
    piece = do_ref.shape[0] // BLOCKS
    take_tokens = local(tokens_hbm, tokens_s, loc_sem.at[0])
    for j, part in enumerate(split_columns(uo_ref[...].astype(f32), n)):
        up_own[j] = part.astype(bf16)
    sems = (send_sem, recv_sem)
    refs = [(small_all, 0), (qkv_all, own), (o_all, gather_edge(own))]
    for j in range(BLOCKS):
        refs += [(up_all.at[j], gather_edge(own)), (down_all.at[j], gather_edge(piece, j == BLOCKS - 1))]
    units = [Gather(place, ref, edge, sems, i * Gather.count(B)) for i, (ref, edge) in enumerate(refs)]
    mine = lambda unit: unit.part(place.outer, place.inner, place.core, "plane")
    fill = [local(small_ref, mine(units[0]), loc_sem.at[1])]
    own_qkv = lambda i: qkv_all.at[place.outer, place.inner, place.core, pl.ds(i * own, own)]
    fill.append(local(ko_ref, own_qkv(1), loc_sem.at[2]))

    @pl.when(place.side == 0)
    def _():
        local(qo_ref, own_qkv(0), loc_sem.at[3]).wait()

    @pl.when(place.side == 1)
    def _():
        local(vo_ref, own_qkv(2), loc_sem.at[3]).wait()

    fill.append(local(oo_ref.at[units[2].rows_of("plane")], mine(units[2]), loc_sem.at[5]))
    for j in range(BLOCKS):
        a, b = units[3 + 2 * j], units[4 + 2 * j]
        fill.append(local(up_own.at[j, a.rows_of("plane")], mine(a), loc_sem.at[6 + 2 * j]))
        rows = b.rows_of("plane")
        fill.append(local(do_ref.at[pl.ds(pl.multiple_of(j * piece + rows.start, 8), rows.size)], mine(b),
                          loc_sem.at[7 + 2 * j]))
    greet(place.neighbours())
    for c in fill:
        c.wait()

    def vectors():
        local(small_all, small_s, loc_sem.at[1]).wait()
        total = jnp.zeros(vec_ref.shape, f32)
        for i in range(n):
            total = total + small_s[i // (2 * B), i // 2 % B, i % 2].astype(f32)
        vec_ref[...] = total

    head, middle, rest = CFG.get("plan", gather_plan)(units[0], units[1:], vectors)
    for one in head:
        one()
    take = local(qkv_all, w_s, loc_sem.at[1])
    take_tokens.wait()
    take.wait()
    rows, feat = tokens_s.shape

    def project_rows(i):
        sl = slice(i * RB, (i + 1) * RB)
        xhat, _q = norm_parts(tokens_s[sl, :].astype(f32))
        fi = (xhat * vec_ref[0:1, :] + vec_ref[1:2, :]).astype(bf16)
        weight = lambda i: w_s[:, :, :, i * own:(i + 1) * own, :].reshape(feat, feat)
        q_s[sl, :] = ((dot(fi, weight(0)) + vec_ref[2:3, :]).astype(bf16).astype(f32) * 0.125).astype(bf16)
        k_s[sl, :] = dot(fi, weight(1)).astype(bf16)
        v_s[sl, :] = (dot(fi, weight(2)) + vec_ref[3:4, :]).astype(bf16)

    for i in range(rows // RB):
        if CFG.get("proj", True):
            project_rows(i)
        for one in middle[i]:
            one()
    keep = [local(a, b, loc_sem.at[2 + i]) for i, (a, b) in enumerate(((q_s, q_hbm), (k_s, k_hbm), (v_s, v_hbm)))]
    blocks = rows // QB
    pieces = feat // 128 * blocks

    def attend_piece(i, _):
        if CFG.get("att", True):
            attend_block(counts_ref, q_s, k_s, v_s, mixed_s, lse_ref, i // blocks, i % blocks)
        for at in range(pieces):
            todo = [one for k, batch in enumerate(rest) if k * pieces // len(rest) == at for one in batch]
            if todo:
                @pl.when(i == at)
                def _(todo=todo):
                    for one in todo:
                        one()
        return 0

    lax.fori_loop(0, pieces, attend_piece, 0)
    keep.append(local(mixed_s, mixed_hbm, loc_sem.at[0]))
    for c in keep:
        c.wait()
    for x in units:
        x.finish()


def gather_attend(sizes, counts, tokens, small, qw, kw, vw, ow, up, down):
    dp_total, n = sizes
    rows, feat = tokens.shape
    own = qw.shape[0]
    B = n // 8
    pairs = feat // 128
    s = jax.ShapeDtypeStruct
    vm = pl.BlockSpec(memory_space=pltpu.VMEM)
    anyspec = pl.BlockSpec(memory_space=pl.ANY)
    full = lambda *dims: (4, B, 2) + dims
    width = up.shape[1] // BLOCKS
    piece = down.shape[0] // BLOCKS
    act = s((rows, feat), bf16)
    copies = (3 + 2 * BLOCKS) * Gather.count(B)
    return pl.pallas_call(
        functools.partial(gather_kernel, dp_total, n),
        in_specs=[pl.BlockSpec(memory_space=pltpu.SMEM), anyspec] + [vm] * 7,
        out_specs=[anyspec] * 3 + [vm, anyspec, vm] + [anyspec] * 5,
        out_shape=[act, act, act, s(small.shape, f32), act, s((pairs, 2, rows), f32), s(full(3 * own, feat), bf16),
                   s(full(own, feat), bf16), s((BLOCKS,) + full(own, width), bf16),
                   s((BLOCKS,) + full(piece, feat), bf16), s(full(*small.shape), bf16)],
        scratch_shapes=[pltpu.VMEM((rows, feat), bf16)] * 5 + [
            pltpu.VMEM(full(3 * own, feat), bf16), pltpu.VMEM(full(*small.shape), bf16),
            pltpu.VMEM((BLOCKS, own, width), bf16), pltpu.SemaphoreType.DMA((copies,)),
            pltpu.SemaphoreType.DMA((copies,)), pltpu.SemaphoreType.DMA((6 + 2 * BLOCKS,))],
        compiler_params=pltpu.CompilerParams(collective_id=1, has_side_effects=True, vmem_limit_bytes=60 * 2**20),
        name="gather_attend",
    )(counts, tokens, small, qw, kw, vw, ow, up, down)


def scatter_edge(width):
    return 128 if width == 768 else width // 4


def feed_kernel(dp_total, n, counts_ref, mixed_ref, tokens_ref, cot_ref, outw_ref, vec_ref, up_hbm, down_hbm,
                layer_ref, gres_ref, gmix_ref, gout_ref, gup_ref, gdown_ref, gvec_ref,
                res_s, si_s, gb_s, hid_s, gi_s, up_s, down_s, ub_s, gub_s, gup_s, *rest):
    rows, feat = tokens_ref.shape
    width = gi_s.shape[1]
    piece = gdown_ref.shape[0] // BLOCKS
    place = Place(dp_total, n)
    B, pairs = place.inner_total, place.pairs
    per = 5 if pairs == 1 else 7
    uterm_s, dterm_s = rest[:2]
    ubufs, dbufs = rest[2:2 + per], rest[2 + per:2 + 2 * per]
    send_sem, recv_sem, loc_sem = rest[2 + 2 * per:]
    load = lambda j: (pltpu.make_async_copy(up_hbm.at[j], up_s.at[j], loc_sem.at[2 * j]),
                      pltpu.make_async_copy(down_hbm.at[j], down_s.at[j], loc_sem.at[2 * j + 1]))
    for j in range(BLOCKS):
        for c in load(j):
            c.start()
    count = Scatter.count(B, pairs)

    def unit_u(j):
        def emit(cols, value):
            gup_s[j, :, cols] = value
        return Scatter(place, uterm_s.at[j % 2], [b.at[j] for b in ubufs], scatter_edge(width), emit,
                       (send_sem, recv_sem), 2 * j * count)

    def unit_d(j):
        def emit(cols, value):
            gdown_ref[pl.ds(pl.multiple_of(j * piece, 8), piece), cols] = value
        return Scatter(place, dterm_s.at[j % 2], [b.at[j] for b in dbufs], scatter_edge(feat), emit,
                       (send_sem, recv_sem), (2 * j + 1) * count)

    def last(unit):
        unit.from_last()
        unit.from_pairs()

    obias, gain, shift, dbias = (vec_ref[i:i + 1, :] for i in range(4, 8))
    ub = jnp.concatenate([vec_ref[8 + i:9 + i, :] for i in range(BLOCKS * width // feat)], axis=1)
    for j, part in enumerate(split_columns(jnp.broadcast_to(ub, (8, ub.shape[1])), n)):
        ub_s[j] = part

    def begin(i, _):
        first = pl.multiple_of(i * RB, RB)
        sl = pl.ds(first, RB)
        res = tokens_ref[sl, :].astype(f32) + (dot(mixed_ref[sl, :], outw_ref[...]) + obias)
        res_s[sl, :] = res
        xhat, _q = norm_parts(res)
        si_s[sl, :] = (xhat * gain + shift).astype(bf16)
        gb_s[sl, :] = jnp.where(live_mask(counts_ref, first, RB), cot_ref[sl, :], jnp.zeros((), bf16))
        gres_ref[sl, :] = jnp.zeros((RB, feat), f32)
        return 0

    lax.fori_loop(0, rows // RB, begin, 0)
    greet(place.neighbours(pairs=True))

    def block(j, _):
        for c in load(j):
            c.wait()
        upw = lambda: up_s[j].reshape(feat, width)
        downw = lambda: down_s[j].reshape(width, feat)
        cols = pl.ds(pl.multiple_of(j * width, 128), width)
        gub_s[j] = jnp.zeros(gub_s.shape[1:], f32)

        def after(back, when, todo):
            @pl.when(when & (j >= back))
            def _():
                todo(j - back)

        def rows_piece(i, _):
            sl = pl.ds(pl.multiple_of(i * RB, RB), RB)
            pre = dot(si_s[sl, :], upw()) + ub_s[j, 0:1, :]
            cdf = 0.5 + 0.5 * lax.erf(pre * INV_SQRT2)
            pdf = jnp.exp(-0.5 * pre * pre) * INV_SQRT2PI
            hid_s[sl, cols] = (pre * cdf).astype(bf16)
            gi = (dot_nt(gb_s[sl, :], downw()) * (cdf + pre * pdf)).astype(bf16)
            gi_s[sl, :] = gi
            gub_s[j, 0:1, :] += jnp.sum(gi.astype(f32), axis=0, keepdims=True)
            after(1, i == 0, lambda k: unit_u(k).from_twin())
            after(2, i == 0, lambda k: unit_u(k).from_outer())
            after(2, i == 1, lambda k: last(unit_d(k)))
            after(2, i == 2, lambda k: last(unit_u(k)))
            after(1, i == 3, lambda k: unit_d(k).from_inner())
            return 0

        lax.fori_loop(0, rows // RB, rows_piece, 0)
        always = j >= 0

        @pl.when(j >= 2)
        def _():
            for c in unit_u(j - 2).copies("core") + unit_d(j - 2).copies("core"):
                c.wait_send()

        dterm_s[j % 2] = dot_tn(hid_s[:, cols], gb_s[...]).astype(bf16).reshape(dterm_s.shape[1:])
        unit_d(j).start()
        after(1, always, lambda k: unit_u(k).from_inner())
        uterm_s[j % 2] = dot_tn(si_s[...], gi_s[...]).astype(bf16).reshape(uterm_s.shape[1:])
        unit_u(j).start()
        unit_d(j).from_core()
        gres_ref[...] += dot_nt(gi_s[...], upw())
        unit_u(j).from_core()
        unit_d(j).from_twin()
        after(1, always, lambda k: unit_d(k).from_outer())
        return 0

    lax.fori_loop(0, BLOCKS, block, 0)
    end, before = BLOCKS - 1, BLOCKS - 2
    gvec_ref[...] = jnp.zeros_like(gvec_ref)

    def finish_rows(i, _):
        first = pl.multiple_of(i * RB, RB)
        sl = pl.ds(first, RB)
        res = res_s[sl, :]
        layer = res + (dot(hid_s[sl, :], down_s[...].reshape(BLOCKS * width, feat)) + dbias)
        layer_ref[sl, :] = jnp.where(live_mask(counts_ref, first, RB), layer, 0.0).astype(bf16)
        xhat, q = norm_parts(res)
        gs = gres_ref[sl, :]
        t = gs * gain
        gb = gb_s[sl, :].astype(f32)
        gres = gb + q * (t - jnp.mean(t, axis=-1, keepdims=True) - xhat * jnp.mean(t * xhat, axis=-1, keepdims=True))
        gres_ref[sl, :] = gres
        ga = gres.astype(bf16)
        si_s[sl, :] = ga
        gvec_ref[7:8, :] += jnp.sum(gb, axis=0, keepdims=True)
        gvec_ref[5:6, :] += jnp.sum(gs * xhat, axis=0, keepdims=True)
        gvec_ref[6:7, :] += jnp.sum(gs, axis=0, keepdims=True)
        gvec_ref[4:5, :] += jnp.sum(ga.astype(f32), axis=0, keepdims=True)
        gmix_ref[sl, :] = dot_nt(ga, outw_ref[...]).astype(bf16)

        def at(k, *todo):
            @pl.when(i == k)
            def _():
                for one in todo:
                    one()

        at(0, unit_u(end).from_twin, unit_u(before).from_outer)
        at(1, lambda: last(unit_d(before)))
        at(2, lambda: last(unit_u(before)), unit_d(end).from_inner)
        return 0

    lax.fori_loop(0, rows // RB, finish_rows, 0)
    unit_u(end).from_inner()
    gout_ref[...] = dot_tn(mixed_ref[...], si_s[...]).astype(bf16)
    total = join_columns([gub_s[j] for j in range(BLOCKS)], n)
    for i in range(total.shape[1] // feat):
        gvec_ref[8 + i:9 + i, :] = total[0:1, i * feat:(i + 1) * feat]
    unit_d(end).from_outer()
    unit_u(end).from_outer()
    last(unit_d(end))
    last(unit_u(end))
    gup_ref[...] = join_columns([gup_s[j] for j in range(BLOCKS)], n)

    def drain(j, _):
        for unit in (unit_u(j), unit_d(j)):
            for stage in ("twin", "inner", "outer", "last") + (("pairs",) if pairs > 1 else ()):
                for c in unit.copies(stage):
                    c.wait_send()

            @pl.when(j >= BLOCKS - 2)
            def _(unit=unit):
                for c in unit.copies("core"):
                    c.wait_send()
        return 0

    lax.fori_loop(0, BLOCKS, drain, 0)


def feed_forward(sizes, counts, mixed, tokens, cot, outw, vec, up_all, down_all):
    dp_total, n = sizes
    rows, feat = tokens.shape
    B, pairs = n // 8, dp_total // 2
    own, width = up_all.shape[-2:]
    piece = down_all.shape[-2]
    s = jax.ShapeDtypeStruct
    vm = pl.BlockSpec(memory_space=pltpu.VMEM)
    anyspec = pl.BlockSpec(memory_space=pl.ANY)
    act = lambda dt: pltpu.VMEM((rows, feat), dt)
    copies = 2 * BLOCKS * Scatter.count(B, pairs)
    return pl.pallas_call(
        functools.partial(feed_kernel, dp_total, n),
        in_specs=[pl.BlockSpec(memory_space=pltpu.SMEM)] + [vm] * 5 + [anyspec] * 2,
        out_specs=[vm] * 7,
        out_shape=[s((rows, feat), bf16), s((rows, feat), f32), s((rows, feat), bf16), s((feat, feat), bf16),
                   s((own, BLOCKS * width), f32), s((BLOCKS * piece, feat), f32), s(vec.shape, f32)],
        scratch_shapes=[act(f32), act(bf16), act(bf16), pltpu.VMEM((rows, BLOCKS * width), bf16),
                        pltpu.VMEM((rows, width), bf16), pltpu.VMEM(up_all.shape, bf16),
                        pltpu.VMEM(down_all.shape, bf16), pltpu.VMEM((BLOCKS, 8, width), f32),
                        pltpu.VMEM((BLOCKS, 8, width), f32), pltpu.VMEM((BLOCKS, own, width), f32),
                        pltpu.VMEM((2,) + up_all.shape[1:], bf16), pltpu.VMEM((2,) + down_all.shape[1:], bf16)]
        + Scatter.shapes(B, pairs, own, width, scatter_edge(width), (BLOCKS,))
        + Scatter.shapes(B, pairs, piece, feat, scatter_edge(feat), (BLOCKS,))
        + [pltpu.SemaphoreType.DMA((copies,)), pltpu.SemaphoreType.DMA((copies,)),
           pltpu.SemaphoreType.DMA((2 * BLOCKS,))],
        compiler_params=pltpu.CompilerParams(collective_id=2, has_side_effects=True, vmem_limit_bytes=67043328),
        name="feed_forward",
    )(counts, mixed, tokens, cot, outw, vec, up_all, down_all)


def back_kernel(dp_total, n, edges, tokens_ref, vec_ref, gres_ref, dq_ref, dk_ref, dv_ref, w_ref, oterm_ref, small_ref,
                gtok_ref, gq_ref, gk_ref, gv_ref, go_ref, total_ref,
                fi_s, small_s, qterm_s, kterm_s, vterm_s, *rest):
    place = Place(dp_total, n)
    B, pairs = place.inner_total, place.pairs
    rows, feat = tokens_ref.shape
    own = gq_ref.shape[0]
    per = 5 if pairs == 1 else 7
    send_sem, recv_sem = rest[-2:]
    sems = (send_sem, recv_sem)

    def into(ref):
        def emit(cols, value):
            ref[:, cols] = value
        return emit

    pieces = [(oterm_ref, go_ref), (qterm_s, gq_ref), (kterm_s, gk_ref), (vterm_s, gv_ref)]
    o, q, k, v = [Scatter(place, term, rest[i * per:(i + 1) * per], edges[i], into(out), sems,
                          i * Scatter.count(B, pairs)) for i, (term, out) in enumerate(pieces)]
    small = Total(place, small_s, rest[4 * per:4 * per + 2], total_ref, sems, 4 * Scatter.count(B, pairs))
    gain, shift = vec_ref[0:1, :], vec_ref[1:2, :]
    greet(place.neighbours(pairs=True))
    o.start()

    def norm_rows(i, _):
        sl = pl.ds(pl.multiple_of(i * RB, RB), RB)
        xhat, _q = norm_parts(tokens_ref[sl, :].astype(f32))
        fi_s[sl, :] = (xhat * gain + shift).astype(bf16)
        return 0

    lax.fori_loop(0, rows // RB, norm_rows, 0)
    grad = lambda d: dot_tn(fi_s[...], d[...]).astype(bf16).reshape(qterm_s.shape)
    o.from_core()
    qterm_s[...] = grad(dq_ref)
    q.start()
    o.from_twin()
    kterm_s[...] = grad(dk_ref)
    k.start()
    q.from_core()
    vterm_s[...] = grad(dv_ref)
    v.start()
    k.from_core()
    q.from_twin()
    small_s[...] = small_ref[...]

    def back_rows(i, _):
        sl = pl.ds(pl.multiple_of(i * RB, RB), RB)
        dq, dk, dv = dq_ref[sl, :], dk_ref[sl, :], dv_ref[sl, :]
        weight = lambda i: w_ref[:, :, :, i * own:(i + 1) * own, :].reshape(feat, feat)
        gs = dot_nt(dq, weight(0)) + dot_nt(dk, weight(1)) + dot_nt(dv, weight(2))
        xhat, q_ = norm_parts(tokens_ref[sl, :].astype(f32))
        t = gs * gain
        gtok_ref[sl, :] = gres_ref[sl, :] + q_ * (t - jnp.mean(t, axis=-1, keepdims=True)
                                                  - xhat * jnp.mean(t * xhat, axis=-1, keepdims=True))
        for r, a in enumerate((gs * xhat, gs, dq.astype(f32), dv.astype(f32))):
            small_s[r:r + 1, :] += jnp.sum(a, axis=0, keepdims=True)

        def at(j, *todo):
            @pl.when(i == j)
            def _():
                for one in todo:
                    one()

        at(0, v.from_core, k.from_twin, o.from_inner)
        at(1, v.from_twin, q.from_inner)
        at(2, o.from_outer)
        at(3, k.from_inner)
        return 0

    lax.fori_loop(0, rows // RB, back_rows, 0)

    def last(unit):
        unit.from_last()
        unit.from_pairs()

    small.start()
    steps = small.steps()
    steps[0]()
    v.from_inner()
    q.from_outer()
    steps[1]()
    last(o)
    k.from_outer()
    steps[2]()
    last(q)
    v.from_outer()
    for one in steps[3:]:
        one()
    last(k)
    last(v)
    for unit in (o, q, k, v, small):
        unit.finish()


def project_back(sizes, tokens, vec, gres, dq, dk, dv, qkv_all, gout, small):
    dp_total, n = sizes
    rows, feat = tokens.shape
    B, pairs = n // 8, dp_total // 2
    own = feat // n
    edges = (128, 256, 128, 256)
    s = jax.ShapeDtypeStruct
    vm = pl.BlockSpec(memory_space=pltpu.VMEM)
    term = (4, B, 2, own, feat)
    scratch = [pltpu.VMEM((rows, feat), bf16), pltpu.VMEM(small.shape, f32)] + [pltpu.VMEM(term, bf16)] * 3
    for e in edges:
        scratch += Scatter.shapes(B, pairs, own, feat, e)
    scratch += Total.shapes(B, pairs, small.shape)
    copies = 4 * Scatter.count(B, pairs) + Total.count(B, pairs)
    scratch += [pltpu.SemaphoreType.DMA((copies,))] * 2
    return pl.pallas_call(
        functools.partial(back_kernel, dp_total, n, edges),
        in_specs=[vm] * 9, out_specs=[vm] * 6,
        out_shape=[s((rows, feat), f32)] + [s((own, feat), f32)] * 4 + [s(small.shape, f32)],
        scratch_shapes=scratch,
        compiler_params=pltpu.CompilerParams(collective_id=3, has_side_effects=True, vmem_limit_bytes=60 * 2**20),
        name="project_back",
    )(tokens, vec, gres, dq, dk, dv, qkv_all, gout.reshape(term), small)

FSDP="fsdp"

def spread(vectors, index, total):
    own = vectors.shape[-1]
    at = lax.broadcasted_iota(jnp.int32, (1, total, own), 1)
    wide = jnp.where(at == index, vectors[:, None, :], jnp.zeros((), vectors.dtype))
    return wide.reshape(vectors.shape[0], total * own)

def on_device(sizes, tokens, image_counts, cotangent, first_gain, first_shift, query_weight, query_bias, key_weight,
              value_weight, value_bias, out_weight, out_bias, second_gain, second_shift, up_weight, up_bias,
              down_weight, down_bias):
    rows, feat = tokens.shape
    own = query_weight.shape[0]
    n = feat // own
    counts = image_counts[0]
    me = lax.axis_index(FSDP)
    eight = jnp.stack([first_gain, first_shift, query_bias, value_bias, out_bias, second_gain, second_shift, down_bias])
    small = jnp.concatenate([spread(eight, me, n), spread(up_bias[None], me, n).reshape(-1, feat)])
    small = jnp.concatenate([small, jnp.zeros((16 - small.shape[0], feat), bf16)])
    q, k, v, vec, mixed, lse, qkv_all, o_all, up_all, down_all, _ = gather_attend(
        sizes, counts, tokens, small, query_weight, key_weight, value_weight, out_weight, up_weight, down_weight)
    layer_out, gres, gmix, gout, gup, gdown, gvec = feed_forward(
        sizes, counts, mixed, tokens, cotangent, o_all.reshape(feat, feat), vec, up_all, down_all)
    dq, dk, dv = attn_bwd(counts, q, k, v, gmix, lse)
    gtok, gq, gk, gv, go, total = project_back(sizes, tokens, vec, gres, dq, dk, dv, qkv_all, gout, gvec)
    mine = lax.dynamic_index_in_dim(total[:8].reshape(8, n, own), me, 1, keepdims=False)
    ub_mine = lax.dynamic_index_in_dim(total[8:12].reshape(n, -1), me, 0, keepdims=False)
    return (layer_out, gtok, mine[0], mine[1], gq, mine[2], gk, gv, mine[3], go, mine[4], mine[5], mine[6],
            gup, ub_mine, gdown, mine[7])


def solution(mesh):
    rows = P(("dp", "fsdp"), None)
    mat = P("fsdp", None)
    vec = P("fsdp")
    return jax.shard_map(
        functools.partial(on_device, (mesh.shape["dp"], mesh.shape["fsdp"])),
        mesh=mesh,
        in_specs=(rows, rows, rows, vec, vec, mat, vec, mat, mat, vec, mat, vec, vec, vec, mat, vec, mat, vec),
        out_specs=(rows, rows, vec, vec, mat, vec, mat, mat, vec, mat, vec, vec, vec, mat, vec, mat, vec),
        check_vma=False,
    )
```

```python
import functools
import math

import jax
import jax.numpy as jnp
from jax import lax
from jax.experimental import pallas as pl
from jax.experimental.pallas import tpu as pltpu
from jax.sharding import PartitionSpec as P

EPS = 1e-06
NT = (((1,), (1,)), ((), ()))
TN = (((0,), (0,)), ((), ()))


SMALL_ROWS=197; LARGE_ROWS=325
QB=256
KB=128
NEG=-1e30

def image_ends(small, large, rows):
    ends=[]
    for i in range(1, rows//SMALL_ROWS+1):
        e = jnp.minimum(i, small)*SMALL_ROWS + jnp.maximum(i-small,0)*LARGE_ROWS
        ends.append(jnp.where(i<=small+large, e, 2*rows))
    return ends

def image_of(places, ends):
    idx = jnp.zeros(places.shape, jnp.int32)
    for e in ends:
        idx = idx + (places>=e).astype(jnp.int32)
    return idx

def key_range(ends, first, last, rows):
    lo = jnp.int32(0); hi = jnp.int32(rows)
    for e in ends:
        lo = jnp.maximum(lo, jnp.where(e<=first, e, 0))
        hi = jnp.minimum(hi, jnp.where(e>last, e, rows))
    return lo, hi

def widths_of(rows):
    ws = [w*KB for w in range(3, rows//KB)]
    ws = [w for w in ws if w<=768]
    return ws+[rows]

def with_window(counts_ref, rows, first, body):
    small=counts_ref[0]; large=counts_ref[1]
    ends=image_ends(small, large, rows)
    lo,hi=key_range(ends, first, first+QB-1, rows)
    base=lo//KB
    need=(hi+KB-1)//KB - base
    done=jnp.int32(0)
    for w in widths_of(rows):
        n=w//KB
        use = (need<=n) & (need>done)
        start = jnp.minimum(base, (rows-w)//KB)*KB
        @pl.when(use)
        def _(start=start, w=w):
            body(pl.multiple_of(start,KB), w, ends)
        done=jnp.int32(n)

def fwd_kernel(counts_ref, q_ref, k_ref, v_ref, o_ref, lse_ref):
    rows=q_ref.shape[0]
    lane=lax.broadcasted_iota(jnp.int32,(QB,128),1)
    def block(b, _):
        first=pl.multiple_of(b*QB,QB)
        def body(start, w, ends):
            q=q_ref[pl.ds(first,QB),:]
            k=k_ref[pl.ds(start,w),:]
            v=v_ref[pl.ds(start,w),:]
            rid=image_of(first+lax.broadcasted_iota(jnp.int32,(QB,1),0), ends)
            cid=image_of(start+lax.broadcasted_iota(jnp.int32,(1,w),1), ends)
            bias=jnp.where(rid==cid, 0.0, NEG)
            outs=[];lses=[]
            for e in range(2):
                qm=jnp.where((lane<64)==(e==0), q, jnp.zeros_like(q))
                s=lax.dot_general(qm,k,(((1,),(1,)),((),())),preferred_element_type=jnp.float32)+bias
                m=jnp.max(s,axis=1,keepdims=True)
                p=jnp.exp(s-m)
                l=jnp.sum(p,axis=1,keepdims=True)
                o=jnp.dot(p.astype(jnp.bfloat16),v,preferred_element_type=jnp.float32)
                outs.append(o*(1.0/l)); lses.append(m+jnp.log(l))
            o_ref[pl.ds(first,QB),:]=jnp.where(lane<64,outs[0],outs[1]).astype(jnp.bfloat16)
            both=jnp.where(lane<64,jnp.broadcast_to(lses[0],(QB,128)),jnp.broadcast_to(lses[1],(QB,128)))
            t=both.T
            lse_ref[0,0:1,pl.ds(first,QB)]=t[0:1,:]
            lse_ref[0,1:2,pl.ds(first,QB)]=t[64:65,:]
        with_window(counts_ref, rows, first, body)
        return 0
    lax.fori_loop(0,rows//QB,block,0)

def attn_fwd(counts,q,k,v):
    rows,feat=q.shape
    pairs=feat//128
    spec=pl.BlockSpec((rows,128),lambda p,c:(0,p))
    return pl.pallas_call(fwd_kernel,
        grid_spec=pltpu.PrefetchScalarGridSpec(num_scalar_prefetch=1,grid=(pairs,),
            in_specs=[spec]*3,out_specs=[spec,pl.BlockSpec((1,2,rows),lambda p,c:(p,0,0))]),
        out_shape=[jax.ShapeDtypeStruct((rows,feat),jnp.bfloat16),jax.ShapeDtypeStruct((pairs,2,rows),jnp.float32)],
        name="attend",
        )(counts,q,k,v)

def bwd_kernel(counts_ref, q_ref, k_ref, v_ref, do_ref, lse_ref, dq_ref, dk_ref, dv_ref, dk_acc, dv_acc):
    rows=q_ref.shape[0]
    lane=lax.broadcasted_iota(jnp.int32,(QB,128),1)
    dk_acc[...]=jnp.zeros_like(dk_acc)
    dv_acc[...]=jnp.zeros_like(dv_acc)
    nt=(((1,),(1,)),((),()))
    tn=(((0,),(0,)),((),()))
    def block(b,_):
        first=pl.multiple_of(b*QB,QB)
        def body(start,w,ends):
            q=q_ref[pl.ds(first,QB),:]
            do=do_ref[pl.ds(first,QB),:]
            k=k_ref[pl.ds(start,w),:]
            v=v_ref[pl.ds(start,w),:]
            rid=image_of(start+lax.broadcasted_iota(jnp.int32,(w,1),0), ends)
            cid=image_of(first+lax.broadcasted_iota(jnp.int32,(1,QB),1), ends)
            bias=jnp.where(rid==cid,0.0,NEG)
            dqs=[]
            dks=None;dvs=None
            for e in range(2):
                mask=(lane<64)==(e==0)
                qm=jnp.where(mask,q,jnp.zeros_like(q))
                dom=jnp.where(mask,do,jnp.zeros_like(do))
                s=lax.dot_general(k,qm,nt,preferred_element_type=jnp.float32)+bias
                p=jnp.exp(s-lse_ref[0,e:e+1,pl.ds(first,QB)])
                dp=lax.dot_general(v,dom,nt,preferred_element_type=jnp.float32)
                delta=jnp.sum(p*dp,axis=0,keepdims=True)
                ds=(p*(dp-delta)).astype(jnp.bfloat16)
                pb=p.astype(jnp.bfloat16)
                dv_e=jnp.dot(pb,dom,preferred_element_type=jnp.float32)
                dk_e=jnp.dot(ds,qm,preferred_element_type=jnp.float32)
                dq_e=lax.dot_general(ds,k,tn,preferred_element_type=jnp.float32)
                dvs=dv_e if dvs is None else dvs+dv_e
                dks=dk_e if dks is None else dks+dk_e
                dqs.append(dq_e)
            dv_acc[pl.ds(start,w),:]+=dvs
            dk_acc[pl.ds(start,w),:]+=dks
            dq_ref[pl.ds(first,QB),:]=(jnp.where(lane<64,dqs[0],dqs[1])*0.125).astype(jnp.bfloat16)
        with_window(counts_ref,rows,first,body)
        return 0
    lax.fori_loop(0,rows//QB,block,0)
    dk_ref[...]=dk_acc[...].astype(jnp.bfloat16)
    dv_ref[...]=dv_acc[...].astype(jnp.bfloat16)

def attn_bwd(counts,q,k,v,do,lse):
    rows,feat=q.shape
    pairs=feat//128
    spec=pl.BlockSpec((rows,128),lambda p,c:(0,p))
    return pl.pallas_call(bwd_kernel,
        grid_spec=pltpu.PrefetchScalarGridSpec(num_scalar_prefetch=1,grid=(pairs,),
            in_specs=[spec]*4+[pl.BlockSpec((1,2,rows),lambda p,c:(p,0,0))],out_specs=[spec]*3,
            scratch_shapes=[pltpu.VMEM((rows,128),jnp.float32)]*2),
        out_shape=[jax.ShapeDtypeStruct((rows,feat),jnp.bfloat16)]*3,
        name="attend_back",
        )(counts,q,k,v,do,lse)

f32=jnp.float32; bf16=jnp.bfloat16
RB=256
INV_SQRT2=1/math.sqrt(2.0); INV_SQRT2PI=1/math.sqrt(2*math.pi)

def dot(a,b): return jnp.dot(a,b,preferred_element_type=f32)
def dot_nt(a,b): return lax.dot_general(a,b,NT,preferred_element_type=f32)
def dot_tn(a,b): return lax.dot_general(a,b,TN,preferred_element_type=f32)

def norm_parts(x):
    mean=jnp.mean(x,axis=-1,keepdims=True)
    cen=x-mean
    var=jnp.mean(cen*cen,axis=-1,keepdims=True)
    q=lax.rsqrt(var+EPS)
    return cen*q, q

def live_mask(counts_ref, first, n):
    end=counts_ref[0]*197+counts_ref[1]*325
    r=first+lax.broadcasted_iota(jnp.int32,(n,1),0)
    return r<end

def mid_kernel(counts_ref, mixed_ref, tokens_ref, cot_ref, outw_ref, vec_ref, up_ref, ub_ref, down_ref,
        layer_ref, gres_ref, gmix_ref, gup_ref, gub_ref, gdown_ref, gout_ref, gvec_ref,
        res_s, si_s, gb_s, accout_s, accgs_s, hid_s, gi_s):
    rows=tokens_ref.shape[0]
    j=pl.program_id(0); nj=pl.num_programs(0)
    obias=vec_ref[0:1,:]; gain=vec_ref[1:2,:]; shift=vec_ref[2:3,:]; dbias=vec_ref[3:4,:]
    @pl.when(j==0)
    def _():
        def step(i,_):
            first=pl.multiple_of(i*RB,RB); sl=pl.ds(first,RB)
            res=tokens_ref[sl,:].astype(f32)+(dot(mixed_ref[sl,:],outw_ref[...])+obias)
            res_s[sl,:]=res
            xhat,_q=norm_parts(res)
            si_s[sl,:]=(xhat*gain+shift).astype(bf16)
            live=live_mask(counts_ref,first,RB)
            gb_s[sl,:]=jnp.where(live,cot_ref[sl,:],jnp.zeros((),bf16))
            return 0
        lax.fori_loop(0,rows//RB,step,0)
        accout_s[...]=jnp.zeros_like(accout_s)
        accgs_s[...]=jnp.zeros_like(accgs_s)
    gub=jnp.zeros(gub_ref.shape,f32)
    for i in range(rows//RB):
        sl=slice(i*RB,(i+1)*RB)
        pre=dot(si_s[sl,:],up_ref[...])+ub_ref[...]
        cdf=0.5+0.5*lax.erf(pre*INV_SQRT2)
        pdf=jnp.exp(-0.5*pre*pre)*INV_SQRT2PI
        hid_s[sl,:]=(pre*cdf).astype(bf16)
        gh=dot_nt(gb_s[sl,:],down_ref[...])
        gi=(gh*(cdf+pre*pdf)).astype(bf16)
        gi_s[sl,:]=gi
        gub=gub+jnp.sum(gi.astype(f32),axis=0,keepdims=True)
    gub_ref[...]=gub
    accout_s[...]+=dot(hid_s[...],down_ref[...])
    accgs_s[...]+=dot_nt(gi_s[...],up_ref[...])
    gdown_ref[...]=dot_tn(hid_s[...],gb_s[...]).astype(bf16)
    gup_ref[...]=dot_tn(si_s[...],gi_s[...]).astype(bf16)
    @pl.when(j==nj-1)
    def _():
        gvec_ref[...]=jnp.zeros_like(gvec_ref)
        def step(i,_):
            first=pl.multiple_of(i*RB,RB); sl=pl.ds(first,RB)
            live=live_mask(counts_ref,first,RB)
            res=res_s[sl,:]
            layer=res+(accout_s[sl,:]+dbias)
            layer_ref[sl,:]=jnp.where(live,layer,0.0).astype(bf16)
            xhat,q=norm_parts(res)
            gs=accgs_s[sl,:]
            t=gs*gain
            gb=gb_s[sl,:].astype(f32)
            gres=gb+q*(t-jnp.mean(t,axis=-1,keepdims=True)-xhat*jnp.mean(t*xhat,axis=-1,keepdims=True))
            gres_ref[sl,:]=gres
            ga=gres.astype(bf16)
            mixed_unused=None
            si_s[sl,:]=ga
            gvec_ref[0:1,:]+=jnp.sum(gb,axis=0,keepdims=True)
            gvec_ref[1:2,:]+=jnp.sum(gs*xhat,axis=0,keepdims=True)
            gvec_ref[2:3,:]+=jnp.sum(gs,axis=0,keepdims=True)
            gvec_ref[3:4,:]+=jnp.sum(ga.astype(f32),axis=0,keepdims=True)
            gmix_ref[sl,:]=dot_nt(ga,outw_ref[...]).astype(bf16)
            return 0
        lax.fori_loop(0,rows//RB,step,0)
        gout_ref[...]=dot_tn(mixed_ref[...],si_s[...]).astype(bf16)

def middle(counts,mixed,tokens,cot,outw,vec,up,ub,down,FB=512):
    rows,D=tokens.shape; FF=up.shape[1]
    nj=FF//FB
    full=lambda a: pl.BlockSpec(a.shape,lambda j,c:(0,)*len(a.shape),pipeline_mode=pl.Buffered(1))
    fo=lambda s: pl.BlockSpec(s,lambda j,c:(0,)*len(s),pipeline_mode=pl.Buffered(1))
    return pl.pallas_call(mid_kernel,
        grid_spec=pltpu.PrefetchScalarGridSpec(num_scalar_prefetch=1,grid=(nj,),
            in_specs=[full(mixed),full(tokens),full(cot),full(outw),full(vec),
                pl.BlockSpec((D,FB),lambda j,c:(0,j)),pl.BlockSpec((1,FB),lambda j,c:(0,j)),pl.BlockSpec((FB,D),lambda j,c:(j,0))],
            out_specs=[fo((rows,D)),fo((rows,D)),fo((rows,D)),
                pl.BlockSpec((D,FB),lambda j,c:(0,j)),pl.BlockSpec((1,FB),lambda j,c:(0,j)),pl.BlockSpec((FB,D),lambda j,c:(j,0)),
                fo((D,D)),fo((8,D))],
            scratch_shapes=[pltpu.VMEM((rows,D),f32),pltpu.VMEM((rows,D),bf16),pltpu.VMEM((rows,D),bf16),
                pltpu.VMEM((rows,D),f32),pltpu.VMEM((rows,D),f32),pltpu.VMEM((rows,FB),bf16),pltpu.VMEM((rows,FB),bf16)]),
        out_shape=[jax.ShapeDtypeStruct((rows,D),bf16),jax.ShapeDtypeStruct((rows,D),f32),jax.ShapeDtypeStruct((rows,D),bf16),
            jax.ShapeDtypeStruct((D,FF),bf16),jax.ShapeDtypeStruct((1,FF),f32),jax.ShapeDtypeStruct((FF,D),bf16),
            jax.ShapeDtypeStruct((D,D),bf16),jax.ShapeDtypeStruct((8,D),f32)],
        compiler_params=pltpu.CompilerParams(vmem_limit_bytes=60*2**20),
        name="feed_forward",
        )(counts,mixed,tokens,cot,outw,vec,up,ub,down)


def qkv_kernel(tokens_ref, vec_ref, qw_ref, kw_ref, vw_ref, fi_ref, q_ref, k_ref, v_ref):
    rows=tokens_ref.shape[0]
    gain=vec_ref[0:1,:]; shift=vec_ref[1:2,:]; qb=vec_ref[2:3,:]; vb=vec_ref[3:4,:]
    for i in range(rows//RB):
        sl=slice(i*RB,(i+1)*RB)
        xhat,_=norm_parts(tokens_ref[sl,:].astype(f32))
        fi=(xhat*gain+shift).astype(bf16)
        fi_ref[sl,:]=fi
        q_ref[sl,:]=((dot(fi,qw_ref[...])+qb).astype(bf16).astype(f32)*0.125).astype(bf16)
        k_ref[sl,:]=dot(fi,kw_ref[...]).astype(bf16)
        v_ref[sl,:]=(dot(fi,vw_ref[...])+vb).astype(bf16)

def project(tokens,vec,qw,kw,vw):
    rows,D=tokens.shape
    return pl.pallas_call(qkv_kernel,out_shape=[jax.ShapeDtypeStruct((rows,D),bf16)]*4,
        compiler_params=pltpu.CompilerParams(vmem_limit_bytes=60*2**20),name="project")(tokens,vec,qw,kw,vw)

def back_kernel(tokens_ref, vec_ref, gres_ref, fi_ref, dq_ref, dk_ref, dv_ref, qw_ref, kw_ref, vw_ref,
        gtok_ref, gq_ref, gk_ref, gv_ref, gvec_ref):
    rows=tokens_ref.shape[0]
    gain=vec_ref[0:1,:]
    gvec=[jnp.zeros((1,tokens_ref.shape[1]),f32)]*4
    for i in range(rows//RB):
        sl=slice(i*RB,(i+1)*RB)
        dq=dq_ref[sl,:];dk=dk_ref[sl,:];dv=dv_ref[sl,:]
        gs=dot_nt(dq,qw_ref[...])+dot_nt(dk,kw_ref[...])+dot_nt(dv,vw_ref[...])
        xhat,q=norm_parts(tokens_ref[sl,:].astype(f32))
        t=gs*gain
        gtok_ref[sl,:]=gres_ref[sl,:]+q*(t-jnp.mean(t,axis=-1,keepdims=True)-xhat*jnp.mean(t*xhat,axis=-1,keepdims=True))
        for n,a in enumerate((gs*xhat,gs,dq.astype(f32),dv.astype(f32))):
            gvec[n]=gvec[n]+jnp.sum(a,axis=0,keepdims=True)
    gvec_ref[...]=jnp.zeros_like(gvec_ref)
    for n in range(4): gvec_ref[n:n+1,:]=gvec[n]
    fi=fi_ref[...]
    gq_ref[...]=dot_tn(fi,dq_ref[...]).astype(bf16)
    gk_ref[...]=dot_tn(fi,dk_ref[...]).astype(bf16)
    gv_ref[...]=dot_tn(fi,dv_ref[...]).astype(bf16)

def project_back(tokens,vec,gres,fi,dq,dk,dv,qw,kw,vw):
    rows,D=tokens.shape
    s=jax.ShapeDtypeStruct
    return pl.pallas_call(back_kernel,out_shape=[s((rows,D),f32),s((D,D),bf16),s((D,D),bf16),s((D,D),bf16),s((8,D),f32)],
        compiler_params=pltpu.CompilerParams(vmem_limit_bytes=60*2**20),name="project_back")(tokens,vec,gres,fi,dq,dk,dv,qw,kw,vw)


MESH = pl.DeviceIdType.MESH


class Place:
    def __init__(self, dp_total, fsdp_total):
        half = fsdp_total // 2
        self.outer_total = 4
        self.inner_total = half // 4
        assert half % 4 == 0
        self.pairs = dp_total // 2
        self.d = lax.axis_index("dp")
        self.f = lax.axis_index("fsdp")
        self.core = self.f % 2
        self.inner = (self.f // 2) % self.inner_total
        self.outer = self.f // (2 * self.inner_total)
        self.side = self.d % 2
        self.twin = self.d + 1 - 2 * self.side
        self.flip = self.outer // 2
        self.mirror = self.unmirror(self.outer)

    def unmirror(self, at):
        return at + self.flip * (3 - 2 * at)

    def arrival(self, step):
        return self.unmirror(step - self.mirror if step == 1 else step)

    def device(self, outer, inner, core):
        return (self.d, (outer * self.inner_total + inner) * 2 + core)

    def at_outer(self, outer):
        return self.device(outer, self.inner, self.core)

    def at_inner(self, t):
        return self.device(self.outer, (self.inner + t) % self.inner_total, self.core)

    def other_core(self):
        return self.device(self.outer, self.inner, 1 - self.core)

    def at_twin(self):
        return (self.twin, self.f)

    def me(self):
        return (self.d, self.f)

    def at_pair(self, k):
        return (self.side + 2 * ((self.d // 2 + k) % self.pairs), self.f)

    def neighbours(self, pairs=False):
        out = [self.at_outer((self.outer + s) % 4) for s in range(1, 4)]
        out += [self.at_inner(t) for t in range(1, self.inner_total)]
        out += [self.at_twin(), self.other_core()]
        if pairs:
            out += [self.at_pair(k) for k in range(1, self.pairs)]
        return out


def greet(others):
    barrier = pltpu.get_barrier_semaphore()
    for other in others:
        pl.semaphore_signal(barrier, inc=1, device_id=other, device_id_type=MESH)
    pl.semaphore_wait(barrier, len(others))


class Gather:
    def __init__(self, place, ref, edge, sems, base):
        self.place, self.ref, self.edge = place, ref, edge
        self.rows = ref.shape[-2]
        self.send_sem, self.recv_sem = sems
        self.base = base
        A, B = place.outer_total, place.inner_total
        keys = [("z", s) for s in range(1, A)] + [("Z", s) for s in range(1, A)]
        keys += [("x", s, t) for s in range(A) for t in range(1, B)]
        keys += [("y", t) for t in range(B)]
        keys += [("c",)]
        self.keys = {key: i for i, key in enumerate(keys)}
        self.sent = []
        self.sent_inside = []

    @staticmethod
    def count(B):
        return 6 + 4 * (B - 1) + B + 1

    def rows_of(self, kind):
        e, r, p = self.edge, self.rows, self.place.side
        if not e or kind == "all":
            return pl.ds(0, r)
        start, size = {"plane": (p * e, r - e), "mine": (p * (r - e), e), "theirs": ((1 - p) * (r - e), e)}[kind]
        return pl.ds(pl.multiple_of(start, 8), size)

    def part(self, outer, inner, core, kind):
        return self.ref.at[outer, inner, core, self.rows_of(kind)]

    def copy(self, key, ref, to):
        i = self.base + self.keys[key]
        into = i
        if key[0] == "Z":
            into = self.base + self.keys["z", 2 if key[1] == 2 else 3]
        return pltpu.make_async_remote_copy(src_ref=ref, dst_ref=ref, send_sem=self.send_sem.at[i],
                                            recv_sem=self.recv_sem.at[into], device_id=to, device_id_type=MESH)

    def send(self, key, make):
        self.copy(key, *make()).start()
        self.sent.append((key, make))

    def send_inside(self, key, make):
        @pl.when(self.place.mirror == 1)
        def _():
            self.copy(key, *make()).start()

        self.sent_inside.append((key, make))

    def got(self, key, ref):
        self.copy(key, ref, self.place.me()).wait_recv()

    def outer_of(self, step):
        return self.place.outer if step == 0 else self.place.arrival(step)

    def own_line(self, step):
        p = self.place
        return self.part(self.outer_of(step), p.inner, p.core, "plane")

    def start(self):
        p = self.place
        self.send(("z", 1), lambda: (self.own_line(0), p.at_outer(p.unmirror(1 - p.mirror))))
        self.send_inside(("z", 2), lambda: (self.own_line(0), p.at_outer(p.unmirror(2))))
        self.pass_inner(0)

    def pass_inner(self, step):
        p = self.place
        for t in range(1, p.inner_total):
            self.send(("x", step, t), lambda t=t: (self.own_line(step), p.at_inner(-t)))

    def from_outer_step(self, step):
        p = self.place
        self.got(("z", step), self.own_line(step))
        self.send_inside(("Z", step), lambda: (self.own_line(step), p.at_outer(p.unmirror(2 if step == 1 else 0))))
        self.pass_inner(step)
        if step == 3:
            self.pass_twin(0)

    def from_outer(self):
        for step in range(1, 4):
            self.from_outer_step(step)

    def line(self, t, kind):
        p = self.place
        return self.part(slice(None), (p.inner + t) % p.inner_total, p.core, kind)

    def pass_twin(self, t):
        if self.edge:
            self.send(("y", t), lambda: (self.line(t, "mine"), self.place.at_twin()))

    def from_inner(self):
        p = self.place
        for t in range(1, p.inner_total):
            for step in range(4):
                self.got(("x", step, t), self.part(self.outer_of(step), (p.inner + t) % p.inner_total, p.core, "plane"))
            self.pass_twin(t)

    def half(self, core):
        return self.part(slice(None), slice(None), core, "all")

    def from_twin(self):
        p = self.place
        if self.edge:
            for t in range(p.inner_total):
                self.got(("y", t), self.line(t, "theirs"))
        self.send(("c",), lambda: (self.half(p.core), p.other_core()))

    def from_core(self):
        self.got(("c",), self.half(1 - self.place.core))

    def finish(self):
        for key, make in self.sent:
            self.copy(key, *make()).wait_send()

        @pl.when(self.place.mirror == 1)
        def _():
            for key, make in self.sent_inside:
                self.copy(key, *make()).wait_send()


class Scatter:
    def __init__(self, place, terms, bufs, edge, emit, sems, base):
        self.place, self.terms, self.edge, self.emit = place, terms, edge, emit
        self.sums, self.twin_buf, self.inner_buf, self.outer_buf, self.last_buf = bufs[:5]
        self.pair_bufs = bufs[5:]
        self.send_sem, self.recv_sem = sems
        self.base = base
        p, e, w = place.side, edge, terms.shape[-1]
        at = lambda start, size: pl.ds(pl.multiple_of(start, 128), size)
        self.plane = at(p * e, w - e)
        self.mine = at(p * (w - e), e)
        self.theirs = at((1 - p) * (w - e), e)
        self.twin_plane = at((1 - p) * e, w - e)
        self.middle = pl.ds(e, w - 2 * e)

    @staticmethod
    def count(B, pairs):
        return 1 + 1 + (B - 1) + 3 + 1 + (pairs - 1)

    @staticmethod
    def shapes(B, pairs, rows, width, edge, lead=()):
        out = [(4, B, rows, width), (4, B, rows, edge), (B - 1, 4, rows, width), (3, rows, width), (rows, width)]
        if pairs > 1:
            out += [(rows, width), (pairs - 1, rows, width)]
        return [pltpu.VMEM(tuple(lead) + s, bf16) for s in out]

    def copy(self, i, src, dst, to):
        return pltpu.make_async_remote_copy(src_ref=src, dst_ref=dst, send_sem=self.send_sem.at[self.base + i],
                                            recv_sem=self.recv_sem.at[self.base + i], device_id=to, device_id_type=MESH)

    def copies(self, stage):
        p = self.place
        A, B = 4, p.inner_total
        if stage == "core":
            return [self.copy(0, self.terms.at[:, :, 1 - p.core], self.sums, p.other_core())]
        if stage == "twin":
            return [self.copy(1, self.sums.at[:, :, :, self.theirs], self.twin_buf, p.at_twin())]
        if stage == "inner":
            return [self.copy(1 + t, self.sums.at[:, (p.inner + B - t) % B, :, self.plane],
                              self.inner_buf.at[t - 1, :, :, self.plane], p.at_inner(-t)) for t in range(1, B)]
        if stage == "outer":
            return [self.copy(B + s, self.sums.at[(p.outer + A - s) % A, p.inner, :, self.plane],
                              self.outer_buf.at[s - 1, :, self.plane], p.at_outer((p.outer + A - s) % A))
                    for s in range(1, A)]
        if stage == "last":
            return [self.copy(A + B, self.sums.at[p.outer, p.inner, :, self.plane], self.last_buf.at[:, self.plane],
                              p.at_twin())]
        half, others = self.pair_bufs
        return [self.copy(A + B + k, half, others.at[k - 1], p.at_pair(p.pairs - k)) for k in range(1, p.pairs)]

    def go(self, stage):
        for c in self.copies(stage):
            c.start()

    def got(self, i, dst):
        self.copy(i, dst, dst, self.place.me()).wait_recv()

    def start(self):
        self.go("core")

    def from_core(self):
        p = self.place
        B = p.inner_total
        self.got(0, self.sums)

        def add(i, _):
            a, b = i // B, i % B
            self.sums[a, b] = (self.sums[a, b].astype(f32) + self.terms[a, b, p.core].astype(f32)).astype(bf16)
            return 0

        lax.fori_loop(0, 4 * B, add, 0)
        self.go("twin")

    def from_twin(self):
        p = self.place
        B = p.inner_total
        self.got(1, self.twin_buf)

        def add(i, _):
            a, b = i // B, i % B
            self.sums[a, b, :, self.mine] = (self.sums[a, b, :, self.mine].astype(f32)
                                             + self.twin_buf[a, b].astype(f32)).astype(bf16)
            return 0

        lax.fori_loop(0, 4 * B, add, 0)
        self.go("inner")

    def from_inner(self):
        p = self.place
        B = p.inner_total
        for t in range(1, B):
            self.got(1 + t, self.inner_buf.at[t - 1, :, :, self.plane])

        def add(a, _):
            total = self.sums[a, p.inner, :, self.plane].astype(f32)
            for t in range(1, B):
                total = total + self.inner_buf[t - 1, a, :, self.plane].astype(f32)
            self.sums[a, p.inner, :, self.plane] = total.astype(bf16)
            return 0

        lax.fori_loop(0, 4, add, 0)
        self.go("outer")

    def from_outer(self):
        p = self.place
        B = p.inner_total
        for s in range(1, 4):
            self.got(B + s, self.outer_buf.at[s - 1, :, self.plane])
        total = self.sums[p.outer, p.inner, :, self.plane].astype(f32)
        for s in range(1, 4):
            total = total + self.outer_buf[s - 1, :, self.plane].astype(f32)
        self.sums[p.outer, p.inner, :, self.plane] = total.astype(bf16)
        self.go("last")

    def from_last(self):
        p = self.place
        self.got(4 + p.inner_total, self.last_buf.at[:, self.twin_plane])
        own = lambda cols: self.sums[p.outer, p.inner, :, cols].astype(f32)
        last = lambda cols: self.last_buf[:, cols].astype(f32)
        if p.pairs == 1:
            self.emit(self.mine, own(self.mine))
            self.emit(self.middle, own(self.middle) + last(self.middle))
            self.emit(self.theirs, last(self.theirs))
            return
        half, others = self.pair_bufs
        half[:, self.mine] = own(self.mine).astype(bf16)
        half[:, self.middle] = (own(self.middle) + last(self.middle)).astype(bf16)
        half[:, self.theirs] = last(self.theirs).astype(bf16)
        self.go("pairs")

    def from_pairs(self):
        p = self.place
        if p.pairs == 1:
            return
        half, others = self.pair_bufs
        total = half[...].astype(f32)
        for k in range(1, p.pairs):
            self.got(4 + p.inner_total + k, others.at[k - 1])
            total = total + others[k - 1].astype(f32)
        self.emit(pl.ds(0, self.terms.shape[-1]), total)

    def finish(self):
        for stage in ("core", "twin", "inner", "outer", "last") + (("pairs",) if self.place.pairs > 1 else ()):
            for c in self.copies(stage):
                c.wait_send()


class Total:
    def __init__(self, place, value, bufs, out, sems, base):
        self.place, self.value, self.bufs, self.out = place, value, bufs, out
        self.send_sem, self.recv_sem = sems
        p = place
        rounds = [[p.other_core()], [p.at_inner(t) for t in range(1, p.inner_total)],
                  [p.at_outer((p.outer + s) % 4) for s in range(1, 4)], [p.at_twin()],
                  [p.at_pair(k) for k in range(1, p.pairs)]]
        self.rounds = [r for r in rounds if r]
        self.base = base

    @staticmethod
    def count(B, pairs):
        return 1 + (B - 1) + 3 + 1 + (pairs - 1)

    @staticmethod
    def shapes(B, pairs, shape):
        return [pltpu.VMEM((Total.count(B, pairs),) + shape, f32), pltpu.VMEM((5,) + shape, f32)]

    def copies(self, r):
        landing, held = self.bufs
        i = sum(len(x) for x in self.rounds[:r])
        return [(pltpu.make_async_remote_copy(src_ref=held.at[r], dst_ref=landing.at[i + k],
                                              send_sem=self.send_sem.at[self.base + i + k],
                                              recv_sem=self.recv_sem.at[self.base + i + k], device_id=to,
                                              device_id_type=MESH), i + k) for k, to in enumerate(self.rounds[r])]

    def start(self):
        self.bufs[1][0] = self.value[...]
        for c, _ in self.copies(0):
            c.start()

    def step(self, r):
        landing, held = self.bufs
        total = held[r]
        for c, i in self.copies(r):
            c.wait_recv()
            total = total + landing[i]
        if r + 1 < len(self.rounds):
            held[r + 1] = total
            for c, _ in self.copies(r + 1):
                c.start()
        else:
            self.out[...] = total

    def steps(self):
        return [functools.partial(self.step, r) for r in range(len(self.rounds))]

    def finish(self):
        for r in range(len(self.rounds)):
            for c, _ in self.copies(r):
                c.wait_send()


def local(src, dst, sem):
    c = pltpu.make_async_copy(src, dst, sem)
    c.start()
    return c


BLOCKS = 3


def lane_tile(source, moves):
    lane = None
    out = None
    for col, to, size in moves:
        tile = source[:, col // 128 * 128:col // 128 * 128 + 128]
        shift = (to - col) % 128
        if shift:
            tile = pltpu.roll(tile, shift, 1)
        if out is None:
            out = tile
            lane = lax.broadcasted_iota(jnp.int32, tile.shape, 1)
        else:
            out = jnp.where((lane >= to) & (lane < to + size), tile, out)
    return out


def split_columns(source, owners):
    piece = source.shape[1] // owners // BLOCKS
    per = 128 // piece
    out = []
    for j in range(BLOCKS):
        tiles = [lane_tile(source, [(((t * per + q) * BLOCKS + j) * piece, q * piece, piece) for q in range(per)])
                 for t in range(owners // per)]
        out.append(jnp.concatenate(tiles, axis=1))
    return out


def join_columns(parts, owners):
    source = jnp.concatenate(parts, axis=1)
    width = parts[0].shape[1]
    piece = width // owners
    per = 128 // piece
    tiles = []
    for t in range(source.shape[1] // 128):
        moves = []
        for q in range(per):
            unit = t * per + q
            moves.append(((unit % BLOCKS) * width + unit // BLOCKS * piece, q * piece, piece))
        tiles.append(lane_tile(source, moves))
    return jnp.concatenate(tiles, axis=1)


CFG = {}


def attend_block(counts_ref, q_ref, k_ref, v_ref, mixed_ref, lse_ref, pair, block):
    rows = q_ref.shape[0]
    lane = lax.broadcasted_iota(jnp.int32, (QB, 128), 1)
    first = pl.multiple_of(block * QB, QB)
    cols = pl.ds(pl.multiple_of(pair * 128, 128), 128)
    q = q_ref[pl.ds(first, QB), cols]
    k = k_ref[:, cols]
    v = v_ref[:, cols]
    ends = image_ends(counts_ref[0], counts_ref[1], rows)
    rid = image_of(first + lax.broadcasted_iota(jnp.int32, (QB, 1), 0), ends)
    cid = image_of(lax.broadcasted_iota(jnp.int32, (1, rows), 1), ends)
    bias = jnp.where(rid == cid, 0.0, NEG)
    outs = []
    lses = []
    for e in range(2):
        qm = jnp.where((lane < 64) == (e == 0), q, jnp.zeros_like(q))
        s = dot_nt(qm, k) + bias
        m = jnp.max(s, axis=1, keepdims=True)
        p = jnp.exp(s - m)
        l = jnp.sum(p, axis=1, keepdims=True)
        o = dot(p.astype(bf16), v)
        outs.append(o * (1.0 / l))
        lses.append(m + jnp.log(l))
    mixed_ref[pl.ds(first, QB), cols] = jnp.where(lane < 64, outs[0], outs[1]).astype(bf16)
    both = jnp.where(lane < 64, jnp.broadcast_to(lses[0], (QB, 128)), jnp.broadcast_to(lses[1], (QB, 128)))
    t = both.T
    lse_ref[pair, 0:1, pl.ds(first, QB)] = t[0:1, :]
    lse_ref[pair, 1:2, pl.ds(first, QB)] = t[64:65, :]


def gather_edge(rows, last=False):
    return rows // 3 if rows % 24 == 0 else rows // 4 if last or rows < 64 else rows * 3 // 8


def gather_plan(sm, u, vectors):
    step = lambda unit, s: functools.partial(unit.from_outer_step, s)
    head = [sm.start, u[0].start, sm.from_outer, u[1].start, u[0].from_outer, sm.from_inner, u[2].start,
            u[1].from_outer, u[0].from_inner, sm.from_twin, u[3].start, u[2].from_outer, u[1].from_inner,
            u[0].from_twin, sm.from_core, vectors, u[4].start, step(u[3], 1), u[0].from_core]
    middle = [[step(u[3], 2)], [step(u[3], 3), u[5].start], [u[2].from_inner], [u[1].from_twin]]
    rest = []
    for t in range(4, len(u)):
        rest += [[step(u[t], 1)] + ([u[t + 2].start] if t + 2 < len(u) else []), [step(u[t], 2)], [step(u[t], 3)],
                 [u[t - 1].from_inner], [u[t - 2].from_twin, u[t - 3].from_core]]
    n = len(u)
    rest += [[u[n - 1].from_inner], [u[n - 2].from_twin, u[n - 3].from_core], [u[n - 1].from_twin, u[n - 2].from_core],
             [u[n - 1].from_core]]
    return head, middle, rest


def gather_kernel(dp_total, n, counts_ref, tokens_hbm, small_ref, qo_ref, ko_ref, vo_ref, oo_ref, uo_ref, do_ref,
                  q_hbm, k_hbm, v_hbm, vec_ref, mixed_hbm, lse_ref, qkv_all, o_all, up_all, down_all, small_all,
                  tokens_s, q_s, k_s, v_s, mixed_s, w_s, small_s, up_own, send_sem, recv_sem, loc_sem):
    place = Place(dp_total, n)
    B = place.inner_total
    own = qo_ref.shape[0]
    piece = do_ref.shape[0] // BLOCKS
    take_tokens = local(tokens_hbm, tokens_s, loc_sem.at[0])
    for j, part in enumerate(split_columns(uo_ref[...].astype(f32), n)):
        up_own[j] = part.astype(bf16)
    sems = (send_sem, recv_sem)
    refs = [(small_all, 0), (qkv_all, own), (o_all, gather_edge(own))]
    for j in range(BLOCKS):
        refs += [(up_all.at[j], gather_edge(own)), (down_all.at[j], gather_edge(piece, j == BLOCKS - 1))]
    units = [Gather(place, ref, edge, sems, i * Gather.count(B)) for i, (ref, edge) in enumerate(refs)]
    mine = lambda unit: unit.part(place.outer, place.inner, place.core, "plane")
    fill = [local(small_ref, mine(units[0]), loc_sem.at[1])]
    own_qkv = lambda i: qkv_all.at[place.outer, place.inner, place.core, pl.ds(i * own, own)]
    fill.append(local(ko_ref, own_qkv(1), loc_sem.at[2]))

    @pl.when(place.side == 0)
    def _():
        local(qo_ref, own_qkv(0), loc_sem.at[3]).wait()

    @pl.when(place.side == 1)
    def _():
        local(vo_ref, own_qkv(2), loc_sem.at[3]).wait()

    fill.append(local(oo_ref.at[units[2].rows_of("plane")], mine(units[2]), loc_sem.at[5]))
    for j in range(BLOCKS):
        a, b = units[3 + 2 * j], units[4 + 2 * j]
        fill.append(local(up_own.at[j, a.rows_of("plane")], mine(a), loc_sem.at[6 + 2 * j]))
        rows = b.rows_of("plane")
        fill.append(local(do_ref.at[pl.ds(pl.multiple_of(j * piece + rows.start, 8), rows.size)], mine(b),
                          loc_sem.at[7 + 2 * j]))
    greet(place.neighbours())
    for c in fill:
        c.wait()

    def vectors():
        local(small_all, small_s, loc_sem.at[1]).wait()
        total = jnp.zeros(vec_ref.shape, f32)
        for i in range(n):
            total = total + small_s[i // (2 * B), i // 2 % B, i % 2].astype(f32)
        vec_ref[...] = total

    head, middle, rest = CFG.get("plan", gather_plan)(units[0], units[1:], vectors)
    for one in head:
        one()
    take = local(qkv_all, w_s, loc_sem.at[1])
    take_tokens.wait()
    take.wait()
    rows, feat = tokens_s.shape

    def project_rows(i):
        sl = slice(i * RB, (i + 1) * RB)
        xhat, _q = norm_parts(tokens_s[sl, :].astype(f32))
        fi = (xhat * vec_ref[0:1, :] + vec_ref[1:2, :]).astype(bf16)
        weight = lambda i: w_s[:, :, :, i * own:(i + 1) * own, :].reshape(feat, feat)
        q_s[sl, :] = ((dot(fi, weight(0)) + vec_ref[2:3, :]).astype(bf16).astype(f32) * 0.125).astype(bf16)
        k_s[sl, :] = dot(fi, weight(1)).astype(bf16)
        v_s[sl, :] = (dot(fi, weight(2)) + vec_ref[3:4, :]).astype(bf16)

    for i in range(rows // RB):
        if CFG.get("proj", True):
            project_rows(i)
        for one in middle[i]:
            one()
    keep = [local(a, b, loc_sem.at[2 + i]) for i, (a, b) in enumerate(((q_s, q_hbm), (k_s, k_hbm), (v_s, v_hbm)))]
    blocks = rows // QB
    pieces = feat // 128 * blocks

    def attend_piece(i, _):
        if CFG.get("att", True):
            attend_block(counts_ref, q_s, k_s, v_s, mixed_s, lse_ref, i // blocks, i % blocks)
        for at in range(pieces):
            todo = [one for k, batch in enumerate(rest) if k * pieces // len(rest) == at for one in batch]
            if todo:
                @pl.when(i == at)
                def _(todo=todo):
                    for one in todo:
                        one()
        return 0

    lax.fori_loop(0, pieces, attend_piece, 0)
    keep.append(local(mixed_s, mixed_hbm, loc_sem.at[0]))
    for c in keep:
        c.wait()
    for x in units:
        x.finish()


def gather_attend(sizes, counts, tokens, small, qw, kw, vw, ow, up, down):
    dp_total, n = sizes
    rows, feat = tokens.shape
    own = qw.shape[0]
    B = n // 8
    pairs = feat // 128
    s = jax.ShapeDtypeStruct
    vm = pl.BlockSpec(memory_space=pltpu.VMEM)
    anyspec = pl.BlockSpec(memory_space=pl.ANY)
    full = lambda *dims: (4, B, 2) + dims
    width = up.shape[1] // BLOCKS
    piece = down.shape[0] // BLOCKS
    act = s((rows, feat), bf16)
    copies = (3 + 2 * BLOCKS) * Gather.count(B)
    return pl.pallas_call(
        functools.partial(gather_kernel, dp_total, n),
        in_specs=[pl.BlockSpec(memory_space=pltpu.SMEM), anyspec] + [vm] * 7,
        out_specs=[anyspec] * 3 + [vm, anyspec, vm] + [anyspec] * 5,
        out_shape=[act, act, act, s(small.shape, f32), act, s((pairs, 2, rows), f32), s(full(3 * own, feat), bf16),
                   s(full(own, feat), bf16), s((BLOCKS,) + full(own, width), bf16),
                   s((BLOCKS,) + full(piece, feat), bf16), s(full(*small.shape), bf16)],
        scratch_shapes=[pltpu.VMEM((rows, feat), bf16)] * 5 + [
            pltpu.VMEM(full(3 * own, feat), bf16), pltpu.VMEM(full(*small.shape), bf16),
            pltpu.VMEM((BLOCKS, own, width), bf16), pltpu.SemaphoreType.DMA((copies,)),
            pltpu.SemaphoreType.DMA((copies,)), pltpu.SemaphoreType.DMA((6 + 2 * BLOCKS,))],
        compiler_params=pltpu.CompilerParams(collective_id=1, has_side_effects=True, vmem_limit_bytes=60 * 2**20),
        name="gather_attend",
    )(counts, tokens, small, qw, kw, vw, ow, up, down)


def scatter_edge(width):
    return 128 if width == 768 else width // 4 if width % 512 == 0 else width // 3


def key_lanes(keys, ends):
    lane = lax.broadcasted_iota(jnp.int32, keys.shape, 1)
    image = image_of(lax.broadcasted_iota(jnp.int32, keys.shape, 0), ends)
    return [jnp.where((lane < 64) == (e == 0), keys, jnp.where(image == lane - 64 * (1 - e), 0.0, NEG).astype(bf16))
            for e in range(2)]


def query_lanes(queries, first, ends, e):
    lane = lax.broadcasted_iota(jnp.int32, queries.shape, 1)
    image = image_of(first + lax.broadcasted_iota(jnp.int32, queries.shape, 0), ends)
    return jnp.where((lane < 64) == (e == 0), queries, jnp.where(image == lane - 64 * (1 - e), 1.0, 0.0).astype(bf16))


def layer_kernel(dp_total, n, counts_ref, mixed_hbm, tokens_ref, cot_hbm, outw_ref, vec_ref, lse_ref, up_hbm, down_hbm,
                 q_hbm, k_hbm, v_hbm, qkv_all,
                 layer_ref, gtok_ref, gup_ref, gdown_ref, gq_ref, gk_ref, gv_ref, go_ref, total_ref,
                 res_s, si_s, gb_s, mixed_s, hid_s, gi_s, up_s, down_s, kt_s, ub_s, gub_s, gqkv_s, small_s, *rest):
    rows, feat = tokens_ref.shape
    width = gi_s.shape[1]
    own = gq_ref.shape[0]
    piece = gdown_ref.shape[0] // BLOCKS
    heads = feat // 128
    place = Place(dp_total, n)
    B, pairs = place.inner_total, place.pairs
    per = 5 if pairs == 1 else 7
    uterm_s, dterm_s = rest[:2]
    ubufs, dbufs, obufs, abufs = (rest[2 + i * per:2 + (i + 1) * per] for i in range(4))
    total_bufs = rest[2 + 4 * per:4 + 4 * per]
    send_sem, recv_sem, loc_sem = rest[4 + 4 * per:]
    sems = (send_sem, recv_sem)
    count = Scatter.count(B, pairs)
    wide = lambda start: pl.ds(start, feat)
    load = lambda j: (pltpu.make_async_copy(up_hbm.at[j], up_s.at[j], loc_sem.at[2 * j]),
                      pltpu.make_async_copy(down_hbm.at[j], down_s.at[j], loc_sem.at[2 * j + 1]))
    at_end = 3 * feat
    first_loads = [local(mixed_hbm, mixed_s, loc_sem.at[2 * BLOCKS]),
                   local(cot_hbm, hid_s.at[:, wide(at_end)], loc_sem.at[2 * BLOCKS + 1])]
    for j in range(BLOCKS):
        for c in load(j):
            c.start()

    def unit_u(j):
        def emit(cols, value):
            gup_ref[:, pl.ds(pl.multiple_of(j * width + cols.start, 128), cols.size)] = value
        return Scatter(place, uterm_s.at[j % 2], [b.at[j] for b in ubufs], scatter_edge(width), emit, sems,
                       2 * j * count)

    def unit_d(j):
        def emit(cols, value):
            gdown_ref[pl.ds(pl.multiple_of(j * piece, 8), piece), cols] = value
        return Scatter(place, dterm_s.at[j % 2], [b.at[j] for b in dbufs], scatter_edge(feat), emit, sems,
                       (2 * j + 1) * count)

    def emit_out(cols, value):
        go_ref[:, cols] = value

    unit_o = Scatter(place, uterm_s.at[1, :, :, :, :, wide(0)], obufs, 256, emit_out, sems, 2 * BLOCKS * count)

    def pair_term(p):
        return dterm_s.at[1, :, :, :, pl.ds(0, own), pl.ds(pl.multiple_of(p % 2 * 384, 128), 384)]

    def unit_a(p):
        def emit(cols, value):
            gqkv_s[p, :, cols] = value
        return Scatter(place, pair_term(p), [b.at[p] for b in abufs], 128, emit, sems,
                       (2 * BLOCKS + 1 + p) * count)

    small = Total(place, small_s, total_bufs, total_ref, sems, (2 * BLOCKS + 1 + heads) * count)

    def last(unit):
        unit.from_last()
        unit.from_pairs()

    def sent(unit, *stages):
        for stage in stages:
            for c in unit.copies(stage):
                c.wait_send()

    rest_stages = ("twin", "inner", "outer", "last") + (("pairs",) if pairs > 1 else ())
    gain_one, shift_one = vec_ref[0:1, :], vec_ref[1:2, :]
    obias, gain, shift, dbias = (vec_ref[i:i + 1, :] for i in range(4, 8))
    ub = jnp.concatenate([vec_ref[8 + i:9 + i, :] for i in range(BLOCKS * width // feat)], axis=1)
    for j, part in enumerate(split_columns(jnp.broadcast_to(ub, (8, ub.shape[1])), n)):
        ub_s[j] = part
    small_s[...] = jnp.zeros_like(small_s)
    for c in first_loads:
        c.wait()

    def begin(i, _):
        first = pl.multiple_of(i * RB, RB)
        sl = pl.ds(first, RB)
        res = tokens_ref[sl, :].astype(f32) + (dot(mixed_s[sl, :], outw_ref[...]) + obias)
        res_s[sl, :] = res
        xhat, _q = norm_parts(res)
        si_s[sl, :] = (xhat * gain + shift).astype(bf16)
        gb_s[sl, :] = jnp.where(live_mask(counts_ref, first, RB), hid_s[sl, wide(at_end)], jnp.zeros((), bf16))
        gtok_ref[sl, :] = jnp.zeros((RB, feat), f32)
        return 0

    lax.fori_loop(0, rows // RB, begin, 0)
    greet(place.neighbours(pairs=True))

    def block(j, _):
        for c in load(j):
            c.wait()
        upw = lambda: up_s[j].reshape(feat, width)
        downw = lambda: down_s[j].reshape(width, feat)
        cols = pl.ds(pl.multiple_of(j * width, 128), width)
        gub_s[j] = jnp.zeros(gub_s.shape[1:], f32)

        def after(back, when, todo):
            @pl.when(when & (j >= back))
            def _():
                todo(j - back)

        def rows_piece(i, _):
            sl = pl.ds(pl.multiple_of(i * RB, RB), RB)
            pre = dot(si_s[sl, :], upw()) + ub_s[j, 0:1, :]
            cdf = 0.5 + 0.5 * lax.erf(pre * INV_SQRT2)
            pdf = jnp.exp(-0.5 * pre * pre) * INV_SQRT2PI
            hid_s[sl, cols] = (pre * cdf).astype(bf16)
            gi = (dot_nt(gb_s[sl, :], downw()) * (cdf + pre * pdf)).astype(bf16)
            gi_s[sl, :] = gi
            gub_s[j, 0:1, :] += jnp.sum(gi.astype(f32), axis=0, keepdims=True)
            after(1, i == 0, lambda k: unit_u(k).from_twin())
            after(2, i == 0, lambda k: unit_u(k).from_outer())
            after(2, i == 1, lambda k: last(unit_d(k)))
            after(2, i == 2, lambda k: last(unit_u(k)))
            after(1, i == 3, lambda k: unit_d(k).from_inner())
            return 0

        lax.fori_loop(0, rows // RB, rows_piece, 0)
        always = j >= 0
        after(2, always, lambda k: (sent(unit_u(k), "core"), sent(unit_d(k), "core")))
        dterm_s[j % 2] = dot_tn(hid_s[:, cols], gb_s[...]).astype(bf16).reshape(dterm_s.shape[1:])
        unit_d(j).start()
        after(1, always, lambda k: unit_u(k).from_inner())
        uterm_s[j % 2] = dot_tn(si_s[...], gi_s[...]).astype(bf16).reshape(uterm_s.shape[1:])
        unit_u(j).start()
        unit_d(j).from_core()
        gtok_ref[...] += dot_nt(gi_s[...], upw())
        unit_u(j).from_core()
        unit_d(j).from_twin()
        after(1, always, lambda k: unit_d(k).from_outer())
        return 0

    lax.fori_loop(0, BLOCKS, block, 0)
    end, before = BLOCKS - 1, BLOCKS - 2
    weights = [local(qkv_all.at[:, :, :, pl.ds(i * own, own)], up_s.at[i, :, :, :, :, wide(0)], loc_sem.at[i])
               for i in range(3)]

    def finish_rows(i, _):
        first = pl.multiple_of(i * RB, RB)
        sl = pl.ds(first, RB)
        res = res_s[sl, :]
        layer = res + (dot(hid_s[sl, :], down_s[...].reshape(BLOCKS * width, feat)) + dbias)
        layer_ref[sl, :] = jnp.where(live_mask(counts_ref, first, RB), layer, 0.0).astype(bf16)
        xhat, q = norm_parts(res)
        gs = gtok_ref[sl, :]
        t = gs * gain
        gb = gb_s[sl, :].astype(f32)
        gres = gb + q * (t - jnp.mean(t, axis=-1, keepdims=True) - xhat * jnp.mean(t * xhat, axis=-1, keepdims=True))
        gtok_ref[sl, :] = gres
        ga = gres.astype(bf16)
        si_s[sl, :] = ga
        small_s[7:8, :] += jnp.sum(gb, axis=0, keepdims=True)
        small_s[5:6, :] += jnp.sum(gs * xhat, axis=0, keepdims=True)
        small_s[6:7, :] += jnp.sum(gs, axis=0, keepdims=True)
        small_s[4:5, :] += jnp.sum(ga.astype(f32), axis=0, keepdims=True)
        hid_s[sl, wide(at_end)] = dot_nt(ga, outw_ref[...]).astype(bf16)

        def at(k, *todo):
            @pl.when(i == k)
            def _():
                for one in todo:
                    one()

        at(0, unit_u(end).from_twin, unit_u(before).from_outer)
        at(1, lambda: last(unit_d(before)))
        at(2, lambda: last(unit_u(before)), unit_d(end).from_inner)
        return 0

    lax.fori_loop(0, rows // RB, finish_rows, 0)
    take = [local(x, hid_s.at[:, wide(i * feat)], loc_sem.at[3 + i]) for i, x in enumerate((q_hbm, k_hbm, v_hbm))]
    sent(unit_u(before), "core")
    sent(unit_d(before), "core")
    unit_o.terms[...] = dot_tn(mixed_s[...], si_s[...]).astype(bf16).reshape(unit_o.terms.shape)
    unit_o.start()
    unit_u(end).from_inner()
    gub = join_columns([gub_s[j] for j in range(BLOCKS)], n)
    for i in range(gub.shape[1] // feat):
        small_s[8 + i:9 + i, :] = gub[0:1, i * feat:(i + 1) * feat]

    def norm_rows(i, _):
        sl = pl.ds(pl.multiple_of(i * RB, RB), RB)
        xhat, _q = norm_parts(tokens_ref[sl, :].astype(f32))
        gi_s[sl, wide(0)] = (xhat * gain_one + shift_one).astype(bf16)
        return 0

    lax.fori_loop(0, rows // RB, norm_rows, 0)
    for c in take:
        c.wait()
    ends = image_ends(counts_ref[0], counts_ref[1], rows)
    key_at = lambda e: pl.ds(feat + e * 128, 128)
    dk_at, dv_at = pl.ds(0, 128), pl.ds(128, 128)

    def pair(p, _):
        part = lambda which: pl.ds(pl.multiple_of(which * feat + p * 128, 128), 128)
        cols = part(0)
        keys = hid_s[:, part(1)]
        for e, x in enumerate(key_lanes(keys, ends)):
            gi_s[:, key_at(e)] = x
        kt_s[...] = keys.T
        res_s[:, pl.ds(0, 256)] = jnp.zeros((rows, 256), f32)

        def attend_back(b, _):
            first = pl.multiple_of(b * QB, QB)
            sl = pl.ds(first, QB)
            q, do = hid_s[sl, part(0)], hid_s[sl, part(3)]
            v = hid_s[:, part(2)]
            lane = lax.broadcasted_iota(jnp.int32, q.shape, 1)
            zero = jnp.zeros_like(q)
            dqs = []
            dks = dvs = None
            for e in range(2):
                mask = (lane < 64) == (e == 0)
                qm, dom = jnp.where(mask, q, zero), jnp.where(mask, do, zero)
                s = dot_nt(gi_s[:, key_at(e)], query_lanes(q, first, ends, e))
                probs = jnp.exp(s - lse_ref[p, e:e + 1, sl])
                dp = dot_nt(v, dom)
                centre = jnp.sum(probs * dp, axis=0, keepdims=True)
                ds = (probs * (dp - centre)).astype(bf16)
                dv_e = dot(probs.astype(bf16), dom)
                dk_e = dot(ds, qm)
                dqs.append(dot(kt_s[e * 64:(e + 1) * 64, :], ds))
                dvs = dv_e if dvs is None else dvs + dv_e
                dks = dk_e if dks is None else dks + dk_e
            res_s[:, dk_at] += dks
            res_s[:, dv_at] += dvs
            gb_s[sl, cols] = (jnp.concatenate(dqs, axis=0).T * 0.125).astype(bf16)

            def at(k, when, todo):
                @pl.when((b == k) & when)
                def _():
                    todo()

            at(0, p == 0, unit_o.from_core)
            at(1, p == 0, lambda: unit_d(end).from_outer())
            at(2, p == 0, unit_o.from_twin)
            at(3, p == 0, lambda: unit_u(end).from_outer())
            at(0, p == 1, lambda: last(unit_d(end)))
            at(1, p == 1, lambda: (last(unit_u(end)), unit_o.from_inner()))
            at(3, p == 1, unit_o.from_outer)
            at(0, p == 2, lambda: last(unit_o))
            at(0, p >= 3, lambda: last(unit_a(p - 3)))
            at(0, p >= 1, lambda: unit_a(p - 1).from_core())
            at(1, p >= 2, lambda: unit_a(p - 2).from_inner())
            at(2, p >= 1, lambda: unit_a(p - 1).from_twin())
            at(3, p >= 2, lambda: unit_a(p - 2).from_outer())
            return 0

        lax.fori_loop(0, rows // QB, attend_back, 0)
        dk, dv = res_s[:, dk_at].astype(bf16), res_s[:, dv_at].astype(bf16)
        mixed_s[:, cols] = dk
        si_s[:, cols] = dv
        both = jnp.concatenate([gb_s[:, cols], dk, dv], axis=1)

        @pl.when(p >= 2)
        def _():
            sent(unit_a(p - 2), "core")

        term = pair_term(p)
        term[...] = dot_tn(gi_s[:, wide(0)], both).astype(bf16).reshape(term.shape)
        unit_a(p).start()
        return 0

    lax.fori_loop(0, heads, pair, 0)
    for c in weights:
        c.wait()

    def back_rows(i, _):
        sl = pl.ds(pl.multiple_of(i * RB, RB), RB)
        dq, dk, dv = gb_s[sl, :], mixed_s[sl, :], si_s[sl, :]
        weight = lambda i: up_s[i, :, :, :, :, wide(0)].reshape(feat, feat)
        gs = dot_nt(dq, weight(0)) + dot_nt(dk, weight(1)) + dot_nt(dv, weight(2))
        xhat, q = norm_parts(tokens_ref[sl, :].astype(f32))
        t = gs * gain_one
        gtok_ref[sl, :] += q * (t - jnp.mean(t, axis=-1, keepdims=True)
                                - xhat * jnp.mean(t * xhat, axis=-1, keepdims=True))
        for r, a in enumerate((gs * xhat, gs, dq.astype(f32), dv.astype(f32))):
            small_s[r:r + 1, :] += jnp.sum(a, axis=0, keepdims=True)

        def at(k, *todo):
            @pl.when(i == k)
            def _():
                for one in todo:
                    one()

        at(0, lambda: last(unit_a(heads - 3)), lambda: unit_a(heads - 1).from_core())
        at(1, lambda: unit_a(heads - 2).from_inner())
        at(2, lambda: unit_a(heads - 1).from_twin())
        at(3, lambda: unit_a(heads - 2).from_outer())
        return 0

    lax.fori_loop(0, rows // RB, back_rows, 0)
    steps = small.steps()
    small.start()
    unit_a(heads - 1).from_inner()
    steps[0]()
    last(unit_a(heads - 2))
    steps[1]()
    unit_a(heads - 1).from_outer()
    gup_ref[...] = join_columns([gup_ref[:, j * width:(j + 1) * width] for j in range(BLOCKS)], n)
    steps[2]()
    last(unit_a(heads - 1))
    for one in steps[3:]:
        one()
    for p in range(heads):
        for i, ref in enumerate((gq_ref, gk_ref, gv_ref)):
            ref[:, p * 128:(p + 1) * 128] = gqkv_s[p, :, i * 128:(i + 1) * 128]

    def drain(j, _):
        sent(unit_u(j), *rest_stages)
        sent(unit_d(j), *rest_stages)
        return 0

    lax.fori_loop(0, BLOCKS, drain, 0)
    sent(unit_u(end), "core")
    sent(unit_d(end), "core")
    sent(unit_o, "core", *rest_stages)

    def drain_pairs(p, _):
        sent(unit_a(p), *rest_stages)

        @pl.when(p >= heads - 2)
        def _():
            sent(unit_a(p), "core")
        return 0

    lax.fori_loop(0, heads, drain_pairs, 0)
    small.finish()


def layer_back(sizes, counts, mixed, tokens, cot, outw, vec, lse, up_all, down_all, q, k, v, qkv_all):
    dp_total, n = sizes
    rows, feat = tokens.shape
    B, pairs = n // 8, dp_total // 2
    own, width = up_all.shape[-2:]
    piece = down_all.shape[-2]
    heads = feat // 128
    s = jax.ShapeDtypeStruct
    vm = pl.BlockSpec(memory_space=pltpu.VMEM)
    anyspec = pl.BlockSpec(memory_space=pl.ANY)
    act = lambda dt, cols=feat: pltpu.VMEM((rows, cols), dt)
    copies = (2 * BLOCKS + 1 + heads) * Scatter.count(B, pairs) + Total.count(B, pairs)
    return pl.pallas_call(
        functools.partial(layer_kernel, dp_total, n),
        in_specs=[pl.BlockSpec(memory_space=pltpu.SMEM), anyspec, vm, anyspec, vm, vm, vm] + [anyspec] * 6,
        out_specs=[vm] * 9,
        out_shape=[s((rows, feat), bf16), s((rows, feat), f32), s((own, BLOCKS * width), f32),
                   s((BLOCKS * piece, feat), f32)] + [s((own, feat), f32)] * 4 + [s(vec.shape, f32)],
        scratch_shapes=[act(f32), act(bf16), act(bf16), act(bf16), act(bf16, BLOCKS * width), act(bf16, width),
                        pltpu.VMEM(up_all.shape, bf16), pltpu.VMEM(down_all.shape, bf16),
                        pltpu.VMEM((128, rows), bf16), pltpu.VMEM((BLOCKS, 8, width), f32),
                        pltpu.VMEM((BLOCKS, 8, width), f32), pltpu.VMEM((heads, own, 384), f32),
                        pltpu.VMEM(vec.shape, f32),
                        pltpu.VMEM((2,) + up_all.shape[1:], bf16), pltpu.VMEM((2,) + down_all.shape[1:], bf16)]
        + Scatter.shapes(B, pairs, own, width, scatter_edge(width), (BLOCKS,))
        + Scatter.shapes(B, pairs, piece, feat, scatter_edge(feat), (BLOCKS,))
        + Scatter.shapes(B, pairs, own, feat, 256)
        + Scatter.shapes(B, pairs, own, 384, 128, (heads,))
        + Total.shapes(B, pairs, vec.shape)
        + [pltpu.SemaphoreType.DMA((copies,)), pltpu.SemaphoreType.DMA((copies,)),
           pltpu.SemaphoreType.DMA((2 * BLOCKS + 2,))],
        compiler_params=pltpu.CompilerParams(collective_id=2, has_side_effects=True, vmem_limit_bytes=67043328),
        name="layer_back",
    )(counts, mixed, tokens, cot, outw, vec, lse, up_all, down_all, q, k, v, qkv_all)

FSDP="fsdp"

def spread(vectors, index, total):
    own = vectors.shape[-1]
    at = lax.broadcasted_iota(jnp.int32, (1, total, own), 1)
    wide = jnp.where(at == index, vectors[:, None, :], jnp.zeros((), vectors.dtype))
    return wide.reshape(vectors.shape[0], total * own)

def on_device(sizes, tokens, image_counts, cotangent, first_gain, first_shift, query_weight, query_bias, key_weight,
              value_weight, value_bias, out_weight, out_bias, second_gain, second_shift, up_weight, up_bias,
              down_weight, down_bias):
    rows, feat = tokens.shape
    own = query_weight.shape[0]
    n = feat // own
    counts = image_counts[0]
    me = lax.axis_index(FSDP)
    eight = jnp.stack([first_gain, first_shift, query_bias, value_bias, out_bias, second_gain, second_shift, down_bias])
    small = jnp.concatenate([spread(eight, me, n), spread(up_bias[None], me, n).reshape(-1, feat)])
    small = jnp.concatenate([small, jnp.zeros((16 - small.shape[0], feat), bf16)])
    q, k, v, vec, mixed, lse, qkv_all, o_all, up_all, down_all, _ = gather_attend(
        sizes, counts, tokens, small, query_weight, key_weight, value_weight, out_weight, up_weight, down_weight)
    layer_out, gtok, gup, gdown, gq, gk, gv, go, total = layer_back(
        sizes, counts, mixed, tokens, cotangent, o_all.reshape(feat, feat), vec, lse, up_all, down_all, q, k, v, qkv_all)
    mine = lax.dynamic_index_in_dim(total[:8].reshape(8, n, own), me, 1, keepdims=False)
    ub_mine = lax.dynamic_index_in_dim(total[8:12].reshape(n, -1), me, 0, keepdims=False)
    return (layer_out, gtok, mine[0], mine[1], gq, mine[2], gk, gv, mine[3], go, mine[4], mine[5], mine[6],
            gup, ub_mine, gdown, mine[7])


def solution(mesh):
    rows = P(("dp", "fsdp"), None)
    mat = P("fsdp", None)
    vec = P("fsdp")
    return jax.shard_map(
        functools.partial(on_device, (mesh.shape["dp"], mesh.shape["fsdp"])),
        mesh=mesh,
        in_specs=(rows, rows, rows, vec, vec, mat, vec, mat, mat, vec, mat, vec, vec, vec, mat, vec, mat, vec),
        out_specs=(rows, rows, vec, vec, mat, vec, mat, mat, vec, mat, vec, vec, vec, mat, vec, mat, vec),
        check_vma=False,
    )
```

```python
import functools
import math

import jax
import jax.numpy as jnp
from jax import lax
from jax.experimental import pallas as pl
from jax.experimental.pallas import tpu as pltpu
from jax.sharding import PartitionSpec as P

EPS = 1e-06
NT = (((1,), (1,)), ((), ()))
TN = (((0,), (0,)), ((), ()))


SMALL_ROWS=197; LARGE_ROWS=325
QB=256
NEG=-1e30

def image_ends(small, large, rows):
    ends=[]
    for i in range(1, rows//SMALL_ROWS+1):
        e = jnp.minimum(i, small)*SMALL_ROWS + jnp.maximum(i-small,0)*LARGE_ROWS
        ends.append(jnp.where(i<=small+large, e, 2*rows))
    return ends

def image_of(places, ends):
    idx = jnp.zeros(places.shape, jnp.int32)
    for e in ends:
        idx = idx + (places>=e).astype(jnp.int32)
    return idx


f32=jnp.float32; bf16=jnp.bfloat16
RB=256
INV_SQRT2=1/math.sqrt(2.0); INV_SQRT2PI=1/math.sqrt(2*math.pi)

def dot(a,b): return jnp.dot(a,b,preferred_element_type=f32)
def dot_nt(a,b): return lax.dot_general(a,b,NT,preferred_element_type=f32)
def dot_tn(a,b): return lax.dot_general(a,b,TN,preferred_element_type=f32)

def norm_parts(x):
    mean=jnp.mean(x,axis=-1,keepdims=True)
    cen=x-mean
    var=jnp.mean(cen*cen,axis=-1,keepdims=True)
    q=lax.rsqrt(var+EPS)
    return cen*q, q

def live_mask(counts_ref, first, n):
    end=counts_ref[0]*197+counts_ref[1]*325
    r=first+lax.broadcasted_iota(jnp.int32,(n,1),0)
    return r<end


MESH = pl.DeviceIdType.MESH


class Place:
    def __init__(self, dp_total, fsdp_total):
        half = fsdp_total // 2
        self.outer_total = 4
        self.inner_total = half // 4
        assert half % 4 == 0
        self.pairs = dp_total // 2
        self.d = lax.axis_index("dp")
        self.f = lax.axis_index("fsdp")
        self.core = self.f % 2
        self.inner = (self.f // 2) % self.inner_total
        self.outer = self.f // (2 * self.inner_total)
        self.side = self.d % 2
        self.twin = self.d + 1 - 2 * self.side
        self.flip = self.outer // 2
        self.mirror = self.unmirror(self.outer)

        B = self.inner_total
        self.outers = [self.outer] + [(self.outer + s) % 4 for s in range(1, 4)]
        self.inners = [self.inner] + [(self.inner + t) % B for t in range(1, B)]
        self.cores = [self.core, 1 - self.core]
        self.ends = [self.unmirror(0), self.unmirror(1), self.unmirror(2)]
        self.next_outer = self.unmirror(1 - self.mirror)
        self.arrivals = [self.outer, self.next_outer, self.ends[2], self.unmirror(3)]
        self.outer_devices = [self.device(o, self.inner, self.core) for o in self.outers]
        self.inner_devices = [self.device(self.outer, i, self.core) for i in self.inners]
        self.core_device = self.device(self.outer, self.inner, self.cores[1])
        self.twin_device = (self.twin, self.f)
        self.pair_devices = [(self.d, self.f)] + [(self.side + 2 * ((self.d // 2 + k) % self.pairs), self.f)
                                                  for k in range(1, self.pairs)]

    def unmirror(self, at):
        return at + self.flip * (3 - 2 * at)

    def device(self, outer, inner, core):
        return (self.d, (outer * self.inner_total + inner) * 2 + core)

    def at_outer(self, outer):
        return self.device(outer, self.inner, self.core)

    def at_inner(self, t):
        return self.inner_devices[t % self.inner_total]

    def other_core(self):
        return self.core_device

    def at_twin(self):
        return self.twin_device

    def me(self):
        return (self.d, self.f)

    def at_pair(self, k):
        return self.pair_devices[k % self.pairs]

    def neighbours(self, pairs=False):
        out = self.outer_devices[1:]
        out += [self.at_inner(t) for t in range(1, self.inner_total)]
        out += [self.at_twin(), self.other_core()]
        if pairs:
            out = self.outer_devices[1:] + Total.near_devices(self)
            out += [self.at_pair(k) for k in range(1, self.pairs)]
        return out


def greet(others):
    barrier = pltpu.get_barrier_semaphore()
    for other in others:
        pl.semaphore_signal(barrier, inc=1, device_id=other, device_id_type=MESH)
    pl.semaphore_wait(barrier, len(others))


class Gather:
    def __init__(self, place, ref, edge, sems, base):
        self.place, self.ref, self.edge = place, ref, edge
        self.rows = ref.shape[-2]
        self.send_sem, self.recv_sem = sems
        self.base = base
        A, B = place.outer_total, place.inner_total
        keys = [("z", s) for s in range(1, A)] + [("Z", s) for s in range(1, A)]
        keys += [("x", s, t) for s in range(A) for t in range(1, B)]
        keys += [("y", t) for t in range(B)]
        keys += [("c",)]
        self.keys = {key: i for i, key in enumerate(keys)}
        self.sent = []
        self.sent_inside = []

    @staticmethod
    def count(B):
        return 6 + 4 * (B - 1) + B + 1

    def rows_of(self, kind):
        e, r, p = self.edge, self.rows, self.place.side
        if not e or kind == "all":
            return pl.ds(0, r)
        start, size = {"plane": (p * e, r - e), "mine": (p * (r - e), e), "theirs": ((1 - p) * (r - e), e)}[kind]
        return pl.ds(pl.multiple_of(start, 8), size)

    def part(self, outer, inner, core, kind):
        return self.ref.at[outer, inner, core, self.rows_of(kind)]

    def copy(self, key, ref, to):
        i = self.base + self.keys[key]
        into = i
        if key[0] == "Z":
            into = self.base + self.keys["z", 2 if key[1] == 2 else 3]
        return pltpu.make_async_remote_copy(src_ref=ref, dst_ref=ref, send_sem=self.send_sem.at[i],
                                            recv_sem=self.recv_sem.at[into], device_id=to, device_id_type=MESH)

    def send(self, key, make):
        self.copy(key, *make()).start()
        self.sent.append((key, make))

    def send_inside(self, key, make):
        @pl.when(self.place.mirror == 1)
        def _():
            self.copy(key, *make()).start()

        self.sent_inside.append((key, make))

    def got(self, key, ref):
        self.copy(key, ref, self.place.me()).wait_recv()

    def outer_of(self, step):
        return self.place.arrivals[step]

    def own_line(self, step):
        p = self.place
        return self.part(self.outer_of(step), p.inner, p.core, "plane")

    def start(self):
        p = self.place
        self.send(("z", 1), lambda: (self.own_line(0), p.at_outer(p.next_outer)))
        self.send_inside(("z", 2), lambda: (self.own_line(0), p.at_outer(p.ends[2])))
        self.pass_inner(0)

    def pass_inner(self, step):
        p = self.place
        for t in range(1, p.inner_total):
            self.send(("x", step, t), lambda t=t: (self.own_line(step), p.at_inner(-t)))

    def onward(self, step):
        p = self.place
        return self.own_line(step), p.at_outer(p.ends[2 if step == 1 else 0])

    def arrived(self, step, record):
        self.got(("z", step), self.own_line(step))
        kept = list(self.sent)
        self.pass_inner(step)
        if step == 3:
            self.pass_twin(0)
        if not record:
            self.sent = kept

    def from_next(self):
        self.arrived(1, True)
        self.send_inside(("Z", 1), functools.partial(self.onward, 1))

    def relay(self, step):
        @pl.when(self.place.mirror == 1)
        def _():
            self.got(("z", step), self.own_line(step))
            self.copy(("Z", step), *self.onward(step)).start()
            kept = list(self.sent)
            self.pass_inner(step)
            if step == 3:
                self.pass_twin(0)
            self.sent = kept

        self.sent_inside.append((("Z", step), functools.partial(self.onward, step)))

    def take(self, step):
        @pl.when(self.place.mirror == 0)
        def _():
            self.arrived(step, False)

        for t in range(1, self.place.inner_total):
            self.sent.append((("x", step, t), lambda t=t: (self.own_line(step), self.place.at_inner(-t))))
        if step == 3 and self.edge:
            self.sent.append((("y", 0), lambda: (self.line(0, "mine"), self.place.at_twin())))

    def relay_2(self):
        self.relay(2)

    def relay_3(self):
        self.relay(3)

    def take_2(self):
        self.take(2)

    def take_3(self):
        self.take(3)

    def line(self, t, kind):
        p = self.place
        return self.part(slice(None), p.inners[t], p.core, kind)

    def pass_twin(self, t):
        if self.edge:
            self.send(("y", t), lambda: (self.line(t, "mine"), self.place.at_twin()))

    def from_inner(self):
        p = self.place
        for t in range(1, p.inner_total):
            for step in range(4):
                self.got(("x", step, t), self.part(self.outer_of(step), p.inners[t], p.core, "plane"))
            self.pass_twin(t)

    def half(self, core):
        return self.part(slice(None), slice(None), core, "all")

    def from_twin(self):
        p = self.place
        if self.edge:
            for t in range(p.inner_total):
                self.got(("y", t), self.line(t, "theirs"))
        self.send(("c",), lambda: (self.half(p.core), p.other_core()))

    def from_core(self):
        self.got(("c",), self.half(self.place.cores[1]))

    def finish(self):
        for key, make in self.sent:
            self.copy(key, *make()).wait_send()

        @pl.when(self.place.mirror == 1)
        def _():
            for key, make in self.sent_inside:
                self.copy(key, *make()).wait_send()


class Scatter:
    def __init__(self, place, terms, bufs, edge, emit, sems, base):
        self.place, self.terms, self.edge, self.emit = place, terms, edge, emit
        self.sums, self.twin_buf, self.inner_buf, self.outer_buf, self.last_buf = bufs[:5]
        self.pair_bufs = bufs[5:]
        self.send_sem, self.recv_sem = sems
        self.base = base
        p, e, w = place.side, edge, terms.shape[-1]
        at = lambda start, size: pl.ds(pl.multiple_of(start, 128), size)
        self.plane = at(p * e, w - e)
        self.mine = at(p * (w - e), e)
        self.theirs = at((1 - p) * (w - e), e)
        self.twin_plane = at((1 - p) * e, w - e)
        self.middle = pl.ds(e, w - 2 * e)

    @staticmethod
    def count(B, pairs):
        return 1 + 1 + (B - 1) + 3 + 1 + (pairs - 1)

    @staticmethod
    def shapes(B, pairs, rows, width, edge, lead=()):
        out = [(4, B, rows, width), (4, B, rows, edge), (B - 1, 4, rows, width), (3, rows, width), (rows, width)]
        if pairs > 1:
            out += [(rows, width), (pairs - 1, rows, width)]
        return [pltpu.VMEM(tuple(lead) + s, bf16) for s in out]

    def copy(self, i, src, dst, to):
        return pltpu.make_async_remote_copy(src_ref=src, dst_ref=dst, send_sem=self.send_sem.at[self.base + i],
                                            recv_sem=self.recv_sem.at[self.base + i], device_id=to, device_id_type=MESH)

    def copies(self, stage):
        p = self.place
        A, B = 4, p.inner_total
        if stage == "core":
            return [self.copy(0, self.terms.at[:, :, p.cores[1]], self.sums, p.other_core())]
        if stage == "twin":
            return [self.copy(1, self.sums.at[:, :, :, self.theirs], self.twin_buf, p.at_twin())]
        if stage == "inner":
            return [self.copy(1 + t, self.sums.at[:, p.inners[(B - t) % B], :, self.plane],
                              self.inner_buf.at[t - 1, :, :, self.plane], p.at_inner(-t)) for t in range(1, B)]
        if stage == "outer":
            return [self.copy(B + s, self.sums.at[p.outers[A - s], p.inner, :, self.plane],
                              self.outer_buf.at[s - 1, :, self.plane], p.outer_devices[A - s])
                    for s in range(1, A)]
        if stage == "last":
            return [self.copy(A + B, self.sums.at[p.outer, p.inner, :, self.plane], self.last_buf.at[:, self.plane],
                              p.at_twin())]
        half, others = self.pair_bufs
        return [self.copy(A + B + k, half, others.at[k - 1], p.at_pair(p.pairs - k)) for k in range(1, p.pairs)]

    def go(self, stage):
        for c in self.copies(stage):
            c.start()

    def got(self, i, dst):
        self.copy(i, dst, dst, self.place.me()).wait_recv()

    def start(self):
        self.go("core")

    def from_core(self):
        p = self.place
        B = p.inner_total
        self.got(0, self.sums)

        def add(i, _):
            a, b = i // B, i % B
            self.sums[a, b] = self.sums[a, b] + self.terms[a, b, p.core]
            return 0

        lax.fori_loop(0, 4 * B, add, 0)
        self.go("twin")

    def from_twin(self):
        p = self.place
        B = p.inner_total
        self.got(1, self.twin_buf)

        def add(i, _):
            a, b = i // B, i % B
            self.sums[a, b, :, self.mine] = self.sums[a, b, :, self.mine] + self.twin_buf[a, b]
            return 0

        lax.fori_loop(0, 4 * B, add, 0)
        self.go("inner")

    def from_inner(self):
        p = self.place
        B = p.inner_total
        for t in range(1, B):
            self.got(1 + t, self.inner_buf.at[t - 1, :, :, self.plane])

        def add(a, _):
            if B == 2:
                self.sums[a, p.inner, :, self.plane] = (self.sums[a, p.inner, :, self.plane]
                                                        + self.inner_buf[0, a, :, self.plane])
                return 0
            total = self.sums[a, p.inner, :, self.plane].astype(f32)
            for t in range(1, B):
                total = total + self.inner_buf[t - 1, a, :, self.plane].astype(f32)
            self.sums[a, p.inner, :, self.plane] = total.astype(bf16)
            return 0

        lax.fori_loop(0, 4, add, 0)
        self.go("outer")

    def from_outer(self):
        p = self.place
        B = p.inner_total
        for s in range(1, 4):
            self.got(B + s, self.outer_buf.at[s - 1, :, self.plane])
        total = self.sums[p.outer, p.inner, :, self.plane].astype(f32)
        for s in range(1, 4):
            total = total + self.outer_buf[s - 1, :, self.plane].astype(f32)
        self.sums[p.outer, p.inner, :, self.plane] = total.astype(bf16)
        self.go("last")

    def from_last(self):
        p = self.place
        self.got(4 + p.inner_total, self.last_buf.at[:, self.twin_plane])
        own = lambda cols: self.sums[p.outer, p.inner, :, cols].astype(f32)
        last = lambda cols: self.last_buf[:, cols].astype(f32)
        if p.pairs == 1:
            self.emit(self.mine, own(self.mine))
            self.emit(self.middle, own(self.middle) + last(self.middle))
            self.emit(self.theirs, last(self.theirs))
            return
        half, others = self.pair_bufs
        half[:, self.mine] = own(self.mine).astype(bf16)
        half[:, self.middle] = (own(self.middle) + last(self.middle)).astype(bf16)
        half[:, self.theirs] = last(self.theirs).astype(bf16)
        self.go("pairs")

    def from_pairs(self):
        p = self.place
        if p.pairs == 1:
            return
        half, others = self.pair_bufs
        total = half[...].astype(f32)
        for k in range(1, p.pairs):
            self.got(4 + p.inner_total + k, others.at[k - 1])
            total = total + others[k - 1].astype(f32)
        self.emit(pl.ds(0, self.terms.shape[-1]), total)

    def finish(self):
        for stage in ("core", "twin", "inner", "outer", "last") + (("pairs",) if self.place.pairs > 1 else ()):
            for c in self.copies(stage):
                c.wait_send()


class Total:
    def __init__(self, place, bufs, out, sems, base):
        self.place, self.landing, self.out = place, bufs[0], out
        self.send_sem, self.recv_sem = sems
        p, B = place, place.inner_total
        near = []
        for side in range(2):
            for t in range(B):
                for core in range(2):
                    if side or t or core:
                        dev = p.device(p.outer, p.inners[t], p.cores[core])[1]
                        near.append((p.d if not side else p.twin, dev))
        self.rounds = [(near, (p.side * B + p.inner) * 2 + p.core, 4 * B),
                       (p.outer_devices[1:], p.outer, 4)]
        if p.pairs > 1:
            self.rounds.append(([p.at_pair(k) for k in range(1, p.pairs)], p.d // 2, p.pairs))
        self.base = base

    @staticmethod
    def near_devices(place):
        return Total(place, [None], None, (None, None), 0).rounds[0][0]

    @staticmethod
    def count(B, pairs):
        return 4 * B + 4 + pairs

    @staticmethod
    def shapes(B, pairs, shape):
        return [pltpu.VMEM((Total.count(B, pairs),) + shape, f32)]

    def first(self, r):
        return sum(x[2] for x in self.rounds[:r])

    def send_copy(self, r, k):
        others, mine, _ = self.rounds[r]
        at = self.landing.at[self.first(r) + mine]
        return pltpu.make_async_remote_copy(src_ref=at, dst_ref=at, send_sem=self.send_sem.at[self.base + self.first(r) + k],
                                            recv_sem=self.recv_sem.at[self.base + self.first(r) + mine],
                                            device_id=others[k], device_id_type=MESH)

    def begin(self, r, value):
        others, mine, _ = self.rounds[r]
        self.landing[self.first(r) + mine] = value
        for k in range(len(others)):
            self.send_copy(r, k).start()

    def start(self, value):
        self.begin(0, value)

    def step(self, r):
        others, mine, members = self.rounds[r]
        for k in range(1, members):
            slot = self.first(r) + (mine + k) % members
            at = self.landing.at[slot]
            pltpu.make_async_remote_copy(src_ref=at, dst_ref=at, send_sem=self.send_sem.at[self.base],
                                         recv_sem=self.recv_sem.at[self.base + slot], device_id=self.place.me(),
                                         device_id_type=MESH).wait_recv()
        total = self.landing[self.first(r)]
        for k in range(1, members):
            total = total + self.landing[self.first(r) + k]
        if r + 1 < len(self.rounds):
            self.begin(r + 1, total)
        else:
            self.out[...] = total

    def steps(self):
        return [functools.partial(self.step, r) for r in range(len(self.rounds))]

    def finish(self):
        for r in range(len(self.rounds)):
            for k in range(len(self.rounds[r][0])):
                self.send_copy(r, k).wait_send()


def local(src, dst, sem):
    c = pltpu.make_async_copy(src, dst, sem)
    c.start()
    return c


BLOCKS = 3


def lane_tile(source, moves):
    lane = None
    out = None
    for col, to, size in moves:
        tile = source[:, col // 128 * 128:col // 128 * 128 + 128]
        shift = (to - col) % 128
        if shift:
            tile = pltpu.roll(tile, shift, 1)
        if out is None:
            out = tile
            lane = lax.broadcasted_iota(jnp.int32, tile.shape, 1)
        else:
            out = jnp.where((lane >= to) & (lane < to + size), tile, out)
    return out


def split_columns(source, owners):
    piece = source.shape[1] // owners // BLOCKS
    per = 128 // piece
    out = []
    for j in range(BLOCKS):
        tiles = [lane_tile(source, [(((t * per + q) * BLOCKS + j) * piece, q * piece, piece) for q in range(per)])
                 for t in range(owners // per)]
        out.append(jnp.concatenate(tiles, axis=1))
    return out


def join_columns(parts, owners):
    source = jnp.concatenate(parts, axis=1)
    width = parts[0].shape[1]
    piece = width // owners
    per = 128 // piece
    tiles = []
    for t in range(source.shape[1] // 128):
        moves = []
        for q in range(per):
            unit = t * per + q
            moves.append(((unit % BLOCKS) * width + unit // BLOCKS * piece, q * piece, piece))
        tiles.append(lane_tile(source, moves))
    return jnp.concatenate(tiles, axis=1)


EARLY = 2
PARTS = 3


def attend_block(counts_ref, q_ref, k_ref, v_ref, mixed_ref, lse_ref, pair, block):
    rows = q_ref.shape[0]
    lane = lax.broadcasted_iota(jnp.int32, (QB, 128), 1)
    first = pl.multiple_of(block * QB, QB)
    cols = pl.ds(pl.multiple_of(pair * 128, 128), 128)
    q = q_ref[pl.ds(first, QB), cols]
    k = k_ref[:, cols]
    v = v_ref[:, cols]
    ends = image_ends(counts_ref[0], counts_ref[1], rows)
    rid = image_of(first + lax.broadcasted_iota(jnp.int32, (QB, 1), 0), ends)
    cid = image_of(lax.broadcasted_iota(jnp.int32, (1, rows), 1), ends)
    bias = jnp.where(rid == cid, 0.0, NEG)
    outs = []
    lses = []
    for e in range(2):
        qm = jnp.where((lane < 64) == (e == 0), q, jnp.zeros_like(q))
        s = dot_nt(qm, k) + bias
        m = jnp.max(s, axis=1, keepdims=True)
        p = jnp.exp(s - m)
        l = jnp.sum(p, axis=1, keepdims=True)
        o = dot(p.astype(bf16), v)
        outs.append(o * (1.0 / l))
        lses.append(m + jnp.log(l))
    mixed_ref[pl.ds(first, QB), cols] = jnp.where(lane < 64, outs[0], outs[1]).astype(bf16)
    both = jnp.where(lane < 64, jnp.broadcast_to(lses[0], (QB, 128)), jnp.broadcast_to(lses[1], (QB, 128)))
    t = both.T
    lse_ref[pair, 0:1, pl.ds(first, QB)] = t[0:1, :]
    lse_ref[pair, 1:2, pl.ds(first, QB)] = t[64:65, :]


def gather_edge(rows, last=False):
    return rows // 3 if rows % 24 == 0 else rows // 4 if last or rows < 64 else rows * 3 // 8


def gather_plan(units, early, pieces):
    n = len(units)
    slots = [[] for _ in range(n + 12)]
    for t, u in enumerate(units):
        if t >= 3:
            slots[t - 2].append(u.start)
    for t, u in enumerate(units):
        inner, twin, core = (4, 5, 6) if t <= early else (5, 7, 9) if t <= PARTS else (6, 9, 11)
        stages = [(0, u.from_next), (1, u.relay_2), (2, u.relay_3), (2, u.take_2), (3, u.take_3),
                  (inner, u.from_inner), (twin, u.from_twin), (core, u.from_core)]
        for at, one in stages:
            slots[t + at].append(one)
    cut = early + 7
    rest = slots[cut:]
    while not rest[-1]:
        rest.pop()
    places = [[] for _ in range(pieces)]
    for k, slot in enumerate(rest):
        places[k * pieces // len(rest)] += slot
    for t in range(2, PARTS + 1):
        assert any(units[t].from_core in place for place in places[:(t - 1) * pieces // PARTS])
    return [one for slot in slots[:cut] for one in slot], places


def gather_kernel(dp_total, n, counts_ref, tokens_hbm, small_ref, qo_ref, ko_ref, vo_ref, oo_ref, uo_ref, do_ref,
                  q_hbm, k_hbm, v_hbm, vec_ref, mixed_hbm, lse_ref, up_last, qkv_all, o_all, up_all, down_all, small_all,
                  tokens_s, fi_s, q_s, k_s, v_s, mixed_s, w_s, small_s, up_own, send_sem, recv_sem, loc_sem):
    place = Place(dp_total, n)
    B = place.inner_total
    own = qo_ref.shape[0]
    piece = do_ref.shape[0] // BLOCKS
    greet(place.neighbours())
    take_tokens = local(tokens_hbm, tokens_s, loc_sem.at[0])
    sems = (send_sem, recv_sem)
    refs = [(small_all, 0)] + [(qkv_all.at[j], own) for j in range(PARTS)] + [(o_all, gather_edge(own))]
    for j in range(EARLY):
        refs += [(up_all.at[j], gather_edge(own)), (down_all.at[j], gather_edge(piece, j == EARLY - 1))]
    units = [Gather(place, ref, edge, sems, i * Gather.count(B))
             for i, (ref, edge) in enumerate(refs)]
    mine = lambda unit: unit.part(place.outer, place.inner, place.core, "plane")
    block = qkv_all.shape[-1]

    def own_part(source, j, i):
        return local(source.at[:, pl.ds(j * block, block)],
                     qkv_all.at[j, place.outer, place.inner, place.core, pl.ds(i * own, own)], loc_sem.at[2 + 2 * j + i % 2])

    fill = [local(small_ref, mine(units[0]), loc_sem.at[1])] + [own_part(ko_ref, j, 1) for j in range(PARTS)]

    @pl.when(place.side == 0)
    def _():
        for c in [own_part(qo_ref, j, 0) for j in range(PARTS)]:
            c.wait()

    @pl.when(place.side == 1)
    def _():
        for c in [own_part(vo_ref, j, 2) for j in range(PARTS)]:
            c.wait()

    for c in fill:
        c.wait()
    units[0].start()
    units[1].start()
    for j, part in enumerate(split_columns(uo_ref[...].astype(f32), n)):
        up_own[j] = part.astype(bf16)
    base = 1 + PARTS
    fill = [local(oo_ref.at[units[base].rows_of("plane")], mine(units[base]), loc_sem.at[1])]
    for j in range(EARLY):
        a, b = units[base + 1 + 2 * j], units[base + 2 + 2 * j]
        fill.append(local(up_own.at[j, a.rows_of("plane")], mine(a), loc_sem.at[2 + 2 * j]))
        rows = b.rows_of("plane")
        fill.append(local(do_ref.at[pl.ds(pl.multiple_of(j * piece + rows.start, 8), rows.size)], mine(b),
                          loc_sem.at[3 + 2 * j]))
    for j in range(EARLY, BLOCKS):
        fill.append(local(up_own.at[j], up_last.at[j - EARLY], loc_sem.at[2 + 2 * j]))
    for c in fill:
        c.wait()
    units[2].start()

    def vectors():
        local(small_all, small_s, loc_sem.at[1]).wait()
        total = jnp.zeros(vec_ref.shape, f32)
        for i in range(n):
            total = total + small_s[i // (2 * B), i // 2 % B, i % 2].astype(f32)
        vec_ref[...] = total

    rows, feat = tokens_s.shape
    blocks = rows // QB
    per = qkv_all.shape[-1] // 128 * blocks
    pieces = PARTS * per
    head, rest = gather_plan(units, 1, pieces)
    for one in head:
        one()
    weight_load = lambda j: pltpu.make_async_copy(qkv_all.at[j], w_s.at[j], loc_sem.at[2 + j])
    weight_load(0).start()
    vectors()
    take_tokens.wait()

    def norm_rows(i, _):
        sl = pl.ds(pl.multiple_of(i * RB, RB), RB)
        xhat, _q = norm_parts(tokens_s[sl, :].astype(f32))
        fi_s[sl, :] = (xhat * vec_ref[0:1, :] + vec_ref[1:2, :]).astype(bf16)
        return 0

    lax.fori_loop(0, rows // RB, norm_rows, 0)
    def project(j):
        cols = pl.ds(pl.multiple_of(j * block, 128), block)
        weight_load(j).wait()

        def project_rows(i, _):
            sl = pl.ds(pl.multiple_of(i * RB, RB), RB)
            fi = fi_s[sl, :]
            weight = lambda i: w_s[j, :, :, :, i * own:(i + 1) * own, :].reshape(feat, block)
            q_s[sl, cols] = ((dot(fi, weight(0)) + vec_ref[2:3, cols]).astype(bf16).astype(f32) * 0.125).astype(bf16)
            k_s[sl, cols] = dot(fi, weight(1)).astype(bf16)
            v_s[sl, cols] = (dot(fi, weight(2)) + vec_ref[3:4, cols]).astype(bf16)
            return 0

        lax.fori_loop(0, rows // RB, project_rows, 0)

    def attend_piece(i, _):
        @pl.when(i % per == 0)
        def _():
            project(i // per)

        attend_block(counts_ref, q_s, k_s, v_s, mixed_s, lse_ref, i // blocks, i % blocks)
        for at, todo in enumerate(rest):
            if todo:
                @pl.when(i == at)
                def _(todo=todo):
                    for one in todo:
                        one()

        @pl.when((i % per == per - 1) & (i < pieces - 1))
        def _():
            weight_load(i // per + 1).start()

        return 0

    lax.fori_loop(0, pieces, attend_piece, 0)
    keep = [local(a, b, loc_sem.at[2 + i]) for i, (a, b) in enumerate(((q_s, q_hbm), (k_s, k_hbm), (v_s, v_hbm)))]
    keep.append(local(mixed_s, mixed_hbm, loc_sem.at[0]))
    for c in keep:
        c.wait()
    for x in units:
        x.finish()


def gather_attend(sizes, counts, tokens, small, qw, kw, vw, ow, up, down):
    dp_total, n = sizes
    rows, feat = tokens.shape
    own = qw.shape[0]
    B = n // 8
    pairs = feat // 128
    s = jax.ShapeDtypeStruct
    vm = pl.BlockSpec(memory_space=pltpu.VMEM)
    anyspec = pl.BlockSpec(memory_space=pl.ANY)
    full = lambda *dims: (4, B, 2) + dims
    width = up.shape[1] // BLOCKS
    piece = down.shape[0] // BLOCKS
    act = s((rows, feat), bf16)
    copies = (2 + PARTS + 2 * EARLY) * Gather.count(B)
    return pl.pallas_call(
        functools.partial(gather_kernel, dp_total, n),
        in_specs=[pl.BlockSpec(memory_space=pltpu.SMEM), anyspec] + [vm] * 7,
        out_specs=[anyspec] * 3 + [vm, anyspec, vm] + [anyspec] * 6,
        out_shape=[act, act, act, s(small.shape, f32), act, s((pairs, 2, rows), f32),
                   s((max(1, BLOCKS - EARLY), own, width), bf16), s((PARTS,) + full(3 * own, feat // PARTS), bf16),
                   s(full(own, feat), bf16), s((EARLY,) + full(own, width), bf16),
                   s((EARLY,) + full(piece, feat), bf16), s(full(*small.shape), bf16)],
        scratch_shapes=[pltpu.VMEM((rows, feat), bf16)] * 6 + [
            pltpu.VMEM((PARTS,) + full(3 * own, feat // PARTS), bf16), pltpu.VMEM(full(*small.shape), bf16),
            pltpu.VMEM((BLOCKS, own, width), bf16), pltpu.SemaphoreType.DMA((copies,)),
            pltpu.SemaphoreType.DMA((copies,)), pltpu.SemaphoreType.DMA((6 + 2 * BLOCKS,))],
        compiler_params=pltpu.CompilerParams(collective_id=1, has_side_effects=True, vmem_limit_bytes=60 * 2**20),
        name="gather_attend",
    )(counts, tokens, small, qw, kw, vw, ow, up, down)


def scatter_edge(width):
    return 128 if width == 768 else width // 4 if width % 512 == 0 else width // 3


def late_edge(rows):
    return 16 if rows % 48 == 0 or rows == 64 else 0


def key_lanes(keys, ends):
    lane = lax.broadcasted_iota(jnp.int32, keys.shape, 1)
    image = image_of(lax.broadcasted_iota(jnp.int32, keys.shape, 0), ends)
    return [jnp.where((lane < 64) == (e == 0), keys, jnp.where(image == lane - 64 * (1 - e), 0.0, NEG).astype(bf16))
            for e in range(2)]


def query_lanes(queries, first, ends, e):
    lane = lax.broadcasted_iota(jnp.int32, queries.shape, 1)
    image = image_of(first + lax.broadcasted_iota(jnp.int32, queries.shape, 0), ends)
    return jnp.where((lane < 64) == (e == 0), queries, jnp.where(image == lane - 64 * (1 - e), 1.0, 0.0).astype(bf16))


def layer_kernel(dp_total, n, counts_ref, mixed_hbm, tokens_ref, cot_hbm, outw_ref, vec_ref, lse_ref, up_hbm, down_hbm,
                 up_last, down_own, q_hbm, k_hbm, v_hbm, qkv_all,
                 layer_ref, gtok_ref, gup_ref, gdown_ref, gq_ref, gk_ref, gv_ref, go_ref, total_ref,
                 res_s, si_s, gb_s, mixed_s, hid_s, gi_s, up_s, down_s, kt_s, ub_s, gub_s, gqkv_s, small_s, *rest):
    rows, feat = tokens_ref.shape
    width = gi_s.shape[1]
    own = gq_ref.shape[0]
    piece = gdown_ref.shape[0] // BLOCKS
    heads = feat // 128
    place = Place(dp_total, n)
    B, pairs = place.inner_total, place.pairs
    per = 5 if pairs == 1 else 7
    uterm_s, dterm_s = rest[:2]
    ubufs, dbufs, obufs, abufs = (rest[2 + i * per:2 + (i + 1) * per] for i in range(4))
    total_bufs = rest[2 + 4 * per:3 + 4 * per]
    send_sem, recv_sem, loc_sem, gather_send, gather_recv, weight_sem = rest[3 + 4 * per:]
    sems = (send_sem, recv_sem)
    count = Scatter.count(B, pairs)
    wide = lambda start: pl.ds(start, feat)
    load = lambda j: (pltpu.make_async_copy(up_hbm.at[j], up_s.at[j], loc_sem.at[2 * j]),
                      pltpu.make_async_copy(down_hbm.at[j], down_s.at[j], loc_sem.at[2 * j + 1]))
    at_end = 3 * feat
    first_loads = [local(mixed_hbm, mixed_s, loc_sem.at[2 * BLOCKS]),
                   local(cot_hbm, hid_s.at[:, wide(at_end)], loc_sem.at[2 * BLOCKS + 1])]
    for j in range(EARLY):
        for c in load(j):
            c.start()
    late = []
    for j in range(EARLY, BLOCKS):
        late += [(up_s.at[j], late_edge(own), up_last.at[j - EARLY], 0), (down_s.at[j], late_edge(piece), down_own, j * piece)]
    gathers = []
    for i, (ref, edge, source, start) in enumerate(late):
        unit = Gather(place, ref, edge, (gather_send, gather_recv), i * Gather.count(B))
        gathers.append(unit)
        part = unit.rows_of("plane")
        first_loads.append(local(source.at[pl.ds(pl.multiple_of(start + part.start, 8), part.size)],
                                 unit.part(place.outer, place.inner, place.core, "plane"),
                                 loc_sem.at[2 * EARLY + i]))
    gu, gd = gathers

    def unit_u(j):
        def emit(cols, value):
            gup_ref[:, pl.ds(pl.multiple_of(j * width + cols.start, 128), cols.size)] = value
        return Scatter(place, uterm_s.at[j % 2], [b.at[j] for b in ubufs], scatter_edge(width), emit, sems,
                       2 * j * count)

    def unit_d(j):
        def emit(cols, value):
            gdown_ref[pl.ds(pl.multiple_of(j * piece, 8), piece), cols] = value
        return Scatter(place, dterm_s.at[j % 2], [b.at[j] for b in dbufs], scatter_edge(feat), emit, sems,
                       (2 * j + 1) * count)

    def emit_out(cols, value):
        go_ref[:, cols] = value

    unit_o = Scatter(place, uterm_s.at[1, :, :, :, :, wide(0)], obufs, 256, emit_out, sems, 2 * BLOCKS * count)

    def pair_term(p):
        return dterm_s.at[1, :, :, :, pl.ds(0, own), pl.ds(pl.multiple_of(p % 2 * 384, 128), 384)]

    def unit_a(p):
        def emit(cols, value):
            gqkv_s[p, :, cols] = value
        return Scatter(place, pair_term(p), [b.at[p] for b in abufs], 128, emit, sems,
                       (2 * BLOCKS + 1 + p) * count)

    small = Total(place, total_bufs, total_ref, sems, (2 * BLOCKS + 1 + heads) * count)

    def last(unit):
        unit.from_last()
        unit.from_pairs()

    def sent(unit, *stages):
        for stage in stages:
            for c in unit.copies(stage):
                c.wait_send()

    rest_stages = ("twin", "inner", "outer", "last") + (("pairs",) if pairs > 1 else ())
    gain_one, shift_one = vec_ref[0:1, :], vec_ref[1:2, :]
    obias, gain, shift, dbias = (vec_ref[i:i + 1, :] for i in range(4, 8))
    ub = jnp.concatenate([vec_ref[8 + i:9 + i, :] for i in range(BLOCKS * width // feat)], axis=1)
    for j, part in enumerate(split_columns(jnp.broadcast_to(ub, (8, ub.shape[1])), n)):
        ub_s[j] = part
    small_s[...] = jnp.zeros_like(small_s)
    for c in first_loads:
        c.wait()

    def begin(i, _):
        first = pl.multiple_of(i * RB, RB)
        sl = pl.ds(first, RB)
        res = tokens_ref[sl, :].astype(f32) + (dot(mixed_s[sl, :], outw_ref[...]) + obias)
        res_s[sl, :] = res
        xhat, _q = norm_parts(res)
        si_s[sl, :] = (xhat * gain + shift).astype(bf16)
        gb_s[sl, :] = jnp.where(live_mask(counts_ref, first, RB), hid_s[sl, wide(at_end)], jnp.zeros((), bf16))
        gtok_ref[sl, :] = jnp.zeros((RB, feat), f32)
        return 0

    lax.fori_loop(0, rows // RB, begin, 0)
    greet(place.neighbours(pairs=True))
    gu.start()
    gd.start()

    def block(j, _):
        @pl.when(j < EARLY)
        def _():
            for c in load(j):
                c.wait()

        upw = lambda: up_s[j].reshape(feat, width)
        downw = lambda: down_s[j].reshape(width, feat)
        cols = pl.ds(pl.multiple_of(j * width, 128), width)
        gub_s[j] = jnp.zeros(gub_s.shape[1:], f32)

        def after(back, when, todo):
            @pl.when(when & (j >= back))
            def _():
                todo(j - back)

        def rows_piece(i, _):
            sl = pl.ds(pl.multiple_of(i * RB, RB), RB)
            pre = dot(si_s[sl, :], upw()) + ub_s[j, 0:1, :]
            cdf = 0.5 + 0.5 * lax.erf(pre * INV_SQRT2)
            pdf = jnp.exp(-0.5 * pre * pre) * INV_SQRT2PI
            hid_s[sl, cols] = (pre * cdf).astype(bf16)
            gi = (dot_nt(gb_s[sl, :], downw()) * (cdf + pre * pdf)).astype(bf16)
            gi_s[sl, :] = gi
            gub_s[j, 0:1, :] += jnp.sum(gi.astype(f32), axis=0, keepdims=True)
            for at, row, todo in ((0, 0, (gu.from_next,)), (0, 1, (gu.relay_2, gd.from_next)),
                                  (0, 2, (gu.relay_3, gu.take_2, gd.relay_2)),
                                  (0, 3, (gu.take_3, gd.relay_3, gd.take_2)), (1, 0, (gd.from_inner,)),
                                  (1, 1, (gu.from_twin,)), (1, 2, (gd.from_twin,)), (1, 3, (gu.from_core,))):
                @pl.when((j == at) & (i == row))
                def _(todo=todo):
                    for one in todo:
                        one()
            after(1, i == 0, lambda k: unit_d(k).from_core())
            after(1, i == 1, lambda k: unit_u(k).from_core())
            after(2, i == 1, lambda k: unit_d(k).from_inner())
            after(1, i == 3, lambda k: unit_d(k).from_twin())
            return 0

        lax.fori_loop(0, rows // RB, rows_piece, 0)
        always = j >= 0
        after(2, always, lambda k: (sent(unit_u(k), "core"), sent(unit_d(k), "core")))
        dterm_s[j % 2] = dot_tn(hid_s[:, cols], gb_s[...]).astype(bf16).reshape(dterm_s.shape[1:])
        unit_d(j).start()

        @pl.when(j == 0)
        def _():
            gd.take_3()

        after(1, always, lambda k: unit_u(k).from_twin())
        after(2, always, lambda k: unit_u(k).from_inner())
        uterm_s[j % 2] = dot_tn(si_s[...], gi_s[...]).astype(bf16).reshape(uterm_s.shape[1:])
        unit_u(j).start()
        gtok_ref[...] += dot_nt(gi_s[...], upw())

        @pl.when(j == 0)
        def _():
            gu.from_inner()

        @pl.when(j == 1)
        def _():
            gd.from_core()

        return 0

    lax.fori_loop(0, BLOCKS, block, 0)
    end, before = BLOCKS - 1, BLOCKS - 2
    gu.finish()
    gd.finish()
    third = qkv_all.shape[-1]
    weights = [local(qkv_all.at[j, :, :, :, pl.ds(i * own, own)], up_s.at[i, :, :, :, :, pl.ds(j * third, third)],
                     weight_sem.at[i * PARTS + j]) for i in range(3) for j in range(PARTS)]

    def finish_rows(i, _):
        first = pl.multiple_of(i * RB, RB)
        sl = pl.ds(first, RB)
        res = res_s[sl, :]
        layer = res + (dot(hid_s[sl, :], down_s[...].reshape(BLOCKS * width, feat)) + dbias)
        layer_ref[sl, :] = jnp.where(live_mask(counts_ref, first, RB), layer, 0.0).astype(bf16)
        xhat, q = norm_parts(res)
        gs = gtok_ref[sl, :]
        t = gs * gain
        gb = gb_s[sl, :].astype(f32)
        gres = gb + q * (t - jnp.mean(t, axis=-1, keepdims=True) - xhat * jnp.mean(t * xhat, axis=-1, keepdims=True))
        gtok_ref[sl, :] = gres
        ga = gres.astype(bf16)
        si_s[sl, :] = ga
        small_s[7:8, :] += jnp.sum(gb, axis=0, keepdims=True)
        small_s[5:6, :] += jnp.sum(gs * xhat, axis=0, keepdims=True)
        small_s[6:7, :] += jnp.sum(gs, axis=0, keepdims=True)
        small_s[4:5, :] += jnp.sum(ga.astype(f32), axis=0, keepdims=True)
        hid_s[sl, wide(at_end)] = dot_nt(ga, outw_ref[...]).astype(bf16)

        def at(k, *todo):
            @pl.when(i == k)
            def _():
                for one in todo:
                    one()

        at(0, lambda: unit_d(end).from_core(), lambda: unit_d(0).from_outer())
        at(1, lambda: unit_u(end).from_core(), lambda: unit_d(before).from_inner())
        at(2, lambda: unit_u(0).from_outer())
        at(3, lambda: unit_d(end).from_twin())
        return 0

    lax.fori_loop(0, rows // RB, finish_rows, 0)
    take = [local(x, hid_s.at[:, wide(i * feat)], loc_sem.at[3 + i]) for i, x in enumerate((q_hbm, k_hbm, v_hbm))]
    sent(unit_u(before), "core")
    sent(unit_d(before), "core")
    unit_o.terms[...] = dot_tn(mixed_s[...], si_s[...]).astype(bf16).reshape(unit_o.terms.shape)
    unit_o.start()
    unit_u(end).from_twin()
    unit_u(before).from_inner()
    gub = join_columns([gub_s[j] for j in range(BLOCKS)], n)
    for i in range(gub.shape[1] // feat):
        small_s[8 + i:9 + i, :] = gub[0:1, i * feat:(i + 1) * feat]

    def norm_rows(i, _):
        sl = pl.ds(pl.multiple_of(i * RB, RB), RB)
        xhat, _q = norm_parts(tokens_ref[sl, :].astype(f32))
        gi_s[sl, wide(0)] = (xhat * gain_one + shift_one).astype(bf16)
        return 0

    lax.fori_loop(0, rows // RB, norm_rows, 0)
    for c in take:
        c.wait()
    ends = image_ends(counts_ref[0], counts_ref[1], rows)
    key_at = lambda e: pl.ds(feat + e * 128, 128)
    dk_at, dv_at = pl.ds(0, 128), pl.ds(128, 128)

    def pair(p, _):
        part = lambda which: pl.ds(pl.multiple_of(which * feat + p * 128, 128), 128)
        cols = part(0)
        keys = hid_s[:, part(1)]
        for e, x in enumerate(key_lanes(keys, ends)):
            gi_s[:, key_at(e)] = x
        kt_s[...] = keys.T
        res_s[:, pl.ds(0, 256)] = jnp.zeros((rows, 256), f32)

        def attend_back(b, _):
            first = pl.multiple_of(b * QB, QB)
            sl = pl.ds(first, QB)
            q, do = hid_s[sl, part(0)], hid_s[sl, part(3)]
            v = hid_s[:, part(2)]
            lane = lax.broadcasted_iota(jnp.int32, q.shape, 1)
            zero = jnp.zeros_like(q)
            dqs = []
            dks = dvs = None
            for e in range(2):
                mask = (lane < 64) == (e == 0)
                qm, dom = jnp.where(mask, q, zero), jnp.where(mask, do, zero)
                s = dot_nt(gi_s[:, key_at(e)], query_lanes(q, first, ends, e))
                probs = jnp.exp(s - lse_ref[p, e:e + 1, sl])
                dp = dot_nt(v, dom)
                centre = jnp.sum(probs * dp, axis=0, keepdims=True)
                ds = (probs * (dp - centre)).astype(bf16)
                dv_e = dot(probs.astype(bf16), dom)
                dk_e = dot(ds, qm)
                dqs.append(dot(kt_s[e * 64:(e + 1) * 64, :], ds))
                dvs = dv_e if dvs is None else dvs + dv_e
                dks = dk_e if dks is None else dks + dk_e
            res_s[:, dk_at] += dks
            res_s[:, dv_at] += dvs
            gb_s[sl, cols] = (jnp.concatenate(dqs, axis=0).T * 0.125).astype(bf16)

            def at(k, when, todo):
                @pl.when((b == k) & when)
                def _():
                    todo()

            at(0, p == 0, lambda: last(unit_d(0)))
            at(1, p == 0, lambda: (unit_o.from_core(), last(unit_u(0))))
            at(2, p == 0, lambda: unit_d(before).from_outer())
            at(3, p == 0, lambda: (unit_u(before).from_outer(), unit_d(end).from_inner()))
            at(0, p == 1, lambda: unit_o.from_twin())
            at(1, p == 1, lambda: (last(unit_d(before)), unit_u(end).from_inner()))
            at(2, p == 1, lambda: last(unit_u(before)))
            at(3, p == 1, lambda: unit_o.from_inner())
            at(0, p == 2, lambda: unit_d(end).from_outer())
            at(2, p == 2, lambda: unit_u(end).from_outer())
            at(3, p == 2, lambda: (last(unit_d(end)), unit_o.from_outer()))
            at(0, p == 3, lambda: last(unit_u(end)))
            at(2, p == 3, lambda: last(unit_o))
            at(1, p >= 1, lambda: unit_a(p - 1).from_core())
            at(3, p >= 1, lambda: unit_a(p - 1).from_twin())
            at(1, p >= 2, lambda: unit_a(p - 2).from_inner())
            at(0, p >= 3, lambda: unit_a(p - 3).from_outer())
            at(2, p >= 3, lambda: last(unit_a(p - 3)))
            return 0

        lax.fori_loop(0, rows // QB, attend_back, 0)
        dk, dv = res_s[:, dk_at].astype(bf16), res_s[:, dv_at].astype(bf16)
        mixed_s[:, cols] = dk
        si_s[:, cols] = dv
        both = jnp.concatenate([gb_s[:, cols], dk, dv], axis=1)

        @pl.when(p >= 2)
        def _():
            sent(unit_a(p - 2), "core")

        term = pair_term(p)
        term[...] = dot_tn(gi_s[:, wide(0)], both).astype(bf16).reshape(term.shape)
        unit_a(p).start()
        return 0

    lax.fori_loop(0, heads, pair, 0)
    for c in weights:
        c.wait()

    def back_rows(i, _):
        sl = pl.ds(pl.multiple_of(i * RB, RB), RB)
        dq, dk, dv = gb_s[sl, :], mixed_s[sl, :], si_s[sl, :]
        weight = lambda i: up_s[i, :, :, :, :, wide(0)].reshape(feat, feat)
        gs = dot_nt(dq, weight(0)) + dot_nt(dk, weight(1)) + dot_nt(dv, weight(2))
        xhat, q = norm_parts(tokens_ref[sl, :].astype(f32))
        t = gs * gain_one
        gtok_ref[sl, :] += q * (t - jnp.mean(t, axis=-1, keepdims=True)
                                - xhat * jnp.mean(t * xhat, axis=-1, keepdims=True))
        for r, a in enumerate((gs * xhat, gs, dq.astype(f32), dv.astype(f32))):
            small_s[r:r + 1, :] += jnp.sum(a, axis=0, keepdims=True)

        def at(k, *todo):
            @pl.when(i == k)
            def _():
                for one in todo:
                    one()

        at(0, lambda: unit_a(heads - 3).from_outer(), lambda: unit_a(heads - 1).from_core())
        at(1, lambda: unit_a(heads - 2).from_inner(), lambda: unit_a(heads - 1).from_twin())
        at(2, lambda: last(unit_a(heads - 3)))
        at(3, lambda: unit_a(heads - 2).from_outer(), lambda: unit_a(heads - 1).from_inner())
        return 0

    lax.fori_loop(0, rows // RB, back_rows, 0)
    small.start(small_s[...])
    steps = small.steps()
    last(unit_a(heads - 2))
    gup_ref[...] = join_columns([gup_ref[:, j * width:(j + 1) * width] for j in range(BLOCKS)], n)
    steps[0]()
    unit_a(heads - 1).from_outer()
    steps[1]()
    last(unit_a(heads - 1))
    for one in steps[2:]:
        one()
    for p in range(heads):
        for i, ref in enumerate((gq_ref, gk_ref, gv_ref)):
            ref[:, p * 128:(p + 1) * 128] = gqkv_s[p, :, i * 128:(i + 1) * 128]

    def drain(j, _):
        sent(unit_u(j), *rest_stages)
        sent(unit_d(j), *rest_stages)
        return 0

    lax.fori_loop(0, BLOCKS, drain, 0)
    sent(unit_u(end), "core")
    sent(unit_d(end), "core")
    sent(unit_o, "core", *rest_stages)

    def drain_pairs(p, _):
        sent(unit_a(p), *rest_stages)

        @pl.when(p >= heads - 2)
        def _():
            sent(unit_a(p), "core")
        return 0

    lax.fori_loop(0, heads, drain_pairs, 0)
    small.finish()


def layer_back(sizes, counts, mixed, tokens, cot, outw, vec, lse, up_all, down_all, up_last, down_own, q, k, v, qkv_all):
    dp_total, n = sizes
    rows, feat = tokens.shape
    B, pairs = n // 8, dp_total // 2
    own, width = up_all.shape[-2:]
    piece = down_all.shape[-2]
    heads = feat // 128
    s = jax.ShapeDtypeStruct
    vm = pl.BlockSpec(memory_space=pltpu.VMEM)
    anyspec = pl.BlockSpec(memory_space=pl.ANY)
    act = lambda dt, cols=feat: pltpu.VMEM((rows, cols), dt)
    copies = (2 * BLOCKS + 1 + heads) * Scatter.count(B, pairs) + Total.count(B, pairs)
    return pl.pallas_call(
        functools.partial(layer_kernel, dp_total, n),
        in_specs=[pl.BlockSpec(memory_space=pltpu.SMEM), anyspec, vm, anyspec, vm, vm, vm] + [anyspec] * 8,
        out_specs=[vm] * 9,
        out_shape=[s((rows, feat), bf16), s((rows, feat), f32), s((own, BLOCKS * width), f32),
                   s((BLOCKS * piece, feat), f32)] + [s((own, feat), f32)] * 4 + [s(vec.shape, f32)],
        scratch_shapes=[act(f32), act(bf16), act(bf16), act(bf16), act(bf16, BLOCKS * width), act(bf16, width),
                        pltpu.VMEM((BLOCKS,) + up_all.shape[1:], bf16), pltpu.VMEM((BLOCKS,) + down_all.shape[1:], bf16),
                        pltpu.VMEM((128, rows), bf16), pltpu.VMEM((BLOCKS, 8, width), f32),
                        pltpu.VMEM((BLOCKS, 8, width), f32), pltpu.VMEM((heads, own, 384), f32),
                        pltpu.VMEM(vec.shape, f32),
                        pltpu.VMEM((2,) + up_all.shape[1:], bf16), pltpu.VMEM((2,) + down_all.shape[1:], bf16)]
        + Scatter.shapes(B, pairs, own, width, scatter_edge(width), (BLOCKS,))
        + Scatter.shapes(B, pairs, piece, feat, scatter_edge(feat), (BLOCKS,))
        + Scatter.shapes(B, pairs, own, feat, 256)
        + Scatter.shapes(B, pairs, own, 384, 128, (heads,))
        + Total.shapes(B, pairs, vec.shape)
        + [pltpu.SemaphoreType.DMA((copies,)), pltpu.SemaphoreType.DMA((copies,)),
           pltpu.SemaphoreType.DMA((2 * BLOCKS + 2,))]
        + [pltpu.SemaphoreType.DMA((2 * (BLOCKS - EARLY) * Gather.count(B),))] * 2
        + [pltpu.SemaphoreType.DMA((3 * PARTS,))],
        compiler_params=pltpu.CompilerParams(collective_id=2, has_side_effects=True, vmem_limit_bytes=67043328),
        name="layer_back",
    )(counts, mixed, tokens, cot, outw, vec, lse, up_all, down_all, up_last, down_own, q, k, v, qkv_all)

FSDP="fsdp"

def hand_kernel(*refs):
    half = len(refs) // 2
    for a, b in zip(refs[:half], refs[half:]):
        b[...] = a[...]


def hand_over(by_rows, by_cols, whole):
    steps = 4
    arrays = list(by_rows) + list(by_cols) + list(whole)
    specs = [pl.BlockSpec((a.shape[0] // steps, a.shape[1]), lambda i: (i, 0)) for a in by_rows]
    specs += [pl.BlockSpec((a.shape[0], a.shape[1] // steps), lambda i: (0, i)) for a in by_cols]
    specs += [pl.BlockSpec(a.shape, lambda i: (0, 0)) for a in whole]
    return pl.pallas_call(hand_kernel, grid=(steps,), in_specs=specs, out_specs=specs,
                          out_shape=[jax.ShapeDtypeStruct(a.shape, a.dtype) for a in arrays], name="hand_over")(*arrays)


def spread(vectors, index, total):
    own = vectors.shape[-1]
    at = lax.broadcasted_iota(jnp.int32, (1, total, own), 1)
    wide = jnp.where(at == index, vectors[:, None, :], jnp.zeros((), vectors.dtype))
    return wide.reshape(vectors.shape[0], total * own)

def on_device(sizes, tokens, image_counts, cotangent, first_gain, first_shift, query_weight, query_bias, key_weight,
              value_weight, value_bias, out_weight, out_bias, second_gain, second_shift, up_weight, up_bias,
              down_weight, down_bias):
    rows, feat = tokens.shape
    own = query_weight.shape[0]
    n = feat // own
    counts = image_counts[0]
    me = lax.axis_index(FSDP)
    eight = jnp.stack([first_gain, first_shift, query_bias, value_bias, out_bias, second_gain, second_shift, down_bias])
    small = jnp.concatenate([spread(eight, me, n), spread(up_bias[None], me, n).reshape(-1, feat)])
    small = jnp.concatenate([small, jnp.zeros((16 - small.shape[0], feat), bf16)])
    q, k, v, vec, mixed, lse, up_last, qkv_all, o_all, up_all, down_all, _ = gather_attend(
        sizes, counts, tokens, small, query_weight, key_weight, value_weight, out_weight, up_weight, down_weight)
    layer_out, gtok, gup, gdown, gq, gk, gv, go, total = layer_back(
        sizes, counts, mixed, tokens, cotangent, o_all.reshape(feat, feat), vec, lse, up_all, down_all, up_last,
        down_weight, q, k, v, qkv_all)
    gtok, layer_out, gdown, gup, gq, gk, gv, go = hand_over((gtok, layer_out, gdown), (gup,), (gq, gk, gv, go))
    mine = lax.dynamic_index_in_dim(total[:8].reshape(8, n, own), me, 1, keepdims=False)
    ub_mine = lax.dynamic_index_in_dim(total[8:12].reshape(n, -1), me, 0, keepdims=False)
    return (layer_out, gtok, mine[0], mine[1], gq, mine[2], gk, gv, mine[3], go, mine[4], mine[5], mine[6],
            gup, ub_mine, gdown, mine[7])


def solution(mesh):
    rows = P(("dp", "fsdp"), None)
    mat = P("fsdp", None)
    vec = P("fsdp")
    return jax.shard_map(
        functools.partial(on_device, (mesh.shape["dp"], mesh.shape["fsdp"])),
        mesh=mesh,
        in_specs=(rows, rows, rows, vec, vec, mat, vec, mat, mat, vec, mat, vec, vec, vec, mat, vec, mat, vec),
        out_specs=(rows, rows, vec, vec, mat, vec, mat, mat, vec, mat, vec, vec, vec, mat, vec, mat, vec),
        check_vma=False,
    )
```

```python
import functools
import math

import jax
import jax.numpy as jnp
from jax import lax
from jax.experimental import pallas as pl
from jax.experimental.pallas import tpu as pltpu
from jax.sharding import PartitionSpec as P

EPS = 1e-06
NT = (((1,), (1,)), ((), ()))
TN = (((0,), (0,)), ((), ()))


SMALL_ROWS=197; LARGE_ROWS=325
QB=256
NEG=-1e30

def image_ends(small, large, rows):
    ends=[]
    for i in range(1, rows//SMALL_ROWS+1):
        e = jnp.minimum(i, small)*SMALL_ROWS + jnp.maximum(i-small,0)*LARGE_ROWS
        ends.append(jnp.where(i<=small+large, e, 2*rows))
    return ends

def image_of(places, ends):
    idx = jnp.zeros(places.shape, jnp.int32)
    for e in ends:
        idx = idx + (places>=e).astype(jnp.int32)
    return idx


f32=jnp.float32; bf16=jnp.bfloat16
RB=256
INV_SQRT2=1/math.sqrt(2.0); INV_SQRT2PI=1/math.sqrt(2*math.pi)

def dot(a,b): return jnp.dot(a,b,preferred_element_type=f32)
def dot_nt(a,b): return lax.dot_general(a,b,NT,preferred_element_type=f32)
def dot_tn(a,b): return lax.dot_general(a,b,TN,preferred_element_type=f32)

def norm_parts(x):
    mean=jnp.mean(x,axis=-1,keepdims=True)
    cen=x-mean
    var=jnp.mean(cen*cen,axis=-1,keepdims=True)
    q=lax.rsqrt(var+EPS)
    return cen*q, q

def live_mask(counts_ref, first, n):
    end=counts_ref[0]*197+counts_ref[1]*325
    r=first+lax.broadcasted_iota(jnp.int32,(n,1),0)
    return r<end


MESH = pl.DeviceIdType.MESH


class Place:
    def __init__(self, dp_total, fsdp_total):
        half = fsdp_total // 2
        self.outer_total = 4
        self.inner_total = half // 4
        assert half % 4 == 0
        self.pairs = dp_total // 2
        self.d = lax.axis_index("dp")
        self.f = lax.axis_index("fsdp")
        self.core = self.f % 2
        self.inner = (self.f // 2) % self.inner_total
        self.outer = self.f // (2 * self.inner_total)
        self.side = self.d % 2
        self.twin = self.d + 1 - 2 * self.side
        self.flip = self.outer // 2
        self.mirror = self.unmirror(self.outer)

        B = self.inner_total
        self.outers = [self.outer] + [(self.outer + s) % 4 for s in range(1, 4)]
        self.inners = [self.inner] + [(self.inner + t) % B for t in range(1, B)]
        self.cores = [self.core, 1 - self.core]
        self.ends = [self.unmirror(0), self.unmirror(1), self.unmirror(2)]
        self.next_outer = self.unmirror(1 - self.mirror)
        self.arrivals = [self.outer, self.next_outer, self.ends[2], self.unmirror(3)]
        self.outer_devices = [self.device(o, self.inner, self.core) for o in self.outers]
        self.inner_devices = [self.device(self.outer, i, self.core) for i in self.inners]
        self.core_device = self.device(self.outer, self.inner, self.cores[1])
        self.twin_device = (self.twin, self.f)
        self.pair_devices = [(self.d, self.f)] + [(self.side + 2 * ((self.d // 2 + k) % self.pairs), self.f)
                                                  for k in range(1, self.pairs)]

    def unmirror(self, at):
        return at + self.flip * (3 - 2 * at)

    def device(self, outer, inner, core):
        return (self.d, (outer * self.inner_total + inner) * 2 + core)

    def at_outer(self, outer):
        return self.device(outer, self.inner, self.core)

    def at_inner(self, t):
        return self.inner_devices[t % self.inner_total]

    def other_core(self):
        return self.core_device

    def at_twin(self):
        return self.twin_device

    def me(self):
        return (self.d, self.f)

    def at_pair(self, k):
        return self.pair_devices[k % self.pairs]

    def neighbours(self, pairs=False):
        out = self.outer_devices[1:]
        out += [self.at_inner(t) for t in range(1, self.inner_total)]
        out += [self.at_twin(), self.other_core()]
        if pairs:
            out = self.outer_devices[1:] + Total.near_devices(self)
            out += [self.at_pair(k) for k in range(1, self.pairs)]
        return out


def greet(others):
    barrier = pltpu.get_barrier_semaphore()
    for other in others:
        pl.semaphore_signal(barrier, inc=1, device_id=other, device_id_type=MESH)
    pl.semaphore_wait(barrier, len(others))


class Gather:
    def __init__(self, place, ref, edge, sems, base):
        self.place, self.ref, self.edge = place, ref, edge
        self.rows = ref.shape[-2]
        self.send_sem, self.recv_sem = sems
        self.base = base
        A, B = place.outer_total, place.inner_total
        keys = [("z", s) for s in range(1, A)] + [("Z", s) for s in range(1, A)]
        keys += [("x", s, t) for s in range(A) for t in range(1, B)]
        keys += [("y", t) for t in range(B)]
        keys += [("c",)]
        self.keys = {key: i for i, key in enumerate(keys)}
        self.sent = []
        self.sent_inside = []

    @staticmethod
    def count(B):
        return 6 + 4 * (B - 1) + B + 1

    def rows_of(self, kind):
        e, r, p = self.edge, self.rows, self.place.side
        if not e or kind == "all":
            return pl.ds(0, r)
        start, size = {"plane": (p * e, r - e), "mine": (p * (r - e), e), "theirs": ((1 - p) * (r - e), e)}[kind]
        return pl.ds(pl.multiple_of(start, 8), size)

    def part(self, outer, inner, core, kind):
        return self.ref.at[outer, inner, core, self.rows_of(kind)]

    def copy(self, key, ref, to):
        i = self.base + self.keys[key]
        into = i
        if key[0] == "Z":
            into = self.base + self.keys["z", 2 if key[1] == 2 else 3]
        return pltpu.make_async_remote_copy(src_ref=ref, dst_ref=ref, send_sem=self.send_sem.at[i],
                                            recv_sem=self.recv_sem.at[into], device_id=to, device_id_type=MESH)

    def send(self, key, make):
        self.copy(key, *make()).start()
        self.sent.append((key, make))

    def send_inside(self, key, make):
        @pl.when(self.place.mirror == 1)
        def _():
            self.copy(key, *make()).start()

        self.sent_inside.append((key, make))

    def got(self, key, ref):
        self.copy(key, ref, self.place.me()).wait_recv()

    def outer_of(self, step):
        return self.place.arrivals[step]

    def own_line(self, step):
        p = self.place
        return self.part(self.outer_of(step), p.inner, p.core, "plane")

    def start(self):
        p = self.place
        self.send(("z", 1), lambda: (self.own_line(0), p.at_outer(p.next_outer)))
        self.send_inside(("z", 2), lambda: (self.own_line(0), p.at_outer(p.ends[2])))
        self.pass_inner(0)

    def pass_inner(self, step):
        p = self.place
        for t in range(1, p.inner_total):
            self.send(("x", step, t), lambda t=t: (self.own_line(step), p.at_inner(-t)))

    def onward(self, step):
        p = self.place
        return self.own_line(step), p.at_outer(p.ends[2 if step == 1 else 0])

    def arrived(self, step, record):
        self.got(("z", step), self.own_line(step))
        kept = list(self.sent)
        self.pass_inner(step)
        if step == 3:
            self.pass_twin(0)
        if not record:
            self.sent = kept

    def from_next(self):
        self.arrived(1, True)
        self.send_inside(("Z", 1), functools.partial(self.onward, 1))

    def relay(self, step):
        @pl.when(self.place.mirror == 1)
        def _():
            self.got(("z", step), self.own_line(step))
            self.copy(("Z", step), *self.onward(step)).start()
            kept = list(self.sent)
            self.pass_inner(step)
            if step == 3:
                self.pass_twin(0)
            self.sent = kept

        self.sent_inside.append((("Z", step), functools.partial(self.onward, step)))

    def take(self, step):
        @pl.when(self.place.mirror == 0)
        def _():
            self.arrived(step, False)

        for t in range(1, self.place.inner_total):
            self.sent.append((("x", step, t), lambda t=t: (self.own_line(step), self.place.at_inner(-t))))
        if step == 3 and self.edge:
            self.sent.append((("y", 0), lambda: (self.line(0, "mine"), self.place.at_twin())))

    def relay_2(self):
        self.relay(2)

    def relay_3(self):
        self.relay(3)

    def take_2(self):
        self.take(2)

    def take_3(self):
        self.take(3)

    def line(self, t, kind):
        p = self.place
        return self.part(slice(None), p.inners[t], p.core, kind)

    def pass_twin(self, t):
        if self.edge:
            self.send(("y", t), lambda: (self.line(t, "mine"), self.place.at_twin()))

    def from_inner(self):
        p = self.place
        for t in range(1, p.inner_total):
            for step in range(4):
                self.got(("x", step, t), self.part(self.outer_of(step), p.inners[t], p.core, "plane"))
            self.pass_twin(t)

    def half(self, core):
        return self.part(slice(None), slice(None), core, "all")

    def from_twin(self):
        p = self.place
        if self.edge:
            for t in range(p.inner_total):
                self.got(("y", t), self.line(t, "theirs"))
        self.send(("c",), lambda: (self.half(p.core), p.other_core()))

    def from_core(self):
        self.got(("c",), self.half(self.place.cores[1]))

    def finish(self):
        for key, make in self.sent:
            self.copy(key, *make()).wait_send()

        @pl.when(self.place.mirror == 1)
        def _():
            for key, make in self.sent_inside:
                self.copy(key, *make()).wait_send()


class Scatter:
    def __init__(self, place, terms, bufs, edge, emit, sems, base):
        self.place, self.terms, self.edge, self.emit = place, terms, edge, emit
        self.sums, self.twin_buf, self.inner_buf, self.outer_buf, self.last_buf = bufs[:5]
        self.pair_bufs = bufs[5:]
        self.send_sem, self.recv_sem = sems
        self.base = base
        p, e, w = place.side, edge, terms.shape[-1]
        at = lambda start, size: pl.ds(pl.multiple_of(start, 128), size)
        self.plane = at(p * e, w - e)
        self.mine = at(p * (w - e), e)
        self.theirs = at((1 - p) * (w - e), e)
        self.twin_plane = at((1 - p) * e, w - e)
        self.middle = pl.ds(e, w - 2 * e)

    @staticmethod
    def count(B, pairs):
        return 1 + 1 + (B - 1) + 3 + 1 + (pairs - 1)

    @staticmethod
    def shapes(B, pairs, rows, width, edge, lead=()):
        out = [(4, B, rows, width), (4, B, rows, edge), (B - 1, 4, rows, width), (3, rows, width), (rows, width)]
        if pairs > 1:
            out += [(rows, width), (pairs - 1, rows, width)]
        return [pltpu.VMEM(tuple(lead) + s, bf16) for s in out]

    def copy(self, i, src, dst, to):
        return pltpu.make_async_remote_copy(src_ref=src, dst_ref=dst, send_sem=self.send_sem.at[self.base + i],
                                            recv_sem=self.recv_sem.at[self.base + i], device_id=to, device_id_type=MESH)

    def copies(self, stage):
        p = self.place
        A, B = 4, p.inner_total
        if stage == "core":
            return [self.copy(0, self.terms.at[:, :, p.cores[1]], self.sums, p.other_core())]
        if stage == "twin":
            return [self.copy(1, self.sums.at[:, :, :, self.theirs], self.twin_buf, p.at_twin())]
        if stage == "inner":
            return [self.copy(1 + t, self.sums.at[:, p.inners[(B - t) % B], :, self.plane],
                              self.inner_buf.at[t - 1, :, :, self.plane], p.at_inner(-t)) for t in range(1, B)]
        if stage == "outer":
            return [self.copy(B + s, self.sums.at[p.outers[A - s], p.inner, :, self.plane],
                              self.outer_buf.at[s - 1, :, self.plane], p.outer_devices[A - s])
                    for s in range(1, A)]
        if stage == "last":
            return [self.copy(A + B, self.sums.at[p.outer, p.inner, :, self.plane], self.last_buf.at[:, self.plane],
                              p.at_twin())]
        half, others = self.pair_bufs
        return [self.copy(A + B + k, half, others.at[k - 1], p.at_pair(p.pairs - k)) for k in range(1, p.pairs)]

    def go(self, stage):
        for c in self.copies(stage):
            c.start()

    def got(self, i, dst):
        self.copy(i, dst, dst, self.place.me()).wait_recv()

    def start(self):
        self.go("core")

    def from_core(self):
        p = self.place
        B = p.inner_total
        self.got(0, self.sums)

        def add(i, _):
            a, b = i // B, i % B
            self.sums[a, b] = self.sums[a, b] + self.terms[a, b, p.core]
            return 0

        lax.fori_loop(0, 4 * B, add, 0)
        self.go("twin")

    def from_twin(self):
        p = self.place
        B = p.inner_total
        self.got(1, self.twin_buf)

        def add(i, _):
            a, b = i // B, i % B
            self.sums[a, b, :, self.mine] = self.sums[a, b, :, self.mine] + self.twin_buf[a, b]
            return 0

        lax.fori_loop(0, 4 * B, add, 0)
        self.go("inner")

    def from_inner(self):
        p = self.place
        B = p.inner_total
        for t in range(1, B):
            self.got(1 + t, self.inner_buf.at[t - 1, :, :, self.plane])

        def add(a, _):
            if B == 2:
                self.sums[a, p.inner, :, self.plane] = (self.sums[a, p.inner, :, self.plane]
                                                        + self.inner_buf[0, a, :, self.plane])
                return 0
            total = self.sums[a, p.inner, :, self.plane].astype(f32)
            for t in range(1, B):
                total = total + self.inner_buf[t - 1, a, :, self.plane].astype(f32)
            self.sums[a, p.inner, :, self.plane] = total.astype(bf16)
            return 0

        lax.fori_loop(0, 4, add, 0)
        self.go("outer")

    def from_outer(self):
        p = self.place
        B = p.inner_total
        for s in range(1, 4):
            self.got(B + s, self.outer_buf.at[s - 1, :, self.plane])
        total = self.sums[p.outer, p.inner, :, self.plane].astype(f32)
        for s in range(1, 4):
            total = total + self.outer_buf[s - 1, :, self.plane].astype(f32)
        self.sums[p.outer, p.inner, :, self.plane] = total.astype(bf16)
        self.go("last")

    def from_last(self):
        p = self.place
        self.got(4 + p.inner_total, self.last_buf.at[:, self.twin_plane])
        own = lambda cols: self.sums[p.outer, p.inner, :, cols].astype(f32)
        last = lambda cols: self.last_buf[:, cols].astype(f32)
        if p.pairs == 1:
            self.emit(self.mine, own(self.mine))
            self.emit(self.middle, own(self.middle) + last(self.middle))
            self.emit(self.theirs, last(self.theirs))
            return
        half, others = self.pair_bufs
        half[:, self.mine] = own(self.mine).astype(bf16)
        half[:, self.middle] = (own(self.middle) + last(self.middle)).astype(bf16)
        half[:, self.theirs] = last(self.theirs).astype(bf16)
        self.go("pairs")

    def from_pairs(self):
        p = self.place
        if p.pairs == 1:
            return
        half, others = self.pair_bufs
        total = half[...].astype(f32)
        for k in range(1, p.pairs):
            self.got(4 + p.inner_total + k, others.at[k - 1])
            total = total + others[k - 1].astype(f32)
        self.emit(pl.ds(0, self.terms.shape[-1]), total)

    def finish(self):
        for stage in ("core", "twin", "inner", "outer", "last") + (("pairs",) if self.place.pairs > 1 else ()):
            for c in self.copies(stage):
                c.wait_send()


class Total:
    def __init__(self, place, bufs, out, sems, base):
        self.place, self.landing, self.out = place, bufs[0], out
        self.send_sem, self.recv_sem = sems
        p, B = place, place.inner_total
        near = []
        for side in range(2):
            for t in range(B):
                for core in range(2):
                    if side or t or core:
                        dev = p.device(p.outer, p.inners[t], p.cores[core])[1]
                        near.append((p.d if not side else p.twin, dev))
        self.rounds = [(near, (p.side * B + p.inner) * 2 + p.core, 4 * B),
                       (p.outer_devices[1:], p.outer, 4)]
        if p.pairs > 1:
            self.rounds.append(([p.at_pair(k) for k in range(1, p.pairs)], p.d // 2, p.pairs))
        self.base = base

    @staticmethod
    def near_devices(place):
        return Total(place, [None], None, (None, None), 0).rounds[0][0]

    @staticmethod
    def count(B, pairs):
        return 4 * B + 4 + pairs

    @staticmethod
    def shapes(B, pairs, shape):
        return [pltpu.VMEM((Total.count(B, pairs),) + shape, f32)]

    def first(self, r):
        return sum(x[2] for x in self.rounds[:r])

    def send_copy(self, r, k):
        others, mine, _ = self.rounds[r]
        at = self.landing.at[self.first(r) + mine]
        return pltpu.make_async_remote_copy(src_ref=at, dst_ref=at, send_sem=self.send_sem.at[self.base + self.first(r) + k],
                                            recv_sem=self.recv_sem.at[self.base + self.first(r) + mine],
                                            device_id=others[k], device_id_type=MESH)

    def begin(self, r, value):
        others, mine, _ = self.rounds[r]
        self.landing[self.first(r) + mine] = value
        for k in range(len(others)):
            self.send_copy(r, k).start()

    def start(self, value):
        self.begin(0, value)

    def step(self, r):
        others, mine, members = self.rounds[r]
        for k in range(1, members):
            slot = self.first(r) + (mine + k) % members
            at = self.landing.at[slot]
            pltpu.make_async_remote_copy(src_ref=at, dst_ref=at, send_sem=self.send_sem.at[self.base],
                                         recv_sem=self.recv_sem.at[self.base + slot], device_id=self.place.me(),
                                         device_id_type=MESH).wait_recv()
        total = self.landing[self.first(r)]
        for k in range(1, members):
            total = total + self.landing[self.first(r) + k]
        if r + 1 < len(self.rounds):
            self.begin(r + 1, total)
        else:
            self.out[...] = total

    def steps(self):
        return [functools.partial(self.step, r) for r in range(len(self.rounds))]

    def finish(self):
        for r in range(len(self.rounds)):
            for k in range(len(self.rounds[r][0])):
                self.send_copy(r, k).wait_send()


def local(src, dst, sem):
    c = pltpu.make_async_copy(src, dst, sem)
    c.start()
    return c


def mask_lanes(shape, first, ends, hit, miss):
    lane = lax.broadcasted_iota(jnp.int32, shape, 1)
    image = image_of(first + lax.broadcasted_iota(jnp.int32, shape, 0), ends)
    return jnp.where(image == jnp.where(lane < 64, lane, lane - 64), hit, miss).astype(bf16)


def head_lanes(values, others, e):
    lane = lax.broadcasted_iota(jnp.int32, values.shape, 1)
    return jnp.where((lane < 64) == (e == 0), values, others)


BLOCKS = 3


def lane_tile(source, moves):
    lane = None
    out = None
    for col, to, size in moves:
        tile = source[:, col // 128 * 128:col // 128 * 128 + 128]
        shift = (to - col) % 128
        if shift:
            tile = pltpu.roll(tile, shift, 1)
        if out is None:
            out = tile
            lane = lax.broadcasted_iota(jnp.int32, tile.shape, 1)
        else:
            out = jnp.where((lane >= to) & (lane < to + size), tile, out)
    return out


def split_columns(source, owners):
    piece = source.shape[1] // owners // BLOCKS
    per = 128 // piece
    out = []
    for j in range(BLOCKS):
        tiles = [lane_tile(source, [(((t * per + q) * BLOCKS + j) * piece, q * piece, piece) for q in range(per)])
                 for t in range(owners // per)]
        out.append(jnp.concatenate(tiles, axis=1))
    return out


def join_columns(parts, owners):
    source = jnp.concatenate(parts, axis=1)
    width = parts[0].shape[1]
    piece = width // owners
    per = 128 // piece
    tiles = []
    for t in range(source.shape[1] // 128):
        moves = []
        for q in range(per):
            unit = t * per + q
            moves.append(((unit % BLOCKS) * width + unit // BLOCKS * piece, q * piece, piece))
        tiles.append(lane_tile(source, moves))
    return jnp.concatenate(tiles, axis=1)


PARTS = 3


def attend_block(q_ref, k_ref, v_ref, own_ref, far_ref, mixed_ref, lse_ref, pair, block):
    lane = lax.broadcasted_iota(jnp.int32, (QB, 128), 1)
    first = pl.multiple_of(block * QB, QB)
    cols = pl.ds(pl.multiple_of(pair * 128, 128), 128)
    q = q_ref[pl.ds(first, QB), cols]
    k = k_ref[:, cols]
    v = v_ref[:, cols]
    outs = []
    lses = []
    for e in range(2):
        s = dot_nt(head_lanes(q, own_ref[pl.ds(first, QB), :], e), head_lanes(k, far_ref[...], e))
        m = jnp.max(s, axis=1, keepdims=True)
        p = jnp.exp(s - m)
        l = jnp.sum(p, axis=1, keepdims=True)
        o = dot(p.astype(bf16), v)
        outs.append(o * (1.0 / l))
        lses.append(m + jnp.log(l))
    mixed_ref[pl.ds(first, QB), cols] = jnp.where(lane < 64, outs[0], outs[1]).astype(bf16)
    both = jnp.where(lane < 64, jnp.broadcast_to(lses[0], (QB, 128)), jnp.broadcast_to(lses[1], (QB, 128)))
    t = both.T
    lse_ref[pair, 0:1, pl.ds(first, QB)] = t[0:1, :]
    lse_ref[pair, 1:2, pl.ds(first, QB)] = t[64:65, :]


def gather_edge(rows, last=False):
    return rows // 3 if rows % 24 == 0 else rows // 4 if last or rows < 64 else rows * 3 // 8


def gather_plan(units, early, pieces):
    n = len(units)
    slots = [[] for _ in range(n + 12)]
    for t, u in enumerate(units):
        if t >= 3:
            slots[t - 2].append(u.start)
    for t, u in enumerate(units):
        inner, twin, core = (4, 5, 6) if t <= early else (5, 7, 9) if t <= PARTS else (5, 7, 9)
        stages = [(0, u.from_next), (1, u.relay_2), (2, u.relay_3), (2, u.take_2), (3, u.take_3),
                  (inner, u.from_inner), (twin, u.from_twin), (core, u.from_core)]
        for at, one in stages:
            slots[t + at].append(one)
    cut = early + 7
    rest = slots[cut:]
    while not rest[-1]:
        rest.pop()
    places = [[] for _ in range(pieces)]
    for k, slot in enumerate(rest):
        places[k * pieces // len(rest)] += slot
    for t in range(2, PARTS + 1):
        assert any(units[t].from_core in place for place in places[:(t - 1) * pieces // PARTS])
    return [one for slot in slots[:cut] for one in slot], places


def gather_kernel(dp_total, n, counts_ref, tokens_hbm, small_ref, qo_ref, ko_ref, vo_ref, oo_ref, uo_ref, do_ref,
                  q_hbm, k_hbm, v_hbm, vec_ref, mixed_hbm, lse_ref, qkv_all, o_all, up_all, down_all, small_all,
                  tokens_s, fi_s, own_s, far_s, q_s, k_s, v_s, mixed_s, w_s, small_s, up_own, send_sem, recv_sem, loc_sem, out_sem):
    place = Place(dp_total, n)
    B = place.inner_total
    own = qo_ref.shape[0]
    piece = do_ref.shape[0] // BLOCKS
    greet(place.neighbours())
    take_tokens = local(tokens_hbm, tokens_s, loc_sem.at[0])
    sems = (send_sem, recv_sem)
    refs = [(small_all, 0)] + [(qkv_all.at[j], own) for j in range(PARTS)] + [(o_all, gather_edge(own))]
    for j in range(BLOCKS):
        refs += [(up_all.at[j], gather_edge(own)), (down_all.at[j], gather_edge(piece, j == BLOCKS - 1))]
    units = [Gather(place, ref, edge, sems, i * Gather.count(B))
             for i, (ref, edge) in enumerate(refs)]
    mine = lambda unit: unit.part(place.outer, place.inner, place.core, "plane")
    block = qkv_all.shape[-1]

    def own_part(source, j, i):
        return local(source.at[:, pl.ds(j * block, block)],
                     qkv_all.at[j, place.outer, place.inner, place.core, pl.ds(i * own, own)], loc_sem.at[2 + 2 * j + i % 2])

    fill = [local(small_ref, mine(units[0]), loc_sem.at[1])] + [own_part(ko_ref, j, 1) for j in range(PARTS)]

    @pl.when(place.side == 0)
    def _():
        for c in [own_part(qo_ref, j, 0) for j in range(PARTS)]:
            c.wait()

    @pl.when(place.side == 1)
    def _():
        for c in [own_part(vo_ref, j, 2) for j in range(PARTS)]:
            c.wait()

    for c in fill:
        c.wait()
    units[0].start()
    units[1].start()
    for j, part in enumerate(split_columns(uo_ref[...].astype(f32), n)):
        up_own[j] = part.astype(bf16)
    base = 1 + PARTS
    fill = [local(oo_ref.at[units[base].rows_of("plane")], mine(units[base]), loc_sem.at[1])]
    for j in range(BLOCKS):
        a, b = units[base + 1 + 2 * j], units[base + 2 + 2 * j]
        fill.append(local(up_own.at[j, a.rows_of("plane")], mine(a), loc_sem.at[2 + 2 * j]))
        rows = b.rows_of("plane")
        fill.append(local(do_ref.at[pl.ds(pl.multiple_of(j * piece + rows.start, 8), rows.size)], mine(b),
                          loc_sem.at[3 + 2 * j]))
    for c in fill:
        c.wait()
    units[2].start()

    def vectors():
        local(small_all, small_s, loc_sem.at[1]).wait()
        total = jnp.zeros(vec_ref.shape, f32)
        for i in range(n):
            total = total + small_s[i // (2 * B), i // 2 % B, i % 2].astype(f32)
        vec_ref[...] = total

    rows, feat = tokens_s.shape
    blocks = rows // QB
    per = qkv_all.shape[-1] // 128 * blocks
    pieces = PARTS * per
    head, rest = gather_plan(units, 1, pieces)
    for one in head:
        one()
    weight_load = lambda j: pltpu.make_async_copy(qkv_all.at[j], w_s.at[j], loc_sem.at[2 + j])
    weight_load(0).start()
    vectors()
    take_tokens.wait()

    ends = image_ends(counts_ref[0], counts_ref[1], rows)

    def norm_rows(i, _):
        first = pl.multiple_of(i * RB, RB)
        sl = pl.ds(first, RB)
        own_s[sl, :] = mask_lanes((RB, 128), first, ends, 1.0, 0.0)
        far_s[sl, :] = mask_lanes((RB, 128), first, ends, 0.0, NEG)
        xhat, _q = norm_parts(tokens_s[sl, :].astype(f32))
        fi_s[sl, :] = (xhat * vec_ref[0:1, :] + vec_ref[1:2, :]).astype(bf16)
        return 0

    lax.fori_loop(0, rows // RB, norm_rows, 0)
    def project(j):
        cols = pl.ds(pl.multiple_of(j * block, 128), block)
        weight_load(j).wait()

        def project_rows(i, _):
            sl = pl.ds(pl.multiple_of(i * RB, RB), RB)
            fi = fi_s[sl, :]
            weight = lambda i: w_s[j, :, :, :, i * own:(i + 1) * own, :].reshape(feat, block)
            q_s[sl, cols] = ((dot(fi, weight(0)) + vec_ref[2:3, cols]).astype(bf16).astype(f32) * 0.125).astype(bf16)
            k_s[sl, cols] = dot(fi, weight(1)).astype(bf16)
            v_s[sl, cols] = (dot(fi, weight(2)) + vec_ref[3:4, cols]).astype(bf16)
            return 0

        lax.fori_loop(0, rows // RB, project_rows, 0)
        for c in out_copies(j)[:3]:
            c.start()

    def out_copies(j):
        cols = pl.ds(pl.multiple_of(j * block, 128), block)
        return [pltpu.make_async_copy(a.at[:, cols], b.at[:, cols], out_sem.at[4 * j + i])
                for i, (a, b) in enumerate(((q_s, q_hbm), (k_s, k_hbm), (v_s, v_hbm), (mixed_s, mixed_hbm)))]

    def attend_piece(i, _):
        @pl.when(i % per == 0)
        def _():
            project(i // per)

        attend_block(q_s, k_s, v_s, own_s, far_s, mixed_s, lse_ref, i // blocks, i % blocks)
        for at, todo in enumerate(rest):
            if todo:
                @pl.when(i == at)
                def _(todo=todo):
                    for one in todo:
                        one()

        @pl.when(i % per == per - 1)
        def _():
            out_copies(i // per)[3].start()

        @pl.when((i % per == per - 1) & (i < pieces - 1))
        def _():
            weight_load(i // per + 1).start()

        return 0

    lax.fori_loop(0, pieces, attend_piece, 0)
    for j in range(PARTS):
        for c in out_copies(j):
            c.wait()
    for x in units:
        x.finish()


def gather_attend(sizes, counts, tokens, small, qw, kw, vw, ow, up, down):
    dp_total, n = sizes
    rows, feat = tokens.shape
    own = qw.shape[0]
    B = n // 8
    pairs = feat // 128
    s = jax.ShapeDtypeStruct
    vm = pl.BlockSpec(memory_space=pltpu.VMEM)
    anyspec = pl.BlockSpec(memory_space=pl.ANY)
    full = lambda *dims: (4, B, 2) + dims
    width = up.shape[1] // BLOCKS
    piece = down.shape[0] // BLOCKS
    act = s((rows, feat), bf16)
    copies = (2 + PARTS + 2 * BLOCKS) * Gather.count(B)
    return pl.pallas_call(
        functools.partial(gather_kernel, dp_total, n),
        in_specs=[pl.BlockSpec(memory_space=pltpu.SMEM), anyspec] + [vm] * 7,
        out_specs=[anyspec] * 3 + [vm, anyspec, vm] + [anyspec] * 5,
        out_shape=[act, act, act, s(small.shape, f32), act, s((pairs, 2, rows), f32), s((PARTS,) + full(3 * own, feat // PARTS), bf16),
                   s(full(own, feat), bf16), s((BLOCKS,) + full(own, width), bf16),
                   s((BLOCKS,) + full(piece, feat), bf16), s(full(*small.shape), bf16)],
        scratch_shapes=[pltpu.VMEM((rows, feat), bf16)] * 2 + [pltpu.VMEM((rows, 128), bf16)] * 2 + [
            pltpu.VMEM((rows, feat), bf16)] * 4 + [
            pltpu.VMEM((PARTS,) + full(3 * own, feat // PARTS), bf16), pltpu.VMEM(full(*small.shape), bf16),
            pltpu.VMEM((BLOCKS, own, width), bf16), pltpu.SemaphoreType.DMA((copies,)),
            pltpu.SemaphoreType.DMA((copies,)), pltpu.SemaphoreType.DMA((6 + 2 * BLOCKS,)),
            pltpu.SemaphoreType.DMA((4 * PARTS,))],
        compiler_params=pltpu.CompilerParams(collective_id=1, has_side_effects=True, vmem_limit_bytes=60 * 2**20),
        name="gather_attend",
    )(counts, tokens, small, qw, kw, vw, ow, up, down)


def scatter_edge(width):
    return 128 if width == 768 else width // 4 if width % 512 == 0 else width // 3


def layer_kernel(dp_total, n, counts_ref, mixed_hbm, tokens_ref, cot_hbm, outw_ref, vec_ref, lse_ref, up_hbm, down_hbm,
                 q_hbm, k_hbm, v_hbm, qkv_all,
                 layer_ref, gtok_ref, gup_ref, gdown_ref, gq_ref, gk_ref, gv_ref, go_ref, total_ref,
                 res_s, si_s, gb_s, mixed_s, hid_s, gi_s, up_s, down_s, kt_s, own_s, far_s, ub_s, gub_s, gqkv_s, small_s, *rest):
    rows, feat = tokens_ref.shape
    width = gi_s.shape[1]
    own = gq_ref.shape[0]
    piece = gdown_ref.shape[0] // BLOCKS
    heads = feat // 128
    place = Place(dp_total, n)
    B, pairs = place.inner_total, place.pairs
    per = 5 if pairs == 1 else 7
    uterm_s, dterm_s = rest[:2]
    ubufs, dbufs, obufs, abufs = (rest[2 + i * per:2 + (i + 1) * per] for i in range(4))
    total_bufs = rest[2 + 4 * per:3 + 4 * per]
    send_sem, recv_sem, loc_sem, weight_sem = rest[3 + 4 * per:]
    sems = (send_sem, recv_sem)
    count = Scatter.count(B, pairs)
    wide = lambda start: pl.ds(start, feat)
    load = lambda j: (pltpu.make_async_copy(up_hbm.at[j], up_s.at[j], loc_sem.at[2 * j]),
                      pltpu.make_async_copy(down_hbm.at[j], down_s.at[j], loc_sem.at[2 * j + 1]))
    at_end = 3 * feat
    first_loads = [local(mixed_hbm, mixed_s, loc_sem.at[2 * BLOCKS]),
                   local(cot_hbm, hid_s.at[:, wide(at_end)], loc_sem.at[2 * BLOCKS + 1])]
    for j in range(BLOCKS):
        for c in load(j):
            c.start()
    def unit_u(j):
        def emit(cols, value):
            gup_ref[:, pl.ds(pl.multiple_of(j * width + cols.start, 128), cols.size)] = value
        return Scatter(place, uterm_s.at[j % 2], [b.at[j] for b in ubufs], scatter_edge(width), emit, sems,
                       2 * j * count)

    def unit_d(j):
        def emit(cols, value):
            gdown_ref[pl.ds(pl.multiple_of(j * piece, 8), piece), cols] = value
        return Scatter(place, dterm_s.at[j % 2], [b.at[j] for b in dbufs], scatter_edge(feat), emit, sems,
                       (2 * j + 1) * count)

    def emit_out(cols, value):
        go_ref[:, cols] = value

    unit_o = Scatter(place, uterm_s.at[1, :, :, :, :, wide(0)], obufs, 256, emit_out, sems, 2 * BLOCKS * count)

    def pair_term(p):
        return dterm_s.at[1, :, :, :, pl.ds(0, own), pl.ds(pl.multiple_of(p % 2 * 384, 128), 384)]

    def unit_a(p):
        def emit(cols, value):
            gqkv_s[p, :, cols] = value
        return Scatter(place, pair_term(p), [b.at[p] for b in abufs], 128, emit, sems,
                       (2 * BLOCKS + 1 + p) * count)

    small = Total(place, total_bufs, total_ref, sems, (2 * BLOCKS + 1 + heads) * count)

    def last(unit):
        unit.from_last()
        unit.from_pairs()

    def sent(unit, *stages):
        for stage in stages:
            for c in unit.copies(stage):
                c.wait_send()

    rest_stages = ("twin", "inner", "outer", "last") + (("pairs",) if pairs > 1 else ())
    gain_one, shift_one = vec_ref[0:1, :], vec_ref[1:2, :]
    obias, gain, shift, dbias = (vec_ref[i:i + 1, :] for i in range(4, 8))
    ub = jnp.concatenate([vec_ref[8 + i:9 + i, :] for i in range(BLOCKS * width // feat)], axis=1)
    for j, part in enumerate(split_columns(jnp.broadcast_to(ub, (8, ub.shape[1])), n)):
        ub_s[j] = part
    small_s[...] = jnp.zeros_like(small_s)
    for c in first_loads:
        c.wait()

    def begin(i, _):
        first = pl.multiple_of(i * RB, RB)
        sl = pl.ds(first, RB)
        res = tokens_ref[sl, :].astype(f32) + (dot(mixed_s[sl, :], outw_ref[...]) + obias)
        res_s[sl, :] = res
        xhat, _q = norm_parts(res)
        si_s[sl, :] = (xhat * gain + shift).astype(bf16)
        gb_s[sl, :] = jnp.where(live_mask(counts_ref, first, RB), hid_s[sl, wide(at_end)], jnp.zeros((), bf16))
        gtok_ref[sl, :] = jnp.zeros((RB, feat), f32)
        return 0

    lax.fori_loop(0, rows // RB, begin, 0)
    greet(place.neighbours(pairs=True))

    def block(j, _):
        for c in load(j):
            c.wait()
        upw = lambda: up_s[j].reshape(feat, width)
        downw = lambda: down_s[j].reshape(width, feat)
        cols = pl.ds(pl.multiple_of(j * width, 128), width)
        gub_s[j] = jnp.zeros(gub_s.shape[1:], f32)

        def after(back, when, todo):
            @pl.when(when & (j >= back))
            def _():
                todo(j - back)

        def rows_piece(i, _):
            sl = pl.ds(pl.multiple_of(i * RB, RB), RB)
            pre = dot(si_s[sl, :], upw()) + ub_s[j, 0:1, :]
            cdf = 0.5 + 0.5 * lax.erf(pre * INV_SQRT2)
            pdf = jnp.exp(-0.5 * pre * pre) * INV_SQRT2PI
            hid_s[sl, cols] = (pre * cdf).astype(bf16)
            gi = (dot_nt(gb_s[sl, :], downw()) * (cdf + pre * pdf)).astype(bf16)
            gi_s[sl, :] = gi
            gub_s[j, 0:1, :] += jnp.sum(gi.astype(f32), axis=0, keepdims=True)
            after(1, i == 0, lambda k: unit_d(k).from_core())
            after(1, i == 1, lambda k: unit_u(k).from_core())
            after(2, i == 1, lambda k: unit_d(k).from_inner())
            after(1, i == 3, lambda k: unit_d(k).from_twin())
            return 0

        lax.fori_loop(0, rows // RB, rows_piece, 0)
        always = j >= 0
        after(2, always, lambda k: (sent(unit_u(k), "core"), sent(unit_d(k), "core")))
        dterm_s[j % 2] = dot_tn(hid_s[:, cols], gb_s[...]).astype(bf16).reshape(dterm_s.shape[1:])
        unit_d(j).start()
        after(1, always, lambda k: unit_u(k).from_twin())
        after(2, always, lambda k: unit_u(k).from_inner())
        uterm_s[j % 2] = dot_tn(si_s[...], gi_s[...]).astype(bf16).reshape(uterm_s.shape[1:])
        unit_u(j).start()
        gtok_ref[...] += dot_nt(gi_s[...], upw())
        return 0

    lax.fori_loop(0, BLOCKS, block, 0)
    end, before = BLOCKS - 1, BLOCKS - 2
    third = qkv_all.shape[-1]
    weights = [local(qkv_all.at[j, :, :, :, pl.ds(i * own, own)], up_s.at[i, :, :, :, :, pl.ds(j * third, third)],
                     weight_sem.at[i * PARTS + j]) for i in range(3) for j in range(PARTS)]

    def finish_rows(i, _):
        first = pl.multiple_of(i * RB, RB)
        sl = pl.ds(first, RB)
        res = res_s[sl, :]
        layer = res + (dot(hid_s[sl, :], down_s[...].reshape(BLOCKS * width, feat)) + dbias)
        layer_ref[sl, :] = jnp.where(live_mask(counts_ref, first, RB), layer, 0.0).astype(bf16)
        xhat, q = norm_parts(res)
        gs = gtok_ref[sl, :]
        t = gs * gain
        gb = gb_s[sl, :].astype(f32)
        gres = gb + q * (t - jnp.mean(t, axis=-1, keepdims=True) - xhat * jnp.mean(t * xhat, axis=-1, keepdims=True))
        gtok_ref[sl, :] = gres
        ga = gres.astype(bf16)
        si_s[sl, :] = ga
        small_s[7:8, :] += jnp.sum(gb, axis=0, keepdims=True)
        small_s[5:6, :] += jnp.sum(gs * xhat, axis=0, keepdims=True)
        small_s[6:7, :] += jnp.sum(gs, axis=0, keepdims=True)
        small_s[4:5, :] += jnp.sum(ga.astype(f32), axis=0, keepdims=True)
        hid_s[sl, wide(at_end)] = dot_nt(ga, outw_ref[...]).astype(bf16)

        def at(k, *todo):
            @pl.when(i == k)
            def _():
                for one in todo:
                    one()

        at(0, lambda: unit_d(end).from_core(), lambda: unit_d(0).from_outer())
        at(1, lambda: unit_u(end).from_core(), lambda: unit_d(before).from_inner())
        at(2, lambda: unit_u(0).from_outer())
        at(3, lambda: unit_d(end).from_twin())
        return 0

    lax.fori_loop(0, rows // RB, finish_rows, 0)
    take = [local(x, hid_s.at[:, wide(i * feat)], loc_sem.at[3 + i]) for i, x in enumerate((q_hbm, k_hbm, v_hbm))]
    sent(unit_u(before), "core")
    sent(unit_d(before), "core")
    unit_o.terms[...] = dot_tn(mixed_s[...], si_s[...]).astype(bf16).reshape(unit_o.terms.shape)
    unit_o.start()
    unit_u(end).from_twin()
    unit_u(before).from_inner()
    gub = join_columns([gub_s[j] for j in range(BLOCKS)], n)
    for i in range(gub.shape[1] // feat):
        small_s[8 + i:9 + i, :] = gub[0:1, i * feat:(i + 1) * feat]

    ends = image_ends(counts_ref[0], counts_ref[1], rows)

    def norm_rows(i, _):
        first = pl.multiple_of(i * RB, RB)
        sl = pl.ds(first, RB)
        own_s[sl, :] = mask_lanes((RB, 128), first, ends, 1.0, 0.0)
        far_s[sl, :] = mask_lanes((RB, 128), first, ends, 0.0, NEG)
        xhat, _q = norm_parts(tokens_ref[sl, :].astype(f32))
        gi_s[sl, wide(0)] = (xhat * gain_one + shift_one).astype(bf16)
        return 0

    lax.fori_loop(0, rows // RB, norm_rows, 0)
    for c in take:
        c.wait()
    key_at = lambda e: pl.ds(feat + e * 128, 128)
    dk_at, dv_at = pl.ds(0, 128), pl.ds(128, 128)

    def pair(p, _):
        part = lambda which: pl.ds(pl.multiple_of(which * feat + p * 128, 128), 128)
        cols = part(0)
        keys = hid_s[:, part(1)]
        for e in range(2):
            gi_s[:, key_at(e)] = head_lanes(keys, far_s[...], e)
        kt_s[...] = keys.T
        res_s[:, pl.ds(0, 256)] = jnp.zeros((rows, 256), f32)

        def attend_back(b, _):
            first = pl.multiple_of(b * QB, QB)
            sl = pl.ds(first, QB)
            q, do = hid_s[sl, part(0)], hid_s[sl, part(3)]
            v = hid_s[:, part(2)]
            lane = lax.broadcasted_iota(jnp.int32, q.shape, 1)
            zero = jnp.zeros_like(q)
            dqs = []
            dks = dvs = None
            for e in range(2):
                mask = (lane < 64) == (e == 0)
                qm, dom = jnp.where(mask, q, zero), jnp.where(mask, do, zero)
                s = dot_nt(gi_s[:, key_at(e)], head_lanes(q, own_s[sl, :], e))
                probs = jnp.exp(s - lse_ref[p, e:e + 1, sl])
                dp = dot_nt(v, dom)
                centre = jnp.sum(probs * dp, axis=0, keepdims=True)
                ds = (probs * (dp - centre)).astype(bf16)
                dv_e = dot(probs.astype(bf16), dom)
                dk_e = dot(ds, qm)
                dqs.append(dot(kt_s[e * 64:(e + 1) * 64, :], ds))
                dvs = dv_e if dvs is None else dvs + dv_e
                dks = dk_e if dks is None else dks + dk_e
            res_s[:, dk_at] += dks
            res_s[:, dv_at] += dvs
            gb_s[sl, cols] = (jnp.concatenate(dqs, axis=0).T * 0.125).astype(bf16)

            def at(k, when, todo):
                @pl.when((b == k) & when)
                def _():
                    todo()

            at(0, p == 0, lambda: last(unit_d(0)))
            at(1, p == 0, lambda: (unit_o.from_core(), last(unit_u(0))))
            at(2, p == 0, lambda: unit_d(before).from_outer())
            at(3, p == 0, lambda: (unit_u(before).from_outer(), unit_d(end).from_inner()))
            at(0, p == 1, lambda: unit_o.from_twin())
            at(1, p == 1, lambda: (last(unit_d(before)), unit_u(end).from_inner()))
            at(2, p == 1, lambda: last(unit_u(before)))
            at(3, p == 1, lambda: unit_o.from_inner())
            at(0, p == 2, lambda: unit_d(end).from_outer())
            at(2, p == 2, lambda: unit_u(end).from_outer())
            at(3, p == 2, lambda: (last(unit_d(end)), unit_o.from_outer()))
            at(0, p == 3, lambda: last(unit_u(end)))
            at(2, p == 3, lambda: last(unit_o))
            at(1, p >= 1, lambda: unit_a(p - 1).from_core())
            at(3, p >= 1, lambda: unit_a(p - 1).from_twin())
            at(1, p >= 2, lambda: unit_a(p - 2).from_inner())
            at(0, p >= 3, lambda: unit_a(p - 3).from_outer())
            at(2, p >= 3, lambda: last(unit_a(p - 3)))
            return 0

        lax.fori_loop(0, rows // QB, attend_back, 0)
        dk, dv = res_s[:, dk_at].astype(bf16), res_s[:, dv_at].astype(bf16)
        mixed_s[:, cols] = dk
        si_s[:, cols] = dv
        both = jnp.concatenate([gb_s[:, cols], dk, dv], axis=1)

        @pl.when(p >= 2)
        def _():
            sent(unit_a(p - 2), "core")

        term = pair_term(p)
        term[...] = dot_tn(gi_s[:, wide(0)], both).astype(bf16).reshape(term.shape)
        unit_a(p).start()
        return 0

    lax.fori_loop(0, heads, pair, 0)
    for c in weights:
        c.wait()

    def back_rows(i, _):
        sl = pl.ds(pl.multiple_of(i * RB, RB), RB)
        dq, dk, dv = gb_s[sl, :], mixed_s[sl, :], si_s[sl, :]
        weight = lambda i: up_s[i, :, :, :, :, wide(0)].reshape(feat, feat)
        gs = dot_nt(dq, weight(0)) + dot_nt(dk, weight(1)) + dot_nt(dv, weight(2))
        xhat, q = norm_parts(tokens_ref[sl, :].astype(f32))
        t = gs * gain_one
        gtok_ref[sl, :] += q * (t - jnp.mean(t, axis=-1, keepdims=True)
                                - xhat * jnp.mean(t * xhat, axis=-1, keepdims=True))
        for r, a in enumerate((gs * xhat, gs, dq.astype(f32), dv.astype(f32))):
            small_s[r:r + 1, :] += jnp.sum(a, axis=0, keepdims=True)

        def at(k, *todo):
            @pl.when(i == k)
            def _():
                for one in todo:
                    one()

        at(0, lambda: unit_a(heads - 3).from_outer(), lambda: unit_a(heads - 1).from_core())
        at(1, lambda: unit_a(heads - 2).from_inner(), lambda: unit_a(heads - 1).from_twin())
        at(2, lambda: last(unit_a(heads - 3)))
        at(3, lambda: unit_a(heads - 2).from_outer(), lambda: unit_a(heads - 1).from_inner())
        return 0

    lax.fori_loop(0, rows // RB, back_rows, 0)
    small.start(small_s[...])
    steps = small.steps()
    last(unit_a(heads - 2))
    gup_ref[...] = join_columns([gup_ref[:, j * width:(j + 1) * width] for j in range(BLOCKS)], n)
    steps[0]()
    unit_a(heads - 1).from_outer()
    steps[1]()
    last(unit_a(heads - 1))
    for one in steps[2:]:
        one()
    for p in range(heads):
        for i, ref in enumerate((gq_ref, gk_ref, gv_ref)):
            ref[:, p * 128:(p + 1) * 128] = gqkv_s[p, :, i * 128:(i + 1) * 128]

    def drain(j, _):
        sent(unit_u(j), *rest_stages)
        sent(unit_d(j), *rest_stages)
        return 0

    lax.fori_loop(0, BLOCKS, drain, 0)
    sent(unit_u(end), "core")
    sent(unit_d(end), "core")
    sent(unit_o, "core", *rest_stages)

    def drain_pairs(p, _):
        sent(unit_a(p), *rest_stages)

        @pl.when(p >= heads - 2)
        def _():
            sent(unit_a(p), "core")
        return 0

    lax.fori_loop(0, heads, drain_pairs, 0)
    small.finish()


def layer_back(sizes, counts, mixed, tokens, cot, outw, vec, lse, up_all, down_all, q, k, v, qkv_all):
    dp_total, n = sizes
    rows, feat = tokens.shape
    B, pairs = n // 8, dp_total // 2
    own, width = up_all.shape[-2:]
    piece = down_all.shape[-2]
    heads = feat // 128
    s = jax.ShapeDtypeStruct
    vm = pl.BlockSpec(memory_space=pltpu.VMEM)
    anyspec = pl.BlockSpec(memory_space=pl.ANY)
    act = lambda dt, cols=feat: pltpu.VMEM((rows, cols), dt)
    copies = (2 * BLOCKS + 1 + heads) * Scatter.count(B, pairs) + Total.count(B, pairs)
    return pl.pallas_call(
        functools.partial(layer_kernel, dp_total, n),
        in_specs=[pl.BlockSpec(memory_space=pltpu.SMEM), anyspec, vm, anyspec, vm, vm, vm] + [anyspec] * 6,
        out_specs=[vm] * 9,
        out_shape=[s((rows, feat), bf16), s((rows, feat), f32), s((own, BLOCKS * width), f32),
                   s((BLOCKS * piece, feat), f32)] + [s((own, feat), f32)] * 4 + [s(vec.shape, f32)],
        scratch_shapes=[act(f32), act(bf16), act(bf16), act(bf16), act(bf16, BLOCKS * width), act(bf16, width),
                        pltpu.VMEM(up_all.shape, bf16), pltpu.VMEM(down_all.shape, bf16),
                        pltpu.VMEM((128, rows), bf16), act(bf16, 128), act(bf16, 128), pltpu.VMEM((BLOCKS, 8, width), f32),
                        pltpu.VMEM((BLOCKS, 8, width), f32), pltpu.VMEM((heads, own, 384), f32),
                        pltpu.VMEM(vec.shape, f32),
                        pltpu.VMEM((2,) + up_all.shape[1:], bf16), pltpu.VMEM((2,) + down_all.shape[1:], bf16)]
        + Scatter.shapes(B, pairs, own, width, scatter_edge(width), (BLOCKS,))
        + Scatter.shapes(B, pairs, piece, feat, scatter_edge(feat), (BLOCKS,))
        + Scatter.shapes(B, pairs, own, feat, 256)
        + Scatter.shapes(B, pairs, own, 384, 128, (heads,))
        + Total.shapes(B, pairs, vec.shape)
        + [pltpu.SemaphoreType.DMA((copies,)), pltpu.SemaphoreType.DMA((copies,)),
           pltpu.SemaphoreType.DMA((2 * BLOCKS + 2,))]
        + [pltpu.SemaphoreType.DMA((3 * PARTS,))],
        compiler_params=pltpu.CompilerParams(collective_id=2, has_side_effects=True, vmem_limit_bytes=67043328),
        name="layer_back",
    )(counts, mixed, tokens, cot, outw, vec, lse, up_all, down_all, q, k, v, qkv_all)

FSDP="fsdp"

def hand_kernel(*refs):
    half = len(refs) // 2
    for a, b in zip(refs[:half], refs[half:]):
        b[...] = a[...]


def hand_over(by_rows, by_cols, whole):
    steps = 4
    arrays = list(by_rows) + list(by_cols) + list(whole)
    specs = [pl.BlockSpec((a.shape[0] // steps, a.shape[1]), lambda i: (i, 0)) for a in by_rows]
    specs += [pl.BlockSpec((a.shape[0], a.shape[1] // steps), lambda i: (0, i)) for a in by_cols]
    specs += [pl.BlockSpec(a.shape, lambda i: (0, 0)) for a in whole]
    return pl.pallas_call(hand_kernel, grid=(steps,), in_specs=specs, out_specs=specs,
                          out_shape=[jax.ShapeDtypeStruct(a.shape, a.dtype) for a in arrays], name="hand_over")(*arrays)


def spread(vectors, index, total):
    own = vectors.shape[-1]
    at = lax.broadcasted_iota(jnp.int32, (1, total, own), 1)
    wide = jnp.where(at == index, vectors[:, None, :], jnp.zeros((), vectors.dtype))
    return wide.reshape(vectors.shape[0], total * own)

def on_device(sizes, tokens, image_counts, cotangent, first_gain, first_shift, query_weight, query_bias, key_weight,
              value_weight, value_bias, out_weight, out_bias, second_gain, second_shift, up_weight, up_bias,
              down_weight, down_bias):
    rows, feat = tokens.shape
    own = query_weight.shape[0]
    n = feat // own
    counts = image_counts[0]
    me = lax.axis_index(FSDP)
    eight = jnp.stack([first_gain, first_shift, query_bias, value_bias, out_bias, second_gain, second_shift, down_bias])
    small = jnp.concatenate([spread(eight, me, n), spread(up_bias[None], me, n).reshape(-1, feat)])
    small = jnp.concatenate([small, jnp.zeros((16 - small.shape[0], feat), bf16)])
    q, k, v, vec, mixed, lse, qkv_all, o_all, up_all, down_all, _ = gather_attend(
        sizes, counts, tokens, small, query_weight, key_weight, value_weight, out_weight, up_weight, down_weight)
    layer_out, gtok, gup, gdown, gq, gk, gv, go, total = layer_back(
        sizes, counts, mixed, tokens, cotangent, o_all.reshape(feat, feat), vec, lse, up_all, down_all, q, k, v, qkv_all)
    gtok, layer_out, gdown, gup, gq, gk, gv, go = hand_over((gtok, layer_out, gdown), (gup,), (gq, gk, gv, go))
    mine = lax.dynamic_index_in_dim(total[:8].reshape(8, n, own), me, 1, keepdims=False)
    ub_mine = lax.dynamic_index_in_dim(total[8:12].reshape(n, -1), me, 0, keepdims=False)
    return (layer_out, gtok, mine[0], mine[1], gq, mine[2], gk, gv, mine[3], go, mine[4], mine[5], mine[6],
            gup, ub_mine, gdown, mine[7])


def solution(mesh):
    rows = P(("dp", "fsdp"), None)
    mat = P("fsdp", None)
    vec = P("fsdp")
    return jax.shard_map(
        functools.partial(on_device, (mesh.shape["dp"], mesh.shape["fsdp"])),
        mesh=mesh,
        in_specs=(rows, rows, rows, vec, vec, mat, vec, mat, mat, vec, mat, vec, vec, vec, mat, vec, mat, vec),
        out_specs=(rows, rows, vec, vec, mat, vec, mat, mat, vec, mat, vec, vec, vec, mat, vec, mat, vec),
        check_vma=False,
    )
```

```python
import functools
import math

import jax
import jax.numpy as jnp
from jax import lax
from jax.experimental import pallas as pl
from jax.experimental.pallas import tpu as pltpu
from jax.sharding import PartitionSpec as P

EPS = 1e-06
NT = (((1,), (1,)), ((), ()))
TN = (((0,), (0,)), ((), ()))


SMALL_ROWS=197; LARGE_ROWS=325
QB=256
NEG=-1e30

def image_ends(small, large, rows):
    ends=[]
    for i in range(1, rows//SMALL_ROWS+1):
        e = jnp.minimum(i, small)*SMALL_ROWS + jnp.maximum(i-small,0)*LARGE_ROWS
        ends.append(jnp.where(i<=small+large, e, 2*rows))
    return ends

def image_of(places, ends):
    idx = jnp.zeros(places.shape, jnp.int32)
    for e in ends:
        idx = idx + (places>=e).astype(jnp.int32)
    return idx


f32=jnp.float32; bf16=jnp.bfloat16
RB=256
INV_SQRT2=1/math.sqrt(2.0); INV_SQRT2PI=1/math.sqrt(2*math.pi)

def dot(a,b): return jnp.dot(a,b,preferred_element_type=f32)
def dot_nt(a,b): return lax.dot_general(a,b,NT,preferred_element_type=f32)
def dot_tn(a,b): return lax.dot_general(a,b,TN,preferred_element_type=f32)

def norm_parts(x):
    mean=jnp.mean(x,axis=-1,keepdims=True)
    cen=x-mean
    var=jnp.mean(cen*cen,axis=-1,keepdims=True)
    q=lax.rsqrt(var+EPS)
    return cen*q, q

def live_mask(counts_ref, first, n):
    end=counts_ref[0]*197+counts_ref[1]*325
    r=first+lax.broadcasted_iota(jnp.int32,(n,1),0)
    return r<end


MESH = pl.DeviceIdType.MESH


class Place:
    def __init__(self, dp_total, fsdp_total):
        half = fsdp_total // 2
        self.outer_total = 4
        self.inner_total = half // 4
        assert half % 4 == 0
        self.pairs = dp_total // 2
        self.d = lax.axis_index("dp")
        self.f = lax.axis_index("fsdp")
        self.core = self.f % 2
        self.inner = (self.f // 2) % self.inner_total
        self.outer = self.f // (2 * self.inner_total)
        self.side = self.d % 2
        self.twin = self.d + 1 - 2 * self.side
        self.flip = self.outer // 2
        self.mirror = self.unmirror(self.outer)

        B = self.inner_total
        self.outers = [self.outer] + [(self.outer + s) % 4 for s in range(1, 4)]
        self.inners = [self.inner] + [(self.inner + t) % B for t in range(1, B)]
        self.cores = [self.core, 1 - self.core]
        self.ends = [self.unmirror(0), self.unmirror(1), self.unmirror(2)]
        self.next_outer = self.unmirror(1 - self.mirror)
        self.arrivals = [self.outer, self.next_outer, self.ends[2], self.unmirror(3)]
        self.outer_devices = [self.device(o, self.inner, self.core) for o in self.outers]
        self.inner_devices = [self.device(self.outer, i, self.core) for i in self.inners]
        self.core_device = self.device(self.outer, self.inner, self.cores[1])
        self.twin_device = (self.twin, self.f)
        self.pair_devices = [(self.d, self.f)] + [(self.side + 2 * ((self.d // 2 + k) % self.pairs), self.f)
                                                  for k in range(1, self.pairs)]

    def unmirror(self, at):
        return at + self.flip * (3 - 2 * at)

    def device(self, outer, inner, core):
        return (self.d, (outer * self.inner_total + inner) * 2 + core)

    def at_outer(self, outer):
        return self.device(outer, self.inner, self.core)

    def at_inner(self, t):
        return self.inner_devices[t % self.inner_total]

    def other_core(self):
        return self.core_device

    def at_twin(self):
        return self.twin_device

    def me(self):
        return (self.d, self.f)

    def at_pair(self, k):
        return self.pair_devices[k % self.pairs]

    def neighbours(self, pairs=False):
        out = self.outer_devices[1:]
        out += [self.at_inner(t) for t in range(1, self.inner_total)]
        out += [self.at_twin(), self.other_core()]
        if pairs:
            out = self.outer_devices[1:] + Total.near_devices(self)
            out += [self.at_pair(k) for k in range(1, self.pairs)]
        return out


def greet(others):
    barrier = pltpu.get_barrier_semaphore()
    for other in others:
        pl.semaphore_signal(barrier, inc=1, device_id=other, device_id_type=MESH)
    pl.semaphore_wait(barrier, len(others))


class Gather:
    def __init__(self, place, ref, edge, sems, base):
        self.place, self.ref, self.edge = place, ref, edge
        self.rows = ref.shape[-2]
        self.send_sem, self.recv_sem = sems
        self.base = base
        A, B = place.outer_total, place.inner_total
        keys = [("z", s) for s in range(1, A)] + [("Z", s) for s in range(1, A)]
        keys += [("x", s, t) for s in range(A) for t in range(1, B)]
        keys += [("y", t) for t in range(B)]
        keys += [("c",)]
        self.keys = {key: i for i, key in enumerate(keys)}
        self.sent = []
        self.sent_inside = []

    @staticmethod
    def count(B):
        return 6 + 4 * (B - 1) + B + 1

    def rows_of(self, kind):
        e, r, p = self.edge, self.rows, self.place.side
        if not e or kind == "all":
            return pl.ds(0, r)
        start, size = {"plane": (p * e, r - e), "mine": (p * (r - e), e), "theirs": ((1 - p) * (r - e), e)}[kind]
        return pl.ds(pl.multiple_of(start, 8), size)

    def part(self, outer, inner, core, kind):
        return self.ref.at[outer, inner, core, self.rows_of(kind)]

    def copy(self, key, ref, to):
        i = self.base + self.keys[key]
        into = i
        if key[0] == "Z":
            into = self.base + self.keys["z", 2 if key[1] == 2 else 3]
        return pltpu.make_async_remote_copy(src_ref=ref, dst_ref=ref, send_sem=self.send_sem.at[i],
                                            recv_sem=self.recv_sem.at[into], device_id=to, device_id_type=MESH)

    def send(self, key, make):
        self.copy(key, *make()).start()
        self.sent.append((key, make))

    def send_inside(self, key, make):
        @pl.when(self.place.mirror == 1)
        def _():
            self.copy(key, *make()).start()

        self.sent_inside.append((key, make))

    def got(self, key, ref):
        self.copy(key, ref, self.place.me()).wait_recv()

    def outer_of(self, step):
        return self.place.arrivals[step]

    def own_line(self, step):
        p = self.place
        return self.part(self.outer_of(step), p.inner, p.core, "plane")

    def start(self):
        p = self.place
        self.send(("z", 1), lambda: (self.own_line(0), p.at_outer(p.next_outer)))
        self.send_inside(("z", 2), lambda: (self.own_line(0), p.at_outer(p.ends[2])))
        self.pass_inner(0)

    def pass_inner(self, step):
        p = self.place
        for t in range(1, p.inner_total):
            self.send(("x", step, t), lambda t=t: (self.own_line(step), p.at_inner(-t)))

    def onward(self, step):
        p = self.place
        return self.own_line(step), p.at_outer(p.ends[2 if step == 1 else 0])

    def arrived(self, step, record):
        self.got(("z", step), self.own_line(step))
        kept = list(self.sent)
        self.pass_inner(step)
        if step == 3:
            self.pass_twin(0)
        if not record:
            self.sent = kept

    def from_next(self):
        self.arrived(1, True)
        self.send_inside(("Z", 1), functools.partial(self.onward, 1))

    def relay(self, step):
        @pl.when(self.place.mirror == 1)
        def _():
            self.got(("z", step), self.own_line(step))
            self.copy(("Z", step), *self.onward(step)).start()
            kept = list(self.sent)
            self.pass_inner(step)
            if step == 3:
                self.pass_twin(0)
            self.sent = kept

        self.sent_inside.append((("Z", step), functools.partial(self.onward, step)))

    def take(self, step):
        @pl.when(self.place.mirror == 0)
        def _():
            self.arrived(step, False)

        for t in range(1, self.place.inner_total):
            self.sent.append((("x", step, t), lambda t=t: (self.own_line(step), self.place.at_inner(-t))))
        if step == 3 and self.edge:
            self.sent.append((("y", 0), lambda: (self.line(0, "mine"), self.place.at_twin())))

    def relay_2(self):
        self.relay(2)

    def relay_3(self):
        self.relay(3)

    def take_2(self):
        self.take(2)

    def take_3(self):
        self.take(3)

    def line(self, t, kind):
        p = self.place
        return self.part(slice(None), p.inners[t], p.core, kind)

    def pass_twin(self, t):
        if self.edge:
            self.send(("y", t), lambda: (self.line(t, "mine"), self.place.at_twin()))

    def from_inner(self):
        p = self.place
        for t in range(1, p.inner_total):
            for step in range(4):
                self.got(("x", step, t), self.part(self.outer_of(step), p.inners[t], p.core, "plane"))
            self.pass_twin(t)

    def half(self, core):
        return self.part(slice(None), slice(None), core, "all")

    def from_twin(self):
        p = self.place
        if self.edge:
            for t in range(p.inner_total):
                self.got(("y", t), self.line(t, "theirs"))
        self.send(("c",), lambda: (self.half(p.core), p.other_core()))

    def from_core(self):
        self.got(("c",), self.half(self.place.cores[1]))

    def finish(self):
        for key, make in self.sent:
            self.copy(key, *make()).wait_send()

        @pl.when(self.place.mirror == 1)
        def _():
            for key, make in self.sent_inside:
                self.copy(key, *make()).wait_send()


class Scatter:
    def __init__(self, place, terms, bufs, edge, emit, sems, base):
        self.place, self.terms, self.edge, self.emit = place, terms, edge, emit
        self.sums, self.twin_buf, self.inner_buf, self.outer_buf, self.last_buf = bufs[:5]
        self.pair_bufs = bufs[5:]
        self.send_sem, self.recv_sem = sems
        self.base = base
        p, e, w = place.side, edge, terms.shape[-1]
        at = lambda start, size: pl.ds(pl.multiple_of(start, 128), size)
        self.plane = at(p * e, w - e)
        self.mine = at(p * (w - e), e)
        self.theirs = at((1 - p) * (w - e), e)
        self.twin_plane = at((1 - p) * e, w - e)
        self.middle = pl.ds(e, w - 2 * e)

    @staticmethod
    def count(B, pairs):
        return 1 + 1 + (B - 1) + 3 + 1 + (pairs - 1)

    @staticmethod
    def shapes(B, pairs, rows, width, edge, lead=()):
        out = [(4, B, rows, width), (4, B, rows, edge), (B - 1, 4, rows, width), (3, rows, width), (rows, width)]
        if pairs > 1:
            out += [(rows, width), (pairs - 1, rows, width)]
        return [pltpu.VMEM(tuple(lead) + s, bf16) for s in out]

    def copy(self, i, src, dst, to):
        return pltpu.make_async_remote_copy(src_ref=src, dst_ref=dst, send_sem=self.send_sem.at[self.base + i],
                                            recv_sem=self.recv_sem.at[self.base + i], device_id=to, device_id_type=MESH)

    def copies(self, stage):
        p = self.place
        A, B = 4, p.inner_total
        if stage == "core":
            return [self.copy(0, self.terms.at[:, :, p.cores[1]], self.sums, p.other_core())]
        if stage == "twin":
            return [self.copy(1, self.sums.at[:, :, :, self.theirs], self.twin_buf, p.at_twin())]
        if stage == "inner":
            return [self.copy(1 + t, self.sums.at[:, p.inners[(B - t) % B], :, self.plane],
                              self.inner_buf.at[t - 1, :, :, self.plane], p.at_inner(-t)) for t in range(1, B)]
        if stage == "outer":
            return [self.copy(B + s, self.sums.at[p.outers[A - s], p.inner, :, self.plane],
                              self.outer_buf.at[s - 1, :, self.plane], p.outer_devices[A - s])
                    for s in range(1, A)]
        if stage == "last":
            return [self.copy(A + B, self.sums.at[p.outer, p.inner, :, self.plane], self.last_buf.at[:, self.plane],
                              p.at_twin())]
        half, others = self.pair_bufs
        return [self.copy(A + B + k, half, others.at[k - 1], p.at_pair(p.pairs - k)) for k in range(1, p.pairs)]

    def go(self, stage):
        for c in self.copies(stage):
            c.start()

    def got(self, i, dst):
        self.copy(i, dst, dst, self.place.me()).wait_recv()

    def start(self):
        self.go("core")

    def from_core(self):
        p = self.place
        B = p.inner_total
        self.got(0, self.sums)

        def add(i, _):
            a, b = i // B, i % B
            self.sums[a, b] = self.sums[a, b] + self.terms[a, b, p.core]
            return 0

        lax.fori_loop(0, 4 * B, add, 0)
        self.go("twin")

    def from_twin(self):
        p = self.place
        B = p.inner_total
        self.got(1, self.twin_buf)

        def add(i, _):
            a, b = i // B, i % B
            self.sums[a, b, :, self.mine] = self.sums[a, b, :, self.mine] + self.twin_buf[a, b]
            return 0

        lax.fori_loop(0, 4 * B, add, 0)
        self.go("inner")

    def from_inner(self):
        p = self.place
        B = p.inner_total
        for t in range(1, B):
            self.got(1 + t, self.inner_buf.at[t - 1, :, :, self.plane])

        def add(a, _):
            if B == 2:
                self.sums[a, p.inner, :, self.plane] = (self.sums[a, p.inner, :, self.plane]
                                                        + self.inner_buf[0, a, :, self.plane])
                return 0
            total = self.sums[a, p.inner, :, self.plane].astype(f32)
            for t in range(1, B):
                total = total + self.inner_buf[t - 1, a, :, self.plane].astype(f32)
            self.sums[a, p.inner, :, self.plane] = total.astype(bf16)
            return 0

        lax.fori_loop(0, 4, add, 0)
        self.go("outer")

    def from_outer(self):
        p = self.place
        B = p.inner_total
        for s in range(1, 4):
            self.got(B + s, self.outer_buf.at[s - 1, :, self.plane])
        total = self.sums[p.outer, p.inner, :, self.plane].astype(f32)
        for s in range(1, 4):
            total = total + self.outer_buf[s - 1, :, self.plane].astype(f32)
        self.sums[p.outer, p.inner, :, self.plane] = total.astype(bf16)
        self.go("last")

    def from_last(self):
        p = self.place
        self.got(4 + p.inner_total, self.last_buf.at[:, self.twin_plane])
        own = lambda cols: self.sums[p.outer, p.inner, :, cols].astype(f32)
        last = lambda cols: self.last_buf[:, cols].astype(f32)
        if p.pairs == 1:
            self.emit(self.mine, own(self.mine))
            self.emit(self.middle, own(self.middle) + last(self.middle))
            self.emit(self.theirs, last(self.theirs))
            return
        half, others = self.pair_bufs
        half[:, self.mine] = own(self.mine).astype(bf16)
        half[:, self.middle] = (own(self.middle) + last(self.middle)).astype(bf16)
        half[:, self.theirs] = last(self.theirs).astype(bf16)
        self.go("pairs")

    def from_pairs(self):
        p = self.place
        if p.pairs == 1:
            return
        half, others = self.pair_bufs
        total = half[...].astype(f32)
        for k in range(1, p.pairs):
            self.got(4 + p.inner_total + k, others.at[k - 1])
            total = total + others[k - 1].astype(f32)
        self.emit(pl.ds(0, self.terms.shape[-1]), total)

    def finish(self):
        for stage in ("core", "twin", "inner", "outer", "last") + (("pairs",) if self.place.pairs > 1 else ()):
            for c in self.copies(stage):
                c.wait_send()


class Total:
    def __init__(self, place, bufs, out, sems, base):
        self.place, self.landing, self.out = place, bufs[0], out
        self.send_sem, self.recv_sem = sems
        p, B = place, place.inner_total
        near = []
        for side in range(2):
            for t in range(B):
                for core in range(2):
                    if side or t or core:
                        dev = p.device(p.outer, p.inners[t], p.cores[core])[1]
                        near.append((p.d if not side else p.twin, dev))
        self.rounds = [(near, (p.side * B + p.inner) * 2 + p.core, 4 * B),
                       (p.outer_devices[1:], p.outer, 4)]
        if p.pairs > 1:
            self.rounds.append(([p.at_pair(k) for k in range(1, p.pairs)], p.d // 2, p.pairs))
        self.base = base

    @staticmethod
    def near_devices(place):
        return Total(place, [None], None, (None, None), 0).rounds[0][0]

    @staticmethod
    def count(B, pairs):
        return 4 * B + 4 + pairs

    @staticmethod
    def shapes(B, pairs, shape):
        return [pltpu.VMEM((Total.count(B, pairs),) + shape, f32)]

    def first(self, r):
        return sum(x[2] for x in self.rounds[:r])

    def send_copy(self, r, k):
        others, mine, _ = self.rounds[r]
        at = self.landing.at[self.first(r) + mine]
        return pltpu.make_async_remote_copy(src_ref=at, dst_ref=at, send_sem=self.send_sem.at[self.base + self.first(r) + k],
                                            recv_sem=self.recv_sem.at[self.base + self.first(r) + mine],
                                            device_id=others[k], device_id_type=MESH)

    def begin(self, r, value):
        others, mine, _ = self.rounds[r]
        self.landing[self.first(r) + mine] = value
        for k in range(len(others)):
            self.send_copy(r, k).start()

    def start(self, value):
        self.begin(0, value)

    def step(self, r):
        others, mine, members = self.rounds[r]
        for k in range(1, members):
            slot = self.first(r) + (mine + k) % members
            at = self.landing.at[slot]
            pltpu.make_async_remote_copy(src_ref=at, dst_ref=at, send_sem=self.send_sem.at[self.base],
                                         recv_sem=self.recv_sem.at[self.base + slot], device_id=self.place.me(),
                                         device_id_type=MESH).wait_recv()
        total = self.landing[self.first(r)]
        for k in range(1, members):
            total = total + self.landing[self.first(r) + k]
        if r + 1 < len(self.rounds):
            self.begin(r + 1, total)
        else:
            self.out[...] = total

    def steps(self):
        return [functools.partial(self.step, r) for r in range(len(self.rounds))]

    def finish(self):
        for r in range(len(self.rounds)):
            for k in range(len(self.rounds[r][0])):
                self.send_copy(r, k).wait_send()


def local(src, dst, sem):
    c = pltpu.make_async_copy(src, dst, sem)
    c.start()
    return c


def mask_lanes(shape, first, ends, hit, miss):
    lane = lax.broadcasted_iota(jnp.int32, shape, 1)
    image = image_of(first + lax.broadcasted_iota(jnp.int32, shape, 0), ends)
    return jnp.where(image == jnp.where(lane < 64, lane, lane - 64), hit, miss).astype(bf16)


def head_lanes(values, others, e):
    lane = lax.broadcasted_iota(jnp.int32, values.shape, 1)
    return jnp.where((lane < 64) == (e == 0), values, others)


BLOCKS = 3


def lane_tile(source, moves):
    lane = None
    out = None
    for col, to, size in moves:
        tile = source[:, col // 128 * 128:col // 128 * 128 + 128]
        shift = (to - col) % 128
        if shift:
            tile = pltpu.roll(tile, shift, 1)
        if out is None:
            out = tile
            lane = lax.broadcasted_iota(jnp.int32, tile.shape, 1)
        else:
            out = jnp.where((lane >= to) & (lane < to + size), tile, out)
    return out


def split_columns(source, owners):
    piece = source.shape[1] // owners // BLOCKS
    per = 128 // piece
    out = []
    for j in range(BLOCKS):
        tiles = [lane_tile(source, [(((t * per + q) * BLOCKS + j) * piece, q * piece, piece) for q in range(per)])
                 for t in range(owners // per)]
        out.append(jnp.concatenate(tiles, axis=1))
    return out


def join_columns(parts, owners):
    source = jnp.concatenate(parts, axis=1)
    width = parts[0].shape[1]
    piece = width // owners
    per = 128 // piece
    tiles = []
    for t in range(source.shape[1] // 128):
        moves = []
        for q in range(per):
            unit = t * per + q
            moves.append(((unit % BLOCKS) * width + unit // BLOCKS * piece, q * piece, piece))
        tiles.append(lane_tile(source, moves))
    return jnp.concatenate(tiles, axis=1)


PARTS = 3


def attend_block(q_ref, k_ref, v_ref, own_ref, far_ref, mixed_ref, lse_ref, pair, block):
    lane = lax.broadcasted_iota(jnp.int32, (QB, 128), 1)
    first = pl.multiple_of(block * QB, QB)
    cols = pl.ds(pl.multiple_of(pair * 128, 128), 128)
    q = q_ref[pl.ds(first, QB), cols]
    k = k_ref[:, cols]
    v = v_ref[:, cols]
    outs = []
    lses = []
    for e in range(2):
        s = dot_nt(head_lanes(q, own_ref[pl.ds(first, QB), :], e), head_lanes(k, far_ref[...], e))
        m = jnp.max(s, axis=1, keepdims=True)
        p = jnp.exp(s - m)
        l = jnp.sum(p, axis=1, keepdims=True)
        o = dot(p.astype(bf16), v)
        outs.append(o * (1.0 / l))
        lses.append(m + jnp.log(l))
    mixed_ref[pl.ds(first, QB), cols] = jnp.where(lane < 64, outs[0], outs[1]).astype(bf16)
    both = jnp.where(lane < 64, jnp.broadcast_to(lses[0], (QB, 128)), jnp.broadcast_to(lses[1], (QB, 128)))
    t = both.T
    lse_ref[pair, 0:1, pl.ds(first, QB)] = t[0:1, :]
    lse_ref[pair, 1:2, pl.ds(first, QB)] = t[64:65, :]


def gather_edge(rows, last=False):
    return rows // 3 if rows % 24 == 0 else rows // 4 if last or rows < 64 else rows * 3 // 8


def gather_plan(units, early, pieces):
    n = len(units)
    slots = [[] for _ in range(n + 12)]
    for t, u in enumerate(units):
        if t >= 3:
            slots[t - 2].append(u.start)
    for t, u in enumerate(units):
        inner, twin, core = (4, 5, 6) if t <= early else (5, 7, 9) if t <= PARTS else (5, 7, 9)
        stages = [(0, u.from_next), (1, u.relay_2), (2, u.relay_3), (2, u.take_2), (3, u.take_3),
                  (inner, u.from_inner), (twin, u.from_twin), (core, u.from_core)]
        for at, one in stages:
            slots[t + at].append(one)
    cut = early + 7
    rest = slots[cut:]
    while not rest[-1]:
        rest.pop()
    places = [[] for _ in range(pieces)]
    for k, slot in enumerate(rest):
        places[k * pieces // len(rest)] += slot
    for t in range(2, PARTS + 1):
        assert any(units[t].from_core in place for place in places[:(t - 1) * pieces // PARTS])
    return [one for slot in slots[:cut] for one in slot], places


def gather_kernel(dp_total, n, counts_ref, tokens_hbm, small_ref, qo_ref, ko_ref, vo_ref, oo_ref, uo_ref, do_ref,
                  q_hbm, k_hbm, v_hbm, vec_ref, mixed_hbm, lse_ref, qkv_all, o_all, up_all, down_all, small_all,
                  tokens_s, fi_s, own_s, far_s, q_s, k_s, v_s, mixed_s, w_s, small_s, up_own, send_sem, recv_sem, loc_sem, out_sem):
    place = Place(dp_total, n)
    B = place.inner_total
    own = qo_ref.shape[0]
    piece = do_ref.shape[0] // BLOCKS
    greet(place.neighbours())
    take_tokens = local(tokens_hbm, tokens_s, loc_sem.at[0])
    sems = (send_sem, recv_sem)
    refs = [(small_all, 0)] + [(qkv_all.at[j], own) for j in range(PARTS)] + [(o_all, gather_edge(own))]
    for j in range(BLOCKS):
        refs += [(up_all.at[j], gather_edge(own)), (down_all.at[j], gather_edge(piece, j == BLOCKS - 1))]
    units = [Gather(place, ref, edge, sems, i * Gather.count(B))
             for i, (ref, edge) in enumerate(refs)]
    mine = lambda unit: unit.part(place.outer, place.inner, place.core, "plane")
    block = qkv_all.shape[-1]

    def own_part(source, j, i):
        return local(source.at[:, pl.ds(j * block, block)],
                     qkv_all.at[j, place.outer, place.inner, place.core, pl.ds(i * own, own)], loc_sem.at[2 + 2 * j + i % 2])

    fill = [local(small_ref, mine(units[0]), loc_sem.at[1])] + [own_part(ko_ref, j, 1) for j in range(PARTS)]

    @pl.when(place.side == 0)
    def _():
        for c in [own_part(qo_ref, j, 0) for j in range(PARTS)]:
            c.wait()

    @pl.when(place.side == 1)
    def _():
        for c in [own_part(vo_ref, j, 2) for j in range(PARTS)]:
            c.wait()

    for c in fill:
        c.wait()
    units[0].start()
    units[1].start()
    for j, part in enumerate(split_columns(uo_ref[...].astype(f32), n)):
        up_own[j] = part.astype(bf16)
    base = 1 + PARTS
    fill = [local(oo_ref.at[units[base].rows_of("plane")], mine(units[base]), loc_sem.at[1])]
    for j in range(BLOCKS):
        a, b = units[base + 1 + 2 * j], units[base + 2 + 2 * j]
        fill.append(local(up_own.at[j, a.rows_of("plane")], mine(a), loc_sem.at[2 + 2 * j]))
        rows = b.rows_of("plane")
        fill.append(local(do_ref.at[pl.ds(pl.multiple_of(j * piece + rows.start, 8), rows.size)], mine(b),
                          loc_sem.at[3 + 2 * j]))
    for c in fill:
        c.wait()
    units[2].start()

    def vectors():
        local(small_all, small_s, loc_sem.at[1]).wait()
        total = jnp.zeros(vec_ref.shape, f32)
        for i in range(n):
            total = total + small_s[i // (2 * B), i // 2 % B, i % 2].astype(f32)
        vec_ref[...] = total

    rows, feat = tokens_s.shape
    blocks = rows // QB
    per = qkv_all.shape[-1] // 128 * blocks
    pieces = PARTS * per
    head, rest = gather_plan(units, 1, pieces)
    for one in head:
        one()
    weight_load = lambda j: pltpu.make_async_copy(qkv_all.at[j], w_s.at[j], loc_sem.at[2 + j])
    weight_load(0).start()
    vectors()
    take_tokens.wait()

    ends = image_ends(counts_ref[0], counts_ref[1], rows)

    def norm_rows(i, _):
        first = pl.multiple_of(i * RB, RB)
        sl = pl.ds(first, RB)
        own_s[sl, :] = mask_lanes((RB, 128), first, ends, 1.0, 0.0)
        far_s[sl, :] = mask_lanes((RB, 128), first, ends, 0.0, NEG)
        xhat, _q = norm_parts(tokens_s[sl, :].astype(f32))
        fi_s[sl, :] = (xhat * vec_ref[0:1, :] + vec_ref[1:2, :]).astype(bf16)
        return 0

    lax.fori_loop(0, rows // RB, norm_rows, 0)
    def project(j):
        cols = pl.ds(pl.multiple_of(j * block, 128), block)
        weight_load(j).wait()

        def project_rows(i, _):
            sl = pl.ds(pl.multiple_of(i * RB, RB), RB)
            fi = fi_s[sl, :]
            weight = lambda i: w_s[j, :, :, :, i * own:(i + 1) * own, :].reshape(feat, block)
            q_s[sl, cols] = ((dot(fi, weight(0)) + vec_ref[2:3, cols]).astype(bf16).astype(f32) * 0.125).astype(bf16)
            k_s[sl, cols] = dot(fi, weight(1)).astype(bf16)
            v_s[sl, cols] = (dot(fi, weight(2)) + vec_ref[3:4, cols]).astype(bf16)
            return 0

        lax.fori_loop(0, rows // RB, project_rows, 0)
        for c in out_copies(j)[:3]:
            c.start()

    def out_copies(j):
        cols = pl.ds(pl.multiple_of(j * block, 128), block)
        return [pltpu.make_async_copy(a.at[:, cols], b.at[:, cols], out_sem.at[4 * j + i])
                for i, (a, b) in enumerate(((q_s, q_hbm), (k_s, k_hbm), (v_s, v_hbm), (mixed_s, mixed_hbm)))]

    def attend_piece(i, _):
        @pl.when(i % per == 0)
        def _():
            project(i // per)

        attend_block(q_s, k_s, v_s, own_s, far_s, mixed_s, lse_ref, i // blocks, i % blocks)
        for at, todo in enumerate(rest):
            if todo:
                @pl.when(i == at)
                def _(todo=todo):
                    for one in todo:
                        one()

        @pl.when(i % per == per - 1)
        def _():
            out_copies(i // per)[3].start()

        @pl.when((i % per == per - 1) & (i < pieces - 1))
        def _():
            weight_load(i // per + 1).start()

        return 0

    lax.fori_loop(0, pieces, attend_piece, 0)
    for j in range(PARTS):
        for c in out_copies(j):
            c.wait()
    for x in units:
        x.finish()


def gather_attend(sizes, counts, tokens, small, qw, kw, vw, ow, up, down):
    dp_total, n = sizes
    rows, feat = tokens.shape
    own = qw.shape[0]
    B = n // 8
    pairs = feat // 128
    s = jax.ShapeDtypeStruct
    vm = pl.BlockSpec(memory_space=pltpu.VMEM)
    anyspec = pl.BlockSpec(memory_space=pl.ANY)
    full = lambda *dims: (4, B, 2) + dims
    width = up.shape[1] // BLOCKS
    piece = down.shape[0] // BLOCKS
    act = s((rows, feat), bf16)
    copies = (2 + PARTS + 2 * BLOCKS) * Gather.count(B)
    return pl.pallas_call(
        functools.partial(gather_kernel, dp_total, n),
        in_specs=[pl.BlockSpec(memory_space=pltpu.SMEM), anyspec] + [vm] * 7,
        out_specs=[anyspec] * 3 + [vm, anyspec, vm] + [anyspec] * 5,
        out_shape=[act, act, act, s(small.shape, f32), act, s((pairs, 2, rows), f32), s((PARTS,) + full(3 * own, feat // PARTS), bf16),
                   s(full(own, feat), bf16), s((BLOCKS,) + full(own, width), bf16),
                   s((BLOCKS,) + full(piece, feat), bf16), s(full(*small.shape), bf16)],
        scratch_shapes=[pltpu.VMEM((rows, feat), bf16)] * 2 + [pltpu.VMEM((rows, 128), bf16)] * 2 + [
            pltpu.VMEM((rows, feat), bf16)] * 4 + [
            pltpu.VMEM((PARTS,) + full(3 * own, feat // PARTS), bf16), pltpu.VMEM(full(*small.shape), bf16),
            pltpu.VMEM((BLOCKS, own, width), bf16), pltpu.SemaphoreType.DMA((copies,)),
            pltpu.SemaphoreType.DMA((copies,)), pltpu.SemaphoreType.DMA((6 + 2 * BLOCKS,)),
            pltpu.SemaphoreType.DMA((4 * PARTS,))],
        compiler_params=pltpu.CompilerParams(collective_id=1, has_side_effects=True, vmem_limit_bytes=60 * 2**20),
        name="gather_attend",
    )(counts, tokens, small, qw, kw, vw, ow, up, down)


def scatter_edge(width):
    return 128 if width == 768 else width // 4 if width % 512 == 0 else width // 3


def layer_kernel(dp_total, n, counts_ref, mixed_hbm, tokens_ref, cot_hbm, outw_ref, vec_ref, lse_ref, up_hbm, down_hbm,
                 q_hbm, k_hbm, v_hbm, qkv_all,
                 layer_ref, gtok_ref, gup_ref, gdown_ref, gq_ref, gk_ref, gv_ref, go_ref, total_ref,
                 res_s, si_s, gb_s, mixed_s, hid_s, gi_s, up_s, down_s, kt_s, own_s, far_s, ub_s, gub_s, gqkv_s, small_s, *rest):
    rows, feat = tokens_ref.shape
    width = gi_s.shape[1]
    own = gq_ref.shape[0]
    piece = gdown_ref.shape[0] // BLOCKS
    heads = feat // 128
    place = Place(dp_total, n)
    B, pairs = place.inner_total, place.pairs
    per = 5 if pairs == 1 else 7
    uterm_s, dterm_s = rest[:2]
    ubufs, dbufs, obufs, abufs = (rest[2 + i * per:2 + (i + 1) * per] for i in range(4))
    total_bufs = rest[2 + 4 * per:3 + 4 * per]
    send_sem, recv_sem, loc_sem, weight_sem = rest[3 + 4 * per:]
    sems = (send_sem, recv_sem)
    count = Scatter.count(B, pairs)
    wide = lambda start: pl.ds(start, feat)
    load = lambda j: (pltpu.make_async_copy(up_hbm.at[j], up_s.at[j], loc_sem.at[2 * j]),
                      pltpu.make_async_copy(down_hbm.at[j], down_s.at[j], loc_sem.at[2 * j + 1]))
    at_end = 3 * feat
    first_loads = [local(mixed_hbm, mixed_s, loc_sem.at[2 * BLOCKS]),
                   local(cot_hbm, hid_s.at[:, wide(at_end)], loc_sem.at[2 * BLOCKS + 1])]
    for j in range(BLOCKS):
        for c in load(j):
            c.start()
    def unit_u(j):
        def emit(cols, value):
            gup_ref[:, pl.ds(pl.multiple_of(j * width + cols.start, 128), cols.size)] = value
        return Scatter(place, uterm_s.at[j % 2], [b.at[j] for b in ubufs], scatter_edge(width), emit, sems,
                       2 * j * count)

    def unit_d(j):
        def emit(cols, value):
            gdown_ref[pl.ds(pl.multiple_of(j * piece, 8), piece), cols] = value
        return Scatter(place, dterm_s.at[j % 2], [b.at[j] for b in dbufs], scatter_edge(feat), emit, sems,
                       (2 * j + 1) * count)

    def emit_out(cols, value):
        go_ref[:, cols] = value

    unit_o = Scatter(place, uterm_s.at[1, :, :, :, :, wide(0)], obufs, 256, emit_out, sems, 2 * BLOCKS * count)

    def pair_term(p):
        return dterm_s.at[1, :, :, :, pl.ds(0, own), pl.ds(pl.multiple_of(p % 2 * 384, 128), 384)]

    def unit_a(p):
        def emit(cols, value):
            gqkv_s[p, :, cols] = value
        return Scatter(place, pair_term(p), [b.at[p] for b in abufs], 128, emit, sems,
                       (2 * BLOCKS + 1 + p) * count)

    small = Total(place, total_bufs, total_ref, sems, (2 * BLOCKS + 1 + heads) * count)

    def last(unit):
        unit.from_last()
        unit.from_pairs()

    def sent(unit, *stages):
        for stage in stages:
            for c in unit.copies(stage):
                c.wait_send()

    rest_stages = ("twin", "inner", "outer", "last") + (("pairs",) if pairs > 1 else ())
    gain_one, shift_one = vec_ref[0:1, :], vec_ref[1:2, :]
    obias, gain, shift, dbias = (vec_ref[i:i + 1, :] for i in range(4, 8))
    ub = jnp.concatenate([vec_ref[8 + i:9 + i, :] for i in range(BLOCKS * width // feat)], axis=1)
    for j, part in enumerate(split_columns(jnp.broadcast_to(ub, (8, ub.shape[1])), n)):
        ub_s[j] = part
    small_s[...] = jnp.zeros_like(small_s)
    for c in first_loads:
        c.wait()

    def begin(i, _):
        first = pl.multiple_of(i * RB, RB)
        sl = pl.ds(first, RB)
        res = tokens_ref[sl, :].astype(f32) + (dot(mixed_s[sl, :], outw_ref[...]) + obias)
        res_s[sl, :] = res
        xhat, _q = norm_parts(res)
        si_s[sl, :] = (xhat * gain + shift).astype(bf16)
        gb_s[sl, :] = jnp.where(live_mask(counts_ref, first, RB), hid_s[sl, wide(at_end)], jnp.zeros((), bf16))
        gtok_ref[sl, :] = jnp.zeros((RB, feat), f32)
        return 0

    lax.fori_loop(0, rows // RB, begin, 0)
    greet(place.neighbours(pairs=True))

    def block(j, _):
        for c in load(j):
            c.wait()
        upw = lambda: up_s[j].reshape(feat, width)
        downw = lambda: down_s[j].reshape(width, feat)
        cols = pl.ds(pl.multiple_of(j * width, 128), width)
        gub_s[j] = jnp.zeros(gub_s.shape[1:], f32)

        def after(back, when, todo):
            @pl.when(when & (j >= back))
            def _():
                todo(j - back)

        def rows_piece(i, _):
            sl = pl.ds(pl.multiple_of(i * RB, RB), RB)
            pre = dot(si_s[sl, :], upw()) + ub_s[j, 0:1, :]
            cdf = 0.5 + 0.5 * lax.erf(pre * INV_SQRT2)
            pdf = jnp.exp(-0.5 * pre * pre) * INV_SQRT2PI
            hid_s[sl, cols] = (pre * cdf).astype(bf16)
            gi = (dot_nt(gb_s[sl, :], downw()) * (cdf + pre * pdf)).astype(bf16)
            gi_s[sl, :] = gi
            gub_s[j, 0:1, :] += jnp.sum(gi.astype(f32), axis=0, keepdims=True)
            after(1, i == 0, lambda k: unit_d(k).from_core())
            after(1, i == 1, lambda k: unit_u(k).from_core())
            after(2, i == 1, lambda k: unit_d(k).from_inner())
            after(1, i == 3, lambda k: unit_d(k).from_twin())
            return 0

        lax.fori_loop(0, rows // RB, rows_piece, 0)
        always = j >= 0
        after(2, always, lambda k: (sent(unit_u(k), "core"), sent(unit_d(k), "core")))
        dterm_s[j % 2] = dot_tn(hid_s[:, cols], gb_s[...]).astype(bf16).reshape(dterm_s.shape[1:])
        unit_d(j).start()
        after(1, always, lambda k: unit_u(k).from_twin())
        after(2, always, lambda k: unit_u(k).from_inner())
        uterm_s[j % 2] = dot_tn(si_s[...], gi_s[...]).astype(bf16).reshape(uterm_s.shape[1:])
        unit_u(j).start()
        gtok_ref[...] += dot_nt(gi_s[...], upw())
        return 0

    lax.fori_loop(0, BLOCKS, block, 0)
    end, before = BLOCKS - 1, BLOCKS - 2
    third = qkv_all.shape[-1]
    weights = [local(qkv_all.at[j, :, :, :, pl.ds(i * own, own)], up_s.at[i, :, :, :, :, pl.ds(j * third, third)],
                     weight_sem.at[i * PARTS + j]) for i in range(3) for j in range(PARTS)]

    def finish_rows(i, _):
        first = pl.multiple_of(i * RB, RB)
        sl = pl.ds(first, RB)
        res = res_s[sl, :]
        layer = res + (dot(hid_s[sl, :], down_s[...].reshape(BLOCKS * width, feat)) + dbias)
        layer_ref[sl, :] = jnp.where(live_mask(counts_ref, first, RB), layer, 0.0).astype(bf16)
        xhat, q = norm_parts(res)
        gs = gtok_ref[sl, :]
        t = gs * gain
        gb = gb_s[sl, :].astype(f32)
        gres = gb + q * (t - jnp.mean(t, axis=-1, keepdims=True) - xhat * jnp.mean(t * xhat, axis=-1, keepdims=True))
        gtok_ref[sl, :] = gres
        ga = gres.astype(bf16)
        si_s[sl, :] = ga
        small_s[7:8, :] += jnp.sum(gb, axis=0, keepdims=True)
        small_s[5:6, :] += jnp.sum(gs * xhat, axis=0, keepdims=True)
        small_s[6:7, :] += jnp.sum(gs, axis=0, keepdims=True)
        small_s[4:5, :] += jnp.sum(ga.astype(f32), axis=0, keepdims=True)
        hid_s[sl, wide(at_end)] = dot_nt(ga, outw_ref[...]).astype(bf16)

        def at(k, *todo):
            @pl.when(i == k)
            def _():
                for one in todo:
                    one()

        at(0, lambda: unit_d(end).from_core(), lambda: unit_d(0).from_outer())
        at(1, lambda: unit_u(end).from_core(), lambda: unit_d(before).from_inner())
        at(2, lambda: unit_u(0).from_outer())
        at(3, lambda: unit_d(end).from_twin())
        return 0

    lax.fori_loop(0, rows // RB, finish_rows, 0)
    take = [local(x, hid_s.at[:, wide(i * feat)], loc_sem.at[3 + i]) for i, x in enumerate((q_hbm, k_hbm, v_hbm))]
    sent(unit_u(before), "core")
    sent(unit_d(before), "core")
    unit_o.terms[...] = dot_tn(mixed_s[...], si_s[...]).astype(bf16).reshape(unit_o.terms.shape)
    unit_o.start()
    unit_u(end).from_twin()
    unit_u(before).from_inner()
    gub = join_columns([gub_s[j] for j in range(BLOCKS)], n)
    for i in range(gub.shape[1] // feat):
        small_s[8 + i:9 + i, :] = gub[0:1, i * feat:(i + 1) * feat]

    ends = image_ends(counts_ref[0], counts_ref[1], rows)

    def norm_rows(i, _):
        first = pl.multiple_of(i * RB, RB)
        sl = pl.ds(first, RB)
        own_s[sl, :] = mask_lanes((RB, 128), first, ends, 1.0, 0.0)
        far_s[sl, :] = mask_lanes((RB, 128), first, ends, 0.0, NEG)
        xhat, _q = norm_parts(tokens_ref[sl, :].astype(f32))
        gi_s[sl, wide(0)] = (xhat * gain_one + shift_one).astype(bf16)
        return 0

    lax.fori_loop(0, rows // RB, norm_rows, 0)
    for c in take:
        c.wait()
    key_at = lambda e: pl.ds(feat + e * 128, 128)
    dk_at, dv_at = pl.ds(0, 128), pl.ds(128, 128)

    def pair(p, _):
        part = lambda which: pl.ds(pl.multiple_of(which * feat + p * 128, 128), 128)
        cols = part(0)
        keys = hid_s[:, part(1)]
        for e in range(2):
            gi_s[:, key_at(e)] = head_lanes(keys, far_s[...], e)
        kt_s[...] = keys.T
        res_s[:, pl.ds(0, 256)] = jnp.zeros((rows, 256), f32)

        def attend_back(b, _):
            first = pl.multiple_of(b * QB, QB)
            sl = pl.ds(first, QB)
            q, do = hid_s[sl, part(0)], hid_s[sl, part(3)]
            v = hid_s[:, part(2)]
            lane = lax.broadcasted_iota(jnp.int32, q.shape, 1)
            zero = jnp.zeros_like(q)
            dqs = []
            dks = dvs = None
            for e in range(2):
                mask = (lane < 64) == (e == 0)
                qm, dom = jnp.where(mask, q, zero), jnp.where(mask, do, zero)
                s = dot_nt(gi_s[:, key_at(e)], head_lanes(q, own_s[sl, :], e))
                probs = jnp.exp(s - lse_ref[p, e:e + 1, sl])
                dp = dot_nt(v, dom)
                centre = jnp.sum(probs * dp, axis=0, keepdims=True)
                ds = (probs * (dp - centre)).astype(bf16)
                dv_e = dot(probs.astype(bf16), dom)
                dk_e = dot(ds, qm)
                dqs.append(dot(kt_s[e * 64:(e + 1) * 64, :], ds))
                dvs = dv_e if dvs is None else dvs + dv_e
                dks = dk_e if dks is None else dks + dk_e
            res_s[:, dk_at] += dks
            res_s[:, dv_at] += dvs
            gb_s[sl, cols] = (jnp.concatenate(dqs, axis=0).T * 0.125).astype(bf16)

            def at(k, when, todo):
                @pl.when((b == k) & when)
                def _():
                    todo()

            at(0, p == 0, lambda: last(unit_d(0)))
            at(1, p == 0, lambda: (unit_o.from_core(), last(unit_u(0))))
            at(2, p == 0, lambda: unit_d(before).from_outer())
            at(3, p == 0, lambda: (unit_u(before).from_outer(), unit_d(end).from_inner()))
            at(0, p == 1, lambda: unit_o.from_twin())
            at(1, p == 1, lambda: (last(unit_d(before)), unit_u(end).from_inner()))
            at(2, p == 1, lambda: last(unit_u(before)))
            at(3, p == 1, lambda: unit_o.from_inner())
            at(0, p == 2, lambda: unit_d(end).from_outer())
            at(2, p == 2, lambda: unit_u(end).from_outer())
            at(3, p == 2, lambda: (last(unit_d(end)), unit_o.from_outer()))
            at(0, p == 3, lambda: last(unit_u(end)))
            at(2, p == 3, lambda: last(unit_o))
            at(1, p >= 1, lambda: unit_a(p - 1).from_core())
            at(3, p >= 1, lambda: unit_a(p - 1).from_twin())
            at(1, p >= 2, lambda: unit_a(p - 2).from_inner())
            at(0, p >= 3, lambda: unit_a(p - 3).from_outer())
            at(2, p >= 3, lambda: last(unit_a(p - 3)))
            return 0

        lax.fori_loop(0, rows // QB, attend_back, 0)
        dk, dv = res_s[:, dk_at].astype(bf16), res_s[:, dv_at].astype(bf16)
        mixed_s[:, cols] = dk
        si_s[:, cols] = dv
        both = jnp.concatenate([gb_s[:, cols], dk, dv], axis=1)

        @pl.when(p >= 2)
        def _():
            sent(unit_a(p - 2), "core")

        term = pair_term(p)
        term[...] = dot_tn(gi_s[:, wide(0)], both).astype(bf16).reshape(term.shape)
        unit_a(p).start()
        return 0

    lax.fori_loop(0, heads, pair, 0)
    for c in weights:
        c.wait()

    def back_rows(i, _):
        sl = pl.ds(pl.multiple_of(i * RB, RB), RB)
        dq, dk, dv = gb_s[sl, :], mixed_s[sl, :], si_s[sl, :]
        weight = lambda i: up_s[i, :, :, :, :, wide(0)].reshape(feat, feat)
        gs = dot_nt(dq, weight(0)) + dot_nt(dk, weight(1)) + dot_nt(dv, weight(2))
        xhat, q = norm_parts(tokens_ref[sl, :].astype(f32))
        t = gs * gain_one
        gtok_ref[sl, :] += q * (t - jnp.mean(t, axis=-1, keepdims=True)
                                - xhat * jnp.mean(t * xhat, axis=-1, keepdims=True))
        for r, a in enumerate((gs * xhat, gs, dq.astype(f32), dv.astype(f32))):
            small_s[r:r + 1, :] += jnp.sum(a, axis=0, keepdims=True)

        def at(k, *todo):
            @pl.when(i == k)
            def _():
                for one in todo:
                    one()

        at(0, lambda: unit_a(heads - 3).from_outer(), lambda: unit_a(heads - 1).from_core())
        at(1, lambda: unit_a(heads - 2).from_inner(), lambda: unit_a(heads - 1).from_twin())
        at(2, lambda: last(unit_a(heads - 3)))
        at(3, lambda: unit_a(heads - 2).from_outer(), lambda: unit_a(heads - 1).from_inner())
        return 0

    lax.fori_loop(0, rows // RB, back_rows, 0)
    small.start(small_s[...])
    steps = small.steps()
    last(unit_a(heads - 2))
    gup_ref[...] = join_columns([gup_ref[:, j * width:(j + 1) * width] for j in range(BLOCKS)], n)

    def drain(j, _):
        sent(unit_u(j), *rest_stages)
        sent(unit_d(j), *rest_stages)
        return 0

    lax.fori_loop(0, BLOCKS, drain, 0)
    sent(unit_u(end), "core")
    sent(unit_d(end), "core")
    sent(unit_o, "core", *rest_stages)

    def drain_pairs(p, _):
        sent(unit_a(p), *rest_stages)
        return 0

    lax.fori_loop(0, heads - 1, drain_pairs, 0)

    def hand_pair(p):
        for i, ref in enumerate((gq_ref, gk_ref, gv_ref)):
            ref[:, p * 128:(p + 1) * 128] = gqkv_s[p, :, i * 128:(i + 1) * 128]

    for p in range(heads - 1):
        hand_pair(p)
    steps[0]()
    unit_a(heads - 1).from_outer()
    steps[1]()
    last(unit_a(heads - 1))
    for one in steps[2:]:
        one()
    hand_pair(heads - 1)
    sent(unit_a(heads - 2), "core")
    sent(unit_a(heads - 1), "core", *rest_stages)
    small.finish()


def layer_back(sizes, counts, mixed, tokens, cot, outw, vec, lse, up_all, down_all, q, k, v, qkv_all):
    dp_total, n = sizes
    rows, feat = tokens.shape
    B, pairs = n // 8, dp_total // 2
    own, width = up_all.shape[-2:]
    piece = down_all.shape[-2]
    heads = feat // 128
    s = jax.ShapeDtypeStruct
    vm = pl.BlockSpec(memory_space=pltpu.VMEM)
    anyspec = pl.BlockSpec(memory_space=pl.ANY)
    act = lambda dt, cols=feat: pltpu.VMEM((rows, cols), dt)
    copies = (2 * BLOCKS + 1 + heads) * Scatter.count(B, pairs) + Total.count(B, pairs)
    return pl.pallas_call(
        functools.partial(layer_kernel, dp_total, n),
        in_specs=[pl.BlockSpec(memory_space=pltpu.SMEM), anyspec, vm, anyspec, vm, vm, vm] + [anyspec] * 6,
        out_specs=[vm] * 9,
        out_shape=[s((rows, feat), bf16), s((rows, feat), f32), s((own, BLOCKS * width), f32),
                   s((BLOCKS * piece, feat), f32)] + [s((own, feat), f32)] * 4 + [s(vec.shape, f32)],
        scratch_shapes=[act(f32), act(bf16), act(bf16), act(bf16), act(bf16, BLOCKS * width), act(bf16, width),
                        pltpu.VMEM(up_all.shape, bf16), pltpu.VMEM(down_all.shape, bf16),
                        pltpu.VMEM((128, rows), bf16), act(bf16, 128), act(bf16, 128), pltpu.VMEM((BLOCKS, 8, width), f32),
                        pltpu.VMEM((BLOCKS, 8, width), f32), pltpu.VMEM((heads, own, 384), f32),
                        pltpu.VMEM(vec.shape, f32),
                        pltpu.VMEM((2,) + up_all.shape[1:], bf16), pltpu.VMEM((2,) + down_all.shape[1:], bf16)]
        + Scatter.shapes(B, pairs, own, width, scatter_edge(width), (BLOCKS,))
        + Scatter.shapes(B, pairs, piece, feat, scatter_edge(feat), (BLOCKS,))
        + Scatter.shapes(B, pairs, own, feat, 256)
        + Scatter.shapes(B, pairs, own, 384, 128, (heads,))
        + Total.shapes(B, pairs, vec.shape)
        + [pltpu.SemaphoreType.DMA((copies,)), pltpu.SemaphoreType.DMA((copies,)),
           pltpu.SemaphoreType.DMA((2 * BLOCKS + 2,))]
        + [pltpu.SemaphoreType.DMA((3 * PARTS,))],
        compiler_params=pltpu.CompilerParams(collective_id=2, has_side_effects=True, vmem_limit_bytes=67043328),
        name="layer_back",
    )(counts, mixed, tokens, cot, outw, vec, lse, up_all, down_all, q, k, v, qkv_all)

FSDP="fsdp"

def hand_kernel(*refs):
    half = len(refs) // 2
    for a, b in zip(refs[:half], refs[half:]):
        b[...] = a[...]


def hand_over(by_rows, by_cols, whole):
    steps = 2
    arrays = list(by_rows) + list(by_cols) + list(whole)
    specs = [pl.BlockSpec((a.shape[0] // steps, a.shape[1]), lambda i: (i, 0)) for a in by_rows]
    specs += [pl.BlockSpec((a.shape[0], a.shape[1] // steps), lambda i: (0, i)) for a in by_cols]
    specs += [pl.BlockSpec(a.shape, lambda i: (0, 0)) for a in whole]
    return pl.pallas_call(hand_kernel, grid=(steps,), in_specs=specs, out_specs=specs,
                          out_shape=[jax.ShapeDtypeStruct(a.shape, a.dtype) for a in arrays], name="hand_over")(*arrays)


def spread(vectors, index, total):
    own = vectors.shape[-1]
    at = lax.broadcasted_iota(jnp.int32, (1, total, own), 1)
    wide = jnp.where(at == index, vectors[:, None, :], jnp.zeros((), vectors.dtype))
    return wide.reshape(vectors.shape[0], total * own)

def on_device(sizes, tokens, image_counts, cotangent, first_gain, first_shift, query_weight, query_bias, key_weight,
              value_weight, value_bias, out_weight, out_bias, second_gain, second_shift, up_weight, up_bias,
              down_weight, down_bias):
    rows, feat = tokens.shape
    own = query_weight.shape[0]
    n = feat // own
    counts = image_counts[0]
    me = lax.axis_index(FSDP)
    eight = jnp.stack([first_gain, first_shift, query_bias, value_bias, out_bias, second_gain, second_shift, down_bias])
    small = jnp.concatenate([spread(eight, me, n), spread(up_bias[None], me, n).reshape(-1, feat)])
    small = jnp.concatenate([small, jnp.zeros((16 - small.shape[0], feat), bf16)])
    q, k, v, vec, mixed, lse, qkv_all, o_all, up_all, down_all, _ = gather_attend(
        sizes, counts, tokens, small, query_weight, key_weight, value_weight, out_weight, up_weight, down_weight)
    layer_out, gtok, gup, gdown, gq, gk, gv, go, total = layer_back(
        sizes, counts, mixed, tokens, cotangent, o_all.reshape(feat, feat), vec, lse, up_all, down_all, q, k, v, qkv_all)
    gtok, layer_out, gdown, gup, gq, gk, gv, go = hand_over((gtok, layer_out, gdown), (gup,), (gq, gk, gv, go))
    mine = lax.dynamic_index_in_dim(total[:8].reshape(8, n, own), me, 1, keepdims=False)
    ub_mine = lax.dynamic_index_in_dim(total[8:12].reshape(n, -1), me, 0, keepdims=False)
    return (layer_out, gtok, mine[0], mine[1], gq, mine[2], gk, gv, mine[3], go, mine[4], mine[5], mine[6],
            gup, ub_mine, gdown, mine[7])


def solution(mesh):
    rows = P(("dp", "fsdp"), None)
    mat = P("fsdp", None)
    vec = P("fsdp")
    return jax.shard_map(
        functools.partial(on_device, (mesh.shape["dp"], mesh.shape["fsdp"])),
        mesh=mesh,
        in_specs=(rows, rows, rows, vec, vec, mat, vec, mat, mat, vec, mat, vec, vec, vec, mat, vec, mat, vec),
        out_specs=(rows, rows, vec, vec, mat, vec, mat, mat, vec, mat, vec, vec, vec, mat, vec, mat, vec),
        check_vma=False,
    )
```
